32 devices in a mesh: dp: 8 (over z, x), tensor: 4 (over y, core).
Axes of the slice: x: 2, y: 2, z: 4, core: 2. Of those that a mesh axis runs over, the one named last changes fastest.
Arguments:
- inputs: float32 [32, 1024, 768], P(('dp', 'tensor')), may hold values from -6 to 6
- w_qkv: float32 [3, 768, 768], P(None, None, 'tensor'), may hold values from -0.21875 to 0.21875
- b_qv: float32 [2, 768], P(None, 'tensor'), may hold values from -3 to 3
- w_out: float32 [768, 768], P('tensor'), may hold values from -0.875 to 0.875
- w_in: float32 [768, 3072], P(None, 'tensor'), may hold values from -0.21875 to 0.21875
- b_in: float32 [3072], P('tensor'), may hold values from -3 to 3
- w_back: float32 [3072, 768], P('tensor'), may hold values from -0.109375 to 0.109375
- norm_gains: float32 [2, 768], replicated, may hold values from 0.5 to 1.5
- shifts: float32 [4, 768], replicated, may hold values from -2 to 2
- segment_ids: int32 [32, 1024], P('dp'), may hold values from 0 to 7, never falling along the last dimension, each value on 1 to 512 neighbouring positions
- valid_lengths: int32 [32], P('dp'), may hold values from 307 to 1024, as said below
- teacher: float32 [32, 1024, 768], P(('dp', 'tensor')), may hold values from -6 to 6
Outputs:
- output: float32 [32, 1024, 768], P(('dp', 'tensor'))
- loss: float32 [], replicated
- grad_inputs: float32 [32, 1024, 768], P(('dp', 'tensor'))
- grad_w_qkv: float32 [3, 768, 768], P(None, None, 'tensor')
- grad_b_qv: float32 [2, 768], P(None, 'tensor')
- grad_w_out: float32 [768, 768], P('tensor')
- grad_w_in: float32 [768, 3072], P(None, 'tensor')
- grad_b_in: float32 [3072], P('tensor')
- grad_w_back: float32 [3072, 768], P('tensor')
- grad_norm_gains: float32 [2, 768], replicated
- grad_shifts: float32 [4, 768], replicated
The draws below stay inside these ranges and needn't reach their ends.
Inputs may be any that keep to these rules, and one draw needn't show every extreme that they name: `valid_lengths`: each sequence's slots at and after its valid length are padding; some sequence has all 1024 slots in use. `segment_ids`: along a sequence the document number never falls; a document holds 1 to 512 slots, one exactly that many.
All inputs are finite; a program needn't handle non-finite values.
Results may differ from the reference program's by a relative error of at most 0.0095.
The reference program's roundings to bfloat16 on the way count: a program that leaves them out, or rounds other values in their place, can miss the bound.
Values may be sent and summed in bfloat16 or wider, within the bound.
A program may use at most 320 MiB of HBM per device.

```python
import math
import jax
import jax.numpy as jnp
import numpy as np
from jax import lax

D = 768
H = 12
HD = 64
FF = 3072
LEN = 1024
SEQS = 32
TOKENS = 32768


def draw_valid_lengths(key, part):
    index = jnp.arange(SEQS, dtype=jnp.int32)
    base_len = LEN * (3 * (SEQS - 1) + 7 * index) // (10 * (SEQS - 1))
    jitter = jax.random.randint(key, (SEQS,), 0, LEN // 8 + 1, dtype=jnp.int32)
    jitter = jnp.where(index > 0, jitter, 0)
    lengths = jnp.minimum(base_len + jitter, LEN)
    return lengths.at[SEQS - 1].set(LEN).astype(jnp.int32)


def block_scale(key, dims, cuts, smallest, high):
    level, own = 1.0, jax.random.fold_in(key, 6)
    for dim, shards_of in cuts:
        heights = jnp.exp(jax.random.uniform(jax.random.fold_in(own, dim), (shards_of,), jnp.float32, smallest / len(cuts), high / len(cuts)))
        level = level * jnp.repeat(heights, dims[dim] // shards_of).reshape([-1 if axis == dim else 1 for axis in range(len(dims))])
    return level


def length_profile(amount, total, reach, skew):
    portions = [(1 << 20) // math.isqrt(standing ** skew) + 1 for standing in range(2, amount + 1)]
    surplus, counts = total - reach - (amount - 1), [1] * (amount - 1)
    while surplus > 0:
        movable = [i for i in range(amount - 1) if counts[i] < reach]
        pool, left = sum([portions[i] for i in movable]), surplus
        for i in movable:
            addition = min(reach - counts[i], max(1, left * portions[i] // pool), surplus)
            counts[i] = counts[i] + addition
            surplus = surplus - addition
    return np.array([reach] + counts)


def uneven_parts(key, count, total, bound, lean):
    if count == 2:
        one = jax.random.randint(key, (), max(1, total - bound), min(bound, total - 1) + 1)
        return jnp.stack([one, total - one])
    tallies = jnp.asarray(length_profile(count, total, bound, lean), jnp.int32)
    couples = (count - 1) // 2
    source_of, taker = tallies[1:1 + 2 * couples:2], tallies[2:2 + 2 * couples:2]
    slack = jnp.minimum(source_of - 1, bound - taker)
    shifted = jax.random.randint(jax.random.fold_in(key, 1), (couples,), 0, 1 << 20) % (slack + 1)
    tallies = tallies.at[1:1 + 2 * couples:2].set(source_of - shifted).at[2:2 + 2 * couples:2].set(taker + shifted)
    return tallies[jax.random.permutation(jax.random.fold_in(key, 2), count)]


def bell_draw(rng, shape, deviation, bound, shards=(), held_as=jnp.bfloat16):
    values = jax.random.normal(rng, shape, jnp.float32) * deviation
    if len(shards) > 0:
        values = block_scale(rng, shape, shards, -0.22, 0.18) * values
    return jnp.clip(values, min=-bound, max=bound).astype(held_as)


def setup_inputs(seed: int = 0) -> dict:
    seeds = jax.random.split(jax.random.key(seed), 13)
    return {
        "inputs": bell_draw(seeds[0], (SEQS, LEN, D), 1.0, 6.0, ((0, 32),), jnp.float32),
        "w_qkv": bell_draw(seeds[1], (3, D, D), D ** -0.5, 0.21875, ((2, 4),), jnp.float32),
        "b_qv": bell_draw(seeds[2], (2, D), 0.5, 3.0, ((1, 4),), jnp.float32),
        "w_out": bell_draw(seeds[3], (D, D), (D // 16) ** -0.5, 0.875, ((0, 4),), jnp.float32),
        "w_in": bell_draw(seeds[4], (D, FF), D ** -0.5, 0.21875, ((1, 4),), jnp.float32),
        "b_in": bell_draw(seeds[5], (FF,), 0.5, 3.0, ((0, 4),), jnp.float32),
        "w_back": bell_draw(seeds[6], (FF, D), FF ** -0.5, 0.109375, ((0, 4),), jnp.float32),
        "norm_gains": jnp.clip(1.0 + 0.1 * jax.random.normal(seeds[7], (2, D), jnp.float32), 0.5, 1.5),
        "shifts": bell_draw(seeds[8], (4, D), 0.3, 2.0, (), jnp.float32),
        "segment_ids": jax.vmap(lambda own: jnp.searchsorted(jnp.cumsum(uneven_parts(own, 8, LEN, LEN // 2, 2)), jnp.arange(LEN), side="right"))(jax.random.split(seeds[9], SEQS)).reshape((SEQS, LEN)).astype(jnp.int32),
        "valid_lengths": draw_valid_lengths(jax.random.fold_in(seeds[12], 71), 0),
        "teacher": bell_draw(seeds[11], (SEQS, LEN, D), 1.0, 6.0, ((0, 32),), jnp.float32),
    }


@jax.custom_vjp
def low(v):
    return lax.optimization_barrier(v.astype(jnp.bfloat16)).astype(jnp.float32)

@jax.custom_vjp
def low_back(v):
    return v

def low_keep(v):
    return (low(v), None)

def low_pass(kept, grad):
    return (grad,)

def back_keep(v):
    return (v, None)

def back_low(kept, grad):
    return (low(grad),)
low.defvjp(low_keep, low_pass)
low_back.defvjp(back_keep, back_low)
LN_EPSILON = 1e-05
MASKED_SCORE = -1000000000.0
HIGHEST = lax.Precision.HIGHEST

def matmul_high(left, right):
    return jnp.dot(left, right, precision=HIGHEST, preferred_element_type=jnp.float32)

def layer_norm(values, gain, shift):
    centred = values - lax.optimization_barrier(jnp.mean(values, axis=-1, keepdims=True))
    spread = lax.optimization_barrier(jnp.mean(centred * centred, axis=-1, keepdims=True))
    return centred * lax.rsqrt(spread + LN_EPSILON) * gain + shift

def exact_gelu(values):
    return jax.nn.gelu(values, approximate=False)

def attend(queries, keys_all, values, segments, valid_len):
    positions = jnp.arange(LEN, dtype=jnp.int32)
    same_doc = segments[:, None] == segments[None, :]
    allowed = same_doc & (positions[None, :] < valid_len) | (positions[:, None] == positions[None, :])
    scores = jnp.einsum('qhd,khd->hqk', queries, keys_all, precision=HIGHEST) * (1.0 / math.sqrt(HD))
    scores = low_back(scores)
    scores = jnp.where(allowed[None], scores, MASKED_SCORE)
    row_max = lax.optimization_barrier(jnp.max(scores, axis=-1, keepdims=True))
    exp_scores = jnp.exp(scores - row_max)
    probs = low(exp_scores / lax.optimization_barrier(jnp.sum(exp_scores, axis=-1, keepdims=True)))
    return jnp.einsum('hqk,khd->qhd', probs, values, precision=HIGHEST)

def attend_one(operands):
    return jax.checkpoint(attend)(*operands)

def forward(inputs, w_qkv, b_qv, w_out, w_in, b_in, w_back, norm_gains, shifts, segment_ids, valid_lengths, teacher):
    x_rows = inputs.reshape(TOKENS, D)
    x_low = low(x_rows)
    query = low(low_back(matmul_high(x_low, low(w_qkv[0])) + b_qv[0]))
    keys_proj = low(low_back(matmul_high(x_low, low(w_qkv[1]))))
    value = low(low_back(matmul_high(x_low, low(w_qkv[2])) + b_qv[1]))
    head_shape = (SEQS, LEN, H, HD)
    context = lax.map(attend_one, (query.reshape(head_shape), keys_proj.reshape(head_shape), value.reshape(head_shape), segment_ids, valid_lengths))
    context = low(low_back(context.reshape(TOKENS, D)))
    attn_rows = low_back(matmul_high(context, low(w_out))) + shifts[0]
    mid_state = layer_norm(attn_rows + x_rows, norm_gains[0], shifts[1])
    mid_low = low(mid_state)
    pre_act = low_back(matmul_high(mid_low, low(w_in)) + b_in)
    hidden = low(exact_gelu(pre_act))
    ffn_rows = low_back(matmul_high(hidden, low(w_back))) + shifts[2]
    output = layer_norm(ffn_rows + mid_state, norm_gains[1], shifts[3])
    live_mask = (jnp.arange(LEN, dtype=jnp.int32)[None, :] < valid_lengths[:, None]).reshape(TOKENS).astype(jnp.float32)
    token_count = jnp.sum(valid_lengths).astype(jnp.float32)
    distance = output - teacher.reshape(TOKENS, D)
    squared_sum = jnp.sum(live_mask * lax.optimization_barrier(jnp.sum(distance * distance, axis=-1)))
    loss = squared_sum / (2.0 * D * token_count)
    objective = TOKENS * D * loss
    return (objective, (output.reshape(SEQS, LEN, D), loss))

def reference(inputs, w_qkv, b_qv, w_out, w_in, b_in, w_back, norm_gains, shifts, segment_ids, valid_lengths, teacher):

    def objective_of(inputs, w_qkv, b_qv, w_out, w_in, b_in, w_back, norm_gains, shifts):
        return forward(inputs, w_qkv, b_qv, w_out, w_in, b_in, w_back, norm_gains, shifts, segment_ids, valid_lengths, teacher)
    objective, pull_back, extras = jax.vjp(objective_of, inputs, w_qkv, b_qv, w_out, w_in, b_in, w_back, norm_gains, shifts, has_aux=True)
    grads = pull_back(jnp.ones_like(objective))
    output, loss = extras
    return (output, loss, grads[0], grads[1], grads[2], grads[3], grads[4], grads[5], grads[6], grads[7], grads[8])
```

```python
import functools
import math

import jax
import jax.numpy as jnp
from jax import lax
from jax.experimental import pallas as pl
from jax.experimental.pallas import tpu as pltpu
from jax.sharding import PartitionSpec as P

HD = 64
LN_EPSILON = 1e-05
MASKED_SCORE = -1000000000.0
QB = 256
KB = 128
NT = ((1,), (1,))


def layer_norm(values, gain, shift):
    centred = values - jnp.mean(values, axis=-1, keepdims=True)
    spread = jnp.mean(centred * centred, axis=-1, keepdims=True)
    return centred * lax.rsqrt(spread + LN_EPSILON) * gain + shift


def exact_gelu(values):
    return jax.nn.gelu(values, approximate=False)


def matmul_f32(left, right):
    return jnp.dot(left, right, preferred_element_type=jnp.float32)


def left_cross(left, right):
    return jnp.einsum("nd,ne->de", left, right, preferred_element_type=jnp.float32)


def right_cross(left, right):
    return jnp.einsum("ne,de->nd", left, right, preferred_element_type=jnp.float32)


def dot(left, right, dims=((1,), (0,))):
    return lax.dot_general(left, right, (dims, ((), ())), preferred_element_type=jnp.float32)


def span_tables(segments, valid, seq):
    blocks = seq // QB
    firsts, lasts = segments[::QB], segments[QB - 1 :: QB]
    low = jnp.sum((segments[None, :] < firsts[:, None]).astype(jnp.int32), axis=1)
    high = jnp.sum((segments[None, :] <= lasts[:, None]).astype(jnp.int32), axis=1)
    own_end = (jnp.arange(blocks, dtype=jnp.int32) + 1) * QB
    high = jnp.maximum(jnp.minimum(high, valid), own_end)
    low_block = low // KB
    high_block = (high + KB - 1) // KB
    return jnp.stack([low_block, high_block - low_block]).astype(jnp.int32)


def make_bias(bias_ref, block, low, count, code_ref, seg_ref):
    shape = (count * KB, QB)
    codes = code_ref[pl.ds(low * KB, count * KB), :]
    segs = seg_ref[:, pl.ds(block * QB, QB)]
    key_at = low * KB + lax.broadcasted_iota(jnp.int32, shape, 0)
    query_at = block * QB + lax.broadcasted_iota(jnp.int32, shape, 1)
    allowed = (codes == segs) | (key_at == query_at)
    bias_ref[block, : count * KB, :] = jnp.where(allowed, 0.0, MASKED_SCORE)


def one_head(values, head):
    lane = lax.broadcasted_iota(jnp.int32, values.shape, 1)
    keep = (lane < HD) if head == 0 else (lane >= HD)
    return jnp.where(keep, values, jnp.zeros_like(values))


def forward_kernel(
    table_ref, q_ref, k_ref, v_ref, code_ref, seg_ref, ctx_ref, lse_ref, vt_ref, bias_ref
):
    pair, block = pl.program_id(0), pl.program_id(1)
    low, total = table_ref[0, block], table_ref[1, block]

    @pl.when(block == 0)
    def _():
        vt_ref[...] = v_ref[...].T

    def run(count):
        @pl.when(pair == 0)
        def _():
            make_bias(bias_ref, block, low, count, code_ref, seg_ref)

        bias = bias_ref[block, : count * KB, :]
        rows = pl.ds(pl.multiple_of(low * KB, KB), count * KB)
        keys = k_ref[rows, :]
        queries = q_ref[...] * jnp.asarray(0.125, q_ref.dtype)
        outs, sums = [], []
        for head in range(2):
            scores = dot(keys, one_head(queries, head), NT) + bias
            peak = jnp.max(scores, axis=0, keepdims=True)
            powers = jnp.exp(scores - peak)
            mass = jnp.sum(powers, axis=0, keepdims=True)
            probs = (powers * (1.0 / mass)).astype(jnp.bfloat16)
            outs.append(dot(vt_ref[head * HD : (head + 1) * HD, rows], probs))
            sums.append(peak + jnp.log(mass))
        ctx_ref[...] = jnp.concatenate(outs, axis=0).T.astype(ctx_ref.dtype)
        lse_ref[0, 0:1, :] = sums[0]
        lse_ref[0, 1:2, :] = sums[1]

    for count in range(2, k_ref.shape[0] // KB + 1):
        pl.when(total == count)(functools.partial(run, count))


def backward_kernel(
    table_ref,
    q_ref,
    k_ref,
    v_ref,
    g_ref,
    lse_ref,
    code_ref,
    seg_ref,
    dq_ref,
    dk_ref,
    dv_ref,
    kt_ref,
    bias_ref,
    dk_sum,
    dv_sum,
):
    pair, block = pl.program_id(0), pl.program_id(1)
    low, total = table_ref[0, block], table_ref[1, block]

    @pl.when(block == 0)
    def _():
        kt_ref[...] = k_ref[...].T
        dk_sum[...] = jnp.zeros_like(dk_sum)
        dv_sum[...] = jnp.zeros_like(dv_sum)

    def run(count):
        @pl.when(pair == 0)
        def _():
            make_bias(bias_ref, block, low, count, code_ref, seg_ref)

        bias = bias_ref[block, : count * KB, :]
        rows = pl.ds(pl.multiple_of(low * KB, KB), count * KB)
        keys, values = k_ref[rows, :], v_ref[rows, :]
        queries = q_ref[...] * jnp.asarray(0.125, q_ref.dtype)
        grads = g_ref[...]
        outs = []
        for head in range(2):
            query, grad = one_head(queries, head), one_head(grads, head)
            probs = jnp.exp(dot(keys, query, NT) + bias - lse_ref[0, head : head + 1, :])
            dv_sum[rows, :] += dot(probs.astype(jnp.bfloat16), grad)
            prob_grad = dot(values, grad, NT)
            delta = jnp.sum(probs * prob_grad, axis=0, keepdims=True)
            score_grad = (probs * (prob_grad - delta)).astype(jnp.bfloat16)
            dk_sum[rows, :] += dot(score_grad, query)
            outs.append(dot(kt_ref[head * HD : (head + 1) * HD, rows], score_grad))
        dq_ref[...] = (jnp.concatenate(outs, axis=0).T * 0.125).astype(dq_ref.dtype)

    for count in range(2, k_ref.shape[0] // KB + 1):
        pl.when(total == count)(functools.partial(run, count))

    @pl.when(block == pl.num_programs(1) - 1)
    def _():
        dk_ref[...] = dk_sum[...].astype(dk_ref.dtype)
        dv_ref[...] = dv_sum[...].astype(dv_ref.dtype)


def attend_forward(table, qkv, code, seg):
    seq, width = qkv.shape[0], qkv.shape[1] // 3
    pairs, blocks = width // 128, seq // QB
    return pl.pallas_call(
        forward_kernel,
        out_shape=(
            jax.ShapeDtypeStruct((seq, width), jnp.bfloat16),
            jax.ShapeDtypeStruct((pairs, 8, seq), jnp.float32),
        ),
        grid_spec=pltpu.PrefetchScalarGridSpec(
            num_scalar_prefetch=1,
            grid=(pairs, blocks),
            in_specs=[
                pl.BlockSpec((QB, 128), lambda p, i, t: (i, p)),
                pl.BlockSpec((seq, 128), lambda p, i, t: (0, pairs + p)),
                pl.BlockSpec((seq, 128), lambda p, i, t: (0, 2 * pairs + p)),
                pl.BlockSpec((seq, 1), lambda p, i, t: (0, 0)),
                pl.BlockSpec((1, seq), lambda p, i, t: (0, 0)),
            ],
            out_specs=[
                pl.BlockSpec((QB, 128), lambda p, i, t: (i, p)),
                pl.BlockSpec((1, 8, QB), lambda p, i, t: (p, 0, i)),
            ],
            scratch_shapes=[
                pltpu.VMEM((128, seq), jnp.bfloat16),
                pltpu.VMEM((blocks, seq, QB), jnp.float32),
            ],
        ),
        compiler_params=pltpu.CompilerParams(vmem_limit_bytes=32 << 20),
        cost_estimate=pl.CostEstimate(
            flops=8 * seq * seq * width, bytes_accessed=8 * seq * width, transcendentals=seq * seq * pairs
        ),
        name="attend_forward",
    )(table, qkv, qkv, qkv, code, seg)


def attend_backward(table, qkv, grad, lse, code, seg):
    seq, width = grad.shape
    pairs, blocks = width // 128, seq // QB
    block = pl.BlockSpec((QB, 128), lambda p, i, t: (i, p))
    return pl.pallas_call(
        backward_kernel,
        out_shape=(jax.ShapeDtypeStruct((seq, width), jnp.bfloat16),) * 3,
        grid_spec=pltpu.PrefetchScalarGridSpec(
            num_scalar_prefetch=1,
            grid=(pairs, blocks),
            in_specs=[
                block,
                pl.BlockSpec((seq, 128), lambda p, i, t: (0, pairs + p)),
                pl.BlockSpec((seq, 128), lambda p, i, t: (0, 2 * pairs + p)),
                block,
                pl.BlockSpec((1, 8, QB), lambda p, i, t: (p, 0, i)),
                pl.BlockSpec((seq, 1), lambda p, i, t: (0, 0)),
                pl.BlockSpec((1, seq), lambda p, i, t: (0, 0)),
            ],
            out_specs=[
                block,
                pl.BlockSpec((seq, 128), lambda p, i, t: (0, p)),
                pl.BlockSpec((seq, 128), lambda p, i, t: (0, p)),
            ],
            scratch_shapes=[
                pltpu.VMEM((128, seq), jnp.bfloat16),
                pltpu.VMEM((blocks, seq, QB), jnp.float32),
                pltpu.VMEM((seq, 128), jnp.float32),
                pltpu.VMEM((seq, 128), jnp.float32),
            ],
        ),
        compiler_params=pltpu.CompilerParams(vmem_limit_bytes=32 << 20),
        cost_estimate=pl.CostEstimate(
            flops=16 * seq * seq * width, bytes_accessed=16 * seq * width, transcendentals=seq * seq * pairs
        ),
        name="attend_backward",
    )(table, qkv, qkv, qkv, grad, lse, code, seg)


def swap(values, axis, bit):
    size = lax.axis_size(axis)
    return lax.ppermute(values, axis, [(i, i ^ (1 << bit)) for i in range(size)])


def bits_of(axis):
    return int(math.log2(lax.axis_size(axis)))


def pick(values, bit_set, axis=0):
    half = values.shape[axis] // 2
    keep = lax.dynamic_slice_in_dim(values, bit_set * half, half, axis)
    send = lax.dynamic_slice_in_dim(values, (1 - bit_set) * half, half, axis)
    return keep, send


def join(mine, other, bit_set, axis=0):
    low = jnp.where(bit_set == 0, mine, other)
    high = jnp.where(bit_set == 0, other, mine)
    return jnp.concatenate([low, high], axis=axis)


def reduce_rows(pieces):
    low = jnp.bfloat16
    from_core = swap(jnp.stack([pieces[1], pieces[3]]).astype(low), "tensor", 0)
    away = (pieces[2] + from_core[1].astype(jnp.float32)).astype(low)
    from_y = swap(away, "tensor", 1)
    total = pieces[0] + from_core[0].astype(jnp.float32) + from_y.astype(jnp.float32)
    place = lax.axis_index("dp")
    count = bits_of("dp")
    sides = [(place >> bit) & 1 for bit in range(count)]
    for bit in range(count):
        keep, send = pick(total, sides[bit])
        total = keep + swap(send.astype(low), "dp", bit).astype(jnp.float32)
    total = total.astype(low)
    for bit in reversed(range(count)):
        total = join(total, swap(total, "dp", bit), sides[bit])
    return total.astype(jnp.float32)


def reduce_all(values):
    for bit in range(bits_of("tensor")):
        values = values + swap(values, "tensor", bit)
    for bit in range(bits_of("dp")):
        values = values + swap(values, "dp", bit)
    return values


def gather(own):
    far = swap(own, "tensor", 1)
    return [own, swap(own, "tensor", 0), far, swap(far, "tensor", 0)]


def per_device(
    inputs,
    w_qkv,
    b_qv,
    w_out,
    w_in,
    b_in,
    w_back,
    norm_gains,
    shifts,
    segment_ids,
    valid_lengths,
    teacher,
):
    own_seqs, seq_len, width = inputs.shape
    assert own_seqs == 1 and lax.axis_size("tensor") == 4
    total_slots = seq_len * lax.axis_size("tensor") * lax.axis_size("dp")
    low = jnp.bfloat16
    index = lax.axis_index("tensor")
    x_rows = inputs.reshape(seq_len, width)
    valid = lax.dynamic_index_in_dim(valid_lengths, index, keepdims=False)
    segments = lax.dynamic_index_in_dim(segment_ids, index, keepdims=False)
    positions = jnp.arange(seq_len, dtype=jnp.int32)
    live = positions < valid
    live_mask = live.astype(jnp.float32)
    code = jnp.where(live, segments, -1)[:, None]
    seg = segments[None, :]
    table = span_tables(segments, valid, seq_len)
    token_count = jnp.sum(valid_lengths)
    for bit in range(bits_of("dp")):
        token_count = token_count + swap(token_count, "dp", bit)
    token_count = token_count.astype(jnp.float32)

    qkv_parts = gather(w_qkv.astype(low))
    bias_parts = gather(jnp.concatenate([b_qv.reshape(-1), b_in]))
    out_parts = gather(w_out.astype(low))
    in_parts = gather(w_in.astype(low))
    back_parts = gather(w_back.astype(low))
    piece = w_qkv.shape[2]
    bias_in = jnp.concatenate([part[2 * piece :] for part in bias_parts])
    out_low = jnp.concatenate(out_parts, axis=0)
    in_low = jnp.concatenate(in_parts, axis=1)
    back_low = jnp.concatenate(back_parts, axis=0)

    x_low = x_rows.astype(low)
    groups = []
    for parts, biases in ((qkv_parts[:2], bias_parts[:2]), (qkv_parts[2:], bias_parts[2:])):
        weights = jnp.concatenate([part[i] for i in range(3) for part in parts], axis=1)
        bias = jnp.concatenate(
            [part[:piece] for part in biases]
            + [jnp.zeros((2 * piece,), jnp.float32)]
            + [part[piece : 2 * piece] for part in biases]
        )
        qkv = (matmul_f32(x_low, weights) + bias).astype(low)
        context, lse = attend_forward(table, qkv, code, seg)
        groups.append((weights, qkv, context, lse))
    context_low = jnp.concatenate([group[2] for group in groups], axis=1)

    attn_rows = matmul_f32(context_low, out_low)
    mid_state, norm_one_back = jax.vjp(
        layer_norm, attn_rows + shifts[0] + x_rows, norm_gains[0], shifts[1]
    )
    mid_low = mid_state.astype(low)
    hidden, gelu_back = jax.vjp(exact_gelu, matmul_f32(mid_low, in_low) + bias_in)
    hidden_low = hidden.astype(low)
    ffn_rows = matmul_f32(hidden_low, back_low)
    output, norm_two_back = jax.vjp(
        layer_norm, ffn_rows + shifts[2] + mid_state, norm_gains[1], shifts[3]
    )
    distance = output - teacher.reshape(seq_len, width)
    squared_sum = jnp.sum(live_mask * jnp.sum(distance * distance, axis=-1))
    out_grad = total_slots / token_count * live_mask[:, None] * distance
    dh_two, gain_two, shift_two = norm_two_back(out_grad)
    dh_two_low = dh_two.astype(low)
    hidden_grad = right_cross(dh_two_low, back_low)
    grad_w_back = left_cross(hidden_low, dh_two_low)
    (pre_grad,) = gelu_back(hidden_grad)
    pre_grad_low = pre_grad.astype(low)
    grad_b_in = jnp.sum(pre_grad_low.astype(jnp.float32), axis=0)
    grad_w_in = left_cross(mid_low, pre_grad_low)
    units = w_in.shape[1]
    grad_w_back = reduce_rows([grad_w_back[i * units : (i + 1) * units] for i in range(4)])
    grad_w_in = reduce_rows([grad_w_in[:, i * units : (i + 1) * units] for i in range(4)])

    mid_grad = right_cross(pre_grad_low, in_low) + dh_two
    dh_one, gain_one, shift_one = norm_one_back(mid_grad)
    dh_one_low = dh_one.astype(low)
    context_grad = right_cross(dh_one_low, out_low).astype(low)
    grad_w_out = left_cross(context_low, dh_one_low)
    grad_w_out = reduce_rows([grad_w_out[i * piece : (i + 1) * piece] for i in range(4)])

    pieces = [None] * 4
    bias_pieces = [None] * 4
    grad_inputs = dh_one
    for at in (1, 0):
        weights, qkv, context, lse = groups[at]
        half = 2 * piece
        grads = attend_backward(
            table, qkv, context_grad[:, at * half : (at + 1) * half], lse, code, seg
        )
        crosses = [left_cross(x_low, grad) for grad in grads]
        sums = [jnp.sum(grads[i].astype(jnp.float32), axis=0) for i in (0, 2)]
        for side in range(2):
            cols = slice(side * piece, (side + 1) * piece)
            pieces[2 * at + side] = jnp.concatenate([c[:, cols] for c in crosses], axis=1)
            bias_pieces[2 * at + side] = jnp.concatenate([s[cols] for s in sums])
        grad_inputs = grad_inputs + right_cross(jnp.concatenate(grads, axis=1), weights)
    grad_w_qkv = reduce_rows(pieces)
    grad_w_qkv = grad_w_qkv.reshape(width, 3, piece).transpose(1, 0, 2)

    bias_grads = jnp.stack(
        [
            jnp.concatenate([bias_pieces[i], grad_b_in[i * units : (i + 1) * units]])
            for i in range(4)
        ]
    )
    wide = bias_grads.shape[1]
    bias_grads = jnp.stack([bias_grads[0], bias_grads[1], bias_grads[2], bias_grads[3]])
    natural = lax.dynamic_index_in_dim(
        jnp.stack([jnp.stack([bias_grads[i ^ j] for i in range(4)]) for j in range(4)]),
        index,
        keepdims=False,
    )
    small = jnp.concatenate(
        [
            natural.reshape(-1),
            gain_one,
            gain_two,
            jnp.sum(dh_one, axis=0),
            shift_one,
            jnp.sum(dh_two, axis=0),
            shift_two,
            squared_sum[None],
        ]
    )
    small = reduce_all(small)
    own = lax.dynamic_slice_in_dim(small, index * wide, wide)
    rest = small[4 * wide :]
    grad_gains = rest[: 2 * width].reshape(2, width)
    grad_shifts = rest[2 * width : 6 * width].reshape(4, width)
    loss = rest[6 * width] / (2.0 * width * token_count)
    return (
        output.reshape(own_seqs, seq_len, width),
        loss,
        grad_inputs.reshape(own_seqs, seq_len, width),
        grad_w_qkv,
        own[: 2 * piece].reshape(2, piece),
        grad_w_out,
        grad_w_in,
        own[2 * piece :],
        grad_w_back,
        grad_gains,
        grad_shifts,
    )


def solution(mesh):
    return jax.shard_map(
        per_device,
        mesh=mesh,
        in_specs=(
            P(("dp", "tensor"), None, None),
            P(None, None, "tensor"),
            P(None, "tensor"),
            P("tensor", None),
            P(None, "tensor"),
            P("tensor"),
            P("tensor", None),
            P(),
            P(),
            P("dp", None),
            P("dp"),
            P(("dp", "tensor"), None, None),
        ),
        out_specs=(
            P(("dp", "tensor"), None, None),
            P(),
            P(("dp", "tensor"), None, None),
            P(None, None, "tensor"),
            P(None, "tensor"),
            P("tensor", None),
            P(None, "tensor"),
            P("tensor"),
            P("tensor", None),
            P(),
            P(),
        ),
        check_vma=False,
    )
```

```python
import functools
import math

import jax
import jax.numpy as jnp
from jax import lax
from jax.experimental import pallas as pl
from jax.experimental.pallas import tpu as pltpu
from jax.sharding import PartitionSpec as P

HD = 64
LN_EPSILON = 1e-05
MASKED_SCORE = -1000000000.0
QB = 256
KB = 128
RB = 256
FR = 256
NT = ((1,), (1,))
TN = ((0,), (0,))
PHI = (
    0.09255110872,
    0.09001568156,
    0.1049848251,
    0.006341010132,
    0.2381524984,
    -0.2150534404,
    0.2551771707,
    -0.07216888208,
)
PHI_STEP = 0.23164188826636045

VMEM = pl.BlockSpec(memory_space=pltpu.VMEM)
SMEM = pl.BlockSpec(memory_space=pltpu.SMEM)
HBM = pl.BlockSpec(memory_space=pl.ANY)
LOW = jnp.bfloat16
F32 = jnp.float32


def dot(left, right, dims=((1,), (0,))):
    return lax.dot_general(left, right, (dims, ((), ())), preferred_element_type=jnp.float32)


def shape(dims, dtype):
    return jax.ShapeDtypeStruct(dims, dtype)


def three_parts(values):
    first = values.astype(LOW)
    rest = values - first.astype(F32)
    second = rest.astype(LOW)
    return first, second, (rest - second.astype(F32)).astype(LOW)


def round_qkv_kernel(side_ref, w_ref, bqv_ref, bin_ref, out_ref):
    piece = w_ref.shape[2]
    width = w_ref.shape[1]
    half = bin_ref.shape[1] // 2
    for i in range(3):
        out_ref[i * piece : (i + 1) * piece, :] = w_ref[i].T.astype(LOW)
    mine = bin_ref[:, pl.ds(pl.multiple_of(side_ref[0] * half, half), half)]
    other = bin_ref[:, pl.ds(pl.multiple_of((1 - side_ref[0]) * half, half), half)]
    pad = jnp.zeros((1, width - piece), F32)
    rows = [jnp.concatenate([mine, other], axis=1)]
    rows += [jnp.concatenate([bqv_ref[i : i + 1, :], pad], axis=1) for i in range(2)]
    parts = [part.astype(F32) for row in rows for part in three_parts(row)]
    parts += [jnp.zeros((1, width), F32)] * 7
    out_ref[3 * piece :, :] = jnp.concatenate(parts, axis=0).astype(LOW)


def round_qkv(side, w_qkv, b_qv, b_in):
    _, width, piece = w_qkv.shape
    return pl.pallas_call(
        round_qkv_kernel,
        out_shape=shape((3 * piece + 16, width), LOW),
        in_specs=[SMEM, VMEM, VMEM, VMEM],
        out_specs=VMEM,
        name="round_qkv",
    )(side, w_qkv, b_qv, b_in)


def round_rest_kernel(side_ref, wo_ref, wi_ref, wb_ref, x_ref, first_ref, second_ref, x_low_ref):
    rows, width = wo_ref.shape
    half = width // 2
    for c in range(2):
        first_ref[c * rows : (c + 1) * rows, :] = wo_ref[:, c * half : (c + 1) * half].astype(LOW)
    for out, base, side in ((first_ref, 2 * rows, side_ref[0]), (second_ref, 0, 1 - side_ref[0])):
        at = pl.ds(pl.multiple_of(side * half, half), half)
        out[base : base + width, :] = wi_ref[:, at].astype(LOW)
        for c in range(2):
            start = base + width + c * half
            out[start : start + half, :] = wb_ref[at, c * half : (c + 1) * half].astype(LOW)
    x_low_ref[...] = x_ref[...].astype(LOW)


def round_rest(side, w_out, w_in, w_back, x):
    rows, width = w_out.shape
    half = width // 2
    return pl.pallas_call(
        round_rest_kernel,
        out_shape=(
            shape((2 * rows + 2 * width, half), LOW),
            shape((2 * width, half), LOW),
            shape(x.shape, LOW),
        ),
        in_specs=[SMEM, VMEM, VMEM, VMEM, VMEM],
        out_specs=(VMEM, VMEM, VMEM),
        compiler_params=pltpu.CompilerParams(vmem_limit_bytes=40 << 20),
        name="round_rest",
    )(side, w_out, w_in, w_back, x)


def span_tables(segments, valid, seq):
    blocks = seq // QB
    firsts, lasts = segments[::QB], segments[QB - 1 :: QB]
    low = jnp.sum((segments[None, :] < firsts[:, None]).astype(jnp.int32), axis=1)
    high = jnp.sum((segments[None, :] <= lasts[:, None]).astype(jnp.int32), axis=1)
    own_end = (jnp.arange(blocks, dtype=jnp.int32) + 1) * QB
    high = jnp.maximum(jnp.minimum(high, valid), own_end)
    low_block = low // KB
    high_block = (high + KB - 1) // KB
    return jnp.stack([low_block, high_block - low_block]).astype(jnp.int32)


def make_bias(bias_ref, block, low, count, code_ref, seg_ref):
    dims = (count * KB, QB)
    codes = code_ref[pl.ds(pl.multiple_of(low * KB, KB), count * KB), :]
    segs = seg_ref[:, pl.ds(pl.multiple_of(block * QB, QB), QB)]
    key_at = low * KB + lax.broadcasted_iota(jnp.int32, dims, 0)
    query_at = block * QB + lax.broadcasted_iota(jnp.int32, dims, 1)
    allowed = (codes == segs) | (key_at == query_at)
    bias_ref[block, : count * KB, :] = jnp.where(allowed, 0.0, MASKED_SCORE)


def one_head(values, head):
    lane = lax.broadcasted_iota(jnp.int32, values.shape, 1)
    keep = (lane < HD) if head == 0 else (lane >= HD)
    return jnp.where(keep, values, jnp.zeros_like(values))


def forward_kernel(
    table_ref,
    x_ref,
    w0_ref,
    w1_ref,
    code_ref,
    seg_ref,
    q_ref,
    k_ref,
    v_ref,
    ctx_ref,
    lse_ref,
    weights,
    biases,
    vt_ref,
    bias_ref,
):
    pair, block = pl.program_id(0), pl.program_id(1)
    low, total = table_ref[0, block], table_ref[1, block]
    piece = (w0_ref.shape[0] - 16) // 3

    @pl.when((pair == 0) & (block == 0))
    def _():
        for i in range(3):
            for n, ref in enumerate((w0_ref, w1_ref)):
                at = 0
                while at < piece:
                    spot = n * piece + at
                    size = min(128 - spot % 128, piece - at)
                    weights[spot // 128, i * 128 + spot % 128 : i * 128 + spot % 128 + size, :] = ref[
                        i * piece + at : i * piece + at + size, :
                    ]
                    at += size
        lane = lax.broadcasted_iota(jnp.int32, (1, x_ref.shape[1]), 1)
        for i in range(3):
            if i == 1:
                continue
            base = 3 * piece + (3 if i == 0 else 6)
            both = [
                sum(ref[base + part : base + part + 1, :].astype(F32) for part in range(3))
                for ref in (w0_ref, w1_ref)
            ]
            row = jnp.where(lane < piece, both[0], pltpu.roll(both[1], piece, 1))
            for p in range(2 * piece // 128):
                biases[p, :, i * 128 : (i + 1) * 128] = row[:, p * 128 : (p + 1) * 128]
        for p in range(2 * piece // 128):
            biases[p, :, 128:256] = jnp.zeros((1, 128), F32)

    @pl.when(block == 0)
    def _():
        qkv = (dot(x_ref[...], weights[pair], NT) + biases[pair]).astype(LOW)
        q_ref[...] = qkv[:, :128]
        k_ref[...] = qkv[:, 128:256]
        v_ref[...] = qkv[:, 256:]
        vt_ref[...] = qkv[:, 256:].T

    def run(count):
        @pl.when(pair == 0)
        def _():
            make_bias(bias_ref, block, low, count, code_ref, seg_ref)

        bias = bias_ref[block, : count * KB, :]
        rows = pl.ds(pl.multiple_of(low * KB, KB), count * KB)
        keys = k_ref[rows, :]
        queries = q_ref[pl.ds(pl.multiple_of(block * QB, QB), QB), :] * jnp.asarray(0.125, LOW)
        outs, sums = [], []
        for head in range(2):
            scores = dot(keys, one_head(queries, head), NT) + bias
            peak = jnp.max(scores, axis=0, keepdims=True)
            powers = jnp.exp(scores - peak)
            mass = jnp.sum(powers, axis=0, keepdims=True)
            probs = (powers * (1.0 / mass)).astype(LOW)
            outs.append(dot(vt_ref[head * HD : (head + 1) * HD, rows], probs))
            sums.append(peak + jnp.log(mass))
        ctx_ref[...] = jnp.concatenate(outs, axis=0).T.astype(LOW)
        lse_ref[0, 0:1, :] = sums[0]
        lse_ref[0, 1:2, :] = sums[1]

    for count in range(2, k_ref.shape[0] // KB + 1):
        pl.when(total == count)(functools.partial(run, count))


def backward_kernel(
    table_ref,
    q_ref,
    k_ref,
    v_ref,
    g_ref,
    lse_ref,
    code_ref,
    seg_ref,
    dq_ref,
    dk_ref,
    dv_ref,
    kt_ref,
    bias_ref,
    dk_sum,
    dv_sum,
):
    pair, block = pl.program_id(0), pl.program_id(1)
    low, total = table_ref[0, block], table_ref[1, block]

    @pl.when(block == 0)
    def _():
        kt_ref[...] = k_ref[...].T
        dk_sum[...] = jnp.zeros_like(dk_sum)
        dv_sum[...] = jnp.zeros_like(dv_sum)

    def run(count):
        @pl.when(pair == 0)
        def _():
            make_bias(bias_ref, block, low, count, code_ref, seg_ref)

        bias = bias_ref[block, : count * KB, :]
        rows = pl.ds(pl.multiple_of(low * KB, KB), count * KB)
        keys, values = k_ref[rows, :], v_ref[rows, :]
        queries = q_ref[...] * jnp.asarray(0.125, LOW)
        grads = g_ref[...]
        outs = []
        for head in range(2):
            query, grad = one_head(queries, head), one_head(grads, head)
            probs = jnp.exp(dot(keys, query, NT) + bias - lse_ref[0, head : head + 1, :])
            dv_sum[rows, :] += dot(probs.astype(LOW), grad)
            prob_grad = dot(values, grad, NT)
            delta = jnp.sum(probs * prob_grad, axis=0, keepdims=True)
            score_grad = (probs * (prob_grad - delta)).astype(LOW)
            dk_sum[rows, :] += dot(score_grad, query)
            outs.append(dot(kt_ref[head * HD : (head + 1) * HD, rows], score_grad))
        dq_ref[...] = (jnp.concatenate(outs, axis=0).T * 0.125).astype(LOW)

    for count in range(2, k_ref.shape[0] // KB + 1):
        pl.when(total == count)(functools.partial(run, count))

    @pl.when(block == pl.num_programs(1) - 1)
    def _():
        dk_ref[...] = dk_sum[...].astype(LOW)
        dv_ref[...] = dv_sum[...].astype(LOW)


def attend_forward(table, x, first, second, code, seg):
    seq, width = x.shape
    piece = (first.shape[0] - 16) // 3
    pairs, blocks = 2 * piece // 128, seq // QB
    column = pl.BlockSpec((seq, 128), lambda p, i, t: (0, p))
    whole = lambda p, i, t: (0, 0)
    return pl.pallas_call(
        forward_kernel,
        out_shape=(shape((seq, 2 * piece), LOW),) * 4 + (shape((pairs, 8, seq), F32),),
        grid_spec=pltpu.PrefetchScalarGridSpec(
            num_scalar_prefetch=1,
            grid=(pairs, blocks),
            in_specs=[
                pl.BlockSpec((seq, width), whole),
                pl.BlockSpec(first.shape, whole),
                pl.BlockSpec(second.shape, whole),
                pl.BlockSpec((seq, 1), whole),
                pl.BlockSpec((1, seq), whole),
            ],
            out_specs=[
                column,
                column,
                column,
                pl.BlockSpec((QB, 128), lambda p, i, t: (i, p)),
                pl.BlockSpec((1, 8, QB), lambda p, i, t: (p, 0, i)),
            ],
            scratch_shapes=[
                pltpu.VMEM((pairs, 384, width), LOW),
                pltpu.VMEM((pairs, 1, 384), F32),
                pltpu.VMEM((128, seq), LOW),
                pltpu.VMEM((blocks, seq, QB), F32),
            ],
        ),
        compiler_params=pltpu.CompilerParams(vmem_limit_bytes=40 << 20),
        cost_estimate=pl.CostEstimate(
            flops=16 * seq * seq * piece + 12 * seq * width * piece,
            bytes_accessed=16 * seq * piece,
            transcendentals=seq * seq * pairs,
        ),
        name="attend_forward",
    )(table, x, first, second, code, seg)


def attend_backward(table, q, k, v, grad, lse, code, seg):
    seq, width = grad.shape
    pairs, blocks = width // 128, seq // QB
    block = pl.BlockSpec((QB, 128), lambda p, i, t: (i, p))
    column = pl.BlockSpec((seq, 128), lambda p, i, t: (0, p))
    return pl.pallas_call(
        backward_kernel,
        out_shape=(shape((seq, width), LOW),) * 3,
        grid_spec=pltpu.PrefetchScalarGridSpec(
            num_scalar_prefetch=1,
            grid=(pairs, blocks),
            in_specs=[
                block,
                column,
                column,
                block,
                pl.BlockSpec((1, 8, QB), lambda p, i, t: (p, 0, i)),
                pl.BlockSpec((seq, 1), lambda p, i, t: (0, 0)),
                pl.BlockSpec((1, seq), lambda p, i, t: (0, 0)),
            ],
            out_specs=[block, column, column],
            scratch_shapes=[
                pltpu.VMEM((128, seq), LOW),
                pltpu.VMEM((blocks, seq, QB), F32),
                pltpu.VMEM((seq, 128), F32),
                pltpu.VMEM((seq, 128), F32),
            ],
        ),
        compiler_params=pltpu.CompilerParams(vmem_limit_bytes=32 << 20),
        cost_estimate=pl.CostEstimate(
            flops=16 * seq * seq * width,
            bytes_accessed=16 * seq * width,
            transcendentals=seq * seq * pairs,
        ),
        name="attend_backward",
    )(table, q, k, v, grad, lse, code, seg)


def gelu_parts(pre):
    t = 1.0 / (1.0 + PHI_STEP * jnp.abs(pre))
    poly = PHI[7] * t + PHI[6]
    for factor in PHI[5::-1]:
        poly = poly * t + factor
    bell = jnp.exp(-0.5 * (pre * pre))
    tail = poly * t * bell
    cdf = jnp.where(pre < 0, tail, 1.0 - tail)
    return pre * cdf, cdf + pre * (bell * 0.3989422804014327)


def norm_stats(values):
    width = values.shape[-1]
    mean = jnp.sum(values, axis=-1, keepdims=True) * (1.0 / width)
    centred = values - mean
    spread = jnp.sum(centred * centred, axis=-1, keepdims=True) * (1.0 / width)
    rate = lax.rsqrt(spread + LN_EPSILON)
    return centred * rate, rate


def norm_back(grad, gain, xhat, rate):
    width = grad.shape[-1]
    scaled = grad * gain
    mean = jnp.sum(scaled, axis=-1, keepdims=True) * (1.0 / width)
    along = jnp.sum(scaled * xhat, axis=-1, keepdims=True) * (1.0 / width)
    return rate * (scaled - mean - xhat * along)


def column_sum(values):
    return jnp.sum(values, axis=0, keepdims=True)


def middle_kernel(
    valid_ref,
    scale_ref,
    ctx_a,
    ctx_b,
    gains,
    shifts,
    bias_in,
    x_hbm,
    teacher_hbm,
    r0a,
    r0b,
    r0c,
    r0d,
    r1a,
    r1b,
    r1c,
    r1d,
    out_hbm,
    dh_hbm,
    cg_a,
    cg_b,
    ffn_send,
    ffn_keep,
    out_send,
    out_keep,
    sums,
    bias_sums,
    w_in,
    w_back,
    w_out,
    xhat_one,
    rate_one,
    mid_low,
    hidden,
    slope,
    acc,
    dh_low,
    pre_grad,
    rows_in,
    rows_out,
    stage16,
    stage32,
    w_sem,
    in_sem,
    out_sem,
    g_sem,
):
    seq, width = acc.shape
    blocks = seq // RB
    half = width // 2
    first, second = (r0a, r0b, r0c, r0d), (r1a, r1b, r1c, r1d)
    out_rows = w_out.shape[0] // 4
    units = w_in.shape[2]
    side = units // 2

    def rows(i):
        return pl.ds(i * RB, RB)

    def fetch(source, i, slot):
        return pltpu.make_async_copy(source.at[rows(i), :], rows_in.at[slot], in_sem.at[slot])

    def out_weights(p, c):
        return pltpu.make_async_copy(
            first[p].at[pl.ds(c * out_rows, out_rows), :],
            w_out.at[pl.ds(p * out_rows, out_rows), pl.ds(c * half, half)],
            w_sem.at[p, c],
        )

    def ffn_weights(p, r):
        source, base = (first[p], 2 * out_rows) if r == 0 else (second[p], 0)
        copies = [
            pltpu.make_async_copy(
                source.at[pl.ds(base, width), :],
                w_in.at[p, :, pl.ds(r * side, side)],
                w_sem.at[p, 2 + 3 * r],
            )
        ]
        for c in range(2):
            copies.append(
                pltpu.make_async_copy(
                    source.at[pl.ds(base + width + c * side, side), :],
                    w_back.at[p, pl.ds(r * side, side), pl.ds(c * half, half)],
                    w_sem.at[p, 3 + 3 * r + c],
                )
            )
        return copies

    out_copies = [out_weights(p, c) for p in range(4) for c in range(2)]
    for copy in out_copies:
        copy.start()
    fetch(x_hbm, 0, 0).start()
    for p in range(4):
        for r in range(2):
            for copy in ffn_weights(p, r):
                copy.start()
    for copy in out_copies:
        copy.wait()

    for i in range(blocks):
        if i + 1 < blocks:
            fetch(x_hbm, i + 1, (i + 1) % 2).start()
        fetch(x_hbm, i, i % 2).wait()
        context = jnp.concatenate([ctx_a[rows(i), :], ctx_b[rows(i), :]], axis=1)
        xhat, rate = norm_stats(dot(context, w_out[...]) + shifts[0:1, :] + rows_in[i % 2])
        xhat_one[rows(i), :] = xhat
        rate_one[rows(i), :] = rate
        mid_low[rows(i), :] = (xhat * gains[0:1, :] + shifts[1:2, :]).astype(LOW)
        acc[rows(i), :] = jnp.zeros((RB, width), F32)
    fetch(teacher_hbm, 0, 0).start()

    for p in range(4):
        for r in range(2):
            for copy in ffn_weights(p, r):
                copy.wait()
        for k in range(seq // FR):
            at = pl.ds(k * FR, FR)
            pre = dot(mid_low[at, :], w_in[p]) + bias_in[:, p * units : (p + 1) * units]
            act, der = gelu_parts(pre)
            act = act.astype(LOW)
            hidden[p, at, :] = act
            slope[p, at, :] = der
            acc[at, :] += dot(act, w_back[p])

    zero = jnp.zeros((1, width), F32)
    squares, gain_two, shift_two, shift_mid = zero, zero, zero, zero
    stores = []
    for i in range(blocks):
        if i + 1 < blocks:
            fetch(teacher_hbm, i + 1, (i + 1) % 2).start()
        fetch(teacher_hbm, i, i % 2).wait()
        mid = xhat_one[rows(i), :] * gains[0:1, :] + shifts[1:2, :]
        xhat, rate = norm_stats(acc[rows(i), :] + shifts[2:3, :] + mid)
        output = xhat * gains[1:2, :] + shifts[3:4, :]
        if i >= 2:
            stores[i - 2].wait()
        rows_out[i % 2] = output
        stores.append(
            pltpu.make_async_copy(rows_out.at[i % 2], out_hbm.at[rows(i), :], out_sem.at[i % 2])
        )
        stores[i].start()
        live = (i * RB + lax.broadcasted_iota(jnp.int32, (RB, 1), 0)) < valid_ref[0]
        distance = jnp.where(live, output - rows_in[i % 2], 0.0)
        squares += column_sum(distance * distance)
        out_grad = scale_ref[0] * distance
        gain_two += column_sum(out_grad * xhat)
        shift_two += column_sum(out_grad)
        dh_two = norm_back(out_grad, gains[1:2, :], xhat, rate)
        shift_mid += column_sum(dh_two)
        acc[rows(i), :] = dh_two
        dh_low[rows(i), :] = dh_two.astype(LOW)
    for store in stores[-2:]:
        store.wait()

    pending = {}
    sides = (pl.ds(0, side), pl.ds(side, side))

    def put(key, values, stage, slot, moves):
        for copy in pending.get(key, ()):
            copy.wait()
        stage[slot] = values.astype(stage.dtype)
        pending[key] = [
            pltpu.make_async_copy(stage.at[slot].at[source], target, g_sem.at[key, n])
            for n, (source, target) in enumerate(moves)
        ]
        for copy in pending[key]:
            copy.start()

    for p in (1, 3, 2, 0):
        total = jnp.zeros((1, units), F32)
        for k in range(seq // FR):
            at = pl.ds(k * FR, FR)
            grad = (dot(dh_low[at, :], w_back[p], NT) * slope[p, at, :]).astype(LOW)
            pre_grad[at, :] = grad
            acc[at, :] += dot(grad, w_in[p], NT)
            total += column_sum(grad.astype(F32))
        bias_sums[:, p * units : (p + 1) * units] = total
        stage, target, key = (stage16, ffn_send, 0) if p % 2 else (stage32, ffn_keep, 2)
        target = target.at[p // 2]
        put(
            key,
            dot(mid_low[...], pre_grad[...], TN),
            stage,
            0,
            [((slice(None), sides[r]), target.at[r, 0]) for r in range(2)],
        )
        put(
            key + 1,
            dot(hidden[p], dh_low[...], TN),
            stage,
            1,
            [
                ((sides[r], sides[c]), target.at[r, 1, sides[c], :])
                for r in range(2)
                for c in range(2)
            ],
        )
    for copies in pending.values():
        for copy in copies:
            copy.wait()

    gain_one, shift_one, shift_out = zero, zero, zero
    stores = []
    for i in range(blocks):
        grad, xhat = acc[rows(i), :], xhat_one[rows(i), :]
        gain_one += column_sum(grad * xhat)
        shift_one += column_sum(grad)
        dh_one = norm_back(grad, gains[0:1, :], xhat, rate_one[rows(i), :])
        shift_out += column_sum(dh_one)
        if i >= 2:
            stores[i - 2].wait()
        rows_out[i % 2] = dh_one
        stores.append(
            pltpu.make_async_copy(rows_out.at[i % 2], dh_hbm.at[rows(i), :], out_sem.at[i % 2])
        )
        stores[i].start()
        dh_one = dh_one.astype(LOW)
        dh_low[rows(i), :] = dh_one
        grad = dot(dh_one, w_out[...], NT).astype(LOW)
        cg_a[rows(i), :] = grad[:, :half]
        cg_b[rows(i), :] = grad[:, half:]
    for store in stores[-2:]:
        store.wait()
    for group, context in enumerate((ctx_a, ctx_b)):
        grad = dot(context[...], dh_low[...], TN)
        out_keep[group] = grad[:out_rows]
        out_send[group] = grad[out_rows:].astype(LOW)
    sums[...] = jnp.concatenate(
        [gain_one, gain_two, shift_out, shift_one, shift_mid, shift_two, squares, zero], axis=0
    )


def middle(valid, scale, ctx_a, ctx_b, gains, shifts, bias_in, x, teacher, first, second):
    seq, width = x.shape
    half = width // 2
    out_rows = ctx_a.shape[1] // 2
    units = bias_in.shape[1] // 4
    return pl.pallas_call(
        middle_kernel,
        out_shape=(
            shape((seq, width), F32),
            shape((seq, width), F32),
            shape((seq, half), LOW),
            shape((seq, half), LOW),
            shape((2, 2, 2, width, units // 2), LOW),
            shape((2, 2, 2, width, units // 2), F32),
            shape((2, out_rows, width), LOW),
            shape((2, out_rows, width), F32),
            shape((8, width), F32),
            shape((1, 4 * units), F32),
        ),
        in_specs=[SMEM, SMEM, VMEM, VMEM, VMEM, VMEM, VMEM, HBM, HBM] + [HBM] * 8,
        out_specs=(HBM, HBM, VMEM, VMEM, HBM, HBM, VMEM, VMEM, VMEM, VMEM),
        scratch_shapes=[
            pltpu.VMEM((4, width, units), LOW),
            pltpu.VMEM((4, units, width), LOW),
            pltpu.VMEM((4 * out_rows, width), LOW),
            pltpu.VMEM((seq, width), F32),
            pltpu.VMEM((seq, 1), F32),
            pltpu.VMEM((seq, width), LOW),
            pltpu.VMEM((4, seq, units), LOW),
            pltpu.VMEM((4, seq, units), F32),
            pltpu.VMEM((seq, width), F32),
            pltpu.VMEM((seq, width), LOW),
            pltpu.VMEM((seq, units), LOW),
            pltpu.VMEM((2, RB, width), F32),
            pltpu.VMEM((2, RB, width), F32),
            pltpu.VMEM((2, width, units), LOW),
            pltpu.VMEM((2, width, units), F32),
            pltpu.SemaphoreType.DMA((4, 8)),
            pltpu.SemaphoreType.DMA((2,)),
            pltpu.SemaphoreType.DMA((2,)),
            pltpu.SemaphoreType.DMA((4, 4)),
        ],
        compiler_params=pltpu.CompilerParams(vmem_limit_bytes=63 << 20),
        cost_estimate=pl.CostEstimate(
            flops=6 * seq * width * (8 * units + width),
            bytes_accessed=30 << 20,
            transcendentals=2 * seq * 4 * units,
        ),
        name="middle",
    )(valid, scale, ctx_a, ctx_b, gains, shifts, bias_in, x, teacher, *first, *second)


def projection_kernel(side_ref, x_ref, w0, w1, w2, w3, dqa, dka, dva, dqb, dkb, dvb, osend, okeep, dh_hbm, gx_hbm, send, keep, bias_ref, rows_in, rows_out, in_sem, out_sem):
    seq, width = x_ref.shape
    half = width // 2
    piece = dqa.shape[1] // 2
    blocks = seq // RB
    grads = ((dqa, dka, dva), (dqb, dkb, dvb))
    mine = pl.ds(pl.multiple_of(side_ref[0] * half, half), half)
    other = pl.ds(pl.multiple_of((1 - side_ref[0]) * half, half), half)

    def fetch(i, slot):
        return pltpu.make_async_copy(dh_hbm.at[pl.ds(i * RB, RB), :], rows_in.at[slot], in_sem.at[slot])

    fetch(0, 0).start()
    for g in range(2):
        for i in range(3):
            cross = dot(grads[g][i][...], x_ref[...], TN)
            rows_out[:2 * piece, :] = cross
            for n, at in enumerate((mine, other)):
                keep[g, n, i * piece : (i + 1) * piece, :] = rows_out[:piece, at]
                send[g, n, i * piece : (i + 1) * piece, :] = rows_out[piece : 2 * piece, at].astype(LOW)
            bias_ref[g, i : i + 1, :] = column_sum(grads[g][i][...].astype(F32))
        for n, at in enumerate((mine, other)):
            keep[g, n, 3 * piece :, :] = okeep[g, :, at]
            send[g, n, 3 * piece :, :] = osend[g, :, at]
    weights = ((w0, w1), (w2, w3))
    stores = []
    for b in range(blocks):
        at = pl.ds(b * RB, RB)
        if b + 1 < blocks:
            fetch(b + 1, (b + 1) % 2).start()
        fetch(b, b % 2).wait()
        total = rows_in[b % 2]
        for g in range(2):
            for i in range(3):
                w = jnp.concatenate([ref[i * piece : (i + 1) * piece, :] for ref in weights[g]], axis=0)
                total += dot(grads[g][i][at, :], w)
        if b >= 1:
            stores[b - 1].wait()
        rows_out[:RB, :] = total
        stores.append(pltpu.make_async_copy(rows_out.at[pl.ds(0, RB), :], gx_hbm.at[at, :], out_sem))
        stores[b].start()
    stores[-1].wait()


def projections(side, x, weights, grads, osend, okeep, dh):
    seq, width = x.shape
    half = width // 2
    piece = grads[0].shape[1] // 2
    total = 3 * piece + osend.shape[1]
    return pl.pallas_call(
        projection_kernel,
        out_shape=(
            shape((seq, width), F32),
            shape((2, 2, total, half), LOW),
            shape((2, 2, total, half), F32),
            shape((2, 8, 2 * piece), F32),
        ),
        in_specs=[SMEM] + [VMEM] * 13 + [HBM],
        out_specs=(HBM, VMEM, VMEM, VMEM),
        scratch_shapes=[
            pltpu.VMEM((2, RB, width), F32),
            pltpu.VMEM((2 * piece, width), F32),
            pltpu.SemaphoreType.DMA((2,)),
            pltpu.SemaphoreType.DMA,
        ],
        compiler_params=pltpu.CompilerParams(vmem_limit_bytes=50 << 20),
        cost_estimate=pl.CostEstimate(
            flops=24 * seq * width * piece * 2, bytes_accessed=30 << 20, transcendentals=0
        ),
        name="projections",
    )(side, x, *weights, *grads, osend, okeep, dh)


def swap(values, axis, bit):
    size = lax.axis_size(axis)
    return lax.ppermute(values, axis, [(i, i ^ (1 << bit)) for i in range(size)])


def bits_of(axis):
    return int(math.log2(lax.axis_size(axis)))


def halves(values, bit_set, axis):
    half = values.shape[axis] // 2
    keep = lax.dynamic_slice_in_dim(values, bit_set * half, half, axis)
    send = lax.dynamic_slice_in_dim(values, (1 - bit_set) * half, half, axis)
    return keep, send


def join(mine, other, bit_set, axis):
    low = jnp.where(bit_set == 0, mine, other)
    high = jnp.where(bit_set == 0, other, mine)
    return jnp.concatenate([low, high], axis=axis)


def reduce_pieces(send, keep):
    from_core = swap(send, "tensor", 0)
    away = (keep[1] + from_core[1].astype(F32)).astype(LOW)
    from_y = swap(away, "tensor", 1)
    total = keep[0] + from_core[0].astype(F32) + from_y.astype(F32)
    total = total[0] + swap(total[1].astype(LOW), "dp", 0).astype(F32)
    place = lax.axis_index("dp")
    for bit in range(1, bits_of("dp")):
        mine, other = halves(total, (place >> bit) & 1, total.ndim - 2)
        total = mine + swap(other.astype(LOW), "dp", bit).astype(F32)
    total = total.astype(LOW)
    for bit in reversed(range(1, bits_of("dp"))):
        total = join(total, swap(total, "dp", bit), (place >> bit) & 1, total.ndim - 2)
    side = place & 1
    other = swap(total, "dp", 0)
    return jnp.where(side == 0, total, other).astype(F32), jnp.where(side == 0, other, total).astype(F32)


def reduce_all(values):
    for bit in range(bits_of("tensor")):
        values = values + swap(values, "tensor", bit)
    for bit in range(bits_of("dp")):
        values = values + swap(values, "dp", bit)
    return values


def per_device(
    inputs,
    w_qkv,
    b_qv,
    w_out,
    w_in,
    b_in,
    w_back,
    norm_gains,
    shifts,
    segment_ids,
    valid_lengths,
    teacher,
):
    own_seqs, seq, width = inputs.shape
    assert own_seqs == 1 and lax.axis_size("tensor") == 4
    total_slots = seq * lax.axis_size("tensor") * lax.axis_size("dp")
    half = width // 2
    piece = w_qkv.shape[2]
    units = w_in.shape[1]
    index = lax.axis_index("tensor")
    side = (lax.axis_index("dp") & 1).astype(jnp.int32)
    side_row = side.reshape(1)
    x = inputs.reshape(seq, width)

    near = round_qkv(side_row, w_qkv, b_qv, b_in[None, :])
    core = swap(near, "tensor", 0)
    far = swap(near, "tensor", 1)
    first, second, x_low = round_rest(side_row, w_out, w_in, w_back, x)
    first_far = swap(first, "tensor", 1)

    valid = lax.dynamic_index_in_dim(valid_lengths, index, keepdims=False)
    segments = lax.dynamic_index_in_dim(segment_ids, index, keepdims=False)
    positions = jnp.arange(seq, dtype=jnp.int32)
    code = jnp.where(positions < valid, segments, -1)[:, None]
    seg = segments[None, :]
    table = span_tables(segments, valid, seq)

    qa, ka, va, ctx_a, lse_a = attend_forward(table, x_low, near, core, code, seg)
    core_far = swap(far, "tensor", 0)
    first_core = swap(first, "tensor", 0)
    second_core = swap(second, "tensor", 0)
    token_count = jnp.sum(valid_lengths)
    for bit in range(bits_of("dp")):
        token_count = token_count + swap(token_count, "dp", bit)
    token_count = token_count.astype(F32)
    qb, kb, vb, ctx_b, lse_b = attend_forward(table, x_low, far, core_far, code, seg)
    second_far = swap(first_far[2 * piece :], "dp", 0)
    first_core_far = swap(first_far, "tensor", 0)
    second_core_far = swap(second_far, "tensor", 0)
    at = 3 * piece
    bias_in = jnp.concatenate(
        [
            part[at : at + 1].astype(F32) + part[at + 1 : at + 2].astype(F32) + part[at + 2 : at + 3].astype(F32)
            for part in (near, core, far, core_far)
        ],
        axis=1,
    )
    scale = (total_slots / token_count).reshape(1)
    output, dh_one, cg_a, cg_b, ffn_send, ffn_keep, out_send, out_keep, sums, bias_sums = middle(
        valid.reshape(1),
        scale,
        ctx_a,
        ctx_b,
        norm_gains,
        shifts,
        bias_in,
        x,
        teacher.reshape(seq, width),
        (first, first_core, first_far, first_core_far),
        (second, second_core, second_far, second_core_far),
    )
    low_ffn, high_ffn = reduce_pieces(ffn_send, ffn_keep)
    grads_a = attend_backward(table, qa, ka, va, cg_a, lse_a, code, seg)
    grads_b = attend_backward(table, qb, kb, vb, cg_b, lse_b, code, seg)
    grad_inputs, send, keep, bias_qv = projections(
        side_row, x_low, (near, core, far, core_far), grads_a + grads_b, out_send, out_keep, dh_one
    )
    low_qkv, high_qkv = reduce_pieces(send, keep)

    grad_w_in = jnp.concatenate([low_ffn[0], high_ffn[0]], axis=1)
    grad_w_back = jnp.concatenate(
        [
            jnp.concatenate([part[1, :half], part[1, half:]], axis=1)
            for part in (low_ffn, high_ffn)
        ],
        axis=0,
    )
    rows = jnp.concatenate([low_qkv, high_qkv], axis=1)
    grad_w_qkv = rows[: 3 * piece].reshape(3, piece, width).transpose(0, 2, 1)
    grad_w_out = rows[3 * piece :]

    bias_in_sums = bias_sums.reshape(4, 2, units // 2)
    bias_in_sums = jnp.where(side == 0, bias_in_sums, bias_in_sums[:, ::-1]).reshape(4, units)
    bias_qv_sums = bias_qv[:, (0, 2), :].reshape(2, 2, 2, piece).transpose(0, 2, 1, 3).reshape(4, 2 * piece)
    by_shard = jnp.concatenate([bias_qv_sums, bias_in_sums], axis=1)
    flipped = jnp.where((index & 1) == 0, by_shard, by_shard[jnp.array([1, 0, 3, 2])])
    natural = jnp.where((index & 2) == 0, flipped, flipped[jnp.array([2, 3, 0, 1])])
    wide = by_shard.shape[1]
    small = reduce_all(jnp.concatenate([natural.reshape(-1), sums[:7].reshape(-1)]))
    own = lax.dynamic_slice_in_dim(small, index * wide, wide)
    rest = small[4 * wide :].reshape(7, width)
    loss = jnp.sum(rest[6]) / (2.0 * width * token_count)
    return (
        output.reshape(own_seqs, seq, width),
        loss,
        grad_inputs.reshape(own_seqs, seq, width),
        grad_w_qkv,
        own[: 2 * piece].reshape(2, piece),
        grad_w_out,
        grad_w_in,
        own[2 * piece :],
        grad_w_back,
        rest[:2],
        rest[2:6],
    )


def solution(mesh):
    return jax.shard_map(
        per_device,
        mesh=mesh,
        in_specs=(
            P(("dp", "tensor"), None, None),
            P(None, None, "tensor"),
            P(None, "tensor"),
            P("tensor", None),
            P(None, "tensor"),
            P("tensor"),
            P("tensor", None),
            P(),
            P(),
            P("dp", None),
            P("dp"),
            P(("dp", "tensor"), None, None),
        ),
        out_specs=(
            P(("dp", "tensor"), None, None),
            P(),
            P(("dp", "tensor"), None, None),
            P(None, None, "tensor"),
            P(None, "tensor"),
            P("tensor", None),
            P(None, "tensor"),
            P("tensor"),
            P("tensor", None),
            P(),
            P(),
        ),
        check_vma=False,
    )
```

```python
import functools
import math

import jax
import jax.numpy as jnp
from jax import lax
from jax.experimental import pallas as pl
from jax.experimental.pallas import tpu as pltpu
from jax.sharding import PartitionSpec as P

HD = 64
LN_EPSILON = 1e-05
MASKED_SCORE = -1000000000.0
QB = 256
KB = 128
RB = 256
FR = 256
NT = ((1,), (1,))
TN = ((0,), (0,))
PHI = (
    0.09255110872,
    0.09001568156,
    0.1049848251,
    0.006341010132,
    0.2381524984,
    -0.2150534404,
    0.2551771707,
    -0.07216888208,
)
PHI_STEP = 0.23164188826636045

VMEM_LIMIT = 63 << 20
VMEM = pl.BlockSpec(memory_space=pltpu.VMEM)
SMEM = pl.BlockSpec(memory_space=pltpu.SMEM)
HBM = pl.BlockSpec(memory_space=pl.ANY)
LOW = jnp.bfloat16
F32 = jnp.float32


def dot(left, right, dims=((1,), (0,))):
    return lax.dot_general(left, right, (dims, ((), ())), preferred_element_type=jnp.float32)


def shape(dims, dtype):
    return jax.ShapeDtypeStruct(dims, dtype)


def three_parts(values):
    first = values.astype(LOW)
    rest = values - first.astype(F32)
    second = rest.astype(LOW)
    return first, second, (rest - second.astype(F32)).astype(LOW)


def round_qkv_kernel(side_ref, w_ref, bqv_ref, bin_ref, out_ref):
    piece = w_ref.shape[2]
    width = w_ref.shape[1]
    half = bin_ref.shape[1] // 2
    for i in range(3):
        out_ref[i * piece : (i + 1) * piece, :] = w_ref[i].T.astype(LOW)
    mine = bin_ref[:, pl.ds(pl.multiple_of(side_ref[0] * half, half), half)]
    other = bin_ref[:, pl.ds(pl.multiple_of((1 - side_ref[0]) * half, half), half)]
    pad = jnp.zeros((1, width - piece), F32)
    rows = [jnp.concatenate([mine, other], axis=1)]
    rows += [jnp.concatenate([bqv_ref[i : i + 1, :], pad], axis=1) for i in range(2)]
    parts = [part.astype(F32) for row in rows for part in three_parts(row)]
    parts += [jnp.zeros((1, width), F32)] * 7
    out_ref[3 * piece :, :] = jnp.concatenate(parts, axis=0).astype(LOW)


def round_qkv(side, w_qkv, b_qv, b_in):
    _, width, piece = w_qkv.shape
    return pl.pallas_call(
        round_qkv_kernel,
        out_shape=shape((3 * piece + 16, width), LOW),
        in_specs=[SMEM, VMEM, VMEM, VMEM],
        out_specs=VMEM,
        compiler_params=pltpu.CompilerParams(vmem_limit_bytes=VMEM_LIMIT),
        name="round_qkv",
    )(side, w_qkv, b_qv, b_in)


def round_rest_kernel(side_ref, wo_ref, wi_ref, wb_ref, x_ref, first_ref, second_ref, x_low_ref):
    rows, width = wo_ref.shape
    half = width // 2
    for c in range(2):
        first_ref[c * rows : (c + 1) * rows, :] = wo_ref[:, c * half : (c + 1) * half].astype(LOW)
    for out, base, side in ((first_ref, 2 * rows, side_ref[0]), (second_ref, 0, 1 - side_ref[0])):
        at = pl.ds(pl.multiple_of(side * half, half), half)
        out[base : base + width, :] = wi_ref[:, at].astype(LOW)
        for c in range(2):
            start = base + width + c * half
            out[start : start + half, :] = wb_ref[at, c * half : (c + 1) * half].astype(LOW)
    x_low_ref[...] = x_ref[...].astype(LOW)


def round_rest(side, w_out, w_in, w_back, x):
    rows, width = w_out.shape
    half = width // 2
    return pl.pallas_call(
        round_rest_kernel,
        out_shape=(
            shape((2 * rows + 2 * width, half), LOW),
            shape((2 * width, half), LOW),
            shape(x.shape, LOW),
        ),
        in_specs=[SMEM, VMEM, VMEM, VMEM, VMEM],
        out_specs=(VMEM, VMEM, VMEM),
        compiler_params=pltpu.CompilerParams(vmem_limit_bytes=VMEM_LIMIT),
        name="round_rest",
    )(side, w_out, w_in, w_back, x)


def span_tables(segments, valid, seq):
    blocks = seq // QB
    firsts, lasts = segments[::QB], segments[QB - 1 :: QB]
    low = jnp.sum((segments[None, :] < firsts[:, None]).astype(jnp.int32), axis=1)
    high = jnp.sum((segments[None, :] <= lasts[:, None]).astype(jnp.int32), axis=1)
    own_end = (jnp.arange(blocks, dtype=jnp.int32) + 1) * QB
    high = jnp.maximum(jnp.minimum(high, valid), own_end)
    low_block = low // KB
    high_block = (high + KB - 1) // KB
    return jnp.stack([low_block, high_block - low_block]).astype(jnp.int32)


def make_bias(bias_ref, block, low, count, code_ref, seg_ref):
    dims = (count * KB, QB)
    codes = code_ref[pl.ds(pl.multiple_of(low * KB, KB), count * KB), :]
    segs = seg_ref[:, pl.ds(pl.multiple_of(block * QB, QB), QB)]
    key_at = low * KB + lax.broadcasted_iota(jnp.int32, dims, 0)
    query_at = block * QB + lax.broadcasted_iota(jnp.int32, dims, 1)
    allowed = (codes == segs) | (key_at == query_at)
    bias_ref[block, : count * KB, :] = jnp.where(allowed, 0.0, MASKED_SCORE)


def one_head(values, head):
    lane = lax.broadcasted_iota(jnp.int32, values.shape, 1)
    keep = (lane < HD) if head == 0 else (lane >= HD)
    return jnp.where(keep, values, jnp.zeros_like(values))


def forward_kernel(
    table_ref,
    x_ref,
    w0_ref,
    w1_ref,
    code_ref,
    seg_ref,
    q_ref,
    k_ref,
    v_ref,
    ctx_ref,
    lse_ref,
    weights,
    biases,
    vt_ref,
    bias_ref,
):
    pair, block = pl.program_id(0), pl.program_id(1)
    low, total = table_ref[0, block], table_ref[1, block]
    piece = (w0_ref.shape[0] - 16) // 3

    @pl.when((pair == 0) & (block == 0))
    def _():
        for i in range(3):
            for n, ref in enumerate((w0_ref, w1_ref)):
                at = 0
                while at < piece:
                    spot = n * piece + at
                    size = min(128 - spot % 128, piece - at)
                    weights[spot // 128, i * 128 + spot % 128 : i * 128 + spot % 128 + size, :] = ref[
                        i * piece + at : i * piece + at + size, :
                    ]
                    at += size
        lane = lax.broadcasted_iota(jnp.int32, (1, x_ref.shape[1]), 1)
        for i in range(3):
            if i == 1:
                continue
            base = 3 * piece + (3 if i == 0 else 6)
            both = [
                sum(ref[base + part : base + part + 1, :].astype(F32) for part in range(3))
                for ref in (w0_ref, w1_ref)
            ]
            row = jnp.where(lane < piece, both[0], pltpu.roll(both[1], piece, 1))
            for p in range(2 * piece // 128):
                biases[p, :, i * 128 : (i + 1) * 128] = row[:, p * 128 : (p + 1) * 128]
        for p in range(2 * piece // 128):
            biases[p, :, 128:256] = jnp.zeros((1, 128), F32)

    @pl.when(block == 0)
    def _():
        qkv = (dot(x_ref[...], weights[pair], NT) + biases[pair]).astype(LOW)
        q_ref[...] = qkv[:, :128]
        k_ref[...] = qkv[:, 128:256]
        v_ref[...] = qkv[:, 256:]
        vt_ref[...] = qkv[:, 256:].T

    def run(count):
        @pl.when(pair == 0)
        def _():
            make_bias(bias_ref, block, low, count, code_ref, seg_ref)

        bias = bias_ref[block, : count * KB, :]
        rows = pl.ds(pl.multiple_of(low * KB, KB), count * KB)
        keys = k_ref[rows, :]
        queries = q_ref[pl.ds(pl.multiple_of(block * QB, QB), QB), :] * jnp.asarray(0.125, LOW)
        outs, sums = [], []
        for head in range(2):
            scores = dot(keys, one_head(queries, head), NT) + bias
            peak = jnp.max(scores, axis=0, keepdims=True)
            powers = jnp.exp(scores - peak)
            mass = jnp.sum(powers, axis=0, keepdims=True)
            probs = (powers * (1.0 / mass)).astype(LOW)
            outs.append(dot(vt_ref[head * HD : (head + 1) * HD, rows], probs))
            sums.append(peak + jnp.log(mass))
        ctx_ref[...] = jnp.concatenate(outs, axis=0).T.astype(LOW)
        lse_ref[0, 0:1, :] = sums[0]
        lse_ref[0, 1:2, :] = sums[1]

    for count in range(2, k_ref.shape[0] // KB + 1):
        pl.when(total == count)(functools.partial(run, count))


def backward_kernel(
    table_ref,
    q_ref,
    k_ref,
    v_ref,
    g_ref,
    lse_ref,
    code_ref,
    seg_ref,
    dq_ref,
    dk_ref,
    dv_ref,
    kt_ref,
    bias_ref,
    dk_sum,
    dv_sum,
):
    pair, block = pl.program_id(0), pl.program_id(1)
    low, total = table_ref[0, block], table_ref[1, block]

    @pl.when(block == 0)
    def _():
        kt_ref[...] = k_ref[...].T
        dk_sum[...] = jnp.zeros_like(dk_sum)
        dv_sum[...] = jnp.zeros_like(dv_sum)

    def run(count):
        @pl.when(pair == 0)
        def _():
            make_bias(bias_ref, block, low, count, code_ref, seg_ref)

        bias = bias_ref[block, : count * KB, :]
        rows = pl.ds(pl.multiple_of(low * KB, KB), count * KB)
        keys, values = k_ref[rows, :], v_ref[rows, :]
        queries = q_ref[...] * jnp.asarray(0.125, LOW)
        grads = g_ref[...]
        outs = []
        for head in range(2):
            query, grad = one_head(queries, head), one_head(grads, head)
            probs = jnp.exp(dot(keys, query, NT) + bias - lse_ref[0, head : head + 1, :])
            dv_sum[rows, :] += dot(probs.astype(LOW), grad)
            prob_grad = dot(values, grad, NT)
            delta = jnp.sum(probs * prob_grad, axis=0, keepdims=True)
            score_grad = (probs * (prob_grad - delta)).astype(LOW)
            dk_sum[rows, :] += dot(score_grad, query)
            outs.append(dot(kt_ref[head * HD : (head + 1) * HD, rows], score_grad))
        dq_ref[...] = (jnp.concatenate(outs, axis=0).T * 0.125).astype(LOW)

    for count in range(2, k_ref.shape[0] // KB + 1):
        pl.when(total == count)(functools.partial(run, count))

    @pl.when(block == pl.num_programs(1) - 1)
    def _():
        dk_ref[...] = dk_sum[...].astype(LOW)
        dv_ref[...] = dv_sum[...].astype(LOW)


def attend_forward(table, x, first, second, code, seg):
    seq, width = x.shape
    piece = (first.shape[0] - 16) // 3
    pairs, blocks = 2 * piece // 128, seq // QB
    column = pl.BlockSpec((seq, 128), lambda p, i, t: (0, p))
    whole = lambda p, i, t: (0, 0)
    return pl.pallas_call(
        forward_kernel,
        out_shape=(shape((seq, 2 * piece), LOW),) * 4 + (shape((pairs, 8, seq), F32),),
        grid_spec=pltpu.PrefetchScalarGridSpec(
            num_scalar_prefetch=1,
            grid=(pairs, blocks),
            in_specs=[
                pl.BlockSpec((seq, width), whole),
                pl.BlockSpec(first.shape, whole),
                pl.BlockSpec(second.shape, whole),
                pl.BlockSpec((seq, 1), whole),
                pl.BlockSpec((1, seq), whole),
            ],
            out_specs=[
                column,
                column,
                column,
                pl.BlockSpec((QB, 128), lambda p, i, t: (i, p)),
                pl.BlockSpec((1, 8, QB), lambda p, i, t: (p, 0, i)),
            ],
            scratch_shapes=[
                pltpu.VMEM((pairs, 384, width), LOW),
                pltpu.VMEM((pairs, 1, 384), F32),
                pltpu.VMEM((128, seq), LOW),
                pltpu.VMEM((blocks, seq, QB), F32),
            ],
        ),
        compiler_params=pltpu.CompilerParams(vmem_limit_bytes=VMEM_LIMIT),
        cost_estimate=pl.CostEstimate(
            flops=16 * seq * seq * piece + 12 * seq * width * piece,
            bytes_accessed=16 * seq * piece,
            transcendentals=seq * seq * pairs,
        ),
        name="attend_forward",
    )(table, x, first, second, code, seg)


def attend_backward(table, q, k, v, grad, lse, code, seg):
    seq, width = grad.shape
    pairs, blocks = width // 128, seq // QB
    block = pl.BlockSpec((QB, 128), lambda p, i, t: (i, p))
    column = pl.BlockSpec((seq, 128), lambda p, i, t: (0, p))
    return pl.pallas_call(
        backward_kernel,
        out_shape=(shape((seq, width), LOW),) * 3,
        grid_spec=pltpu.PrefetchScalarGridSpec(
            num_scalar_prefetch=1,
            grid=(pairs, blocks),
            in_specs=[
                block,
                column,
                column,
                block,
                pl.BlockSpec((1, 8, QB), lambda p, i, t: (p, 0, i)),
                pl.BlockSpec((seq, 1), lambda p, i, t: (0, 0)),
                pl.BlockSpec((1, seq), lambda p, i, t: (0, 0)),
            ],
            out_specs=[block, column, column],
            scratch_shapes=[
                pltpu.VMEM((128, seq), LOW),
                pltpu.VMEM((blocks, seq, QB), F32),
                pltpu.VMEM((seq, 128), F32),
                pltpu.VMEM((seq, 128), F32),
            ],
        ),
        compiler_params=pltpu.CompilerParams(vmem_limit_bytes=VMEM_LIMIT),
        cost_estimate=pl.CostEstimate(
            flops=16 * seq * seq * width,
            bytes_accessed=16 * seq * width,
            transcendentals=seq * seq * pairs,
        ),
        name="attend_backward",
    )(table, q, k, v, grad, lse, code, seg)


def gelu_parts(pre):
    t = 1.0 / (1.0 + PHI_STEP * jnp.abs(pre))
    poly = PHI[7] * t + PHI[6]
    for factor in PHI[5::-1]:
        poly = poly * t + factor
    bell = jnp.exp(-0.5 * (pre * pre))
    tail = poly * t * bell
    cdf = jnp.where(pre < 0, tail, 1.0 - tail)
    return pre * cdf, cdf + pre * (bell * 0.3989422804014327)


def norm_stats(values):
    width = values.shape[-1]
    mean = jnp.sum(values, axis=-1, keepdims=True) * (1.0 / width)
    centred = values - mean
    spread = jnp.sum(centred * centred, axis=-1, keepdims=True) * (1.0 / width)
    rate = lax.rsqrt(spread + LN_EPSILON)
    return centred * rate, rate


def norm_back(grad, gain, xhat, rate):
    width = grad.shape[-1]
    scaled = grad * gain
    mean = jnp.sum(scaled, axis=-1, keepdims=True) * (1.0 / width)
    along = jnp.sum(scaled * xhat, axis=-1, keepdims=True) * (1.0 / width)
    return rate * (scaled - mean - xhat * along)


def column_sum(values):
    return jnp.sum(values, axis=0, keepdims=True)


def middle_kernel(
    valid_ref,
    scale_ref,
    ctx_a,
    ctx_b,
    gains,
    shifts,
    bias_in,
    x_hbm,
    teacher_hbm,
    r0a,
    r0b,
    r0c,
    r0d,
    r1a,
    r1b,
    r1c,
    r1d,
    out_hbm,
    dh_hbm,
    cg_a,
    cg_b,
    ffn_send,
    ffn_keep,
    out_send,
    out_keep,
    sums,
    bias_sums,
    w_in,
    w_back,
    w_out,
    xhat_one,
    rate_one,
    mid_low,
    hidden,
    slope,
    acc,
    dh_low,
    pre_grad,
    rows_in,
    rows_out,
    stage16,
    stage32,
    w_sem,
    in_sem,
    out_sem,
    g_sem,
):
    seq, width = acc.shape
    blocks = seq // RB
    half = width // 2
    first, second = (r0a, r0b, r0c, r0d), (r1a, r1b, r1c, r1d)
    out_rows = w_out.shape[0] // 4
    units = w_in.shape[2]
    side = units // 2

    def rows(i):
        return pl.ds(i * RB, RB)

    def fetch(source, i, slot):
        return pltpu.make_async_copy(source.at[rows(i), :], rows_in.at[slot], in_sem.at[slot])

    def out_weights(p, c):
        return pltpu.make_async_copy(
            first[p].at[pl.ds(c * out_rows, out_rows), :],
            w_out.at[pl.ds(p * out_rows, out_rows), pl.ds(c * half, half)],
            w_sem.at[p, c],
        )

    def ffn_weights(p, r):
        source, base = (first[p], 2 * out_rows) if r == 0 else (second[p], 0)
        copies = [
            pltpu.make_async_copy(
                source.at[pl.ds(base, width), :],
                w_in.at[p, :, pl.ds(r * side, side)],
                w_sem.at[p, 2 + 3 * r],
            )
        ]
        for c in range(2):
            copies.append(
                pltpu.make_async_copy(
                    source.at[pl.ds(base + width + c * side, side), :],
                    w_back.at[p, pl.ds(r * side, side), pl.ds(c * half, half)],
                    w_sem.at[p, 3 + 3 * r + c],
                )
            )
        return copies

    out_copies = [out_weights(p, c) for p in range(4) for c in range(2)]
    for copy in out_copies:
        copy.start()
    fetch(x_hbm, 0, 0).start()
    for p in range(4):
        for r in range(2):
            for copy in ffn_weights(p, r):
                copy.start()
    for copy in out_copies:
        copy.wait()

    for i in range(blocks):
        if i + 1 < blocks:
            fetch(x_hbm, i + 1, (i + 1) % 2).start()
        fetch(x_hbm, i, i % 2).wait()
        context = jnp.concatenate([ctx_a[rows(i), :], ctx_b[rows(i), :]], axis=1)
        xhat, rate = norm_stats(dot(context, w_out[...]) + shifts[0:1, :] + rows_in[i % 2])
        xhat_one[rows(i), :] = xhat
        rate_one[rows(i), :] = rate
        mid_low[rows(i), :] = (xhat * gains[0:1, :] + shifts[1:2, :]).astype(LOW)
        acc[rows(i), :] = jnp.zeros((RB, width), F32)
    fetch(teacher_hbm, 0, 0).start()

    def up(p, carry):
        for r in range(2):
            pltpu.make_async_copy(
                first[0].at[pl.ds(0, width), :],
                w_in.at[p, :, pl.ds(r * side, side)],
                w_sem.at[p, 2 + 3 * r],
            ).wait()
            for c in range(2):
                pltpu.make_async_copy(
                    first[0].at[pl.ds(0, side), :],
                    w_back.at[p, pl.ds(r * side, side), pl.ds(c * half, half)],
                    w_sem.at[p, 3 + 3 * r + c],
                ).wait()
        for k in range(seq // FR):
            at = pl.ds(k * FR, FR)
            bias = bias_in[:, pl.ds(pl.multiple_of(p * units, units), units)]
            pre = dot(mid_low[at, :], w_in[p]) + bias
            act, der = gelu_parts(pre)
            act = act.astype(LOW)
            hidden[p, at, :] = act
            slope[p, at, :] = der
            acc[at, :] += dot(act, w_back[p])
        return carry

    lax.fori_loop(0, 4, up, 0)

    zero = jnp.zeros((1, width), F32)
    squares, gain_two, shift_two, shift_mid = zero, zero, zero, zero
    stores = []
    for i in range(blocks):
        if i + 1 < blocks:
            fetch(teacher_hbm, i + 1, (i + 1) % 2).start()
        fetch(teacher_hbm, i, i % 2).wait()
        mid = xhat_one[rows(i), :] * gains[0:1, :] + shifts[1:2, :]
        xhat, rate = norm_stats(acc[rows(i), :] + shifts[2:3, :] + mid)
        output = xhat * gains[1:2, :] + shifts[3:4, :]
        if i >= 2:
            stores[i - 2].wait()
        rows_out[i % 2] = output
        stores.append(
            pltpu.make_async_copy(rows_out.at[i % 2], out_hbm.at[rows(i), :], out_sem.at[i % 2])
        )
        stores[i].start()
        live = (i * RB + lax.broadcasted_iota(jnp.int32, (RB, 1), 0)) < valid_ref[0]
        distance = jnp.where(live, output - rows_in[i % 2], 0.0)
        squares += column_sum(distance * distance)
        out_grad = scale_ref[0] * distance
        gain_two += column_sum(out_grad * xhat)
        shift_two += column_sum(out_grad)
        dh_two = norm_back(out_grad, gains[1:2, :], xhat, rate)
        shift_mid += column_sum(dh_two)
        acc[rows(i), :] = dh_two
        dh_low[rows(i), :] = dh_two.astype(LOW)
    for store in stores[-2:]:
        store.wait()

    sides = (pl.ds(0, side), pl.ds(side, side))

    def moves(stage, target, key):
        copies = [
            (stage.at[0, :, sides[r]], target.at[r, 0], key) for r in range(2)
        ] + [
            (stage.at[1, sides[r], sides[c]], target.at[r, 1, sides[c], :], key)
            for r in range(2)
            for c in range(2)
        ]
        return [
            pltpu.make_async_copy(source, to, g_sem.at[key, n])
            for n, (source, to, key) in enumerate(copies)
        ]

    def down(n, carry, low_turn):
        pair = n if low_turn else 1 - n
        p = 2 * pair + (1 if low_turn else 0)
        total = jnp.zeros((1, units), F32)
        for k in range(seq // FR):
            at = pl.ds(k * FR, FR)
            grad = (dot(dh_low[at, :], w_back[p], NT) * slope[p, at, :]).astype(LOW)
            pre_grad[at, :] = grad
            acc[at, :] += dot(grad, w_in[p], NT)
            total += column_sum(grad.astype(F32))
        bias_sums[:, pl.ds(pl.multiple_of(p * units, units), units)] = total
        stage, target, key = (stage16, ffn_send, 0) if low_turn else (stage32, ffn_keep, 1)
        copies = moves(stage, target.at[pair], key)

        @pl.when(n > 0)
        def _():
            for copy in copies:
                copy.wait()

        stage[0] = dot(mid_low[...], pre_grad[...], TN).astype(stage.dtype)
        stage[1] = dot(hidden[p], dh_low[...], TN).astype(stage.dtype)
        for copy in copies:
            copy.start()
        return carry

    lax.fori_loop(0, 2, functools.partial(down, low_turn=True), 0)
    lax.fori_loop(0, 2, functools.partial(down, low_turn=False), 0)
    for stage, target, key in ((stage16, ffn_send, 0), (stage32, ffn_keep, 1)):
        for copy in moves(stage, target.at[0], key):
            copy.wait()

    gain_one, shift_one, shift_out = zero, zero, zero
    stores = []
    for i in range(blocks):
        grad, xhat = acc[rows(i), :], xhat_one[rows(i), :]
        gain_one += column_sum(grad * xhat)
        shift_one += column_sum(grad)
        dh_one = norm_back(grad, gains[0:1, :], xhat, rate_one[rows(i), :])
        shift_out += column_sum(dh_one)
        if i >= 2:
            stores[i - 2].wait()
        rows_out[i % 2] = dh_one
        stores.append(
            pltpu.make_async_copy(rows_out.at[i % 2], dh_hbm.at[rows(i), :], out_sem.at[i % 2])
        )
        stores[i].start()
        dh_one = dh_one.astype(LOW)
        dh_low[rows(i), :] = dh_one
        grad = dot(dh_one, w_out[...], NT).astype(LOW)
        cg_a[rows(i), :] = grad[:, :half]
        cg_b[rows(i), :] = grad[:, half:]
    for store in stores[-2:]:
        store.wait()
    for group, context in enumerate((ctx_a, ctx_b)):
        grad = dot(context[...], dh_low[...], TN)
        out_keep[group] = grad[:out_rows]
        out_send[group] = grad[out_rows:].astype(LOW)
    sums[...] = jnp.concatenate(
        [gain_one, gain_two, shift_out, shift_one, shift_mid, shift_two, squares, zero], axis=0
    )


def middle(valid, scale, ctx_a, ctx_b, gains, shifts, bias_in, x, teacher, first, second):
    seq, width = x.shape
    half = width // 2
    out_rows = ctx_a.shape[1] // 2
    units = bias_in.shape[1] // 4
    return pl.pallas_call(
        middle_kernel,
        out_shape=(
            shape((seq, width), F32),
            shape((seq, width), F32),
            shape((seq, half), LOW),
            shape((seq, half), LOW),
            shape((2, 2, 2, width, units // 2), LOW),
            shape((2, 2, 2, width, units // 2), F32),
            shape((2, out_rows, width), LOW),
            shape((2, out_rows, width), F32),
            shape((8, width), F32),
            shape((1, 4 * units), F32),
        ),
        in_specs=[SMEM, SMEM, VMEM, VMEM, VMEM, VMEM, VMEM, HBM, HBM] + [HBM] * 8,
        out_specs=(HBM, HBM, VMEM, VMEM, HBM, HBM, VMEM, VMEM, VMEM, VMEM),
        scratch_shapes=[
            pltpu.VMEM((4, width, units), LOW),
            pltpu.VMEM((4, units, width), LOW),
            pltpu.VMEM((4 * out_rows, width), LOW),
            pltpu.VMEM((seq, width), F32),
            pltpu.VMEM((seq, 1), F32),
            pltpu.VMEM((seq, width), LOW),
            pltpu.VMEM((4, seq, units), LOW),
            pltpu.VMEM((4, seq, units), F32),
            pltpu.VMEM((seq, width), F32),
            pltpu.VMEM((seq, width), LOW),
            pltpu.VMEM((seq, units), LOW),
            pltpu.VMEM((2, RB, width), F32),
            pltpu.VMEM((2, RB, width), F32),
            pltpu.VMEM((2, width, units), LOW),
            pltpu.VMEM((2, width, units), F32),
            pltpu.SemaphoreType.DMA((4, 8)),
            pltpu.SemaphoreType.DMA((2,)),
            pltpu.SemaphoreType.DMA((2,)),
            pltpu.SemaphoreType.DMA((2, 6)),
        ],
        compiler_params=pltpu.CompilerParams(vmem_limit_bytes=VMEM_LIMIT),
        cost_estimate=pl.CostEstimate(
            flops=6 * seq * width * (8 * units + width),
            bytes_accessed=30 << 20,
            transcendentals=2 * seq * 4 * units,
        ),
        name="middle",
    )(valid, scale, ctx_a, ctx_b, gains, shifts, bias_in, x, teacher, *first, *second)


def swap(values, axis, bit):
    size = lax.axis_size(axis)
    return lax.ppermute(values, axis, [(i, i ^ (1 << bit)) for i in range(size)])


def bits_of(axis):
    return int(math.log2(lax.axis_size(axis)))


def partner(axis, bit):
    here = {name: lax.axis_index(name) for name in ("dp", "tensor")}
    here[axis] = here[axis] ^ (1 << bit)
    return here["dp"], here["tensor"]


def greet(partners):
    barrier = pltpu.get_barrier_semaphore()
    for device in partners:
        pl.semaphore_signal(
            barrier, inc=1, device_id=device, device_id_type=pl.DeviceIdType.MESH
        )
    pl.semaphore_wait(barrier, len(partners))


def count_kernel(dp_bits, lengths_ref, out_ref, held, send_sem, recv_sem):
    greet([partner("dp", bit) for bit in range(dp_bits)])
    total = jnp.full(out_ref.shape, 0, jnp.int32)
    for i in range(lengths_ref.shape[0]):
        total += lengths_ref[i]
    for bit in range(dp_bits):
        held[2 * bit] = total
        copy = pltpu.make_async_remote_copy(
            src_ref=held.at[2 * bit],
            dst_ref=held.at[2 * bit + 1],
            send_sem=send_sem.at[bit],
            recv_sem=recv_sem.at[bit],
            device_id=partner("dp", bit),
            device_id_type=pl.DeviceIdType.MESH,
        )
        copy.start()
        copy.wait()
        total = total + held[2 * bit + 1]
    out_ref[...] = total


def count_tokens(lengths):
    dp_bits = bits_of("dp")
    return pl.pallas_call(
        functools.partial(count_kernel, dp_bits),
        out_shape=shape((8, 128), jnp.int32),
        in_specs=[SMEM],
        out_specs=VMEM,
        scratch_shapes=[
            pltpu.VMEM((2 * dp_bits, 8, 128), jnp.int32),
            pltpu.SemaphoreType.DMA((dp_bits,)),
            pltpu.SemaphoreType.DMA((dp_bits,)),
        ],
        compiler_params=pltpu.CompilerParams(collective_id=1, has_side_effects=True),
        name="count_tokens",
    )(lengths)


def add_rows(out, terms, chunk=96):
    rows = out.shape[0]
    chunk = min(chunk, rows)

    def step(i, carry):
        at = pl.ds(pl.multiple_of(i * chunk, chunk), chunk)
        total = terms[0][at, :].astype(F32)
        for term in terms[1:]:
            total += term[at, :].astype(F32)
        out[at, :] = total.astype(out.dtype)
        return carry

    lax.fori_loop(0, rows // chunk, step, 0)


def finish_kernel(
    dp_bits,
    x_ref,
    w0,
    w1,
    w2,
    w3,
    dqa,
    dka,
    dva,
    dqb,
    dkb,
    dvb,
    osend,
    okeep,
    dh_hbm,
    ffn_keep,
    ffn_core,
    ffn_x,
    ffn_y,
    small_ref,
    gx_hbm,
    result,
    small_out,
    loads,
    loads16,
    keep,
    send,
    core,
    y_send,
    y_recv,
    x_send,
    x_recv,
    total,
    z_send,
    z_recv,
    bias_ref,
    small_held,
    rows_in,
    rows_out,
    cross,
    load_sem,
    send_sem,
    recv_sem,
    in_sem,
    out_sem,
):
    seq, width = x_ref.shape
    half = width // 2
    piece = dqa.shape[1] // 2
    blocks = seq // RB
    place = lax.axis_index("dp")
    index = lax.axis_index("tensor")
    side = place & 1
    core_at, y_at = partner("tensor", 0), partner("tensor", 1)
    dp_at = [partner("dp", bit) for bit in range(dp_bits)]
    greet([core_at, y_at] + dp_at)
    started = {}

    def remote(key, source, target, device):
        n = len(started)
        started[key] = pltpu.make_async_remote_copy(
            src_ref=source,
            dst_ref=target,
            send_sem=send_sem.at[n],
            recv_sem=recv_sem.at[n],
            device_id=device,
            device_id_type=pl.DeviceIdType.MESH,
        )
        started[key].start()

    def arrive(key):
        started[key].wait_recv()

    own = []
    for n, (pair, r, w) in enumerate(((1, 0, 0), (0, 1, 1), (0, 0, 0), (0, 0, 1))):
        own.append(
            [
                pltpu.make_async_copy(ffn_keep.at[pair, r, w], loads.at[n], load_sem.at[n, 0]),
                pltpu.make_async_copy(ffn_core.at[pair, r, w], loads16.at[n, 0], load_sem.at[n, 1]),
                pltpu.make_async_copy(
                    ffn_x.at[pair] if w == 0 else ffn_y.at[r], loads16.at[n, 1], load_sem.at[n, 2]
                ),
            ]
        )
        for copy in own[n]:
            copy.start()

    def fetch(i):
        return pltpu.make_async_copy(
            dh_hbm.at[pl.ds(i * RB, RB), :], rows_in.at[i % 2], in_sem.at[i % 2]
        )

    fetch(0).start()

    def load(n, out):
        for copy in own[n]:
            copy.wait()
        add_rows(out, [loads.at[n], loads16.at[n, 0], loads16.at[n, 1]])

    load(0, y_send.at[2])
    remote("in y", y_send.at[2], y_recv.at[2], y_at)
    load(1, x_send.at[1])
    remote("back x", x_send.at[1], x_recv.at[1], dp_at[0])

    grads = ((dqa, dka, dva), (dqb, dkb, dvb))
    mine = pl.ds(pl.multiple_of(side * half, half), half)
    other = pl.ds(pl.multiple_of((1 - side) * half, half), half)
    for g in (1, 0):
        for i in range(3):
            cross[...] = dot(grads[g][i][...], x_ref[...], TN)
            at = slice(i * piece, (i + 1) * piece)
            for n, lanes in enumerate((mine, other)):
                keep[g, n, at, :] = cross[:piece, lanes]
                send[g, n, at, :] = cross[piece:, lanes].astype(LOW)
            bias_ref[g, i : i + 1, :] = column_sum(grads[g][i][...].astype(F32))
        for n, lanes in enumerate((mine, other)):
            keep[g, n, 3 * piece :, :] = okeep[g, :, lanes]
            send[g, n, 3 * piece :, :] = osend[g, :, lanes]
        for n in (1, 0):
            remote(("core", g, n), send.at[g, n], core.at[g, n], core_at)
    for n in (1, 0):
        arrive(("core", 1, n))
        add_rows(y_send.at[n], [keep.at[1, n], core.at[1, n]])
        remote(("y", n), y_send.at[n], y_recv.at[n], y_at)

    small_held[0] = jnp.zeros(small_held.shape[1:], F32)
    small_held[0, 16:24, :] = small_ref[0:8, :]
    for p in range(4):
        row = 4 * (index ^ p)
        g, n = p // 2, p % 2
        half_mine = small_ref[8 + p : 9 + p, :half]
        half_other = small_ref[8 + p : 9 + p, half:]
        low_half = jnp.where(side == 0, half_mine, half_other)
        high_half = jnp.where(side == 0, half_other, half_mine)
        small_held[0, pl.ds(row, 1), :] = jnp.concatenate([low_half, high_half], axis=1)
        for i, k in enumerate((0, 2)):
            values = bias_ref[g, k : k + 1, :]
            if n == 1:
                values = pltpu.roll(values, 2 * piece - piece, 1)
            small_held[0, pl.ds(row + 1 + i, 1), :half] = values

    weights = ((w0, w1), (w2, w3))
    stores = []

    def inputs_rows(b):
        at = pl.ds(b * RB, RB)
        if b + 1 < blocks:
            fetch(b + 1).start()
        fetch(b).wait()
        grad = rows_in[b % 2]
        for g in range(2):
            for i in range(3):
                rows = slice(i * piece, (i + 1) * piece)
                w = jnp.concatenate([ref[rows, :] for ref in weights[g]], axis=0)
                grad += dot(grads[g][i][at, :], w)
        if b >= 2:
            stores[b - 2].wait()
        rows_out[b % 2] = grad
        stores.append(
            pltpu.make_async_copy(rows_out.at[b % 2], gx_hbm.at[at, :], out_sem.at[b % 2])
        )
        stores[b].start()

    def small_step(n):
        bits = [core_at, y_at] + dp_at
        remote(("small", n), small_held.at[2 * n], small_held.at[2 * n + 1], bits[n])

    def small_sum(n):
        arrive(("small", n))
        out = small_held.at[2 * n + 2] if n < dp_bits + 1 else small_out
        out[...] = small_held[2 * n] + small_held[2 * n + 1]

    rows_of = [width]
    for bit in range(1, min(dp_bits, 3)):
        rows_of.append(rows_of[-1] // 2)

    def offset(level):
        at = 0
        for bit in range(1, level + 1):
            at = at + ((place >> bit) & 1) * rows_of[bit]
        return pl.multiple_of(at, rows_of[level])

    def other_offset(level):
        return pl.multiple_of(
            offset(level - 1) + (1 - ((place >> level) & 1)) * rows_of[level], rows_of[level]
        )

    levels = min(dp_bits, 3) - 1

    def scatter(w, level):
        size = rows_of[level]
        out = z_send.at[w, pl.ds(0, size), :] if level == 1 else z_send.at[w, pl.ds(rows_of[1], size), :]
        into = z_recv.at[w, pl.ds(0, size), :] if level == 1 else z_recv.at[w, pl.ds(rows_of[1], size), :]
        add_rows(out, [total.at[w, pl.ds(other_offset(level), size), :]])
        remote((w, "z", level), out, into, dp_at[level])

    def collect(w, level):
        size = rows_of[level]
        arrive((w, "z", level))
        into = z_recv.at[w, pl.ds(0, size), :] if level == 1 else z_recv.at[w, pl.ds(rows_of[1], size), :]
        mine = total.at[w, pl.ds(offset(level), size), :]
        add_rows(mine, [mine, into])

    def settle(w):
        size = rows_of[levels]
        at = pl.ds(offset(levels), size)
        add_rows(result.at[w, 0, at, :], [total.at[w, at, :]])
        for bit in range(levels + 1, dp_bits):
            spare = result.at[w, 0, at, :]
            into = z_recv.at[w, pl.ds(rows_of[1] + (bit - levels) * size, size), :]
            remote((w, "all", bit), spare, into, dp_at[bit])
            started[(w, "all", bit)].wait_send()
            arrive((w, "all", bit))
            add_rows(spare, [spare, into])

    def spread(w, level):
        if level == 0:
            remote((w, "gather", 0), result.at[w, 0], result.at[w, 1], dp_at[0])
        else:
            rows = result.at[w, 0, pl.ds(offset(level), rows_of[level]), :]
            remote((w, "gather", level), rows, rows, dp_at[level])

    small_step(0)
    for b in range(blocks):
        inputs_rows(b)
        if b < dp_bits + 2:
            small_sum(b)
            if b + 1 < dp_bits + 2:
                small_step(b + 1)

    load(2, total.at[0])
    load(3, total.at[1])
    arrive("in y")
    add_rows(total.at[0], [total.at[0], y_recv.at[2]])
    scatter(0, 1)
    arrive("back x")
    add_rows(total.at[1], [total.at[1], x_recv.at[1]])
    scatter(1, 1)
    for n in range(blocks, dp_bits + 2):
        small_sum(n)
        if n + 1 < dp_bits + 2:
            small_step(n + 1)
    arrive(("core", 0, 1))
    arrive(("core", 0, 0))
    collect(0, 1)
    scatter(0, 2)
    arrive(("y", 1))
    add_rows(x_send.at[0], [keep.at[0, 1], core.at[0, 1], y_recv.at[1]])
    remote("qkv x", x_send.at[0], x_recv.at[0], dp_at[0])
    collect(1, 1)
    scatter(1, 2)
    collect(0, 2)
    settle(0)
    spread(0, 2)
    collect(1, 2)
    settle(1)
    spread(1, 2)
    arrive((0, "gather", 2))
    spread(0, 1)
    arrive(("y", 0))
    add_rows(total.at[2], [keep.at[0, 0], core.at[0, 0], y_recv.at[0]])
    arrive("qkv x")
    add_rows(total.at[2], [total.at[2], x_recv.at[0]])
    scatter(2, 1)
    arrive((1, "gather", 2))
    spread(1, 1)
    arrive((0, "gather", 1))
    spread(0, 0)
    collect(2, 1)
    scatter(2, 2)
    arrive((1, "gather", 1))
    spread(1, 0)
    collect(2, 2)
    settle(2)
    spread(2, 2)
    arrive((2, "gather", 2))
    spread(2, 1)
    arrive((2, "gather", 1))
    spread(2, 0)
    for w in range(3):
        arrive((w, "gather", 0))
    for key, copy in started.items():
        if not (isinstance(key, tuple) and len(key) == 3 and key[1] == "all"):
            copy.wait_send()
    for store in stores[-2:]:
        store.wait()


def finish(x, weights, grads, osend, okeep, dh, ffn_keep, ffn_core, ffn_x, ffn_y, small):
    seq, width = x.shape
    half = width // 2
    piece = grads[0].shape[1] // 2
    dp_bits = bits_of("dp")
    slab = (width, half)
    copies = 9 + dp_bits + 2 + 3 * (2 + 3 + max(dp_bits - 3, 0))
    return pl.pallas_call(
        functools.partial(finish_kernel, dp_bits),
        out_shape=(
            shape((seq, width), F32),
            shape((3, 2) + slab, LOW),
            shape((24, width), F32),
        ),
        in_specs=[VMEM] * 13 + [HBM] * 5 + [VMEM],
        out_specs=(HBM, VMEM, VMEM),
        scratch_shapes=[
            pltpu.VMEM((4,) + slab, F32),
            pltpu.VMEM((4, 2) + slab, LOW),
            pltpu.VMEM((2, 2) + slab, F32),
            pltpu.VMEM((2, 2) + slab, LOW),
            pltpu.VMEM((2, 2) + slab, LOW),
            pltpu.VMEM((3,) + slab, LOW),
            pltpu.VMEM((3,) + slab, LOW),
            pltpu.VMEM((2,) + slab, LOW),
            pltpu.VMEM((2,) + slab, LOW),
            pltpu.VMEM((3,) + slab, F32),
            pltpu.VMEM((3, width, half), LOW),
            pltpu.VMEM((3, 2 * width, half), LOW),
            pltpu.VMEM((2, 8, 2 * piece), F32),
            pltpu.VMEM((2 * dp_bits + 4, 24, width), F32),
            pltpu.VMEM((2, RB, width), F32),
            pltpu.VMEM((2, RB, width), F32),
            pltpu.VMEM((2 * piece, width), F32),
            pltpu.SemaphoreType.DMA((4, 3)),
            pltpu.SemaphoreType.DMA((copies,)),
            pltpu.SemaphoreType.DMA((copies,)),
            pltpu.SemaphoreType.DMA((2,)),
            pltpu.SemaphoreType.DMA((2,)),
        ],
        compiler_params=pltpu.CompilerParams(
            vmem_limit_bytes=VMEM_LIMIT, collective_id=2, has_side_effects=True
        ),
        cost_estimate=pl.CostEstimate(
            flops=48 * seq * width * piece, bytes_accessed=50 << 20, transcendentals=0
        ),
        name="finish",
    )(x, *weights, *grads, osend, okeep, dh, ffn_keep, ffn_core, ffn_x, ffn_y, small)


def widen_kernel(side_ref, result, qkv_ref, out_ref, in_ref, back_ref):
    half = result.shape[3]
    rows = out_ref.shape[0]
    piece = qkv_ref.shape[2]
    side = side_ref[0]
    for n in range(2):
        natural = (side + n) % 2
        at = pl.ds(pl.multiple_of(natural * half, half), half)
        in_ref[:, at] = result[0, n].astype(F32)
        for c in range(2):
            back_ref[at, c * half : (c + 1) * half] = result[1, n, c * half : (c + 1) * half, :].astype(F32)
        for i in range(3):
            qkv_ref[i, at, :] = result[2, n, i * piece : (i + 1) * piece, :].astype(F32).T
        out_ref[:, at] = result[2, n, 3 * piece :, :].astype(F32)


def widen(side, result, piece, rows):
    width, half = result.shape[2:]
    return pl.pallas_call(
        widen_kernel,
        out_shape=(
            shape((3, width, piece), F32),
            shape((rows, width), F32),
            shape((width, 2 * half), F32),
            shape((2 * half, width), F32),
        ),
        in_specs=[SMEM, VMEM],
        out_specs=(VMEM,) * 4,
        compiler_params=pltpu.CompilerParams(vmem_limit_bytes=VMEM_LIMIT),
        name="widen",
    )(side, result)


def per_device(
    inputs,
    w_qkv,
    b_qv,
    w_out,
    w_in,
    b_in,
    w_back,
    norm_gains,
    shifts,
    segment_ids,
    valid_lengths,
    teacher,
):
    own_seqs, seq, width = inputs.shape
    assert own_seqs == 1 and lax.axis_size("tensor") == 4
    total_slots = seq * lax.axis_size("tensor") * lax.axis_size("dp")
    half = width // 2
    piece = w_qkv.shape[2]
    units = w_in.shape[1]
    index = lax.axis_index("tensor")
    side = (lax.axis_index("dp") & 1).astype(jnp.int32)
    side_row = side.reshape(1)
    x = inputs.reshape(seq, width)

    near = round_qkv(side_row, w_qkv, b_qv, b_in[None, :])
    core = swap(near, "tensor", 0)
    far = swap(near, "tensor", 1)
    first, second, x_low = round_rest(side_row, w_out, w_in, w_back, x)
    first_far = swap(first, "tensor", 1)

    valid = lax.dynamic_index_in_dim(valid_lengths, index, keepdims=False)
    segments = lax.dynamic_index_in_dim(segment_ids, index, keepdims=False)
    positions = jnp.arange(seq, dtype=jnp.int32)
    code = jnp.where(positions < valid, segments, -1)[:, None]
    seg = segments[None, :]
    table = span_tables(segments, valid, seq)

    qa, ka, va, ctx_a, lse_a = attend_forward(table, x_low, near, core, code, seg)
    first, second, far, first_far, lengths, ctx_a = lax.optimization_barrier(
        (first, second, far, first_far, valid_lengths, ctx_a)
    )
    core_far = swap(far, "tensor", 0)
    second_far = swap(first_far[2 * piece :], "dp", 0)
    first_core = swap(first, "tensor", 0)
    second_core = swap(second, "tensor", 0)
    first_core_far = swap(first_far, "tensor", 0)
    token_count = count_tokens(lengths)[0, 0].astype(F32)
    qb, kb, vb, ctx_b, lse_b = attend_forward(table, x_low, far, core_far, code, seg)
    second_far, ctx_b = lax.optimization_barrier((second_far, ctx_b))
    second_core_far = swap(second_far, "tensor", 0)
    at = 3 * piece
    bias_in = jnp.concatenate(
        [
            part[at : at + 1].astype(F32)
            + part[at + 1 : at + 2].astype(F32)
            + part[at + 2 : at + 3].astype(F32)
            for part in (near, core, far, core_far)
        ],
        axis=1,
    )
    scale = (total_slots / token_count).reshape(1)
    output, dh_one, cg_a, cg_b, ffn_send, ffn_keep, out_send, out_keep, sums, bias_sums = middle(
        valid.reshape(1),
        scale,
        ctx_a,
        ctx_b,
        norm_gains,
        shifts,
        bias_in,
        x,
        teacher.reshape(seq, width),
        (first, first_core, first_far, first_core_far),
        (second, second_core, second_far, second_core_far),
    )
    ffn_core = swap(ffn_send, "tensor", 0)
    grads_b = attend_backward(table, qb, kb, vb, cg_b, lse_b, code, seg)
    ffn_core, ffn_keep, *grads_b = lax.optimization_barrier((ffn_core, ffn_keep, *grads_b))
    to_x = (ffn_keep[:, 1, 0] + ffn_core[:, 1, 0].astype(F32)).astype(LOW)
    to_y = (ffn_keep[1, :, 1] + ffn_core[1, :, 1].astype(F32)).astype(LOW)
    to_x, to_y, cg_a = lax.optimization_barrier((to_x, to_y, cg_a))
    ffn_x = swap(to_x, "dp", 0)
    ffn_y = swap(to_y, "tensor", 1)
    grads_a = attend_backward(table, qa, ka, va, cg_a, lse_a, code, seg)
    small = jnp.concatenate([sums, bias_sums.reshape(4, units), jnp.zeros((4, width), F32)], axis=0)
    grad_inputs, slabs, small = finish(
        x_low,
        (near, core, far, core_far),
        (*grads_a, *grads_b),
        out_send,
        out_keep,
        dh_one,
        ffn_keep,
        ffn_core,
        ffn_x,
        ffn_y,
        small,
    )
    grad_w_qkv, grad_w_out, grad_w_in, grad_w_back = widen(side_row, slabs, piece, w_out.shape[0])
    own = lax.dynamic_slice_in_dim(small, 4 * index, 4)
    loss = jnp.sum(small[22]) / (2.0 * width * token_count)
    return (
        output.reshape(own_seqs, seq, width),
        loss,
        grad_inputs.reshape(own_seqs, seq, width),
        grad_w_qkv,
        own[1:3, :piece],
        grad_w_out,
        grad_w_in,
        own[0],
        grad_w_back,
        small[16:18],
        small[18:22],
    )


def solution(mesh):
    return jax.shard_map(
        per_device,
        mesh=mesh,
        in_specs=(
            P(("dp", "tensor"), None, None),
            P(None, None, "tensor"),
            P(None, "tensor"),
            P("tensor", None),
            P(None, "tensor"),
            P("tensor"),
            P("tensor", None),
            P(),
            P(),
            P("dp", None),
            P("dp"),
            P(("dp", "tensor"), None, None),
        ),
        out_specs=(
            P(("dp", "tensor"), None, None),
            P(),
            P(("dp", "tensor"), None, None),
            P(None, None, "tensor"),
            P(None, "tensor"),
            P("tensor", None),
            P(None, "tensor"),
            P("tensor"),
            P("tensor", None),
            P(),
            P(),
        ),
        check_vma=False,
    )
```

```python
import functools
import math

import jax
import jax.numpy as jnp
from jax import lax
from jax.experimental import pallas as pl
from jax.experimental.pallas import tpu as pltpu
from jax.sharding import PartitionSpec as P

HD = 64
LN_EPSILON = 1e-05
MASKED_SCORE = -1000000000.0
QB = 256
KB = 128
RB = 256
FR = 256
NT = ((1,), (1,))
TN = ((0,), (0,))
PHI = (
    0.09255110872,
    0.09001568156,
    0.1049848251,
    0.006341010132,
    0.2381524984,
    -0.2150534404,
    0.2551771707,
    -0.07216888208,
)
PHI_STEP = 0.23164188826636045

VMEM_LIMIT = 63 << 20
VMEM = pl.BlockSpec(memory_space=pltpu.VMEM)
SMEM = pl.BlockSpec(memory_space=pltpu.SMEM)
HBM = pl.BlockSpec(memory_space=pl.ANY)
LOW = jnp.bfloat16
F32 = jnp.float32


def dot(left, right, dims=((1,), (0,))):
    return lax.dot_general(left, right, (dims, ((), ())), preferred_element_type=jnp.float32)


def shape(dims, dtype):
    return jax.ShapeDtypeStruct(dims, dtype)


def swap(values, axis, bit):
    size = lax.axis_size(axis)
    return lax.ppermute(values, axis, [(i, i ^ (1 << bit)) for i in range(size)])


def bits_of(axis):
    return int(math.log2(lax.axis_size(axis)))


def partner(axis, bit):
    here = {name: lax.axis_index(name) for name in ("dp", "tensor")}
    here[axis] = here[axis] ^ (1 << bit)
    return here["dp"], here["tensor"]


def greet(partners):
    barrier = pltpu.get_barrier_semaphore()
    for device in partners:
        pl.semaphore_signal(
            barrier, inc=1, device_id=device, device_id_type=pl.DeviceIdType.MESH
        )
    pl.semaphore_wait(barrier, len(partners))


def three_parts(values):
    first = values.astype(LOW)
    rest = values - first.astype(F32)
    second = rest.astype(LOW)
    return first, second, (rest - second.astype(F32)).astype(LOW)


def round_qkv_kernel(side_ref, w_ref, bqv_ref, bin_ref, out_ref):
    piece = w_ref.shape[1]
    width = w_ref.shape[2]
    half = bin_ref.shape[1] // 2
    for i in range(3):
        out_ref[i * piece : (i + 1) * piece, :] = w_ref[i].astype(LOW)
    mine = bin_ref[:, pl.ds(pl.multiple_of(side_ref[0] * half, half), half)]
    other = bin_ref[:, pl.ds(pl.multiple_of((1 - side_ref[0]) * half, half), half)]
    pad = jnp.zeros((1, width - piece), F32)
    rows = [jnp.concatenate([mine, other], axis=1)]
    rows += [jnp.concatenate([bqv_ref[i : i + 1, :], pad], axis=1) for i in range(2)]
    parts = [part.astype(F32) for row in rows for part in three_parts(row)]
    parts += [jnp.zeros((1, width), F32)] * 7
    out_ref[3 * piece :, :] = jnp.concatenate(parts, axis=0).astype(LOW)


def round_qkv(side, w_qkv, b_qv, b_in):
    _, piece, width = w_qkv.shape
    return pl.pallas_call(
        round_qkv_kernel,
        out_shape=shape((3 * piece + 16, width), LOW),
        in_specs=[SMEM, VMEM, VMEM, VMEM],
        out_specs=VMEM,
        compiler_params=pltpu.CompilerParams(vmem_limit_bytes=VMEM_LIMIT),
        name="round_qkv",
    )(side, w_qkv, b_qv, b_in)


def round_rest_kernel(side_ref, wo_ref, wi_ref, wb_ref, x_ref, first_ref, second_ref, x_low_ref):
    rows, width = wo_ref.shape
    half = width // 2
    for c in range(2):
        first_ref[c * rows : (c + 1) * rows, :] = wo_ref[:, c * half : (c + 1) * half].astype(LOW)
    for out, base, side in ((first_ref, 2 * rows, side_ref[0]), (second_ref, 0, 1 - side_ref[0])):
        at = pl.ds(pl.multiple_of(side * half, half), half)
        out[base : base + width, :] = wi_ref[:, at].astype(LOW)
        for c in range(2):
            start = base + width + c * half
            out[start : start + half, :] = wb_ref[at, c * half : (c + 1) * half].astype(LOW)
    x_low_ref[...] = x_ref[...].astype(LOW)


def round_rest(side, w_out, w_in, w_back, x):
    rows, width = w_out.shape
    half = width // 2
    return pl.pallas_call(
        round_rest_kernel,
        out_shape=(
            shape((2 * rows + 2 * width, half), LOW),
            shape((2 * width, half), LOW),
            shape(x.shape, LOW),
        ),
        in_specs=[SMEM, VMEM, VMEM, VMEM, VMEM],
        out_specs=(VMEM, VMEM, VMEM),
        compiler_params=pltpu.CompilerParams(vmem_limit_bytes=VMEM_LIMIT),
        name="round_rest",
    )(side, w_out, w_in, w_back, x)


def span_tables(segments, valid, seq):
    blocks = seq // QB
    firsts, lasts = segments[::QB], segments[QB - 1 :: QB]
    low = jnp.sum((segments[None, :] < firsts[:, None]).astype(jnp.int32), axis=1)
    high = jnp.sum((segments[None, :] <= lasts[:, None]).astype(jnp.int32), axis=1)
    own_end = (jnp.arange(blocks, dtype=jnp.int32) + 1) * QB
    high = jnp.maximum(jnp.minimum(high, valid), own_end)
    low_block = low // KB
    high_block = (high + KB - 1) // KB
    return jnp.stack([low_block, high_block - low_block]).astype(jnp.int32)


def make_bias(bias_ref, block, low, count, code_ref, seg_ref):
    dims = (count * KB, QB)
    codes = code_ref[pl.ds(pl.multiple_of(low * KB, KB), count * KB), :]
    segs = seg_ref[:, pl.ds(pl.multiple_of(block * QB, QB), QB)]
    key_at = low * KB + lax.broadcasted_iota(jnp.int32, dims, 0)
    query_at = block * QB + lax.broadcasted_iota(jnp.int32, dims, 1)
    allowed = (codes == segs) | (key_at == query_at)
    bias_ref[block, : count * KB, :] = jnp.where(allowed, 0.0, MASKED_SCORE)


def one_head(values, head):
    lane = lax.broadcasted_iota(jnp.int32, values.shape, 1)
    keep = (lane < HD) if head == 0 else (lane >= HD)
    return jnp.where(keep, values, jnp.zeros_like(values))


def forward_kernel(
    table_ref,
    x_ref,
    w0_ref,
    w1_ref,
    code_ref,
    seg_ref,
    q_ref,
    k_ref,
    v_ref,
    ctx_ref,
    lse_ref,
    weights,
    biases,
    vt_ref,
    bias_ref,
):
    pair, block = pl.program_id(0), pl.program_id(1)
    low, total = table_ref[0, block], table_ref[1, block]
    piece = (w0_ref.shape[0] - 16) // 3

    @pl.when((pair == 0) & (block == 0))
    def _():
        for i in range(3):
            for n, ref in enumerate((w0_ref, w1_ref)):
                at = 0
                while at < piece:
                    spot = n * piece + at
                    size = min(128 - spot % 128, piece - at)
                    weights[spot // 128, i * 128 + spot % 128 : i * 128 + spot % 128 + size, :] = ref[
                        i * piece + at : i * piece + at + size, :
                    ]
                    at += size
        lane = lax.broadcasted_iota(jnp.int32, (1, x_ref.shape[1]), 1)
        for i in range(3):
            if i == 1:
                continue
            base = 3 * piece + (3 if i == 0 else 6)
            both = [
                sum(ref[base + part : base + part + 1, :].astype(F32) for part in range(3))
                for ref in (w0_ref, w1_ref)
            ]
            row = jnp.where(lane < piece, both[0], pltpu.roll(both[1], piece, 1))
            for p in range(2 * piece // 128):
                biases[p, :, i * 128 : (i + 1) * 128] = row[:, p * 128 : (p + 1) * 128]
        for p in range(2 * piece // 128):
            biases[p, :, 128:256] = jnp.zeros((1, 128), F32)

    @pl.when(block == 0)
    def _():
        qkv = (dot(x_ref[...], weights[pair], NT) + biases[pair]).astype(LOW)
        q_ref[...] = qkv[:, :128]
        k_ref[...] = qkv[:, 128:256]
        v_ref[...] = qkv[:, 256:]
        vt_ref[...] = qkv[:, 256:].T

    def run(count):
        @pl.when(pair == 0)
        def _():
            make_bias(bias_ref, block, low, count, code_ref, seg_ref)

        bias = bias_ref[block, : count * KB, :]
        rows = pl.ds(pl.multiple_of(low * KB, KB), count * KB)
        keys = k_ref[rows, :]
        queries = q_ref[pl.ds(pl.multiple_of(block * QB, QB), QB), :] * jnp.asarray(0.125, LOW)
        outs, sums = [], []
        for head in range(2):
            scores = dot(keys, one_head(queries, head), NT) + bias
            peak = jnp.max(scores, axis=0, keepdims=True)
            powers = jnp.exp(scores - peak)
            mass = jnp.sum(powers, axis=0, keepdims=True)
            probs = (powers * (1.0 / mass)).astype(LOW)
            outs.append(dot(vt_ref[head * HD : (head + 1) * HD, rows], probs))
            sums.append(peak + jnp.log(mass))
        ctx_ref[...] = jnp.concatenate(outs, axis=0).T.astype(LOW)
        lse_ref[0, 0:1, :] = sums[0]
        lse_ref[0, 1:2, :] = sums[1]

    for count in range(2, k_ref.shape[0] // KB + 1):
        pl.when(total == count)(functools.partial(run, count))


def backward_kernel(
    table_ref,
    q_ref,
    k_ref,
    v_ref,
    g_ref,
    lse_ref,
    code_ref,
    seg_ref,
    dq_ref,
    dk_ref,
    dv_ref,
    kt_ref,
    bias_ref,
    dk_sum,
    dv_sum,
):
    pair, block = pl.program_id(0), pl.program_id(1)
    low, total = table_ref[0, block], table_ref[1, block]

    @pl.when(block == 0)
    def _():
        kt_ref[...] = k_ref[...].T
        dk_sum[...] = jnp.zeros_like(dk_sum)
        dv_sum[...] = jnp.zeros_like(dv_sum)

    def run(count):
        @pl.when(pair == 0)
        def _():
            make_bias(bias_ref, block, low, count, code_ref, seg_ref)

        bias = bias_ref[block, : count * KB, :]
        rows = pl.ds(pl.multiple_of(low * KB, KB), count * KB)
        keys, values = k_ref[rows, :], v_ref[rows, :]
        queries = q_ref[...] * jnp.asarray(0.125, LOW)
        grads = g_ref[...]
        outs = []
        for head in range(2):
            query, grad = one_head(queries, head), one_head(grads, head)
            probs = jnp.exp(dot(keys, query, NT) + bias - lse_ref[0, head : head + 1, :])
            dv_sum[rows, :] += dot(probs.astype(LOW), grad)
            prob_grad = dot(values, grad, NT)
            delta = jnp.sum(probs * prob_grad, axis=0, keepdims=True)
            score_grad = (probs * (prob_grad - delta)).astype(LOW)
            dk_sum[rows, :] += dot(score_grad, query)
            outs.append(dot(kt_ref[head * HD : (head + 1) * HD, rows], score_grad))
        dq_ref[...] = (jnp.concatenate(outs, axis=0).T * 0.125).astype(LOW)

    for count in range(2, k_ref.shape[0] // KB + 1):
        pl.when(total == count)(functools.partial(run, count))

    @pl.when(block == pl.num_programs(1) - 1)
    def _():
        dk_ref[...] = dk_sum[...].astype(LOW)
        dv_ref[...] = dv_sum[...].astype(LOW)


def attend_forward(table, x, first, second, code, seg):
    seq, width = x.shape
    piece = (first.shape[0] - 16) // 3
    pairs, blocks = 2 * piece // 128, seq // QB
    column = pl.BlockSpec((seq, 128), lambda p, i, t: (0, p))
    whole = lambda p, i, t: (0, 0)
    return pl.pallas_call(
        forward_kernel,
        out_shape=(shape((seq, 2 * piece), LOW),) * 4 + (shape((pairs, 8, seq), F32),),
        grid_spec=pltpu.PrefetchScalarGridSpec(
            num_scalar_prefetch=1,
            grid=(pairs, blocks),
            in_specs=[
                pl.BlockSpec((seq, width), whole),
                pl.BlockSpec(first.shape, whole),
                pl.BlockSpec(second.shape, whole),
                pl.BlockSpec((seq, 1), whole),
                pl.BlockSpec((1, seq), whole),
            ],
            out_specs=[
                column,
                column,
                column,
                pl.BlockSpec((QB, 128), lambda p, i, t: (i, p)),
                pl.BlockSpec((1, 8, QB), lambda p, i, t: (p, 0, i)),
            ],
            scratch_shapes=[
                pltpu.VMEM((pairs, 384, width), LOW),
                pltpu.VMEM((pairs, 1, 384), F32),
                pltpu.VMEM((128, seq), LOW),
                pltpu.VMEM((blocks, seq, QB), F32),
            ],
        ),
        compiler_params=pltpu.CompilerParams(vmem_limit_bytes=VMEM_LIMIT),
        cost_estimate=pl.CostEstimate(
            flops=16 * seq * seq * piece + 12 * seq * width * piece,
            bytes_accessed=16 * seq * piece,
            transcendentals=seq * seq * pairs,
        ),
        name="attend_forward",
    )(table, x, first, second, code, seg)


def attend_backward(table, q, k, v, grad, lse, code, seg):
    seq, width = grad.shape
    pairs, blocks = width // 128, seq // QB
    block = pl.BlockSpec((QB, 128), lambda p, i, t: (i, p))
    column = pl.BlockSpec((seq, 128), lambda p, i, t: (0, p))
    return pl.pallas_call(
        backward_kernel,
        out_shape=(shape((seq, width), LOW),) * 3,
        grid_spec=pltpu.PrefetchScalarGridSpec(
            num_scalar_prefetch=1,
            grid=(pairs, blocks),
            in_specs=[
                block,
                column,
                column,
                block,
                pl.BlockSpec((1, 8, QB), lambda p, i, t: (p, 0, i)),
                pl.BlockSpec((seq, 1), lambda p, i, t: (0, 0)),
                pl.BlockSpec((1, seq), lambda p, i, t: (0, 0)),
            ],
            out_specs=[block, column, column],
            scratch_shapes=[
                pltpu.VMEM((128, seq), LOW),
                pltpu.VMEM((blocks, seq, QB), F32),
                pltpu.VMEM((seq, 128), F32),
                pltpu.VMEM((seq, 128), F32),
            ],
        ),
        compiler_params=pltpu.CompilerParams(vmem_limit_bytes=VMEM_LIMIT),
        cost_estimate=pl.CostEstimate(
            flops=16 * seq * seq * width,
            bytes_accessed=16 * seq * width,
            transcendentals=seq * seq * pairs,
        ),
        name="attend_backward",
    )(table, q, k, v, grad, lse, code, seg)


def gelu_parts(pre):
    t = 1.0 / (1.0 + PHI_STEP * jnp.abs(pre))
    poly = PHI[7] * t + PHI[6]
    for factor in PHI[5::-1]:
        poly = poly * t + factor
    bell = jnp.exp(-0.5 * (pre * pre))
    tail = poly * t * bell
    cdf = jnp.where(pre < 0, tail, 1.0 - tail)
    return pre * cdf, cdf + pre * (bell * 0.3989422804014327)


def norm_stats(values):
    width = values.shape[-1]
    mean = jnp.sum(values, axis=-1, keepdims=True) * (1.0 / width)
    centred = values - mean
    spread = jnp.sum(centred * centred, axis=-1, keepdims=True) * (1.0 / width)
    rate = lax.rsqrt(spread + LN_EPSILON)
    return centred * rate, rate


def norm_back(grad, gain, xhat, rate):
    width = grad.shape[-1]
    scaled = grad * gain
    mean = jnp.sum(scaled, axis=-1, keepdims=True) * (1.0 / width)
    along = jnp.sum(scaled * xhat, axis=-1, keepdims=True) * (1.0 / width)
    return rate * (scaled - mean - xhat * along)


def column_sum(values):
    return jnp.sum(values, axis=0, keepdims=True)


def middle_kernel(
    total_slots,
    dp_bits,
    valid_ref,
    lengths_ref,
    ctx_a,
    ctx_b,
    gains,
    shifts,
    x_hbm,
    teacher_hbm,
    qa,
    qb,
    qc,
    qd,
    r0a,
    r0b,
    r0c,
    r0d,
    r1a,
    r1b,
    r1c,
    r1d,
    out_hbm,
    dh_hbm,
    cg_a,
    cg_b,
    core_hbm,
    to_x,
    to_y,
    rest,
    out_send,
    out_keep,
    sums,
    bias_sums,
    count_ref,
    w_in,
    w_back,
    w_out,
    bias_parts,
    bias_in,
    xhat_one,
    rate_one,
    mid_low,
    hidden,
    slope,
    acc,
    dh_low,
    pre_grad,
    rows_in,
    rows_out,
    stage16,
    stage32,
    from_core,
    held,
    w_sem,
    in_sem,
    out_sem,
    load_sem,
    store_sem,
    send_sem,
    recv_sem,
    count_send,
    count_recv,
):
    seq, width = acc.shape
    blocks = seq // RB
    half = width // 2
    first, second = (r0a, r0b, r0c, r0d), (r1a, r1b, r1c, r1d)
    out_rows = w_out.shape[0] // 4
    units = w_in.shape[2]
    side = units // 2
    core_at = partner("tensor", 0)
    greet([core_at] + [partner("dp", bit) for bit in range(dp_bits)])

    def rows(i):
        return pl.ds(i * RB, RB)

    def fetch(source, i, slot):
        return pltpu.make_async_copy(source.at[rows(i), :], rows_in.at[slot], in_sem.at[slot])

    def out_weights(p, c):
        return pltpu.make_async_copy(
            first[p].at[pl.ds(c * out_rows, out_rows), :],
            w_out.at[pl.ds(p * out_rows, out_rows), pl.ds(c * half, half)],
            w_sem.at[p, c],
        )

    def bias_rows(p):
        source = (qa, qb, qc, qd)[p]
        return pltpu.make_async_copy(
            source.at[pl.ds(source.shape[0] - 16, 16), :], bias_parts.at[p], w_sem.at[p, 8]
        )

    def ffn_weights(p, r):
        source = first[p] if r == 0 else second[p]
        base = source.shape[0] - 2 * width
        copies = [
            pltpu.make_async_copy(
                source.at[pl.ds(base, width), :],
                w_in.at[p, :, pl.ds(r * side, side)],
                w_sem.at[p, 2 + 3 * r],
            )
        ]
        for c in range(2):
            copies.append(
                pltpu.make_async_copy(
                    source.at[pl.ds(base + width + c * side, side), :],
                    w_back.at[p, pl.ds(r * side, side), pl.ds(c * half, half)],
                    w_sem.at[p, 3 + 3 * r + c],
                )
            )
        return copies

    early = [out_weights(p, c) for p in range(4) for c in range(2)]
    for copy in early:
        copy.start()
    fetch(x_hbm, 0, 0).start()
    for p in range(4):
        bias_rows(p).start()
        for r in range(2):
            for copy in ffn_weights(p, r):
                copy.start()

    def count_step(bit):
        return pltpu.make_async_remote_copy(
            src_ref=held.at[2 * bit],
            dst_ref=held.at[2 * bit + 1],
            send_sem=count_send.at[bit],
            recv_sem=count_recv.at[bit],
            device_id=partner("dp", bit),
            device_id_type=pl.DeviceIdType.MESH,
        )

    tokens = jnp.full(held.shape[1:], 0, jnp.int32)
    for i in range(lengths_ref.shape[0]):
        tokens += lengths_ref[i]
    held[0] = tokens
    count_step(0).start()

    def count_on(bit):
        count_step(bit).wait()
        held[2 * bit + 2] = held[2 * bit] + held[2 * bit + 1]
        if bit + 1 < dp_bits:
            count_step(bit + 1).start()

    for copy in early:
        copy.wait()

    for i in range(blocks):
        if i + 1 < blocks:
            fetch(x_hbm, i + 1, (i + 1) % 2).start()
        fetch(x_hbm, i, i % 2).wait()
        context = jnp.concatenate([ctx_a[rows(i), :], ctx_b[rows(i), :]], axis=1)
        xhat, rate = norm_stats(dot(context, w_out[...]) + shifts[0:1, :] + rows_in[i % 2])
        xhat_one[rows(i), :] = xhat
        rate_one[rows(i), :] = rate
        mid_low[rows(i), :] = (xhat * gains[0:1, :] + shifts[1:2, :]).astype(LOW)
        acc[rows(i), :] = jnp.zeros((RB, width), F32)
        if i < dp_bits:
            count_on(i)
    for bit in range(blocks, dp_bits):
        count_on(bit)
    count_ref[...] = held[2 * dp_bits]
    fetch(teacher_hbm, 0, 0).start()
    for p in range(4):
        bias_rows(p).wait()
        part = bias_parts[p, 0:3, :].astype(F32)
        bias_in[p] = part[0:1] + part[1:2] + part[2:3]

    def up(p, carry):
        for r in range(2):
            pltpu.make_async_copy(
                first[0].at[pl.ds(0, width), :],
                w_in.at[p, :, pl.ds(r * side, side)],
                w_sem.at[p, 2 + 3 * r],
            ).wait()
            for c in range(2):
                pltpu.make_async_copy(
                    first[0].at[pl.ds(0, side), :],
                    w_back.at[p, pl.ds(r * side, side), pl.ds(c * half, half)],
                    w_sem.at[p, 3 + 3 * r + c],
                ).wait()
        for k in range(seq // FR):
            at = pl.ds(k * FR, FR)
            act, der = gelu_parts(dot(mid_low[at, :], w_in[p]) + bias_in[p])
            act = act.astype(LOW)
            hidden[p, at, :] = act
            slope[p, at, :] = der
            acc[at, :] += dot(act, w_back[p])
        return carry

    lax.fori_loop(0, 4, up, 0)

    zero = jnp.zeros((1, width), F32)
    squares, gain_two, shift_two, shift_mid = zero, zero, zero, zero
    scale = total_slots / held[2 * dp_bits, 0:1, 0:1].astype(F32)
    stores = []
    for i in range(blocks):
        if i + 1 < blocks:
            fetch(teacher_hbm, i + 1, (i + 1) % 2).start()
        fetch(teacher_hbm, i, i % 2).wait()
        mid = xhat_one[rows(i), :] * gains[0:1, :] + shifts[1:2, :]
        xhat, rate = norm_stats(acc[rows(i), :] + shifts[2:3, :] + mid)
        output = xhat * gains[1:2, :] + shifts[3:4, :]
        if i >= 2:
            stores[i - 2].wait()
        rows_out[i % 2] = output
        stores.append(
            pltpu.make_async_copy(rows_out.at[i % 2], out_hbm.at[rows(i), :], out_sem.at[i % 2])
        )
        stores[i].start()
        live = (i * RB + lax.broadcasted_iota(jnp.int32, (RB, 1), 0)) < valid_ref[0]
        distance = jnp.where(live, output - rows_in[i % 2], 0.0)
        squares += column_sum(distance * distance)
        out_grad = scale * distance
        gain_two += column_sum(out_grad * xhat)
        shift_two += column_sum(out_grad)
        dh_two = norm_back(out_grad, gains[1:2, :], xhat, rate)
        shift_mid += column_sum(dh_two)
        acc[rows(i), :] = dh_two
        dh_low[rows(i), :] = dh_two.astype(LOW)
    for store in stores[-2:]:
        store.wait()

    sides = (pl.ds(0, side), pl.ds(side, side))

    def ffn_back(p):
        total = jnp.zeros((1, units), F32)
        for k in range(seq // FR):
            at = pl.ds(k * FR, FR)
            grad = (dot(dh_low[at, :], w_back[p], NT) * slope[p, at, :]).astype(LOW)
            pre_grad[at, :] = grad
            acc[at, :] += dot(grad, w_in[p], NT)
            total += column_sum(grad.astype(F32))
        bias_sums[pl.ds(p, 1), :] = total

    def to_core(pair, w):
        return pltpu.make_async_remote_copy(
            src_ref=stage16.at[w],
            dst_ref=core_hbm.at[pair, w],
            send_sem=send_sem.at[w],
            recv_sem=recv_sem.at[pair, w],
            device_id=core_at,
            device_id_type=pl.DeviceIdType.MESH,
        )

    def away(n, carry):
        p = 2 * n + 1
        ffn_back(p)

        @pl.when(n > 0)
        def _():
            for w in range(2):
                to_core(0, w).wait_send()

        stage16[0] = dot(mid_low[...], pre_grad[...], TN).astype(LOW)
        stage16[1] = dot(hidden[p], dh_low[...], TN).astype(LOW)
        for w in range(2):
            to_core(n, w).start()
        return carry

    lax.fori_loop(0, 2, away, 0)

    def in_moves(pair):
        return [
            pltpu.make_async_copy(stage32.at[0, :, sides[0]], rest.at[pair], store_sem.at[0]),
            pltpu.make_async_copy(stage16.at[0, :, sides[1]], to_x.at[pair], store_sem.at[1]),
        ]

    def back_moves(stage, target):
        return [
            pltpu.make_async_copy(
                stage.at[1, sides[r], sides[c]],
                target.at[r, sides[c], :],
                store_sem.at[2 + 2 * r + c],
            )
            for r in range(2)
            for c in range(2)
        ]

    moves = {1: in_moves(1) + back_moves(stage16, to_y), 0: in_moves(0) + back_moves(stage32, rest.at[pl.ds(2, 2)])}

    def home(n, carry):
        pair = 1 - n
        p = 2 * pair
        for w in range(2):
            to_core(pair, w).wait_recv()
            pltpu.make_async_copy(core_hbm.at[pair, w], from_core.at[w], load_sem.at[w]).start()
        ffn_back(p)

        @pl.when(n == 0)
        def _():
            for w in range(2):
                to_core(1, w).wait_send()

        @pl.when(n == 1)
        def _():
            for copy in moves[1]:
                copy.wait()

        stage32[0] = dot(mid_low[...], pre_grad[...], TN)
        stage32[1] = dot(hidden[p], dh_low[...], TN)
        for w in range(2):
            pltpu.make_async_copy(core_hbm.at[pair, w], from_core.at[w], load_sem.at[w]).wait()
            for k in range(0, width, 128):
                total = stage32[w, k : k + 128, :] + from_core[w, k : k + 128, :].astype(F32)
                stage32[w, k : k + 128, :] = total
                stage16[w, k : k + 128, :] = total.astype(LOW)

        @pl.when(n == 0)
        def _():
            for copy in moves[1]:
                copy.start()

        @pl.when(n == 1)
        def _():
            for copy in moves[0]:
                copy.start()

        return carry

    lax.fori_loop(0, 2, home, 0)

    gain_one, shift_one, shift_out = zero, zero, zero
    stores = []
    for i in range(blocks):
        grad, xhat = acc[rows(i), :], xhat_one[rows(i), :]
        gain_one += column_sum(grad * xhat)
        shift_one += column_sum(grad)
        dh_one = norm_back(grad, gains[0:1, :], xhat, rate_one[rows(i), :])
        shift_out += column_sum(dh_one)
        if i >= 2:
            stores[i - 2].wait()
        rows_out[i % 2] = dh_one
        stores.append(
            pltpu.make_async_copy(rows_out.at[i % 2], dh_hbm.at[rows(i), :], out_sem.at[i % 2])
        )
        stores[i].start()
        dh_one = dh_one.astype(LOW)
        dh_low[rows(i), :] = dh_one
        grad = dot(dh_one, w_out[...], NT).astype(LOW)
        cg_a[rows(i), :] = grad[:, :half]
        cg_b[rows(i), :] = grad[:, half:]
    for group, context in enumerate((ctx_a, ctx_b)):
        grad = dot(context[...], dh_low[...], TN)
        out_keep[group] = grad[:out_rows]
        out_send[group] = grad[out_rows:].astype(LOW)
    sums[...] = jnp.concatenate(
        [gain_one, gain_two, shift_out, shift_one, shift_mid, shift_two, squares, zero], axis=0
    )
    for store in stores[-2:]:
        store.wait()
    for copy in moves[0]:
        copy.wait()


def middle(total_slots, valid, lengths, ctx_a, ctx_b, gains, shifts, x, teacher, near, first, second):
    seq, width = x.shape
    half = width // 2
    out_rows = ctx_a.shape[1] // 2
    units = width
    dp_bits = bits_of("dp")
    slab = (width, units // 2)
    return pl.pallas_call(
        functools.partial(middle_kernel, float(total_slots), dp_bits),
        out_shape=(
            shape((seq, width), F32),
            shape((seq, width), F32),
            shape((seq, half), LOW),
            shape((seq, half), LOW),
            shape((2, 2, width, units), LOW),
            shape((2,) + slab, LOW),
            shape((2,) + slab, LOW),
            shape((4,) + slab, F32),
            shape((2, out_rows, width), LOW),
            shape((2, out_rows, width), F32),
            shape((8, width), F32),
            shape((4, units), F32),
            shape((8, 128), jnp.int32),
        ),
        in_specs=[SMEM, SMEM, VMEM, VMEM, VMEM, VMEM, HBM, HBM] + [HBM] * 12,
        out_specs=(HBM, HBM, VMEM, VMEM, HBM, HBM, HBM, HBM) + (VMEM,) * 5,
        scratch_shapes=[
            pltpu.VMEM((4, width, units), LOW),
            pltpu.VMEM((4, units, width), LOW),
            pltpu.VMEM((4 * out_rows, width), LOW),
            pltpu.VMEM((4, 16, width), LOW),
            pltpu.VMEM((4, 1, units), F32),
            pltpu.VMEM((seq, width), F32),
            pltpu.VMEM((seq, 1), F32),
            pltpu.VMEM((seq, width), LOW),
            pltpu.VMEM((4, seq, units), LOW),
            pltpu.VMEM((4, seq, units), F32),
            pltpu.VMEM((seq, width), F32),
            pltpu.VMEM((seq, width), LOW),
            pltpu.VMEM((seq, units), LOW),
            pltpu.VMEM((2, RB, width), F32),
            pltpu.VMEM((2, RB, width), F32),
            pltpu.VMEM((2, width, units), LOW),
            pltpu.VMEM((2, width, units), F32),
            pltpu.VMEM((2, width, units), LOW),
            pltpu.VMEM((2 * dp_bits + 1, 8, 128), jnp.int32),
            pltpu.SemaphoreType.DMA((4, 9)),
            pltpu.SemaphoreType.DMA((2,)),
            pltpu.SemaphoreType.DMA((2,)),
            pltpu.SemaphoreType.DMA((2,)),
            pltpu.SemaphoreType.DMA((6,)),
            pltpu.SemaphoreType.DMA((2,)),
            pltpu.SemaphoreType.DMA((2, 2)),
            pltpu.SemaphoreType.DMA((dp_bits,)),
            pltpu.SemaphoreType.DMA((dp_bits,)),
        ],
        compiler_params=pltpu.CompilerParams(
            vmem_limit_bytes=VMEM_LIMIT, collective_id=1, has_side_effects=True
        ),
        cost_estimate=pl.CostEstimate(
            flops=6 * seq * width * (8 * units + width),
            bytes_accessed=30 << 20,
            transcendentals=2 * seq * 4 * units,
        ),
        name="middle",
    )(valid, lengths, ctx_a, ctx_b, gains, shifts, x, teacher, *near, *first, *second)


def add_rows(out, terms, chunk=96):
    rows = out.shape[0]
    chunk = min(chunk, rows)

    def step(i, carry):
        at = pl.ds(pl.multiple_of(i * chunk, chunk), chunk)
        total = terms[0][at, :].astype(F32)
        for term in terms[1:]:
            total += term[at, :].astype(F32)
        out[at, :] = total.astype(out.dtype)
        return carry

    lax.fori_loop(0, rows // chunk, step, 0)


def cross_rows(x_ref, grads, okeep, osend, side, cross, keep, send, bias_ref):
    half = x_ref.shape[1] // 2
    piece = grads[0].shape[1] // 2
    mine = pl.ds(pl.multiple_of(side * half, half), half)
    other = pl.ds(pl.multiple_of((1 - side) * half, half), half)
    for i in range(3):
        cross[...] = dot(grads[i][...], x_ref[...], TN)
        at = slice(i * piece, (i + 1) * piece)
        for n, lanes in enumerate((mine, other)):
            keep[n, at, :] = cross[:piece, lanes]
            send[n, at, :] = cross[piece:, lanes].astype(send.dtype)
        bias_ref[i : i + 1, :] = column_sum(grads[i][...].astype(F32))
    for n, lanes in enumerate((mine, other)):
        keep[n, 3 * piece :, :] = okeep[:, lanes]
        send[n, 3 * piece :, :] = osend[:, lanes].astype(send.dtype)


def far_kernel(
    x_ref,
    dq,
    dk,
    dv,
    osend,
    okeep,
    away,
    bias_ref,
    keep,
    send,
    core,
    cross,
    send_sem,
    recv_sem,
):
    core_at = partner("tensor", 0)
    greet([core_at])
    bias_ref[...] = jnp.zeros(bias_ref.shape, F32)
    cross_rows(
        x_ref, (dq, dk, dv), okeep, osend, lax.axis_index("dp") & 1, cross, keep, send, bias_ref
    )
    copies = [
        pltpu.make_async_remote_copy(
            src_ref=send.at[n],
            dst_ref=core.at[n],
            send_sem=send_sem.at[n],
            recv_sem=recv_sem.at[n],
            device_id=core_at,
            device_id_type=pl.DeviceIdType.MESH,
        )
        for n in range(2)
    ]
    for n in (1, 0):
        copies[n].start()
    for n in (1, 0):
        copies[n].wait_recv()
        add_rows(away.at[n], [keep.at[n], core.at[n]])
    for n in (1, 0):
        copies[n].wait_send()


def far_projections(x, grads, osend, okeep):
    seq, width = x.shape
    half = width // 2
    piece = grads[0].shape[1] // 2
    slabs = (2, width, half)
    return pl.pallas_call(
        far_kernel,
        out_shape=(shape(slabs, LOW), shape((8, 2 * piece), F32)),
        in_specs=[VMEM] * 6,
        out_specs=(VMEM, VMEM),
        scratch_shapes=[
            pltpu.VMEM(slabs, F32),
            pltpu.VMEM(slabs, F32),
            pltpu.VMEM(slabs, F32),
            pltpu.VMEM((2 * piece, width), F32),
            pltpu.SemaphoreType.DMA((2,)),
            pltpu.SemaphoreType.DMA((2,)),
        ],
        compiler_params=pltpu.CompilerParams(
            vmem_limit_bytes=VMEM_LIMIT, collective_id=3, has_side_effects=True
        ),
        cost_estimate=pl.CostEstimate(
            flops=12 * seq * width * piece, bytes_accessed=10 << 20, transcendentals=0
        ),
        name="far_projections",
    )(x, *grads, osend, okeep)


def finish_kernel(
    dp_bits,
    x_ref,
    w0,
    w1,
    w2,
    w3,
    dqa,
    dka,
    dva,
    dqb,
    dkb,
    dvb,
    osend,
    okeep,
    dh_hbm,
    rest,
    ffn_x,
    ffn_y,
    in_y,
    back_x,
    away,
    qkv_y,
    small_ref,
    bias_far,
    gx_hbm,
    result,
    small_out,
    own,
    own16,
    keep,
    send,
    core,
    y_recv,
    x_send,
    x_recv,
    total,
    z_send,
    z_recv,
    last_send,
    last_recv,
    extra,
    bias_ref,
    small_held,
    rows_in,
    rows_out,
    cross,
    load_sem,
    send_sem,
    recv_sem,
    in_sem,
    out_sem,
):
    seq, width = x_ref.shape
    half = width // 2
    piece = dqa.shape[1] // 2
    blocks = seq // RB
    place = lax.axis_index("dp")
    index = lax.axis_index("tensor")
    side = place & 1
    core_at, y_at = partner("tensor", 0), partner("tensor", 1)
    dp_at = [partner("dp", bit) for bit in range(dp_bits)]
    greet([core_at, y_at] + dp_at)
    started = {}

    def remote(key, source, target, device):
        n = len(started)
        started[key] = pltpu.make_async_remote_copy(
            src_ref=source,
            dst_ref=target,
            send_sem=send_sem.at[n],
            recv_sem=recv_sem.at[n],
            device_id=device,
            device_id_type=pl.DeviceIdType.MESH,
        )
        started[key].start()

    def arrive(key):
        started[key].wait_recv()

    remote("y", away.at[0], y_recv, y_at)
    loads = []
    for w, terms in enumerate(((rest.at[0], ffn_x.at[0], in_y), (rest.at[2], ffn_y.at[0], back_x))):
        targets = (own.at[w], own16.at[w, 0], own16.at[w, 1])
        loads.append(
            [
                pltpu.make_async_copy(term, target, load_sem.at[w, n])
                for n, (term, target) in enumerate(zip(terms, targets))
            ]
        )
        for copy in loads[w]:
            copy.start()

    def fetch(i):
        return pltpu.make_async_copy(
            dh_hbm.at[pl.ds(i * RB, RB), :], rows_in.at[i % 2], in_sem.at[i % 2]
        )

    fetch(0).start()

    rows_of = [width]
    for bit in range(1, min(dp_bits, 3)):
        rows_of.append(rows_of[-1] // 2)
    levels = min(dp_bits, 3) - 1

    def offset(level):
        at = 0
        for bit in range(1, level + 1):
            at = at + ((place >> bit) & 1) * rows_of[bit]
        return pl.multiple_of(at, rows_of[level])

    def other_offset(level):
        return pl.multiple_of(
            offset(level - 1) + (1 - ((place >> level) & 1)) * rows_of[level], rows_of[level]
        )

    def scatter(w, level):
        size = rows_of[level]
        out, into = ((z_send, z_recv) if level == 1 else (last_send, last_recv))
        add_rows(out.at[w], [total.at[w, pl.ds(other_offset(level), size), :]])
        remote((w, "z", level), out.at[w], into.at[w], dp_at[level])

    def collect(w, level):
        size = rows_of[level]
        arrive((w, "z", level))
        into = z_recv if level == 1 else last_recv
        mine = total.at[w, pl.ds(offset(level), size), :]
        if level < levels:
            add_rows(mine, [mine, into.at[w]])
        else:
            add_rows(result.at[w, 0, pl.ds(offset(level), size), :], [mine, into.at[w]])

    def settle(w):
        size = rows_of[levels]
        at = pl.ds(offset(levels), size)
        for bit in range(levels + 1, dp_bits):
            spare = result.at[w, 0, at, :]
            into = extra.at[w, bit - levels - 1]
            remote((w, "all", bit), spare, into, dp_at[bit])
            started[(w, "all", bit)].wait_send()
            arrive((w, "all", bit))
            add_rows(spare, [spare, into])

    def spread(w, level):
        if level == 0:
            remote((w, "gather", 0), result.at[w, 0], result.at[w, 1], dp_at[0])
        else:
            rows = result.at[w, 0, pl.ds(offset(level), rows_of[level]), :]
            remote((w, "gather", level), rows, rows, dp_at[level])

    for w in range(2):
        for copy in loads[w]:
            copy.wait()
        add_rows(total.at[w], [own.at[w], own16.at[w, 0], own16.at[w, 1]])
        scatter(w, 1)

    cross_rows(x_ref, (dqa, dka, dva), okeep, osend, side, cross, keep, send, bias_ref)
    for n in (1, 0):
        remote(("core", n), send.at[n], core.at[n], core_at)

    small_held[0] = jnp.zeros(small_held.shape[1:], F32)
    small_held[0, 16:24, :] = small_ref[0:8, :]
    for p in range(4):
        row = 4 * (index ^ p)
        half_mine = small_ref[8 + p : 9 + p, :half]
        half_other = small_ref[8 + p : 9 + p, half:]
        low_half = jnp.where(side == 0, half_mine, half_other)
        high_half = jnp.where(side == 0, half_other, half_mine)
        small_held[0, pl.ds(row, 1), :] = jnp.concatenate([low_half, high_half], axis=1)
        for i, k in enumerate((0, 2)):
            values = (bias_ref, bias_far)[p // 2][k : k + 1, :]
            if p % 2 == 1:
                values = pltpu.roll(values, piece, 1)
            small_held[0, pl.ds(row + 1 + i, 1), :half] = values

    def small_step(n):
        bits = [core_at, y_at] + dp_at
        remote(("small", n), small_held.at[2 * n], small_held.at[2 * n + 1], bits[n])

    def small_sum(n):
        arrive(("small", n))
        out = small_held.at[2 * n + 2] if n < dp_bits + 1 else small_out
        out[...] = small_held[2 * n] + small_held[2 * n + 1]

    weights = ((w0, w1), (w2, w3))
    grads = ((dqa, dka, dva), (dqb, dkb, dvb))
    stores = []

    def inputs_rows(b):
        at = pl.ds(b * RB, RB)
        if b + 1 < blocks:
            fetch(b + 1).start()
        fetch(b).wait()
        grad = rows_in[b % 2]
        for g in range(2):
            for i in range(3):
                rows = slice(i * piece, (i + 1) * piece)
                w = jnp.concatenate([ref[rows, :] for ref in weights[g]], axis=0)
                grad += dot(grads[g][i][at, :], w)
        if b >= 2:
            stores[b - 2].wait()
        rows_out[b % 2] = grad
        stores.append(
            pltpu.make_async_copy(rows_out.at[b % 2], gx_hbm.at[at, :], out_sem.at[b % 2])
        )
        stores[b].start()

    small_step(0)
    arrive(("core", 1))
    add_rows(x_send, [keep.at[1], core.at[1], qkv_y])
    remote("qkv x", x_send, x_recv, dp_at[0])
    collect(0, 1)
    scatter(0, 2)
    inputs_rows(0)
    small_sum(0)
    small_step(1)
    collect(1, 1)
    scatter(1, 2)
    inputs_rows(1)
    small_sum(1)
    small_step(2)
    collect(0, 2)
    settle(0)
    spread(0, 2)
    inputs_rows(2)
    small_sum(2)
    if dp_bits > 1:
        small_step(3)
    collect(1, 2)
    settle(1)
    spread(1, 2)
    inputs_rows(3)
    arrive((0, "gather", 2))
    spread(0, 1)
    for n in range(3, dp_bits + 2):
        small_sum(n)
        if n + 1 < dp_bits + 2:
            small_step(n + 1)
    arrive(("core", 0))
    arrive("y")
    add_rows(total.at[2], [keep.at[0], core.at[0], y_recv])
    arrive((1, "gather", 2))
    spread(1, 1)
    arrive("qkv x")
    add_rows(total.at[2], [total.at[2], x_recv])
    scatter(2, 1)
    arrive((0, "gather", 1))
    spread(0, 0)
    collect(2, 1)
    scatter(2, 2)
    arrive((1, "gather", 1))
    spread(1, 0)
    collect(2, 2)
    settle(2)
    spread(2, 2)
    arrive((2, "gather", 2))
    spread(2, 1)
    arrive((2, "gather", 1))
    spread(2, 0)
    for w in range(3):
        arrive((w, "gather", 0))
    for key, copy in started.items():
        if not (isinstance(key, tuple) and key[1] == "all"):
            copy.wait_send()
    for store in stores[-2:]:
        store.wait()


def finish(x, weights, grads, osend, okeep, dh, rest, ffn_x, ffn_y, in_y, back_x, away, qkv_y, small, bias_far):
    seq, width = x.shape
    half = width // 2
    piece = grads[0].shape[1] // 2
    dp_bits = bits_of("dp")
    slab = (width, half)
    copies = 4 + dp_bits + 2 + 3 * (2 + 3 + max(dp_bits - 3, 0))
    return pl.pallas_call(
        functools.partial(finish_kernel, dp_bits),
        out_shape=(
            shape((seq, width), F32),
            shape((3, 2) + slab, LOW),
            shape((24, width), F32),
        ),
        in_specs=[VMEM] * 13 + [HBM] * 6 + [HBM, VMEM, VMEM, VMEM],
        out_specs=(HBM, VMEM, VMEM),
        scratch_shapes=[
            pltpu.VMEM((2,) + slab, F32),
            pltpu.VMEM((2, 2) + slab, LOW),
            pltpu.VMEM((2,) + slab, F32),
            pltpu.VMEM((2,) + slab, F32),
            pltpu.VMEM((2,) + slab, F32),
            pltpu.VMEM(slab, LOW),
            pltpu.VMEM(slab, LOW),
            pltpu.VMEM(slab, LOW),
            pltpu.VMEM((3,) + slab, F32),
            pltpu.VMEM((3, width // 2, half), LOW),
            pltpu.VMEM((3, width // 2, half), LOW),
            pltpu.VMEM((3, width // 4, half), F32),
            pltpu.VMEM((3, width // 4, half), F32),
            pltpu.VMEM((3, max(dp_bits - 3, 1), width // 4, half), LOW),
            pltpu.VMEM((8, 2 * piece), F32),
            pltpu.VMEM((2 * dp_bits + 4, 24, width), F32),
            pltpu.VMEM((2, RB, width), F32),
            pltpu.VMEM((2, RB, width), F32),
            pltpu.VMEM((2 * piece, width), F32),
            pltpu.SemaphoreType.DMA((2, 3)),
            pltpu.SemaphoreType.DMA((copies,)),
            pltpu.SemaphoreType.DMA((copies,)),
            pltpu.SemaphoreType.DMA((2,)),
            pltpu.SemaphoreType.DMA((2,)),
        ],
        compiler_params=pltpu.CompilerParams(
            vmem_limit_bytes=VMEM_LIMIT, collective_id=2, has_side_effects=True
        ),
        cost_estimate=pl.CostEstimate(
            flops=36 * seq * width * piece, bytes_accessed=50 << 20, transcendentals=0
        ),
        name="finish",
    )(x, *weights, *grads, osend, okeep, dh, rest, ffn_x, ffn_y, in_y, back_x, away, qkv_y, small, bias_far)


def widen_kernel(
    place_ref,
    result,
    small,
    count,
    loss_ref,
    qkv_ref,
    bqv_ref,
    out_ref,
    in_ref,
    bin_ref,
    back_ref,
    gains_ref,
    shifts_ref,
):
    half = result.shape[3]
    piece = qkv_ref.shape[1]
    side = place_ref[0]
    for n in range(2):
        natural = (side + n) % 2
        at = pl.ds(pl.multiple_of(natural * half, half), half)
        in_ref[:, at] = result[0, n].astype(F32)
        for c in range(2):
            rows = result[1, n, c * half : (c + 1) * half, :]
            back_ref[at, c * half : (c + 1) * half] = rows.astype(F32)
        for i in range(3):
            qkv_ref[i, :, at] = result[2, n, i * piece : (i + 1) * piece, :].astype(F32)
        out_ref[:, at] = result[2, n, 3 * piece :, :].astype(F32)
    row = 4 * place_ref[1]
    bin_ref[...] = small[pl.ds(row, 1), :]
    for i in range(2):
        bqv_ref[i : i + 1, :] = small[pl.ds(row + 1 + i, 1), :piece]
    gains_ref[...] = small[16:18, :]
    shifts_ref[...] = small[18:22, :]
    tokens = count[0:1, 0:1].astype(F32)
    total = jnp.sum(small[22:23, :], axis=1, keepdims=True)
    loss_ref[...] = total / (2.0 * small.shape[1] * tokens)


def widen(place, result, small, count, piece, rows):
    width, half = result.shape[2:]
    return pl.pallas_call(
        widen_kernel,
        out_shape=(
            shape((1, 1), F32),
            shape((3, piece, width), F32),
            shape((2, piece), F32),
            shape((rows, width), F32),
            shape((width, 2 * half), F32),
            shape((1, 2 * half), F32),
            shape((2 * half, width), F32),
            shape((2, width), F32),
            shape((4, width), F32),
        ),
        in_specs=[SMEM, VMEM, VMEM, VMEM],
        out_specs=(VMEM,) * 9,
        compiler_params=pltpu.CompilerParams(vmem_limit_bytes=VMEM_LIMIT),
        name="widen",
    )(place, result, small, count)


def per_device(
    inputs,
    w_qkv,
    b_qv,
    w_out,
    w_in,
    b_in,
    w_back,
    norm_gains,
    shifts,
    segment_ids,
    valid_lengths,
    teacher,
):
    own_seqs, seq, width = inputs.shape
    assert own_seqs == 1 and lax.axis_size("tensor") == 4
    total_slots = seq * lax.axis_size("tensor") * lax.axis_size("dp")
    half = width // 2
    piece = w_qkv.shape[2]
    units = w_in.shape[1]
    index = lax.axis_index("tensor")
    side = (lax.axis_index("dp") & 1).astype(jnp.int32)
    side_row = side.reshape(1)
    x = inputs.reshape(seq, width)

    near = round_qkv(side_row, w_qkv.transpose(0, 2, 1), b_qv, b_in[None, :])
    core = swap(near, "tensor", 0)
    far = swap(near, "tensor", 1)
    near_done, w_in, w_back, w_out, x = lax.optimization_barrier((near, w_in, w_back, w_out, x))
    first, second, x_low = round_rest(side_row, w_out, w_in, w_back, x)
    first_far = swap(first, "tensor", 1)

    valid = lax.dynamic_index_in_dim(valid_lengths, index, keepdims=False)
    segments = lax.dynamic_index_in_dim(segment_ids, index, keepdims=False)
    positions = jnp.arange(seq, dtype=jnp.int32)
    code = jnp.where(positions < valid, segments, -1)[:, None]
    seg = segments[None, :]
    table = span_tables(segments, valid, seq)

    qa, ka, va, ctx_a, lse_a = attend_forward(table, x_low, near, core, code, seg)
    first, second, far, first_far, ctx_a = lax.optimization_barrier(
        (first, second, far, first_far, ctx_a)
    )
    core_far = swap(far, "tensor", 0)
    second_far = swap(first_far, "dp", 0)
    first_core = swap(first, "tensor", 0)
    second_core = swap(second, "tensor", 0)
    first_core_far = swap(first_far, "tensor", 0)
    qb, kb, vb, ctx_b, lse_b = attend_forward(table, x_low, far, core_far, code, seg)
    second_far, ctx_b = lax.optimization_barrier((second_far, ctx_b))
    second_core_far = swap(second_far, "tensor", 0)
    (
        output,
        dh_one,
        cg_a,
        cg_b,
        _,
        to_x,
        to_y,
        rest,
        out_send,
        out_keep,
        sums,
        bias_sums,
        count,
    ) = middle(
        total_slots,
        valid.reshape(1),
        valid_lengths,
        ctx_a,
        ctx_b,
        norm_gains,
        shifts,
        x,
        teacher.reshape(seq, width),
        (near, core, far, core_far),
        (first, first_core, first_far, first_core_far),
        (second, second_core, second_far, second_core_far),
    )
    ffn_x = swap(to_x, "dp", 0)
    ffn_y = swap(to_y, "tensor", 1)
    grads_b = attend_backward(table, qb, kb, vb, cg_b, lse_b, code, seg)
    away, bias_far = far_projections(x_low, grads_b, out_send[1], out_keep[1])
    ffn_x, ffn_y, away = lax.optimization_barrier((ffn_x, ffn_y, away))
    in_away = (rest[1] + ffn_x[1].astype(F32)).astype(LOW)
    back_away = (rest[3] + ffn_y[1].astype(F32)).astype(LOW)
    in_away, back_away, away, cg_a = lax.optimization_barrier((in_away, back_away, away, cg_a))
    in_y = swap(in_away, "tensor", 1)
    back_x = swap(back_away, "dp", 0)
    qkv_y = swap(away[1], "tensor", 1)
    grads_a = attend_backward(table, qa, ka, va, cg_a, lse_a, code, seg)
    small = jnp.concatenate([sums, bias_sums, jnp.zeros((4, width), F32)], axis=0)
    grad_inputs, slabs, small = finish(
        x_low,
        (near, core, far, core_far),
        (*grads_a, *grads_b),
        out_send[0],
        out_keep[0],
        dh_one,
        rest,
        ffn_x,
        ffn_y,
        in_y,
        back_x,
        away,
        qkv_y,
        small,
        bias_far,
    )
    (
        loss,
        grad_w_qkv,
        grad_b_qv,
        grad_w_out,
        grad_w_in,
        grad_b_in,
        grad_w_back,
        grad_gains,
        grad_shifts,
    ) = widen(jnp.stack([side, index]), slabs, small, count, piece, w_out.shape[0])
    return (
        output.reshape(own_seqs, seq, width),
        loss[0, 0],
        grad_inputs.reshape(own_seqs, seq, width),
        grad_w_qkv.transpose(0, 2, 1),
        grad_b_qv,
        grad_w_out,
        grad_w_in,
        grad_b_in[0],
        grad_w_back,
        grad_gains,
        grad_shifts,
    )


def solution(mesh):
    return jax.shard_map(
        per_device,
        mesh=mesh,
        in_specs=(
            P(("dp", "tensor"), None, None),
            P(None, None, "tensor"),
            P(None, "tensor"),
            P("tensor", None),
            P(None, "tensor"),
            P("tensor"),
            P("tensor", None),
            P(),
            P(),
            P("dp", None),
            P("dp"),
            P(("dp", "tensor"), None, None),
        ),
        out_specs=(
            P(("dp", "tensor"), None, None),
            P(),
            P(("dp", "tensor"), None, None),
            P(None, None, "tensor"),
            P(None, "tensor"),
            P("tensor", None),
            P(None, "tensor"),
            P("tensor"),
            P("tensor", None),
            P(),
            P(),
        ),
        check_vma=False,
    )
```

```python
import functools
import math

import jax
import jax.numpy as jnp
from jax import lax
from jax.experimental import pallas as pl
from jax.experimental.pallas import tpu as pltpu
from jax.sharding import PartitionSpec as P

HD = 64
LN_EPSILON = 1e-05
MASKED_SCORE = -1000000000.0
QB = 256
KB = 128
RB = 256
FR = 256
NT = ((1,), (1,))
TN = ((0,), (0,))
PHI = (
    0.09255110872,
    0.09001568156,
    0.1049848251,
    0.006341010132,
    0.2381524984,
    -0.2150534404,
    0.2551771707,
    -0.07216888208,
)
PHI_STEP = 0.23164188826636045

VMEM_LIMIT = 63 << 20
VMEM = pl.BlockSpec(memory_space=pltpu.VMEM)
SMEM = pl.BlockSpec(memory_space=pltpu.SMEM)
HBM = pl.BlockSpec(memory_space=pl.ANY)
LOW = jnp.bfloat16
F32 = jnp.float32


def dot(left, right, dims=((1,), (0,))):
    return lax.dot_general(left, right, (dims, ((), ())), preferred_element_type=jnp.float32)


def shape(dims, dtype):
    return jax.ShapeDtypeStruct(dims, dtype)


def swap(values, axis, bit):
    size = lax.axis_size(axis)
    return lax.ppermute(values, axis, [(i, i ^ (1 << bit)) for i in range(size)])


def bits_of(axis):
    return int(math.log2(lax.axis_size(axis)))


def partner(axis, bit):
    here = {name: lax.axis_index(name) for name in ("dp", "tensor")}
    here[axis] = here[axis] ^ (1 << bit)
    return here["dp"], here["tensor"]


def greet(partners):
    barrier = pltpu.get_barrier_semaphore()
    for device in partners:
        pl.semaphore_signal(
            barrier, inc=1, device_id=device, device_id_type=pl.DeviceIdType.MESH
        )
    pl.semaphore_wait(barrier, len(partners))


def three_parts(values):
    first = values.astype(LOW)
    rest = values - first.astype(F32)
    second = rest.astype(LOW)
    return first, second, (rest - second.astype(F32)).astype(LOW)


def round_qkv_kernel(side_ref, w_ref, bqv_ref, bin_ref, out_ref):
    piece = w_ref.shape[1]
    width = w_ref.shape[2]
    half = bin_ref.shape[1] // 2
    for i in range(3):
        out_ref[i * piece : (i + 1) * piece, :] = w_ref[i].astype(LOW)
    mine = bin_ref[:, pl.ds(pl.multiple_of(side_ref[0] * half, half), half)]
    other = bin_ref[:, pl.ds(pl.multiple_of((1 - side_ref[0]) * half, half), half)]
    pad = jnp.zeros((1, width - piece), F32)
    rows = [jnp.concatenate([mine, other], axis=1)]
    rows += [jnp.concatenate([bqv_ref[i : i + 1, :], pad], axis=1) for i in range(2)]
    parts = [part.astype(F32) for row in rows for part in three_parts(row)]
    parts += [jnp.zeros((1, width), F32)] * 7
    out_ref[3 * piece :, :] = jnp.concatenate(parts, axis=0).astype(LOW)


def round_qkv(side, w_qkv, b_qv, b_in):
    _, piece, width = w_qkv.shape
    return pl.pallas_call(
        round_qkv_kernel,
        out_shape=shape((3 * piece + 16, width), LOW),
        in_specs=[SMEM, VMEM, VMEM, VMEM],
        out_specs=VMEM,
        compiler_params=pltpu.CompilerParams(vmem_limit_bytes=VMEM_LIMIT),
        name="round_qkv",
    )(side, w_qkv, b_qv, b_in)


def round_rest_kernel(side_ref, wo_ref, wi_ref, wb_ref, x_ref, out_in, back, second, x_low_ref):
    rows, width = wo_ref.shape
    half = width // 2
    for c in range(2):
        out_in[c * rows : (c + 1) * rows, :] = wo_ref[:, c * half : (c + 1) * half].astype(LOW)
    x_low_ref[...] = x_ref[...].astype(LOW)
    parts = (
        (out_in, 2 * rows, back, 0, side_ref[0]),
        (second, 0, second, width, 1 - side_ref[0]),
    )
    for to_in, in_base, to_back, back_base, side in parts:
        at = pl.ds(pl.multiple_of(side * half, half), half)
        to_in[in_base : in_base + width, :] = wi_ref[:, at].astype(LOW)
        for c in range(2):
            start = back_base + c * half
            to_back[start : start + half, :] = wb_ref[at, c * half : (c + 1) * half].astype(LOW)


def round_rest(side, w_out, w_in, w_back, x):
    rows, width = w_out.shape
    half = width // 2
    return pl.pallas_call(
        round_rest_kernel,
        out_shape=(
            shape((2 * rows + width, half), LOW),
            shape((width, half), LOW),
            shape((2 * width, half), LOW),
            shape(x.shape, LOW),
        ),
        in_specs=[SMEM, VMEM, VMEM, VMEM, VMEM],
        out_specs=(VMEM,) * 4,
        compiler_params=pltpu.CompilerParams(vmem_limit_bytes=VMEM_LIMIT),
        name="round_rest",
    )(side, w_out, w_in, w_back, x)


def span_tables(segments, valid, seq):
    blocks = seq // QB
    firsts, lasts = segments[::QB], segments[QB - 1 :: QB]
    low = jnp.sum((segments[None, :] < firsts[:, None]).astype(jnp.int32), axis=1)
    high = jnp.sum((segments[None, :] <= lasts[:, None]).astype(jnp.int32), axis=1)
    own_end = (jnp.arange(blocks, dtype=jnp.int32) + 1) * QB
    high = jnp.maximum(jnp.minimum(high, valid), own_end)
    low_block = low // KB
    high_block = (high + KB - 1) // KB
    return jnp.stack([low_block, high_block - low_block]).astype(jnp.int32)


def make_bias(bias_ref, block, low, count, code_ref, seg_ref):
    dims = (count * KB, QB)
    codes = code_ref[pl.ds(pl.multiple_of(low * KB, KB), count * KB), :]
    segs = seg_ref[:, pl.ds(pl.multiple_of(block * QB, QB), QB)]
    key_at = low * KB + lax.broadcasted_iota(jnp.int32, dims, 0)
    query_at = block * QB + lax.broadcasted_iota(jnp.int32, dims, 1)
    allowed = (codes == segs) | (key_at == query_at)
    bias_ref[: count * KB, :] = jnp.where(allowed, 0.0, MASKED_SCORE)


def one_head(values, head):
    lane = lax.broadcasted_iota(jnp.int32, values.shape, 1)
    keep = (lane < HD) if head == 0 else (lane >= HD)
    return jnp.where(keep, values, jnp.zeros_like(values))


def forward_kernel(
    table_ref,
    x_ref,
    w0_ref,
    w1_ref,
    code_ref,
    seg_ref,
    q_ref,
    k_ref,
    v_ref,
    ctx_ref,
    lse_ref,
    weights,
    biases,
    vt_ref,
    bias_ref,
):
    block = pl.program_id(0)
    low, total = table_ref[0, block], table_ref[1, block]
    piece = (w0_ref.shape[0] - 16) // 3
    pairs = 2 * piece // 128

    @pl.when(block == 0)
    def _():
        for i in range(3):
            for n, ref in enumerate((w0_ref, w1_ref)):
                rows = ref[i * piece : (i + 1) * piece, :]
                weights[i, n * piece : (n + 1) * piece, :] = rows
        lane = lax.broadcasted_iota(jnp.int32, (1, x_ref.shape[1]), 1)
        for i in (0, 2):
            base = 3 * piece + (3 if i == 0 else 6)
            both = [
                sum(ref[base + part : base + part + 1, :].astype(F32) for part in range(3))
                for ref in (w0_ref, w1_ref)
            ]
            row = jnp.where(lane < piece, both[0], pltpu.roll(both[1], piece, 1))
            biases[i : i + 1, :] = row[:, : 2 * piece]
        biases[1:2, :] = jnp.zeros((1, 2 * piece), F32)

        def project(b, carry):
            at = pl.ds(pl.multiple_of(b * QB, QB), QB)
            for i, ref in enumerate((q_ref, k_ref, v_ref)):
                ref[at, :] = (dot(x_ref[at, :], weights[i], NT) + biases[i : i + 1, :]).astype(LOW)
            vt_ref[:, at] = v_ref[at, :].T
            return carry

        lax.fori_loop(0, x_ref.shape[0] // QB, project, 0)

    def run(count):
        make_bias(bias_ref, block, low, count, code_ref, seg_ref)
        bias = bias_ref[: count * KB, :]
        rows = pl.ds(pl.multiple_of(low * KB, KB), count * KB)
        queries = pl.ds(pl.multiple_of(block * QB, QB), QB)

        def scores(head):
            lanes = slice(head // 2 * 128, head // 2 * 128 + 128)
            query = q_ref[queries, lanes] * jnp.asarray(0.125, LOW)
            return dot(k_ref[rows, lanes], one_head(query, head % 2), NT) + bias

        def soft(values, head):
            peak = jnp.max(values, axis=0, keepdims=True)
            powers = jnp.exp(values - peak)
            mass = jnp.sum(powers, axis=0, keepdims=True)
            lse_ref[head : head + 1, :] = peak + jnp.log(mass)
            return (powers * (1.0 / mass)).astype(LOW)

        outs = []

        def context(probs, head):
            outs.append(dot(vt_ref[head * HD : (head + 1) * HD, rows], probs))
            if head % 2 == 1:
                both = jnp.concatenate(outs[-2:], axis=0).T
                ctx_ref[:, head // 2 * 128 : head // 2 * 128 + 128] = both.astype(LOW)

        values, probs = scores(0), None
        for head in range(2 * pairs):
            later = scores(head + 1) if head + 1 < 2 * pairs else None
            now = soft(values, head)
            if head > 0:
                context(probs, head - 1)
            values, probs = later, now
        context(probs, 2 * pairs - 1)

    for count in range(2, k_ref.shape[0] // KB + 1):
        pl.when(total == count)(functools.partial(run, count))


def backward_kernel(carried, table_ref, q_ref, k_ref, v_ref, g_ref, lse_ref, code_ref, seg_ref, *refs):
    block = pl.program_id(0)
    refs = list(refs)
    if carried:
        source, target, copy_sem = refs.pop(0), refs.pop(3), refs.pop()
        passing = pltpu.make_async_copy(source, target, copy_sem)
        pl.when(block == 0)(passing.start)
        pl.when(block == pl.num_programs(0) - 1)(passing.wait)
    dq_ref, dk_ref, dv_ref, kt_ref, bias_ref, dk_sum, dv_sum = refs
    low, total = table_ref[0, block], table_ref[1, block]
    heads = q_ref.shape[1] // HD

    @pl.when(block == 0)
    def _():
        kt_ref[...] = k_ref[...].T
        dk_sum[...] = jnp.zeros_like(dk_sum)
        dv_sum[...] = jnp.zeros_like(dv_sum)

    def run(count):
        make_bias(bias_ref, block, low, count, code_ref, seg_ref)
        bias = bias_ref[: count * KB, :]
        rows = pl.ds(pl.multiple_of(low * KB, KB), count * KB)

        def first(head):
            lanes = slice(head // 2 * 128, head // 2 * 128 + 128)
            query = one_head(q_ref[:, lanes] * jnp.asarray(0.125, LOW), head % 2)
            grad = one_head(g_ref[:, lanes], head % 2)
            scores = dot(k_ref[rows, lanes], query, NT) + bias
            return scores, dot(v_ref[rows, lanes], grad, NT), query, grad

        def second(head, scores, prob_grad, query, grad):
            probs = jnp.exp(scores - lse_ref[head : head + 1, :])
            delta = jnp.sum(probs * prob_grad, axis=0, keepdims=True)
            return probs.astype(LOW), (probs * (prob_grad - delta)).astype(LOW), query, grad

        outs = []

        def third(head, probs, score_grad, query, grad):
            lanes = slice(head // 2 * 128, head // 2 * 128 + 128)
            dv_sum[rows, lanes] += dot(probs, grad)
            dk_sum[rows, lanes] += dot(score_grad, query)
            outs.append(dot(kt_ref[head * HD : (head + 1) * HD, rows], score_grad))
            if head % 2 == 1:
                both = jnp.concatenate(outs[-2:], axis=0).T * 0.125
                dq_ref[:, lanes] = both.astype(LOW)

        start, middle_of = first(0), None
        for head in range(heads):
            later = first(head + 1) if head + 1 < heads else None
            now = second(head, *start)
            if head > 0:
                third(head - 1, *middle_of)
            start, middle_of = later, now
        third(heads - 1, *middle_of)

    for count in range(2, k_ref.shape[0] // KB + 1):
        pl.when(total == count)(functools.partial(run, count))

    @pl.when(block == pl.num_programs(0) - 1)
    def _():
        dk_ref[...] = dk_sum[...].astype(LOW)
        dv_ref[...] = dv_sum[...].astype(LOW)


def attend_forward(table, x, first, second, code, seg):
    seq, width = x.shape
    piece = (first.shape[0] - 16) // 3
    heads, blocks = 2 * piece // HD, seq // QB
    whole = lambda i, t: (0, 0)
    column = pl.BlockSpec((seq, 2 * piece), whole)
    return pl.pallas_call(
        forward_kernel,
        out_shape=(shape((seq, 2 * piece), LOW),) * 4 + (shape((8, seq), F32),),
        grid_spec=pltpu.PrefetchScalarGridSpec(
            num_scalar_prefetch=1,
            grid=(blocks,),
            in_specs=[
                pl.BlockSpec((seq, width), whole),
                pl.BlockSpec(first.shape, whole),
                pl.BlockSpec(second.shape, whole),
                pl.BlockSpec((seq, 1), whole),
                pl.BlockSpec((1, seq), whole),
            ],
            out_specs=[
                column,
                column,
                column,
                pl.BlockSpec((QB, 2 * piece), lambda i, t: (i, 0)),
                pl.BlockSpec((8, QB), lambda i, t: (0, i)),
            ],
            scratch_shapes=[
                pltpu.VMEM((3, 2 * piece, width), LOW),
                pltpu.VMEM((3, 2 * piece), F32),
                pltpu.VMEM((2 * piece, seq), LOW),
                pltpu.VMEM((seq, QB), F32),
            ],
        ),
        compiler_params=pltpu.CompilerParams(vmem_limit_bytes=VMEM_LIMIT),
        cost_estimate=pl.CostEstimate(
            flops=16 * seq * seq * piece + 12 * seq * width * piece,
            bytes_accessed=16 * seq * piece,
            transcendentals=seq * seq * heads // 2,
        ),
        name="attend_forward",
    )(table, x, first, second, code, seg)


def attend_backward(table, q, k, v, grad, lse, code, seg, *carried):
    seq, width = grad.shape
    blocks = seq // QB
    block = pl.BlockSpec((QB, width), lambda i, t: (i, 0))
    column = pl.BlockSpec((seq, width), lambda i, t: (0, 0))
    return pl.pallas_call(
        functools.partial(backward_kernel, len(carried)),
        out_shape=(shape((seq, width), LOW),) * 3 + tuple(shape(c.shape, c.dtype) for c in carried),
        grid_spec=pltpu.PrefetchScalarGridSpec(
            num_scalar_prefetch=1,
            grid=(blocks,),
            in_specs=[
                block,
                column,
                column,
                block,
                pl.BlockSpec((8, QB), lambda i, t: (0, i)),
                pl.BlockSpec((seq, 1), lambda i, t: (0, 0)),
                pl.BlockSpec((1, seq), lambda i, t: (0, 0)),
            ]
            + [HBM] * len(carried),
            out_specs=[block, column, column] + [HBM] * len(carried),
            scratch_shapes=[
                pltpu.VMEM((width, seq), LOW),
                pltpu.VMEM((seq, QB), F32),
                pltpu.VMEM((seq, width), F32),
                pltpu.VMEM((seq, width), F32),
            ]
            + [pltpu.SemaphoreType.DMA] * len(carried),
        ),
        compiler_params=pltpu.CompilerParams(vmem_limit_bytes=VMEM_LIMIT),
        cost_estimate=pl.CostEstimate(
            flops=16 * seq * seq * width,
            bytes_accessed=16 * seq * width,
            transcendentals=seq * seq * width // 128,
        ),
        name="attend_backward",
    )(table, q, k, v, grad, lse, code, seg, *carried)


def gelu_parts(pre):
    t = 1.0 / (1.0 + PHI_STEP * jnp.abs(pre))
    poly = PHI[7] * t + PHI[6]
    for factor in PHI[5::-1]:
        poly = poly * t + factor
    bell = jnp.exp(-0.5 * (pre * pre))
    tail = poly * t * bell
    cdf = jnp.where(pre < 0, tail, 1.0 - tail)
    return pre * cdf, cdf + pre * (bell * 0.3989422804014327)


def norm_stats(values):
    width = values.shape[-1]
    mean = jnp.sum(values, axis=-1, keepdims=True) * (1.0 / width)
    centred = values - mean
    spread = jnp.sum(centred * centred, axis=-1, keepdims=True) * (1.0 / width)
    rate = lax.rsqrt(spread + LN_EPSILON)
    return centred * rate, rate


def norm_back(grad, gain, xhat, rate):
    width = grad.shape[-1]
    scaled = grad * gain
    mean = jnp.sum(scaled, axis=-1, keepdims=True) * (1.0 / width)
    along = jnp.sum(scaled * xhat, axis=-1, keepdims=True) * (1.0 / width)
    return rate * (scaled - mean - xhat * along)


def column_sum(values):
    return jnp.sum(values, axis=0, keepdims=True)


def middle_kernel(
    total_slots,
    dp_bits,
    valid_ref,
    lengths_ref,
    ctx_a,
    ctx_b,
    gains,
    shifts,
    x_hbm,
    teacher_hbm,
    qa,
    qb,
    qc,
    qd,
    outin_own,
    outin_core,
    outin_far,
    back_own,
    back_core,
    second_own,
    second_core,
    out_hbm,
    dh_hbm,
    cg_a,
    cg_b,
    core_hbm,
    to_x,
    to_y,
    rest,
    out_send_a,
    out_send_b,
    out_keep_a,
    out_keep_b,
    sums,
    bias_sums,
    count_ref,
    outin_far_core,
    in_far,
    back_far,
    in_far_core,
    back_far_core,
    w_in,
    w_back,
    w_out,
    bias_parts,
    bias_in,
    xhat_one,
    rate_one,
    mid_low,
    hidden,
    slope,
    acc,
    dh_low,
    pre_grad,
    rows_in,
    rows_out,
    stage16,
    stage32,
    from_core,
    held,
    w_sem,
    in_sem,
    out_sem,
    load_sem,
    store_sem,
    send_sem,
    recv_sem,
    count_send,
    count_recv,
    far_send,
    far_recv,
):
    seq, width = acc.shape
    blocks = seq // RB
    half = width // 2
    out_rows = w_out.shape[0] // 4
    units = w_in.shape[2]
    side = units // 2
    core_at, y_at, x_at = partner("tensor", 0), partner("tensor", 1), partner("dp", 0)
    greet([core_at, y_at] + [partner("dp", bit) for bit in range(dp_bits)])

    def far_copy(n, source, target, device):
        return pltpu.make_async_remote_copy(
            src_ref=source,
            dst_ref=target,
            send_sem=far_send.at[n],
            recv_sem=far_recv.at[n],
            device_id=device,
            device_id_type=pl.DeviceIdType.MESH,
        )

    in_at = pl.ds(2 * out_rows, width)
    far = [
        far_copy(0, outin_far, outin_far_core, core_at),
        far_copy(1, back_own, back_far.at[0], y_at),
        far_copy(2, second_own.at[pl.ds(width, width), :], back_far.at[1], y_at),
        far_copy(3, outin_far.at[in_at, :], in_far, x_at),
        far_copy(4, in_far, in_far_core, core_at),
        far_copy(5, back_far.at[0], back_far_core.at[0], core_at),
        far_copy(6, back_far.at[1], back_far_core.at[1], core_at),
    ]
    for copy in far[:4]:
        copy.start()
    out_in = (outin_own, outin_core, outin_far, outin_far_core)
    in_parts = tuple(ref.at[in_at, :] for ref in out_in)
    in_other = (
        second_own.at[pl.ds(0, width), :],
        second_core.at[pl.ds(0, width), :],
        in_far,
        in_far_core,
    )
    back_parts = (back_own, back_core, back_far.at[0], back_far_core.at[0])
    back_other = (
        second_own.at[pl.ds(width, width), :],
        second_core.at[pl.ds(width, width), :],
        back_far.at[1],
        back_far_core.at[1],
    )

    def rows(i):
        return pl.ds(i * RB, RB)

    def fetch(source, i, slot):
        return pltpu.make_async_copy(source.at[rows(i), :], rows_in.at[slot], in_sem.at[slot])

    def out_weights(p, c):
        return pltpu.make_async_copy(
            out_in[p].at[pl.ds(c * out_rows, out_rows), :],
            w_out.at[pl.ds(p * out_rows, out_rows), pl.ds(c * half, half)],
            w_sem.at[p, c],
        )

    def bias_rows(p):
        source = (qa, qb, qc, qd)[p]
        return pltpu.make_async_copy(
            source.at[pl.ds(source.shape[0] - 16, 16), :], bias_parts.at[p], w_sem.at[p, 8]
        )

    def load_in(source, p, r):
        return pltpu.make_async_copy(
            source, w_in.at[p, :, pl.ds(r * side, side)], w_sem.at[p, 2 + 3 * r]
        )

    def load_back(source, p, r, c):
        return pltpu.make_async_copy(
            source.at[pl.ds(c * side, side), :],
            w_back.at[p, pl.ds(r * side, side), pl.ds(c * half, half)],
            w_sem.at[p, 3 + 3 * r + c],
        )

    def ffn_weights(p):
        load_in(in_parts[p], p, 0).start()
        load_in(in_other[p], p, 1).start()
        for c in range(2):
            load_back(back_parts[p], p, 0, c).start()
            load_back(back_other[p], p, 1, c).start()

    early = [out_weights(p, c) for p in range(4) for c in range(2)]
    for copy in early[:6]:
        copy.start()
    fetch(x_hbm, 0, 0).start()
    for p in range(4):
        bias_rows(p).start()
    for p in range(2):
        ffn_weights(p)

    def count_step(bit):
        return pltpu.make_async_remote_copy(
            src_ref=held.at[2 * bit],
            dst_ref=held.at[2 * bit + 1],
            send_sem=count_send.at[bit],
            recv_sem=count_recv.at[bit],
            device_id=partner("dp", bit),
            device_id_type=pl.DeviceIdType.MESH,
        )

    tokens = jnp.full(held.shape[1:], 0, jnp.int32)
    for i in range(lengths_ref.shape[0]):
        tokens += lengths_ref[i]
    held[0] = tokens
    count_step(0).start()

    def count_on(bit):
        count_step(bit).wait()
        held[2 * bit + 2] = held[2 * bit] + held[2 * bit + 1]
        if bit + 1 < dp_bits:
            count_step(bit + 1).start()

    far[0].wait_recv()
    for copy in early[6:]:
        copy.start()
    for copy in early:
        copy.wait()

    for i in range(blocks):
        if i + 1 < blocks:
            fetch(x_hbm, i + 1, (i + 1) % 2).start()
        fetch(x_hbm, i, i % 2).wait()
        context = jnp.concatenate([ctx_a[rows(i), :], ctx_b[rows(i), :]], axis=1)
        xhat, rate = norm_stats(dot(context, w_out[...]) + shifts[0:1, :] + rows_in[i % 2])
        xhat_one[rows(i), :] = xhat
        rate_one[rows(i), :] = rate
        mid_low[rows(i), :] = (xhat * gains[0:1, :] + shifts[1:2, :]).astype(LOW)
        acc[rows(i), :] = jnp.zeros((RB, width), F32)
        if i < dp_bits:
            count_on(i)
    for bit in range(blocks, dp_bits):
        count_on(bit)
    count_ref[...] = held[2 * dp_bits]
    fetch(teacher_hbm, 0, 0).start()
    for p in range(4):
        bias_rows(p).wait()
        part = bias_parts[p, 0:3, :].astype(F32)
        bias_in[p] = part[0:1] + part[1:2] + part[2:3]

    def up(p, carry):
        @pl.when(p == 2)
        def _():
            for n, then in ((3, 4), (1, 5), (2, 6)):
                far[n].wait_recv()
                far[then].start()
            ffn_weights(2)

        @pl.when(p == 3)
        def _():
            for n in (4, 5, 6):
                far[n].wait_recv()
            ffn_weights(3)

        for r in range(2):
            load_in(in_other[0], p, r).wait()
            for c in range(2):
                load_back(back_own, p, r, c).wait()
        def lift(k):
            return dot(mid_low[pl.ds(k * FR, FR), :], w_in[p]) + bias_in[p]

        def lower(k):
            at = pl.ds(k * FR, FR)
            acc[at, :] += dot(hidden[p, at, :], w_back[p])

        pre = lift(0)
        for k in range(seq // FR):
            later = lift(k + 1) if k + 1 < seq // FR else None
            at = pl.ds(k * FR, FR)
            act, der = gelu_parts(pre)
            hidden[p, at, :] = act.astype(LOW)
            slope[p, at, :] = der
            if k > 0:
                lower(k - 1)
            pre = later
        lower(seq // FR - 1)
        return carry

    lax.fori_loop(0, 4, up, 0)

    zero = jnp.zeros((1, width), F32)
    squares, gain_two, shift_two, shift_mid = zero, zero, zero, zero
    scale = total_slots / held[2 * dp_bits, 0:1, 0:1].astype(F32)
    stores = []
    for i in range(blocks):
        if i + 1 < blocks:
            fetch(teacher_hbm, i + 1, (i + 1) % 2).start()
        fetch(teacher_hbm, i, i % 2).wait()
        mid = xhat_one[rows(i), :] * gains[0:1, :] + shifts[1:2, :]
        xhat, rate = norm_stats(acc[rows(i), :] + shifts[2:3, :] + mid)
        output = xhat * gains[1:2, :] + shifts[3:4, :]
        if i >= 2:
            stores[i - 2].wait()
        rows_out[i % 2] = output
        stores.append(
            pltpu.make_async_copy(rows_out.at[i % 2], out_hbm.at[rows(i), :], out_sem.at[i % 2])
        )
        stores[i].start()
        live = (i * RB + lax.broadcasted_iota(jnp.int32, (RB, 1), 0)) < valid_ref[0]
        distance = jnp.where(live, output - rows_in[i % 2], 0.0)
        squares += column_sum(distance * distance)
        out_grad = scale * distance
        gain_two += column_sum(out_grad * xhat)
        shift_two += column_sum(out_grad)
        dh_two = norm_back(out_grad, gains[1:2, :], xhat, rate)
        shift_mid += column_sum(dh_two)
        acc[rows(i), :] = dh_two
        dh_low[rows(i), :] = dh_two.astype(LOW)
    for store in stores[-2:]:
        store.wait()

    sides = (pl.ds(0, side), pl.ds(side, side))

    def ffn_back(p):
        total = jnp.zeros((1, units), F32)

        def lift(k):
            return dot(dh_low[pl.ds(k * FR, FR), :], w_back[p], NT)

        def lower(k):
            at = pl.ds(k * FR, FR)
            acc[at, :] += dot(pre_grad[at, :], w_in[p], NT)

        raised = lift(0)
        for k in range(seq // FR):
            later = lift(k + 1) if k + 1 < seq // FR else None
            at = pl.ds(k * FR, FR)
            grad = (raised * slope[p, at, :]).astype(LOW)
            pre_grad[at, :] = grad
            total += column_sum(grad.astype(F32))
            if k > 0:
                lower(k - 1)
            raised = later
        lower(seq // FR - 1)
        bias_sums[pl.ds(p, 1), :] = total

    def to_core(pair, w):
        return pltpu.make_async_remote_copy(
            src_ref=stage16.at[w],
            dst_ref=core_hbm.at[pair, w],
            send_sem=send_sem.at[w],
            recv_sem=recv_sem.at[pair, w],
            device_id=core_at,
            device_id_type=pl.DeviceIdType.MESH,
        )

    def away(n, carry):
        p = 2 * n + 1
        ffn_back(p)

        @pl.when(n > 0)
        def _():
            for w in range(2):
                to_core(0, w).wait_send()

        stage16[0] = dot(mid_low[...], pre_grad[...], TN).astype(LOW)
        stage16[1] = dot(hidden[p], dh_low[...], TN).astype(LOW)
        for w in range(2):
            to_core(n, w).start()
        return carry

    lax.fori_loop(0, 2, away, 0)

    def in_moves(pair):
        return [
            pltpu.make_async_copy(stage32.at[0, :, sides[0]], rest.at[pair], store_sem.at[0]),
            pltpu.make_async_copy(stage16.at[0, :, sides[1]], to_x.at[pair], store_sem.at[1]),
        ]

    def back_moves(stage, target):
        return [
            pltpu.make_async_copy(
                stage.at[1, sides[r], sides[c]],
                target.at[r, sides[c], :],
                store_sem.at[2 + 2 * r + c],
            )
            for r in range(2)
            for c in range(2)
        ]

    moves = {1: in_moves(1) + back_moves(stage16, to_y), 0: in_moves(0) + back_moves(stage32, rest.at[pl.ds(2, 2)])}

    def home(n, carry):
        pair = 1 - n
        p = 2 * pair
        for w in range(2):
            to_core(pair, w).wait_recv()
            pltpu.make_async_copy(core_hbm.at[pair, w], from_core.at[w], load_sem.at[w]).start()
        ffn_back(p)

        @pl.when(n == 0)
        def _():
            for w in range(2):
                to_core(1, w).wait_send()

        @pl.when(n == 1)
        def _():
            for copy in moves[1]:
                copy.wait()

        stage32[0] = dot(mid_low[...], pre_grad[...], TN)
        stage32[1] = dot(hidden[p], dh_low[...], TN)
        for w in range(2):
            pltpu.make_async_copy(core_hbm.at[pair, w], from_core.at[w], load_sem.at[w]).wait()
            for k in range(0, width, 128):
                total = stage32[w, k : k + 128, :] + from_core[w, k : k + 128, :].astype(F32)
                stage32[w, k : k + 128, :] = total
                stage16[w, k : k + 128, :] = total.astype(LOW)

        @pl.when(n == 0)
        def _():
            for copy in moves[1]:
                copy.start()

        @pl.when(n == 1)
        def _():
            for copy in moves[0]:
                copy.start()

        return carry

    lax.fori_loop(0, 2, home, 0)

    gain_one, shift_one, shift_out = zero, zero, zero
    stores = []
    for i in range(blocks):
        grad, xhat = acc[rows(i), :], xhat_one[rows(i), :]
        gain_one += column_sum(grad * xhat)
        shift_one += column_sum(grad)
        dh_one = norm_back(grad, gains[0:1, :], xhat, rate_one[rows(i), :])
        shift_out += column_sum(dh_one)
        if i >= 2:
            stores[i - 2].wait()
        rows_out[i % 2] = dh_one
        stores.append(
            pltpu.make_async_copy(rows_out.at[i % 2], dh_hbm.at[rows(i), :], out_sem.at[i % 2])
        )
        stores[i].start()
        dh_one = dh_one.astype(LOW)
        dh_low[rows(i), :] = dh_one
        grad = dot(dh_one, w_out[...], NT).astype(LOW)
        cg_a[rows(i), :] = grad[:, :half]
        cg_b[rows(i), :] = grad[:, half:]
    for context, out_keep, out_send in (
        (ctx_a, out_keep_a, out_send_a),
        (ctx_b, out_keep_b, out_send_b),
    ):
        grad = dot(context[...], dh_low[...], TN)
        out_keep[...] = grad[:out_rows]
        out_send[...] = grad[out_rows:].astype(LOW)
    sums[...] = jnp.concatenate(
        [gain_one, gain_two, shift_out, shift_one, shift_mid, shift_two, squares, zero], axis=0
    )
    for store in stores[-2:]:
        store.wait()
    for copy in moves[0]:
        copy.wait()
    for copy in far:
        copy.wait_send()


def middle(
    total_slots, valid, lengths, ctx_a, ctx_b, gains, shifts, x, teacher, near, out_in, back, second
):
    seq, width = x.shape
    half = width // 2
    out_rows = ctx_a.shape[1] // 2
    units = width
    dp_bits = bits_of("dp")
    slab = (width, units // 2)
    return pl.pallas_call(
        functools.partial(middle_kernel, float(total_slots), dp_bits),
        out_shape=(
            shape((seq, width), F32),
            shape((seq, width), F32),
            shape((seq, half), LOW),
            shape((seq, half), LOW),
            shape((2, 2, width, units), LOW),
            shape((2,) + slab, LOW),
            shape((2,) + slab, LOW),
            shape((4,) + slab, F32),
            shape((out_rows, width), LOW),
            shape((out_rows, width), LOW),
            shape((out_rows, width), F32),
            shape((out_rows, width), F32),
            shape((8, width), F32),
            shape((4, units), F32),
            shape((8, 128), jnp.int32),
            shape(out_in[0].shape, LOW),
            shape(slab, LOW),
            shape((2,) + slab, LOW),
            shape(slab, LOW),
            shape((2,) + slab, LOW),
        ),
        in_specs=[SMEM, SMEM, VMEM, VMEM, VMEM, VMEM, HBM, HBM] + [HBM] * 11,
        out_specs=(HBM, HBM, VMEM, VMEM, HBM, HBM, HBM, HBM) + (VMEM,) * 7 + (HBM,) * 5,
        scratch_shapes=[
            pltpu.VMEM((4, width, units), LOW),
            pltpu.VMEM((4, units, width), LOW),
            pltpu.VMEM((4 * out_rows, width), LOW),
            pltpu.VMEM((4, 16, width), LOW),
            pltpu.VMEM((4, 1, units), F32),
            pltpu.VMEM((seq, width), F32),
            pltpu.VMEM((seq, 1), F32),
            pltpu.VMEM((seq, width), LOW),
            pltpu.VMEM((4, seq, units), LOW),
            pltpu.VMEM((4, seq, units), F32),
            pltpu.VMEM((seq, width), F32),
            pltpu.VMEM((seq, width), LOW),
            pltpu.VMEM((seq, units), LOW),
            pltpu.VMEM((2, RB, width), F32),
            pltpu.VMEM((2, RB, width), F32),
            pltpu.VMEM((2, width, units), LOW),
            pltpu.VMEM((2, width, units), F32),
            pltpu.VMEM((2, width, units), LOW),
            pltpu.VMEM((2 * dp_bits + 1, 8, 128), jnp.int32),
            pltpu.SemaphoreType.DMA((4, 9)),
            pltpu.SemaphoreType.DMA((2,)),
            pltpu.SemaphoreType.DMA((2,)),
            pltpu.SemaphoreType.DMA((2,)),
            pltpu.SemaphoreType.DMA((6,)),
            pltpu.SemaphoreType.DMA((2,)),
            pltpu.SemaphoreType.DMA((2, 2)),
            pltpu.SemaphoreType.DMA((dp_bits,)),
            pltpu.SemaphoreType.DMA((dp_bits,)),
            pltpu.SemaphoreType.DMA((7,)),
            pltpu.SemaphoreType.DMA((7,)),
        ],
        compiler_params=pltpu.CompilerParams(
            vmem_limit_bytes=VMEM_LIMIT, collective_id=1, has_side_effects=True
        ),
        cost_estimate=pl.CostEstimate(
            flops=6 * seq * width * (8 * units + width),
            bytes_accessed=30 << 20,
            transcendentals=2 * seq * 4 * units,
        ),
        name="middle",
    )(valid, lengths, ctx_a, ctx_b, gains, shifts, x, teacher, *near, *out_in, *back, *second)


def add_rows(out, terms, chunk=96):
    rows = out.shape[0]
    chunk = min(chunk, rows)

    def step(i, carry):
        at = pl.ds(pl.multiple_of(i * chunk, chunk), chunk)
        total = terms[0][at, :].astype(F32)
        for term in terms[1:]:
            total += term[at, :].astype(F32)
        out[at, :] = total.astype(out.dtype)
        return carry

    lax.fori_loop(0, rows // chunk, step, 0)


def cross_rows(x_ref, grads, okeep, osend, side, cross, keep, send, bias_ref):
    half = x_ref.shape[1] // 2
    piece = grads[0].shape[1] // 2
    mine = pl.ds(pl.multiple_of(side * half, half), half)
    other = pl.ds(pl.multiple_of((1 - side) * half, half), half)
    for i in range(3):
        cross[...] = dot(grads[i][...], x_ref[...], TN)
        at = slice(i * piece, (i + 1) * piece)
        for n, lanes in enumerate((mine, other)):
            keep[n, at, :] = cross[:piece, lanes]
            send[n, at, :] = cross[piece:, lanes].astype(send.dtype)
        bias_ref[i : i + 1, :] = column_sum(grads[i][...].astype(F32))
    for n, lanes in enumerate((mine, other)):
        keep[n, 3 * piece :, :] = okeep[:, lanes]
        send[n, 3 * piece :, :] = osend[:, lanes].astype(send.dtype)


def far_kernel(
    x_ref,
    dq,
    dk,
    dv,
    osend,
    okeep,
    away,
    away_first,
    bias_ref,
    keep,
    send,
    core,
    cross,
    send_sem,
    recv_sem,
):
    core_at = partner("tensor", 0)
    greet([core_at])
    bias_ref[...] = jnp.zeros(bias_ref.shape, F32)
    cross_rows(
        x_ref, (dq, dk, dv), okeep, osend, lax.axis_index("dp") & 1, cross, keep, send, bias_ref
    )
    copies = [
        pltpu.make_async_remote_copy(
            src_ref=send.at[n],
            dst_ref=core.at[n],
            send_sem=send_sem.at[n],
            recv_sem=recv_sem.at[n],
            device_id=core_at,
            device_id_type=pl.DeviceIdType.MESH,
        )
        for n in range(2)
    ]
    for n in (1, 0):
        copies[n].start()
    for n in (1, 0):
        copies[n].wait_recv()
        add_rows((away, away_first)[n], [keep.at[n], core.at[n]])
    for n in (1, 0):
        copies[n].wait_send()


def far_projections(x, grads, osend, okeep):
    seq, width = x.shape
    half = width // 2
    piece = grads[0].shape[1] // 2
    slabs = (2, width, half)
    return pl.pallas_call(
        far_kernel,
        out_shape=(shape(slabs[1:], LOW), shape(slabs[1:], LOW), shape((8, 2 * piece), F32)),
        in_specs=[VMEM] * 6,
        out_specs=(VMEM, VMEM, VMEM),
        scratch_shapes=[
            pltpu.VMEM(slabs, F32),
            pltpu.VMEM(slabs, F32),
            pltpu.VMEM(slabs, F32),
            pltpu.VMEM((2 * piece, width), F32),
            pltpu.SemaphoreType.DMA((2,)),
            pltpu.SemaphoreType.DMA((2,)),
        ],
        compiler_params=pltpu.CompilerParams(
            vmem_limit_bytes=VMEM_LIMIT, collective_id=3, has_side_effects=True
        ),
        cost_estimate=pl.CostEstimate(
            flops=12 * seq * width * piece, bytes_accessed=10 << 20, transcendentals=0
        ),
        name="far_projections",
    )(x, *grads, osend, okeep)


def finish_kernel(
    dp_bits,
    x_ref,
    w0,
    w1,
    w2,
    w3,
    dqa,
    dka,
    dva,
    dqb,
    dkb,
    dvb,
    osend,
    okeep,
    dh_hbm,
    rest,
    ffn_x,
    ffn_y,
    in_y,
    back_x,
    away,
    qkv_y,
    small_ref,
    bias_far,
    gx_hbm,
    result,
    small_out,
    own,
    own16,
    keep,
    send,
    core,
    y_recv,
    x_send,
    x_recv,
    total,
    z_send,
    z_recv,
    last_send,
    last_recv,
    extra,
    bias_ref,
    small_held,
    rows_in,
    rows_out,
    cross,
    load_sem,
    send_sem,
    recv_sem,
    in_sem,
    out_sem,
):
    seq, width = x_ref.shape
    half = width // 2
    piece = dqa.shape[1] // 2
    blocks = seq // RB
    place = lax.axis_index("dp")
    index = lax.axis_index("tensor")
    side = place & 1
    core_at, y_at = partner("tensor", 0), partner("tensor", 1)
    dp_at = [partner("dp", bit) for bit in range(dp_bits)]
    greet([core_at, y_at] + dp_at)
    started = {}

    def remote(key, source, target, device):
        n = len(started)
        started[key] = pltpu.make_async_remote_copy(
            src_ref=source,
            dst_ref=target,
            send_sem=send_sem.at[n],
            recv_sem=recv_sem.at[n],
            device_id=device,
            device_id_type=pl.DeviceIdType.MESH,
        )
        started[key].start()

    def arrive(key):
        started[key].wait_recv()

    remote("y", away, y_recv, y_at)
    loads = []
    for w, terms in enumerate(((rest.at[0], ffn_x.at[0], in_y), (rest.at[2], ffn_y.at[0], back_x))):
        targets = (own.at[w], own16.at[w, 0], own16.at[w, 1])
        loads.append(
            [
                pltpu.make_async_copy(term, target, load_sem.at[w, n])
                for n, (term, target) in enumerate(zip(terms, targets))
            ]
        )
        for copy in loads[w]:
            copy.start()

    def fetch(i):
        return pltpu.make_async_copy(
            dh_hbm.at[pl.ds(i * RB, RB), :], rows_in.at[i % 2], in_sem.at[i % 2]
        )

    fetch(0).start()

    rows_of = [width]
    for bit in range(1, min(dp_bits, 3)):
        rows_of.append(rows_of[-1] // 2)
    levels = min(dp_bits, 3) - 1

    def offset(level):
        at = 0
        for bit in range(1, level + 1):
            at = at + ((place >> bit) & 1) * rows_of[bit]
        return pl.multiple_of(at, rows_of[level])

    def other_offset(level):
        return pl.multiple_of(
            offset(level - 1) + (1 - ((place >> level) & 1)) * rows_of[level], rows_of[level]
        )

    def scatter(w, level):
        size = rows_of[level]
        out, into = ((z_send, z_recv) if level == 1 else (last_send, last_recv))
        add_rows(out.at[w], [total.at[w, pl.ds(other_offset(level), size), :]])
        remote((w, "z", level), out.at[w], into.at[w], dp_at[level])

    def collect(w, level):
        size = rows_of[level]
        arrive((w, "z", level))
        into = z_recv if level == 1 else last_recv
        mine = total.at[w, pl.ds(offset(level), size), :]
        if level < levels:
            add_rows(mine, [mine, into.at[w]])
        else:
            add_rows(result.at[w, 0, pl.ds(offset(level), size), :], [mine, into.at[w]])

    def settle(w):
        size = rows_of[levels]
        at = pl.ds(offset(levels), size)
        for bit in range(levels + 1, dp_bits):
            spare = result.at[w, 0, at, :]
            into = extra.at[w, bit - levels - 1]
            remote((w, "all", bit), spare, into, dp_at[bit])
            started[(w, "all", bit)].wait_send()
            arrive((w, "all", bit))
            add_rows(spare, [spare, into])

    def spread(w, level):
        if level == 0:
            remote((w, "gather", 0), result.at[w, 0], result.at[w, 1], dp_at[0])
        else:
            rows = result.at[w, 0, pl.ds(offset(level), rows_of[level]), :]
            remote((w, "gather", level), rows, rows, dp_at[level])

    for w in range(2):
        for copy in loads[w]:
            copy.wait()
        add_rows(total.at[w], [own.at[w], own16.at[w, 0], own16.at[w, 1]])
        scatter(w, 1)

    cross_rows(x_ref, (dqa, dka, dva), okeep, osend, side, cross, keep, send, bias_ref)
    for n in (1, 0):
        remote(("core", n), send.at[n], core.at[n], core_at)

    small_held[0] = jnp.zeros(small_held.shape[1:], F32)
    small_held[0, 16:24, :] = small_ref[0:8, :]
    for p in range(4):
        row = 4 * (index ^ p)
        half_mine = small_ref[8 + p : 9 + p, :half]
        half_other = small_ref[8 + p : 9 + p, half:]
        low_half = jnp.where(side == 0, half_mine, half_other)
        high_half = jnp.where(side == 0, half_other, half_mine)
        small_held[0, pl.ds(row, 1), :] = jnp.concatenate([low_half, high_half], axis=1)
        for i, k in enumerate((0, 2)):
            values = (bias_ref, bias_far)[p // 2][k : k + 1, :]
            if p % 2 == 1:
                values = pltpu.roll(values, piece, 1)
            small_held[0, pl.ds(row + 1 + i, 1), :half] = values

    def small_step(n):
        bits = [core_at, y_at] + dp_at
        remote(("small", n), small_held.at[2 * n], small_held.at[2 * n + 1], bits[n])

    def small_sum(n):
        arrive(("small", n))
        out = small_held.at[2 * n + 2] if n < dp_bits + 1 else small_out
        out[...] = small_held[2 * n] + small_held[2 * n + 1]

    weights = ((w0, w1), (w2, w3))
    grads = ((dqa, dka, dva), (dqb, dkb, dvb))
    stores = []

    def inputs_rows(b):
        at = pl.ds(b * RB, RB)
        if b + 1 < blocks:
            fetch(b + 1).start()
        fetch(b).wait()
        grad = rows_in[b % 2]
        for g in range(2):
            for i in range(3):
                rows = slice(i * piece, (i + 1) * piece)
                w = jnp.concatenate([ref[rows, :] for ref in weights[g]], axis=0)
                grad += dot(grads[g][i][at, :], w)
        if b >= 2:
            stores[b - 2].wait()
        rows_out[b % 2] = grad
        stores.append(
            pltpu.make_async_copy(rows_out.at[b % 2], gx_hbm.at[at, :], out_sem.at[b % 2])
        )
        stores[b].start()

    small_step(0)
    collect(0, 1)
    scatter(0, 2)
    arrive(("core", 1))
    add_rows(x_send, [keep.at[1], core.at[1], qkv_y])
    remote("qkv x", x_send, x_recv, dp_at[0])
    collect(1, 1)
    scatter(1, 2)
    inputs_rows(0)
    small_sum(0)
    small_step(1)
    collect(0, 2)
    settle(0)
    spread(0, 2)
    inputs_rows(1)
    small_sum(1)
    small_step(2)
    collect(1, 2)
    settle(1)
    spread(1, 2)
    arrive(("core", 0))
    arrive("y")
    add_rows(total.at[2], [keep.at[0], core.at[0], y_recv])
    arrive("qkv x")
    add_rows(total.at[2], [total.at[2], x_recv])
    scatter(2, 1)
    arrive((0, "gather", 2))
    spread(0, 1)
    inputs_rows(2)
    small_sum(2)
    small_step(3)
    arrive((1, "gather", 2))
    spread(1, 1)
    collect(2, 1)
    scatter(2, 2)
    arrive((0, "gather", 1))
    spread(0, 0)
    inputs_rows(3)
    small_sum(3)
    small_step(4)
    collect(2, 2)
    settle(2)
    spread(2, 2)
    arrive((1, "gather", 1))
    spread(1, 0)
    for n in range(4, dp_bits + 2):
        small_sum(n)
        if n + 1 < dp_bits + 2:
            small_step(n + 1)
    arrive((2, "gather", 2))
    spread(2, 1)
    arrive((2, "gather", 1))
    spread(2, 0)
    for w in range(3):
        arrive((w, "gather", 0))
    for key, copy in started.items():
        if not (isinstance(key, tuple) and key[1] == "all"):
            copy.wait_send()
    for store in stores[-2:]:
        store.wait()


def finish(x, weights, grads, osend, okeep, dh, rest, ffn_x, ffn_y, in_y, back_x, away, qkv_y, small, bias_far):
    seq, width = x.shape
    half = width // 2
    piece = grads[0].shape[1] // 2
    dp_bits = bits_of("dp")
    slab = (width, half)
    copies = 4 + dp_bits + 2 + 3 * (2 + 3 + max(dp_bits - 3, 0))
    return pl.pallas_call(
        functools.partial(finish_kernel, dp_bits),
        out_shape=(
            shape((seq, width), F32),
            shape((3, 2) + slab, LOW),
            shape((24, width), F32),
        ),
        in_specs=[VMEM] * 13 + [HBM] * 6 + [HBM, VMEM, VMEM, VMEM],
        out_specs=(HBM, VMEM, VMEM),
        scratch_shapes=[
            pltpu.VMEM((2,) + slab, F32),
            pltpu.VMEM((2, 2) + slab, LOW),
            pltpu.VMEM((2,) + slab, F32),
            pltpu.VMEM((2,) + slab, F32),
            pltpu.VMEM((2,) + slab, F32),
            pltpu.VMEM(slab, LOW),
            pltpu.VMEM(slab, LOW),
            pltpu.VMEM(slab, LOW),
            pltpu.VMEM((3,) + slab, F32),
            pltpu.VMEM((3, width // 2, half), LOW),
            pltpu.VMEM((3, width // 2, half), LOW),
            pltpu.VMEM((3, width // 4, half), LOW),
            pltpu.VMEM((3, width // 4, half), LOW),
            pltpu.VMEM((3, max(dp_bits - 3, 1), width // 4, half), LOW),
            pltpu.VMEM((8, 2 * piece), F32),
            pltpu.VMEM((2 * dp_bits + 4, 24, width), F32),
            pltpu.VMEM((2, RB, width), F32),
            pltpu.VMEM((2, RB, width), F32),
            pltpu.VMEM((2 * piece, width), F32),
            pltpu.SemaphoreType.DMA((2, 3)),
            pltpu.SemaphoreType.DMA((copies,)),
            pltpu.SemaphoreType.DMA((copies,)),
            pltpu.SemaphoreType.DMA((2,)),
            pltpu.SemaphoreType.DMA((2,)),
        ],
        compiler_params=pltpu.CompilerParams(
            vmem_limit_bytes=VMEM_LIMIT, collective_id=2, has_side_effects=True
        ),
        cost_estimate=pl.CostEstimate(
            flops=36 * seq * width * piece, bytes_accessed=50 << 20, transcendentals=0
        ),
        name="finish",
    )(x, *weights, *grads, osend, okeep, dh, rest, ffn_x, ffn_y, in_y, back_x, away, qkv_y, small, bias_far)


def widen_kernel(
    place_ref,
    result,
    small,
    count,
    source,
    loss_ref,
    qkv_ref,
    bqv_ref,
    out_ref,
    in_ref,
    bin_ref,
    back_ref,
    gains_ref,
    shifts_ref,
    target,
    copy_sem,
):
    passing = pltpu.make_async_copy(source, target, copy_sem)
    passing.start()
    half = result.shape[3]
    piece = qkv_ref.shape[1]
    side = place_ref[0]
    for n in range(2):
        natural = (side + n) % 2
        at = pl.ds(pl.multiple_of(natural * half, half), half)
        in_ref[:, at] = result[0, n].astype(F32)
        for c in range(2):
            rows = result[1, n, c * half : (c + 1) * half, :]
            back_ref[at, c * half : (c + 1) * half] = rows.astype(F32)
        for i in range(3):
            qkv_ref[i, :, at] = result[2, n, i * piece : (i + 1) * piece, :].astype(F32)
        out_ref[:, at] = result[2, n, 3 * piece :, :].astype(F32)
    row = 4 * place_ref[1]
    bin_ref[...] = small[pl.ds(row, 1), :]
    for i in range(2):
        bqv_ref[i : i + 1, :] = small[pl.ds(row + 1 + i, 1), :piece]
    gains_ref[...] = small[16:18, :]
    shifts_ref[...] = small[18:22, :]
    tokens = count[0:1, 0:1].astype(F32)
    total = jnp.sum(small[22:23, :], axis=1, keepdims=True)
    loss_ref[...] = total / (2.0 * small.shape[1] * tokens)
    passing.wait()


def widen(place, result, small, count, inputs_grad, piece, rows):
    width, half = result.shape[2:]
    return pl.pallas_call(
        widen_kernel,
        out_shape=(
            shape((1, 1), F32),
            shape((3, piece, width), F32),
            shape((2, piece), F32),
            shape((rows, width), F32),
            shape((width, 2 * half), F32),
            shape((1, 2 * half), F32),
            shape((2 * half, width), F32),
            shape((2, width), F32),
            shape((4, width), F32),
            shape(inputs_grad.shape, F32),
        ),
        in_specs=[SMEM, VMEM, VMEM, VMEM, HBM],
        out_specs=(VMEM,) * 9 + (HBM,),
        scratch_shapes=[pltpu.SemaphoreType.DMA],
        compiler_params=pltpu.CompilerParams(vmem_limit_bytes=VMEM_LIMIT),
        name="widen",
    )(place, result, small, count, inputs_grad)


def per_device(
    inputs,
    w_qkv,
    b_qv,
    w_out,
    w_in,
    b_in,
    w_back,
    norm_gains,
    shifts,
    segment_ids,
    valid_lengths,
    teacher,
):
    own_seqs, seq, width = inputs.shape
    assert own_seqs == 1 and lax.axis_size("tensor") == 4
    total_slots = seq * lax.axis_size("tensor") * lax.axis_size("dp")
    half = width // 2
    piece = w_qkv.shape[2]
    units = w_in.shape[1]
    index = lax.axis_index("tensor")
    side = (lax.axis_index("dp") & 1).astype(jnp.int32)
    side_row = side.reshape(1)
    x = inputs.reshape(seq, width)

    near = round_qkv(side_row, w_qkv.transpose(0, 2, 1), b_qv, b_in[None, :])
    core = swap(near, "tensor", 0)
    far = swap(near, "tensor", 1)
    core, w_in, w_back, w_out = lax.optimization_barrier((core, w_in, w_back, w_out))
    out_in, back, second, x_low = round_rest(side_row, w_out, w_in, w_back, x)
    out_in_far = swap(out_in, "tensor", 1)

    valid = lax.dynamic_index_in_dim(valid_lengths, index, keepdims=False)
    segments = lax.dynamic_index_in_dim(segment_ids, index, keepdims=False)
    positions = jnp.arange(seq, dtype=jnp.int32)
    code = jnp.where(positions < valid, segments, -1)[:, None]
    seg = segments[None, :]
    table = span_tables(segments, valid, seq)

    qa, ka, va, ctx_a, lse_a = attend_forward(table, x_low, near, core, code, seg)
    out_in, back, second, far, ctx_a = lax.optimization_barrier((out_in, back, second, far, ctx_a))
    core_far = swap(far, "tensor", 0)
    out_in_core = swap(out_in, "tensor", 0)
    back_core = swap(back, "tensor", 0)
    second_core = swap(second, "tensor", 0)
    qb, kb, vb, ctx_b, lse_b = attend_forward(table, x_low, far, core_far, code, seg)
    (
        output,
        dh_one,
        cg_a,
        cg_b,
        _,
        to_x,
        to_y,
        rest,
        out_send_a,
        out_send_b,
        out_keep_a,
        out_keep_b,
        sums,
        bias_sums,
        count,
        *_,
    ) = middle(
        total_slots,
        valid.reshape(1),
        valid_lengths,
        ctx_a,
        ctx_b,
        norm_gains,
        shifts,
        x,
        teacher.reshape(seq, width),
        (near, core, far, core_far),
        (out_in, out_in_core, out_in_far),
        (back, back_core),
        (second, second_core),
    )
    ffn_x = swap(to_x, "dp", 0)
    ffn_y = swap(to_y, "tensor", 1)
    grads_b = attend_backward(table, qb, kb, vb, cg_b, lse_b, code, seg)
    away, away_first, bias_far = far_projections(x_low, grads_b, out_send_b, out_keep_b)
    ffn_x, ffn_y, away_first = lax.optimization_barrier((ffn_x, ffn_y, away_first))
    in_away = (rest[1] + ffn_x[1].astype(F32)).astype(LOW)
    back_away = (rest[3] + ffn_y[1].astype(F32)).astype(LOW)
    in_away, back_away, away_first, cg_a = lax.optimization_barrier(
        (in_away, back_away, away_first, cg_a)
    )
    in_y = swap(in_away, "tensor", 1)
    back_x = swap(back_away, "dp", 0)
    qkv_y = swap(away_first, "tensor", 1)
    *grads_a, output = attend_backward(table, qa, ka, va, cg_a, lse_a, code, seg, output)
    small = jnp.concatenate([sums, bias_sums, jnp.zeros((4, width), F32)], axis=0)
    grad_inputs, slabs, small = finish(
        x_low,
        (near, core, far, core_far),
        (*grads_a, *grads_b),
        out_send_a,
        out_keep_a,
        dh_one,
        rest,
        ffn_x,
        ffn_y,
        in_y,
        back_x,
        away,
        qkv_y,
        small,
        bias_far,
    )
    (
        loss,
        grad_w_qkv,
        grad_b_qv,
        grad_w_out,
        grad_w_in,
        grad_b_in,
        grad_w_back,
        grad_gains,
        grad_shifts,
        grad_inputs,
    ) = widen(jnp.stack([side, index]), slabs, small, count, grad_inputs, piece, w_out.shape[0])
    return (
        output.reshape(own_seqs, seq, width),
        loss[0, 0],
        grad_inputs.reshape(own_seqs, seq, width),
        grad_w_qkv.transpose(0, 2, 1),
        grad_b_qv,
        grad_w_out,
        grad_w_in,
        grad_b_in[0],
        grad_w_back,
        grad_gains,
        grad_shifts,
    )


def solution(mesh):
    return jax.shard_map(
        per_device,
        mesh=mesh,
        in_specs=(
            P(("dp", "tensor"), None, None),
            P(None, None, "tensor"),
            P(None, "tensor"),
            P("tensor", None),
            P(None, "tensor"),
            P("tensor"),
            P("tensor", None),
            P(),
            P(),
            P("dp", None),
            P("dp"),
            P(("dp", "tensor"), None, None),
        ),
        out_specs=(
            P(("dp", "tensor"), None, None),
            P(),
            P(("dp", "tensor"), None, None),
            P(None, None, "tensor"),
            P(None, "tensor"),
            P("tensor", None),
            P(None, "tensor"),
            P("tensor"),
            P("tensor", None),
            P(),
            P(),
        ),
        check_vma=False,
    )
```

```python
import functools
import math

import jax
import jax.numpy as jnp
from jax import lax
from jax.experimental import pallas as pl
from jax.experimental.pallas import tpu as pltpu
from jax.sharding import PartitionSpec as P

HD = 64
LN_EPSILON = 1e-05
MASKED_SCORE = -1000000000.0
QB = 256
KB = 128
RB = 256
FR = 256
NT = ((1,), (1,))
TN = ((0,), (0,))
PHI = (
    0.09255110872,
    0.09001568156,
    0.1049848251,
    0.006341010132,
    0.2381524984,
    -0.2150534404,
    0.2551771707,
    -0.07216888208,
)
PHI_STEP = 0.23164188826636045

VMEM_LIMIT = 63 << 20
VMEM = pl.BlockSpec(memory_space=pltpu.VMEM)
SMEM = pl.BlockSpec(memory_space=pltpu.SMEM)
HBM = pl.BlockSpec(memory_space=pl.ANY)
LOW = jnp.bfloat16
F32 = jnp.float32


def dot(left, right, dims=((1,), (0,))):
    return lax.dot_general(left, right, (dims, ((), ())), preferred_element_type=jnp.float32)


def shape(dims, dtype):
    return jax.ShapeDtypeStruct(dims, dtype)


def swap(values, axis, bit):
    size = lax.axis_size(axis)
    return lax.ppermute(values, axis, [(i, i ^ (1 << bit)) for i in range(size)])


def bits_of(axis):
    return int(math.log2(lax.axis_size(axis)))


def partner(axis, bit):
    here = {name: lax.axis_index(name) for name in ("dp", "tensor")}
    here[axis] = here[axis] ^ (1 << bit)
    return here["dp"], here["tensor"]


def greet(partners):
    barrier = pltpu.get_barrier_semaphore()
    for device in partners:
        pl.semaphore_signal(
            barrier, inc=1, device_id=device, device_id_type=pl.DeviceIdType.MESH
        )
    pl.semaphore_wait(barrier, len(partners))


def three_parts(values):
    first = values.astype(LOW)
    rest = values - first.astype(F32)
    second = rest.astype(LOW)
    return first, second, (rest - second.astype(F32)).astype(LOW)


def round_qkv_kernel(side_ref, w_ref, bqv_ref, bin_ref, out_ref):
    piece = w_ref.shape[1]
    width = w_ref.shape[2]
    half = bin_ref.shape[1] // 2
    for i in range(3):
        out_ref[i * piece : (i + 1) * piece, :] = w_ref[i].astype(LOW)
    mine = bin_ref[:, pl.ds(pl.multiple_of(side_ref[0] * half, half), half)]
    other = bin_ref[:, pl.ds(pl.multiple_of((1 - side_ref[0]) * half, half), half)]
    pad = jnp.zeros((1, width - piece), F32)
    rows = [jnp.concatenate([mine, other], axis=1)]
    rows += [jnp.concatenate([bqv_ref[i : i + 1, :], pad], axis=1) for i in range(2)]
    parts = [part.astype(F32) for row in rows for part in three_parts(row)]
    parts += [jnp.zeros((1, width), F32)] * 7
    out_ref[3 * piece :, :] = jnp.concatenate(parts, axis=0).astype(LOW)


def round_qkv(side, w_qkv, b_qv, b_in):
    _, piece, width = w_qkv.shape
    return pl.pallas_call(
        round_qkv_kernel,
        out_shape=shape((3 * piece + 16, width), LOW),
        in_specs=[SMEM, VMEM, VMEM, VMEM],
        out_specs=VMEM,
        compiler_params=pltpu.CompilerParams(vmem_limit_bytes=VMEM_LIMIT),
        name="round_qkv",
    )(side, w_qkv, b_qv, b_in)


def round_rest_kernel(side_ref, wo_ref, wi_ref, wb_ref, x_ref, out_in, back, second, x_low_ref):
    rows, width = wo_ref.shape
    half = width // 2
    for c in range(2):
        out_in[c * rows : (c + 1) * rows, :] = wo_ref[:, c * half : (c + 1) * half].astype(LOW)
    x_low_ref[...] = x_ref[...].astype(LOW)
    parts = (
        (out_in, 2 * rows, back, 0, side_ref[0]),
        (second, 0, second, width, 1 - side_ref[0]),
    )
    for to_in, in_base, to_back, back_base, side in parts:
        at = pl.ds(pl.multiple_of(side * half, half), half)
        to_in[in_base : in_base + width, :] = wi_ref[:, at].astype(LOW)
        for c in range(2):
            start = back_base + c * half
            to_back[start : start + half, :] = wb_ref[at, c * half : (c + 1) * half].astype(LOW)


def round_rest(side, w_out, w_in, w_back, x):
    rows, width = w_out.shape
    half = width // 2
    return pl.pallas_call(
        round_rest_kernel,
        out_shape=(
            shape((2 * rows + width, half), LOW),
            shape((width, half), LOW),
            shape((2 * width, half), LOW),
            shape(x.shape, LOW),
        ),
        in_specs=[SMEM, VMEM, VMEM, VMEM, VMEM],
        out_specs=(VMEM,) * 4,
        compiler_params=pltpu.CompilerParams(vmem_limit_bytes=VMEM_LIMIT),
        name="round_rest",
    )(side, w_out, w_in, w_back, x)


def span_tables(segments, valid, seq):
    blocks = seq // QB
    firsts, lasts = segments[::QB], segments[QB - 1 :: QB]
    low = jnp.sum((segments[None, :] < firsts[:, None]).astype(jnp.int32), axis=1)
    high = jnp.sum((segments[None, :] <= lasts[:, None]).astype(jnp.int32), axis=1)
    own_end = (jnp.arange(blocks, dtype=jnp.int32) + 1) * QB
    high = jnp.maximum(jnp.minimum(high, valid), own_end)
    low_block = low // KB
    high_block = (high + KB - 1) // KB
    return jnp.stack([low_block, high_block - low_block]).astype(jnp.int32)


def make_bias(bias_ref, block, low, count, code_ref, seg_ref):
    dims = (count * KB, QB)
    codes = code_ref[pl.ds(pl.multiple_of(low * KB, KB), count * KB), :]
    segs = seg_ref[:, pl.ds(pl.multiple_of(block * QB, QB), QB)]
    key_at = low * KB + lax.broadcasted_iota(jnp.int32, dims, 0)
    query_at = block * QB + lax.broadcasted_iota(jnp.int32, dims, 1)
    allowed = (codes == segs) | (key_at == query_at)
    bias_ref[: count * KB, :] = jnp.where(allowed, 0.0, MASKED_SCORE)


def one_head(values, head):
    lane = lax.broadcasted_iota(jnp.int32, values.shape, 1)
    keep = (lane < HD) if head == 0 else (lane >= HD)
    return jnp.where(keep, values, jnp.zeros_like(values))


def forward_kernel(
    table_ref,
    x_ref,
    w0_ref,
    w1_ref,
    code_ref,
    seg_ref,
    q_ref,
    k_ref,
    v_ref,
    ctx_ref,
    lse_ref,
    weights,
    biases,
    vt_ref,
    bias_ref,
):
    block = pl.program_id(0)
    low, total = table_ref[0, block], table_ref[1, block]
    piece = (w0_ref.shape[0] - 16) // 3
    pairs = 2 * piece // 128

    @pl.when(block == 0)
    def _():
        for i in range(3):
            for n, ref in enumerate((w0_ref, w1_ref)):
                rows = ref[i * piece : (i + 1) * piece, :]
                weights[i, n * piece : (n + 1) * piece, :] = rows
        lane = lax.broadcasted_iota(jnp.int32, (1, x_ref.shape[1]), 1)
        for i in (0, 2):
            base = 3 * piece + (3 if i == 0 else 6)
            both = [
                sum(ref[base + part : base + part + 1, :].astype(F32) for part in range(3))
                for ref in (w0_ref, w1_ref)
            ]
            row = jnp.where(lane < piece, both[0], pltpu.roll(both[1], piece, 1))
            biases[i : i + 1, :] = row[:, : 2 * piece]
        biases[1:2, :] = jnp.zeros((1, 2 * piece), F32)

        def project(b, carry):
            at = pl.ds(pl.multiple_of(b * QB, QB), QB)
            for i, ref in enumerate((q_ref, k_ref, v_ref)):
                ref[at, :] = (dot(x_ref[at, :], weights[i], NT) + biases[i : i + 1, :]).astype(LOW)
            vt_ref[:, at] = v_ref[at, :].T
            return carry

        lax.fori_loop(0, x_ref.shape[0] // QB, project, 0)

    def run(count):
        make_bias(bias_ref, block, low, count, code_ref, seg_ref)
        bias = bias_ref[: count * KB, :]
        rows = pl.ds(pl.multiple_of(low * KB, KB), count * KB)
        queries = pl.ds(pl.multiple_of(block * QB, QB), QB)

        def scores(head):
            lanes = slice(head // 2 * 128, head // 2 * 128 + 128)
            query = q_ref[queries, lanes] * jnp.asarray(0.125, LOW)
            return dot(k_ref[rows, lanes], one_head(query, head % 2), NT) + bias

        def soft(values, head):
            peak = jnp.max(values, axis=0, keepdims=True)
            powers = jnp.exp(values - peak)
            mass = jnp.sum(powers, axis=0, keepdims=True)
            lse_ref[head : head + 1, :] = peak + jnp.log(mass)
            return (powers * (1.0 / mass)).astype(LOW)

        outs = []

        def context(probs, head):
            outs.append(dot(vt_ref[head * HD : (head + 1) * HD, rows], probs))
            if head % 2 == 1:
                both = jnp.concatenate(outs[-2:], axis=0).T
                ctx_ref[:, head // 2 * 128 : head // 2 * 128 + 128] = both.astype(LOW)

        values, probs = scores(0), None
        for head in range(2 * pairs):
            later = scores(head + 1) if head + 1 < 2 * pairs else None
            now = soft(values, head)
            if head > 0:
                context(probs, head - 1)
            values, probs = later, now
        context(probs, 2 * pairs - 1)

    for count in range(2, k_ref.shape[0] // KB + 1):
        pl.when(total == count)(functools.partial(run, count))


def backward_kernel(carried, table_ref, q_ref, k_ref, v_ref, g_ref, lse_ref, code_ref, seg_ref, *refs):
    block = pl.program_id(0)
    refs = list(refs)
    if carried:
        source, target = refs.pop(0), refs.pop(3)
        target[...] = source[...]
    dq_ref, dk_ref, dv_ref, kt_ref, bias_ref, dk_sum, dv_sum = refs
    low, total = table_ref[0, block], table_ref[1, block]
    heads = q_ref.shape[1] // HD

    @pl.when(block == 0)
    def _():
        kt_ref[...] = k_ref[...].T
        dk_sum[...] = jnp.zeros_like(dk_sum)
        dv_sum[...] = jnp.zeros_like(dv_sum)

    def run(count):
        make_bias(bias_ref, block, low, count, code_ref, seg_ref)
        bias = bias_ref[: count * KB, :]
        rows = pl.ds(pl.multiple_of(low * KB, KB), count * KB)

        def first(head):
            lanes = slice(head // 2 * 128, head // 2 * 128 + 128)
            query = one_head(q_ref[:, lanes] * jnp.asarray(0.125, LOW), head % 2)
            grad = one_head(g_ref[:, lanes], head % 2)
            scores = dot(k_ref[rows, lanes], query, NT) + bias
            return scores, dot(v_ref[rows, lanes], grad, NT), query, grad

        def second(head, scores, prob_grad, query, grad):
            probs = jnp.exp(scores - lse_ref[head : head + 1, :])
            delta = jnp.sum(probs * prob_grad, axis=0, keepdims=True)
            return probs.astype(LOW), (probs * (prob_grad - delta)).astype(LOW), query, grad

        outs = []

        def third(head, probs, score_grad, query, grad):
            lanes = slice(head // 2 * 128, head // 2 * 128 + 128)
            dv_sum[rows, lanes] += dot(probs, grad)
            dk_sum[rows, lanes] += dot(score_grad, query)
            outs.append(dot(kt_ref[head * HD : (head + 1) * HD, rows], score_grad))
            if head % 2 == 1:
                both = jnp.concatenate(outs[-2:], axis=0).T * 0.125
                dq_ref[:, lanes] = both.astype(LOW)

        start, middle_of = first(0), None
        for head in range(heads):
            later = first(head + 1) if head + 1 < heads else None
            now = second(head, *start)
            if head > 0:
                third(head - 1, *middle_of)
            start, middle_of = later, now
        third(heads - 1, *middle_of)

    for count in range(2, k_ref.shape[0] // KB + 1):
        pl.when(total == count)(functools.partial(run, count))

    @pl.when(block == pl.num_programs(0) - 1)
    def _():
        dk_ref[...] = dk_sum[...].astype(LOW)
        dv_ref[...] = dv_sum[...].astype(LOW)


def attend_forward(table, x, first, second, code, seg):
    seq, width = x.shape
    piece = (first.shape[0] - 16) // 3
    heads, blocks = 2 * piece // HD, seq // QB
    whole = lambda i, t: (0, 0)
    column = pl.BlockSpec((seq, 2 * piece), whole)
    return pl.pallas_call(
        forward_kernel,
        out_shape=(shape((seq, 2 * piece), LOW),) * 4 + (shape((8, seq), F32),),
        grid_spec=pltpu.PrefetchScalarGridSpec(
            num_scalar_prefetch=1,
            grid=(blocks,),
            in_specs=[
                pl.BlockSpec((seq, width), whole),
                pl.BlockSpec(first.shape, whole),
                pl.BlockSpec(second.shape, whole),
                pl.BlockSpec((seq, 1), whole),
                pl.BlockSpec((1, seq), whole),
            ],
            out_specs=[
                column,
                column,
                column,
                pl.BlockSpec((QB, 2 * piece), lambda i, t: (i, 0)),
                pl.BlockSpec((8, QB), lambda i, t: (0, i)),
            ],
            scratch_shapes=[
                pltpu.VMEM((3, 2 * piece, width), LOW),
                pltpu.VMEM((3, 2 * piece), F32),
                pltpu.VMEM((2 * piece, seq), LOW),
                pltpu.VMEM((seq, QB), F32),
            ],
        ),
        compiler_params=pltpu.CompilerParams(vmem_limit_bytes=VMEM_LIMIT),
        cost_estimate=pl.CostEstimate(
            flops=16 * seq * seq * piece + 12 * seq * width * piece,
            bytes_accessed=16 * seq * piece,
            transcendentals=seq * seq * heads // 2,
        ),
        name="attend_forward",
    )(table, x, first, second, code, seg)


def attend_backward(table, q, k, v, grad, lse, code, seg, *carried):
    seq, width = grad.shape
    blocks = seq // QB
    block = pl.BlockSpec((QB, width), lambda i, t: (i, 0))
    column = pl.BlockSpec((seq, width), lambda i, t: (0, 0))
    return pl.pallas_call(
        functools.partial(backward_kernel, len(carried)),
        out_shape=(shape((seq, width), LOW),) * 3 + tuple(shape(c.shape, c.dtype) for c in carried),
        grid_spec=pltpu.PrefetchScalarGridSpec(
            num_scalar_prefetch=1,
            grid=(blocks,),
            in_specs=[
                block,
                column,
                column,
                block,
                pl.BlockSpec((8, QB), lambda i, t: (0, i)),
                pl.BlockSpec((seq, 1), lambda i, t: (0, 0)),
                pl.BlockSpec((1, seq), lambda i, t: (0, 0)),
            ]
            + [pl.BlockSpec((QB, c.shape[1]), lambda i, t: (i, 0)) for c in carried],
            out_specs=[block, column, column]
            + [pl.BlockSpec((QB, c.shape[1]), lambda i, t: (i, 0)) for c in carried],
            scratch_shapes=[
                pltpu.VMEM((width, seq), LOW),
                pltpu.VMEM((seq, QB), F32),
                pltpu.VMEM((seq, width), F32),
                pltpu.VMEM((seq, width), F32),
            ],
        ),
        compiler_params=pltpu.CompilerParams(vmem_limit_bytes=VMEM_LIMIT),
        cost_estimate=pl.CostEstimate(
            flops=16 * seq * seq * width,
            bytes_accessed=16 * seq * width,
            transcendentals=seq * seq * width // 128,
        ),
        name="attend_backward",
    )(table, q, k, v, grad, lse, code, seg, *carried)


def gelu_parts(pre):
    t = 1.0 / (1.0 + PHI_STEP * jnp.abs(pre))
    poly = PHI[7] * t + PHI[6]
    for factor in PHI[5::-1]:
        poly = poly * t + factor
    bell = jnp.exp(-0.5 * (pre * pre))
    tail = poly * t * bell
    cdf = jnp.where(pre < 0, tail, 1.0 - tail)
    return pre * cdf, cdf + pre * (bell * 0.3989422804014327)


def norm_stats(values):
    width = values.shape[-1]
    mean = jnp.sum(values, axis=-1, keepdims=True) * (1.0 / width)
    centred = values - mean
    spread = jnp.sum(centred * centred, axis=-1, keepdims=True) * (1.0 / width)
    rate = lax.rsqrt(spread + LN_EPSILON)
    return centred * rate, rate


def norm_back(grad, gain, xhat, rate):
    width = grad.shape[-1]
    scaled = grad * gain
    mean = jnp.sum(scaled, axis=-1, keepdims=True) * (1.0 / width)
    along = jnp.sum(scaled * xhat, axis=-1, keepdims=True) * (1.0 / width)
    return rate * (scaled - mean - xhat * along)


def column_sum(values):
    return jnp.sum(values, axis=0, keepdims=True)


def middle_kernel(
    total_slots,
    dp_bits,
    valid_ref,
    lengths_ref,
    ctx_a,
    ctx_b,
    gains,
    shifts,
    x_hbm,
    teacher_hbm,
    qa,
    qb,
    qc,
    qd,
    outin_own,
    outin_core,
    outin_far,
    back_own,
    back_core,
    second_own,
    second_core,
    out_hbm,
    dh_hbm,
    cg_a,
    cg_b,
    core_hbm,
    to_x,
    to_y,
    rest,
    out_send_a,
    out_send_b,
    out_keep_a,
    out_keep_b,
    sums,
    bias_sums,
    count_ref,
    outin_far_core,
    in_far,
    back_far,
    in_far_core,
    back_far_core,
    w_in,
    w_back,
    w_out,
    bias_parts,
    bias_in,
    xhat_one,
    rate_one,
    mid_low,
    hidden,
    slope,
    acc,
    dh_low,
    pre_grad,
    rows_in,
    rows_out,
    stage16,
    stage32,
    from_core,
    held,
    w_sem,
    in_sem,
    out_sem,
    load_sem,
    store_sem,
    send_sem,
    recv_sem,
    count_send,
    count_recv,
    far_send,
    far_recv,
):
    seq, width = acc.shape
    blocks = seq // RB
    half = width // 2
    out_rows = w_out.shape[0] // 4
    units = w_in.shape[2]
    side = units // 2
    core_at, y_at, x_at = partner("tensor", 0), partner("tensor", 1), partner("dp", 0)
    greet([core_at, y_at] + [partner("dp", bit) for bit in range(dp_bits)])

    def far_copy(n, source, target, device):
        return pltpu.make_async_remote_copy(
            src_ref=source,
            dst_ref=target,
            send_sem=far_send.at[n],
            recv_sem=far_recv.at[n],
            device_id=device,
            device_id_type=pl.DeviceIdType.MESH,
        )

    in_at = pl.ds(2 * out_rows, width)
    far = [
        far_copy(0, outin_far, outin_far_core, core_at),
        far_copy(1, back_own, back_far.at[0], y_at),
        far_copy(2, second_own.at[pl.ds(width, width), :], back_far.at[1], y_at),
        far_copy(3, outin_far.at[in_at, :], in_far, x_at),
        far_copy(4, in_far, in_far_core, core_at),
        far_copy(5, back_far.at[0], back_far_core.at[0], core_at),
        far_copy(6, back_far.at[1], back_far_core.at[1], core_at),
    ]
    for copy in far[:4]:
        copy.start()
    out_in = (outin_own, outin_core, outin_far, outin_far_core)
    in_parts = tuple(ref.at[in_at, :] for ref in out_in)
    in_other = (
        second_own.at[pl.ds(0, width), :],
        second_core.at[pl.ds(0, width), :],
        in_far,
        in_far_core,
    )
    back_parts = (back_own, back_core, back_far.at[0], back_far_core.at[0])
    back_other = (
        second_own.at[pl.ds(width, width), :],
        second_core.at[pl.ds(width, width), :],
        back_far.at[1],
        back_far_core.at[1],
    )

    def rows(i):
        return pl.ds(i * RB, RB)

    def fetch(source, i, slot):
        return pltpu.make_async_copy(source.at[rows(i), :], rows_in.at[slot], in_sem.at[slot])

    def out_weights(p, c):
        return pltpu.make_async_copy(
            out_in[p].at[pl.ds(c * out_rows, out_rows), :],
            w_out.at[pl.ds(p * out_rows, out_rows), pl.ds(c * half, half)],
            w_sem.at[p, c],
        )

    def bias_rows(p):
        source = (qa, qb, qc, qd)[p]
        return pltpu.make_async_copy(
            source.at[pl.ds(source.shape[0] - 16, 16), :], bias_parts.at[p], w_sem.at[p, 8]
        )

    def load_in(source, p, r):
        return pltpu.make_async_copy(
            source, w_in.at[p, :, pl.ds(r * side, side)], w_sem.at[p, 2 + 3 * r]
        )

    def load_back(source, p, r, c):
        return pltpu.make_async_copy(
            source.at[pl.ds(c * side, side), :],
            w_back.at[p, pl.ds(r * side, side), pl.ds(c * half, half)],
            w_sem.at[p, 3 + 3 * r + c],
        )

    def ffn_weights(p):
        load_in(in_parts[p], p, 0).start()
        load_in(in_other[p], p, 1).start()
        for c in range(2):
            load_back(back_parts[p], p, 0, c).start()
            load_back(back_other[p], p, 1, c).start()

    early = [out_weights(p, c) for p in range(4) for c in range(2)]
    for copy in early[:6]:
        copy.start()
    fetch(x_hbm, 0, 0).start()
    for p in range(4):
        bias_rows(p).start()
    for p in range(2):
        ffn_weights(p)

    def count_step(bit):
        return pltpu.make_async_remote_copy(
            src_ref=held.at[2 * bit],
            dst_ref=held.at[2 * bit + 1],
            send_sem=count_send.at[bit],
            recv_sem=count_recv.at[bit],
            device_id=partner("dp", bit),
            device_id_type=pl.DeviceIdType.MESH,
        )

    tokens = jnp.full(held.shape[1:], 0, jnp.int32)
    for i in range(lengths_ref.shape[0]):
        tokens += lengths_ref[i]
    held[0] = tokens
    count_step(0).start()

    def count_on(bit):
        count_step(bit).wait()
        held[2 * bit + 2] = held[2 * bit] + held[2 * bit + 1]
        if bit + 1 < dp_bits:
            count_step(bit + 1).start()

    far[0].wait_recv()
    for copy in early[6:]:
        copy.start()
    for copy in early:
        copy.wait()

    for i in range(blocks):
        if i + 1 < blocks:
            fetch(x_hbm, i + 1, (i + 1) % 2).start()
        fetch(x_hbm, i, i % 2).wait()
        context = jnp.concatenate([ctx_a[rows(i), :], ctx_b[rows(i), :]], axis=1)
        xhat, rate = norm_stats(dot(context, w_out[...]) + shifts[0:1, :] + rows_in[i % 2])
        xhat_one[rows(i), :] = xhat
        rate_one[rows(i), :] = rate
        mid_low[rows(i), :] = (xhat * gains[0:1, :] + shifts[1:2, :]).astype(LOW)
        acc[rows(i), :] = jnp.zeros((RB, width), F32)
        if i < dp_bits:
            count_on(i)
    for bit in range(blocks, dp_bits):
        count_on(bit)
    count_ref[...] = held[2 * dp_bits]
    fetch(teacher_hbm, 0, 0).start()
    for p in range(4):
        bias_rows(p).wait()
        part = bias_parts[p, 0:3, :].astype(F32)
        bias_in[p] = part[0:1] + part[1:2] + part[2:3]

    def up(p, carry):
        @pl.when(p == 2)
        def _():
            for n, then in ((3, 4), (1, 5), (2, 6)):
                far[n].wait_recv()
                far[then].start()
            ffn_weights(2)

        @pl.when(p == 3)
        def _():
            for n in (4, 5, 6):
                far[n].wait_recv()
            ffn_weights(3)

        for r in range(2):
            load_in(in_other[0], p, r).wait()
            for c in range(2):
                load_back(back_own, p, r, c).wait()
        def lift(k):
            return dot(mid_low[pl.ds(k * FR, FR), :], w_in[p]) + bias_in[p]

        def lower(k):
            at = pl.ds(k * FR, FR)
            acc[at, :] += dot(hidden[p, at, :], w_back[p])

        pre = lift(0)
        for k in range(seq // FR):
            later = lift(k + 1) if k + 1 < seq // FR else None
            at = pl.ds(k * FR, FR)
            act, der = gelu_parts(pre)
            hidden[p, at, :] = act.astype(LOW)
            slope[p, at, :] = der
            if k > 0:
                lower(k - 1)
            pre = later
        lower(seq // FR - 1)
        return carry

    lax.fori_loop(0, 4, up, 0)

    zero = jnp.zeros((1, width), F32)
    squares, gain_two, shift_two, shift_mid = zero, zero, zero, zero
    scale = total_slots / held[2 * dp_bits, 0:1, 0:1].astype(F32)
    stores = []
    for i in range(blocks):
        if i + 1 < blocks:
            fetch(teacher_hbm, i + 1, (i + 1) % 2).start()
        fetch(teacher_hbm, i, i % 2).wait()
        mid = xhat_one[rows(i), :] * gains[0:1, :] + shifts[1:2, :]
        xhat, rate = norm_stats(acc[rows(i), :] + shifts[2:3, :] + mid)
        output = xhat * gains[1:2, :] + shifts[3:4, :]
        if i >= 2:
            stores[i - 2].wait()
        rows_out[i % 2] = output
        stores.append(
            pltpu.make_async_copy(rows_out.at[i % 2], out_hbm.at[rows(i), :], out_sem.at[i % 2])
        )
        stores[i].start()
        live = (i * RB + lax.broadcasted_iota(jnp.int32, (RB, 1), 0)) < valid_ref[0]
        distance = jnp.where(live, output - rows_in[i % 2], 0.0)
        squares += column_sum(distance * distance)
        out_grad = scale * distance
        gain_two += column_sum(out_grad * xhat)
        shift_two += column_sum(out_grad)
        dh_two = norm_back(out_grad, gains[1:2, :], xhat, rate)
        shift_mid += column_sum(dh_two)
        acc[rows(i), :] = dh_two
        dh_low[rows(i), :] = dh_two.astype(LOW)
    for store in stores[-2:]:
        store.wait()

    sides = (pl.ds(0, side), pl.ds(side, side))

    def ffn_back(p):
        total = jnp.zeros((1, units), F32)

        def lift(k):
            return dot(dh_low[pl.ds(k * FR, FR), :], w_back[p], NT)

        def lower(k):
            at = pl.ds(k * FR, FR)
            acc[at, :] += dot(pre_grad[at, :], w_in[p], NT)

        raised = lift(0)
        for k in range(seq // FR):
            later = lift(k + 1) if k + 1 < seq // FR else None
            at = pl.ds(k * FR, FR)
            grad = (raised * slope[p, at, :]).astype(LOW)
            pre_grad[at, :] = grad
            total += column_sum(grad.astype(F32))
            if k > 0:
                lower(k - 1)
            raised = later
        lower(seq // FR - 1)
        bias_sums[pl.ds(p, 1), :] = total

    def to_core(pair, w):
        return pltpu.make_async_remote_copy(
            src_ref=stage16.at[w],
            dst_ref=core_hbm.at[pair, w],
            send_sem=send_sem.at[w],
            recv_sem=recv_sem.at[pair, w],
            device_id=core_at,
            device_id_type=pl.DeviceIdType.MESH,
        )

    def away(n, carry):
        p = 2 * n + 1
        ffn_back(p)

        @pl.when(n > 0)
        def _():
            for w in range(2):
                to_core(0, w).wait_send()

        stage16[0] = dot(mid_low[...], pre_grad[...], TN).astype(LOW)
        stage16[1] = dot(hidden[p], dh_low[...], TN).astype(LOW)
        for w in range(2):
            to_core(n, w).start()
        return carry

    lax.fori_loop(0, 2, away, 0)

    def in_moves(pair):
        return [
            pltpu.make_async_copy(stage32.at[0, :, sides[0]], rest.at[pair], store_sem.at[0]),
            pltpu.make_async_copy(stage16.at[0, :, sides[1]], to_x.at[pair], store_sem.at[1]),
        ]

    def back_moves(stage, target):
        return [
            pltpu.make_async_copy(
                stage.at[1, sides[r], sides[c]],
                target.at[r, sides[c], :],
                store_sem.at[2 + 2 * r + c],
            )
            for r in range(2)
            for c in range(2)
        ]

    moves = {1: in_moves(1) + back_moves(stage16, to_y), 0: in_moves(0) + back_moves(stage32, rest.at[pl.ds(2, 2)])}

    def home(n, carry):
        pair = 1 - n
        p = 2 * pair
        for w in range(2):
            to_core(pair, w).wait_recv()
            pltpu.make_async_copy(core_hbm.at[pair, w], from_core.at[w], load_sem.at[w]).start()
        ffn_back(p)

        @pl.when(n == 0)
        def _():
            for w in range(2):
                to_core(1, w).wait_send()

        @pl.when(n == 1)
        def _():
            for copy in moves[1]:
                copy.wait()

        stage32[0] = dot(mid_low[...], pre_grad[...], TN)
        stage32[1] = dot(hidden[p], dh_low[...], TN)
        for w in range(2):
            pltpu.make_async_copy(core_hbm.at[pair, w], from_core.at[w], load_sem.at[w]).wait()
            for k in range(0, width, 128):
                total = stage32[w, k : k + 128, :] + from_core[w, k : k + 128, :].astype(F32)
                stage32[w, k : k + 128, :] = total
                stage16[w, k : k + 128, :] = total.astype(LOW)

        @pl.when(n == 0)
        def _():
            for copy in moves[1]:
                copy.start()

        @pl.when(n == 1)
        def _():
            for copy in moves[0]:
                copy.start()

        return carry

    lax.fori_loop(0, 2, home, 0)

    gain_one, shift_one, shift_out = zero, zero, zero
    stores = []
    for i in range(blocks):
        grad, xhat = acc[rows(i), :], xhat_one[rows(i), :]
        gain_one += column_sum(grad * xhat)
        shift_one += column_sum(grad)
        dh_one = norm_back(grad, gains[0:1, :], xhat, rate_one[rows(i), :])
        shift_out += column_sum(dh_one)
        if i >= 2:
            stores[i - 2].wait()
        rows_out[i % 2] = dh_one
        stores.append(
            pltpu.make_async_copy(rows_out.at[i % 2], dh_hbm.at[rows(i), :], out_sem.at[i % 2])
        )
        stores[i].start()
        dh_one = dh_one.astype(LOW)
        dh_low[rows(i), :] = dh_one
        grad = dot(dh_one, w_out[...], NT).astype(LOW)
        cg_a[rows(i), :] = grad[:, :half]
        cg_b[rows(i), :] = grad[:, half:]
    for context, out_keep, out_send in (
        (ctx_a, out_keep_a, out_send_a),
        (ctx_b, out_keep_b, out_send_b),
    ):
        grad = dot(context[...], dh_low[...], TN)
        out_keep[...] = grad[:out_rows]
        out_send[...] = grad[out_rows:].astype(LOW)
    sums[...] = jnp.concatenate(
        [gain_one, gain_two, shift_out, shift_one, shift_mid, shift_two, squares, zero], axis=0
    )
    for store in stores[-2:]:
        store.wait()
    for copy in moves[0]:
        copy.wait()
    for copy in far:
        copy.wait_send()


def middle(
    total_slots, valid, lengths, ctx_a, ctx_b, gains, shifts, x, teacher, near, out_in, back, second
):
    seq, width = x.shape
    half = width // 2
    out_rows = ctx_a.shape[1] // 2
    units = width
    dp_bits = bits_of("dp")
    slab = (width, units // 2)
    return pl.pallas_call(
        functools.partial(middle_kernel, float(total_slots), dp_bits),
        out_shape=(
            shape((seq, width), F32),
            shape((seq, width), F32),
            shape((seq, half), LOW),
            shape((seq, half), LOW),
            shape((2, 2, width, units), LOW),
            shape((2,) + slab, LOW),
            shape((2,) + slab, LOW),
            shape((4,) + slab, F32),
            shape((out_rows, width), LOW),
            shape((out_rows, width), LOW),
            shape((out_rows, width), F32),
            shape((out_rows, width), F32),
            shape((8, width), F32),
            shape((4, units), F32),
            shape((8, 128), jnp.int32),
            shape(out_in[0].shape, LOW),
            shape(slab, LOW),
            shape((2,) + slab, LOW),
            shape(slab, LOW),
            shape((2,) + slab, LOW),
        ),
        in_specs=[SMEM, SMEM, VMEM, VMEM, VMEM, VMEM, HBM, HBM] + [HBM] * 11,
        out_specs=(HBM, HBM, VMEM, VMEM, HBM, HBM, HBM, HBM) + (VMEM,) * 7 + (HBM,) * 5,
        scratch_shapes=[
            pltpu.VMEM((4, width, units), LOW),
            pltpu.VMEM((4, units, width), LOW),
            pltpu.VMEM((4 * out_rows, width), LOW),
            pltpu.VMEM((4, 16, width), LOW),
            pltpu.VMEM((4, 1, units), F32),
            pltpu.VMEM((seq, width), F32),
            pltpu.VMEM((seq, 1), F32),
            pltpu.VMEM((seq, width), LOW),
            pltpu.VMEM((4, seq, units), LOW),
            pltpu.VMEM((4, seq, units), F32),
            pltpu.VMEM((seq, width), F32),
            pltpu.VMEM((seq, width), LOW),
            pltpu.VMEM((seq, units), LOW),
            pltpu.VMEM((2, RB, width), F32),
            pltpu.VMEM((2, RB, width), F32),
            pltpu.VMEM((2, width, units), LOW),
            pltpu.VMEM((2, width, units), F32),
            pltpu.VMEM((2, width, units), LOW),
            pltpu.VMEM((2 * dp_bits + 1, 8, 128), jnp.int32),
            pltpu.SemaphoreType.DMA((4, 9)),
            pltpu.SemaphoreType.DMA((2,)),
            pltpu.SemaphoreType.DMA((2,)),
            pltpu.SemaphoreType.DMA((2,)),
            pltpu.SemaphoreType.DMA((6,)),
            pltpu.SemaphoreType.DMA((2,)),
            pltpu.SemaphoreType.DMA((2, 2)),
            pltpu.SemaphoreType.DMA((dp_bits,)),
            pltpu.SemaphoreType.DMA((dp_bits,)),
            pltpu.SemaphoreType.DMA((7,)),
            pltpu.SemaphoreType.DMA((7,)),
        ],
        compiler_params=pltpu.CompilerParams(
            vmem_limit_bytes=VMEM_LIMIT, collective_id=1, has_side_effects=True
        ),
        cost_estimate=pl.CostEstimate(
            flops=6 * seq * width * (8 * units + width),
            bytes_accessed=30 << 20,
            transcendentals=2 * seq * 4 * units,
        ),
        name="middle",
    )(valid, lengths, ctx_a, ctx_b, gains, shifts, x, teacher, *near, *out_in, *back, *second)


def add_rows(out, terms, chunk=96):
    rows = out.shape[0]
    chunk = min(chunk, rows)

    def step(i, carry):
        at = pl.ds(pl.multiple_of(i * chunk, chunk), chunk)
        total = terms[0][at, :].astype(F32)
        for term in terms[1:]:
            total += term[at, :].astype(F32)
        out[at, :] = total.astype(out.dtype)
        return carry

    lax.fori_loop(0, rows // chunk, step, 0)


def cross_rows(x_ref, grads, okeep, osend, side, cross, keep, send, bias_ref):
    half = x_ref.shape[1] // 2
    piece = grads[0].shape[1] // 2
    mine = pl.ds(pl.multiple_of(side * half, half), half)
    other = pl.ds(pl.multiple_of((1 - side) * half, half), half)
    for i in range(3):
        cross[...] = dot(grads[i][...], x_ref[...], TN)
        at = slice(i * piece, (i + 1) * piece)
        for n, lanes in enumerate((mine, other)):
            keep[n, at, :] = cross[:piece, lanes]
            send[n, at, :] = cross[piece:, lanes].astype(send.dtype)
        bias_ref[i : i + 1, :] = column_sum(grads[i][...].astype(F32))
    for n, lanes in enumerate((mine, other)):
        keep[n, 3 * piece :, :] = okeep[:, lanes]
        send[n, 3 * piece :, :] = osend[:, lanes].astype(send.dtype)


def far_kernel(
    x_ref,
    dq,
    dk,
    dv,
    osend,
    okeep,
    away,
    away_first,
    bias_ref,
    keep,
    send,
    core,
    cross,
    send_sem,
    recv_sem,
):
    core_at = partner("tensor", 0)
    greet([core_at])
    bias_ref[...] = jnp.zeros(bias_ref.shape, F32)
    cross_rows(
        x_ref, (dq, dk, dv), okeep, osend, lax.axis_index("dp") & 1, cross, keep, send, bias_ref
    )
    copies = [
        pltpu.make_async_remote_copy(
            src_ref=send.at[n],
            dst_ref=core.at[n],
            send_sem=send_sem.at[n],
            recv_sem=recv_sem.at[n],
            device_id=core_at,
            device_id_type=pl.DeviceIdType.MESH,
        )
        for n in range(2)
    ]
    for n in (1, 0):
        copies[n].start()
    for n in (1, 0):
        copies[n].wait_recv()
        add_rows((away, away_first)[n], [keep.at[n], core.at[n]])
    for n in (1, 0):
        copies[n].wait_send()


def far_projections(x, grads, osend, okeep):
    seq, width = x.shape
    half = width // 2
    piece = grads[0].shape[1] // 2
    slabs = (2, width, half)
    return pl.pallas_call(
        far_kernel,
        out_shape=(shape(slabs[1:], LOW), shape(slabs[1:], LOW), shape((8, 2 * piece), F32)),
        in_specs=[VMEM] * 6,
        out_specs=(VMEM, VMEM, VMEM),
        scratch_shapes=[
            pltpu.VMEM(slabs, F32),
            pltpu.VMEM(slabs, F32),
            pltpu.VMEM(slabs, F32),
            pltpu.VMEM((2 * piece, width), F32),
            pltpu.SemaphoreType.DMA((2,)),
            pltpu.SemaphoreType.DMA((2,)),
        ],
        compiler_params=pltpu.CompilerParams(
            vmem_limit_bytes=VMEM_LIMIT, collective_id=3, has_side_effects=True
        ),
        cost_estimate=pl.CostEstimate(
            flops=12 * seq * width * piece, bytes_accessed=10 << 20, transcendentals=0
        ),
        name="far_projections",
    )(x, *grads, osend, okeep)


def finish_kernel(
    dp_bits,
    x_ref,
    w0,
    w1,
    w2,
    w3,
    dqa,
    dka,
    dva,
    dqb,
    dkb,
    dvb,
    osend,
    okeep,
    dh_hbm,
    rest,
    ffn_x,
    ffn_y,
    in_y,
    back_x,
    away,
    qkv_y,
    small_ref,
    bias_far,
    gx_hbm,
    result,
    small_out,
    own,
    own16,
    keep,
    send,
    core,
    y_recv,
    x_send,
    x_recv,
    total,
    z_send,
    z_recv,
    last_send,
    last_recv,
    extra,
    bias_ref,
    small_held,
    rows_in,
    rows_out,
    cross,
    load_sem,
    send_sem,
    recv_sem,
    in_sem,
    out_sem,
):
    seq, width = x_ref.shape
    half = width // 2
    piece = dqa.shape[1] // 2
    blocks = seq // RB
    place = lax.axis_index("dp")
    index = lax.axis_index("tensor")
    side = place & 1
    core_at, y_at = partner("tensor", 0), partner("tensor", 1)
    dp_at = [partner("dp", bit) for bit in range(dp_bits)]
    greet([core_at, y_at] + dp_at)
    started = {}

    def remote(key, source, target, device):
        n = len(started)
        started[key] = pltpu.make_async_remote_copy(
            src_ref=source,
            dst_ref=target,
            send_sem=send_sem.at[n],
            recv_sem=recv_sem.at[n],
            device_id=device,
            device_id_type=pl.DeviceIdType.MESH,
        )
        started[key].start()

    def arrive(key):
        started[key].wait_recv()

    remote("y", away, y_recv, y_at)
    loads = []
    for w, terms in enumerate(((rest.at[0], ffn_x.at[0], in_y), (rest.at[2], ffn_y.at[0], back_x))):
        targets = (own.at[w], own16.at[w, 0], own16.at[w, 1])
        loads.append(
            [
                pltpu.make_async_copy(term, target, load_sem.at[w, n])
                for n, (term, target) in enumerate(zip(terms, targets))
            ]
        )
        for copy in loads[w]:
            copy.start()

    def fetch(i):
        return pltpu.make_async_copy(
            dh_hbm.at[pl.ds(i * RB, RB), :], rows_in.at[i % 2], in_sem.at[i % 2]
        )

    fetch(0).start()

    rows_of = [width]
    for bit in range(1, min(dp_bits, 3)):
        rows_of.append(rows_of[-1] // 2)
    levels = min(dp_bits, 3) - 1

    def offset(level):
        at = 0
        for bit in range(1, level + 1):
            at = at + ((place >> bit) & 1) * rows_of[bit]
        return pl.multiple_of(at, rows_of[level])

    def other_offset(level):
        return pl.multiple_of(
            offset(level - 1) + (1 - ((place >> level) & 1)) * rows_of[level], rows_of[level]
        )

    def scatter(w, level):
        size = rows_of[level]
        out, into = ((z_send, z_recv) if level == 1 else (last_send, last_recv))
        add_rows(out.at[w], [total.at[w, pl.ds(other_offset(level), size), :]])
        remote((w, "z", level), out.at[w], into.at[w], dp_at[level])

    def collect(w, level):
        size = rows_of[level]
        arrive((w, "z", level))
        into = z_recv if level == 1 else last_recv
        mine = total.at[w, pl.ds(offset(level), size), :]
        if level < levels:
            add_rows(mine, [mine, into.at[w]])
        else:
            add_rows(result.at[w, 0, pl.ds(offset(level), size), :], [mine, into.at[w]])

    def settle(w):
        size = rows_of[levels]
        at = pl.ds(offset(levels), size)
        for bit in range(levels + 1, dp_bits):
            spare = result.at[w, 0, at, :]
            into = extra.at[w, bit - levels - 1]
            remote((w, "all", bit), spare, into, dp_at[bit])
            started[(w, "all", bit)].wait_send()
            arrive((w, "all", bit))
            add_rows(spare, [spare, into])

    def spread(w, level):
        if level == 0:
            remote((w, "gather", 0), result.at[w, 0], result.at[w, 1], dp_at[0])
        else:
            rows = result.at[w, 0, pl.ds(offset(level), rows_of[level]), :]
            remote((w, "gather", level), rows, rows, dp_at[level])

    for w in range(2):
        for copy in loads[w]:
            copy.wait()
        add_rows(total.at[w], [own.at[w], own16.at[w, 0], own16.at[w, 1]])
        scatter(w, 1)

    cross_rows(x_ref, (dqa, dka, dva), okeep, osend, side, cross, keep, send, bias_ref)
    for n in (1, 0):
        remote(("core", n), send.at[n], core.at[n], core_at)

    small_held[0] = jnp.zeros(small_held.shape[1:], F32)
    small_held[0, 16:24, :] = small_ref[0:8, :]
    for p in range(4):
        row = 4 * (index ^ p)
        half_mine = small_ref[8 + p : 9 + p, :half]
        half_other = small_ref[8 + p : 9 + p, half:]
        low_half = jnp.where(side == 0, half_mine, half_other)
        high_half = jnp.where(side == 0, half_other, half_mine)
        small_held[0, pl.ds(row, 1), :] = jnp.concatenate([low_half, high_half], axis=1)
        for i, k in enumerate((0, 2)):
            values = (bias_ref, bias_far)[p // 2][k : k + 1, :]
            if p % 2 == 1:
                values = pltpu.roll(values, piece, 1)
            small_held[0, pl.ds(row + 1 + i, 1), :half] = values

    def small_step(n):
        bits = [core_at, y_at] + dp_at
        remote(("small", n), small_held.at[2 * n], small_held.at[2 * n + 1], bits[n])

    def small_sum(n):
        arrive(("small", n))
        out = small_held.at[2 * n + 2] if n < dp_bits + 1 else small_out
        out[...] = small_held[2 * n] + small_held[2 * n + 1]

    weights = ((w0, w1), (w2, w3))
    grads = ((dqa, dka, dva), (dqb, dkb, dvb))
    stores = []

    def inputs_rows(b):
        at = pl.ds(b * RB, RB)
        if b + 1 < blocks:
            fetch(b + 1).start()
        fetch(b).wait()
        grad = rows_in[b % 2]
        for g in range(2):
            for i in range(3):
                rows = slice(i * piece, (i + 1) * piece)
                w = jnp.concatenate([ref[rows, :] for ref in weights[g]], axis=0)
                grad += dot(grads[g][i][at, :], w)
        if b >= 2:
            stores[b - 2].wait()
        rows_out[b % 2] = grad
        stores.append(
            pltpu.make_async_copy(rows_out.at[b % 2], gx_hbm.at[at, :], out_sem.at[b % 2])
        )
        stores[b].start()

    small_step(0)
    collect(0, 1)
    scatter(0, 2)
    arrive(("core", 1))
    add_rows(x_send, [keep.at[1], core.at[1], qkv_y])
    remote("qkv x", x_send, x_recv, dp_at[0])
    collect(1, 1)
    scatter(1, 2)
    inputs_rows(0)
    small_sum(0)
    small_step(1)
    collect(0, 2)
    settle(0)
    spread(0, 2)
    inputs_rows(1)
    small_sum(1)
    small_step(2)
    collect(1, 2)
    settle(1)
    spread(1, 2)
    arrive(("core", 0))
    arrive("y")
    add_rows(total.at[2], [keep.at[0], core.at[0], y_recv])
    arrive("qkv x")
    add_rows(total.at[2], [total.at[2], x_recv])
    scatter(2, 1)
    arrive((0, "gather", 2))
    spread(0, 1)
    inputs_rows(2)
    small_sum(2)
    small_step(3)
    arrive((1, "gather", 2))
    spread(1, 1)
    collect(2, 1)
    scatter(2, 2)
    arrive((0, "gather", 1))
    spread(0, 0)
    inputs_rows(3)
    small_sum(3)
    small_step(4)
    collect(2, 2)
    settle(2)
    spread(2, 2)
    arrive((1, "gather", 1))
    spread(1, 0)
    for n in range(4, dp_bits + 2):
        small_sum(n)
        if n + 1 < dp_bits + 2:
            small_step(n + 1)
    arrive((2, "gather", 2))
    spread(2, 1)
    arrive((2, "gather", 1))
    spread(2, 0)
    for w in range(3):
        arrive((w, "gather", 0))
    for key, copy in started.items():
        if not (isinstance(key, tuple) and key[1] == "all"):
            copy.wait_send()
    for store in stores[-2:]:
        store.wait()


def finish(x, weights, grads, osend, okeep, dh, rest, ffn_x, ffn_y, in_y, back_x, away, qkv_y, small, bias_far):
    seq, width = x.shape
    half = width // 2
    piece = grads[0].shape[1] // 2
    dp_bits = bits_of("dp")
    slab = (width, half)
    copies = 4 + dp_bits + 2 + 3 * (2 + 3 + max(dp_bits - 3, 0))
    return pl.pallas_call(
        functools.partial(finish_kernel, dp_bits),
        out_shape=(
            shape((seq, width), F32),
            shape((3, 2) + slab, LOW),
            shape((24, width), F32),
        ),
        in_specs=[VMEM] * 13 + [HBM] * 6 + [HBM, VMEM, VMEM, VMEM],
        out_specs=(HBM, VMEM, VMEM),
        scratch_shapes=[
            pltpu.VMEM((2,) + slab, F32),
            pltpu.VMEM((2, 2) + slab, LOW),
            pltpu.VMEM((2,) + slab, F32),
            pltpu.VMEM((2,) + slab, F32),
            pltpu.VMEM((2,) + slab, F32),
            pltpu.VMEM(slab, LOW),
            pltpu.VMEM(slab, LOW),
            pltpu.VMEM(slab, LOW),
            pltpu.VMEM((3,) + slab, F32),
            pltpu.VMEM((3, width // 2, half), LOW),
            pltpu.VMEM((3, width // 2, half), LOW),
            pltpu.VMEM((3, width // 4, half), LOW),
            pltpu.VMEM((3, width // 4, half), LOW),
            pltpu.VMEM((3, max(dp_bits - 3, 1), width // 4, half), LOW),
            pltpu.VMEM((8, 2 * piece), F32),
            pltpu.VMEM((2 * dp_bits + 4, 24, width), F32),
            pltpu.VMEM((2, RB, width), F32),
            pltpu.VMEM((2, RB, width), F32),
            pltpu.VMEM((2 * piece, width), F32),
            pltpu.SemaphoreType.DMA((2, 3)),
            pltpu.SemaphoreType.DMA((copies,)),
            pltpu.SemaphoreType.DMA((copies,)),
            pltpu.SemaphoreType.DMA((2,)),
            pltpu.SemaphoreType.DMA((2,)),
        ],
        compiler_params=pltpu.CompilerParams(
            vmem_limit_bytes=VMEM_LIMIT, collective_id=2, has_side_effects=True
        ),
        cost_estimate=pl.CostEstimate(
            flops=36 * seq * width * piece, bytes_accessed=50 << 20, transcendentals=0
        ),
        name="finish",
    )(x, *weights, *grads, osend, okeep, dh, rest, ffn_x, ffn_y, in_y, back_x, away, qkv_y, small, bias_far)


def widen_kernel(
    place_ref,
    result,
    small,
    count,
    source,
    loss_ref,
    qkv_ref,
    bqv_ref,
    out_ref,
    in_ref,
    bin_ref,
    back_ref,
    gains_ref,
    shifts_ref,
    target,
):
    target[...] = source[...]
    half = result.shape[3]
    piece = qkv_ref.shape[1]
    side = place_ref[0]
    for n in range(2):
        natural = (side + n) % 2
        at = pl.ds(pl.multiple_of(natural * half, half), half)
        in_ref[:, at] = result[0, n].astype(F32)
        for c in range(2):
            rows = result[1, n, c * half : (c + 1) * half, :]
            back_ref[at, c * half : (c + 1) * half] = rows.astype(F32)
        for i in range(3):
            qkv_ref[i, :, at] = result[2, n, i * piece : (i + 1) * piece, :].astype(F32)
        out_ref[:, at] = result[2, n, 3 * piece :, :].astype(F32)
    row = 4 * place_ref[1]
    bin_ref[...] = small[pl.ds(row, 1), :]
    for i in range(2):
        bqv_ref[i : i + 1, :] = small[pl.ds(row + 1 + i, 1), :piece]
    gains_ref[...] = small[16:18, :]
    shifts_ref[...] = small[18:22, :]
    tokens = count[0:1, 0:1].astype(F32)
    total = jnp.sum(small[22:23, :], axis=1, keepdims=True)
    loss_ref[...] = total / (2.0 * small.shape[1] * tokens)


def widen(place, result, small, count, inputs_grad, piece, rows):
    width, half = result.shape[2:]
    return pl.pallas_call(
        widen_kernel,
        out_shape=(
            shape((1, 1), F32),
            shape((3, piece, width), F32),
            shape((2, piece), F32),
            shape((rows, width), F32),
            shape((width, 2 * half), F32),
            shape((1, 2 * half), F32),
            shape((2 * half, width), F32),
            shape((2, width), F32),
            shape((4, width), F32),
            shape(inputs_grad.shape, F32),
        ),
        in_specs=[SMEM, VMEM, VMEM, VMEM, VMEM],
        out_specs=(VMEM,) * 10,
        compiler_params=pltpu.CompilerParams(vmem_limit_bytes=VMEM_LIMIT),
        name="widen",
    )(place, result, small, count, inputs_grad)


def per_device(
    inputs,
    w_qkv,
    b_qv,
    w_out,
    w_in,
    b_in,
    w_back,
    norm_gains,
    shifts,
    segment_ids,
    valid_lengths,
    teacher,
):
    own_seqs, seq, width = inputs.shape
    assert own_seqs == 1 and lax.axis_size("tensor") == 4
    total_slots = seq * lax.axis_size("tensor") * lax.axis_size("dp")
    half = width // 2
    piece = w_qkv.shape[2]
    units = w_in.shape[1]
    index = lax.axis_index("tensor")
    side = (lax.axis_index("dp") & 1).astype(jnp.int32)
    side_row = side.reshape(1)
    x = inputs.reshape(seq, width)

    near = round_qkv(side_row, w_qkv.transpose(0, 2, 1), b_qv, b_in[None, :])
    core = swap(near, "tensor", 0)
    far = swap(near, "tensor", 1)
    core, w_in, w_back, w_out = lax.optimization_barrier((core, w_in, w_back, w_out))
    out_in, back, second, x_low = round_rest(side_row, w_out, w_in, w_back, x)
    out_in_far = swap(out_in, "tensor", 1)

    valid = lax.dynamic_index_in_dim(valid_lengths, index, keepdims=False)
    segments = lax.dynamic_index_in_dim(segment_ids, index, keepdims=False)
    positions = jnp.arange(seq, dtype=jnp.int32)
    code = jnp.where(positions < valid, segments, -1)[:, None]
    seg = segments[None, :]
    table = span_tables(segments, valid, seq)

    qa, ka, va, ctx_a, lse_a = attend_forward(table, x_low, near, core, code, seg)
    out_in, back, second, far, ctx_a = lax.optimization_barrier((out_in, back, second, far, ctx_a))
    core_far = swap(far, "tensor", 0)
    out_in_core = swap(out_in, "tensor", 0)
    back_core = swap(back, "tensor", 0)
    second_core = swap(second, "tensor", 0)
    qb, kb, vb, ctx_b, lse_b = attend_forward(table, x_low, far, core_far, code, seg)
    (
        output,
        dh_one,
        cg_a,
        cg_b,
        _,
        to_x,
        to_y,
        rest,
        out_send_a,
        out_send_b,
        out_keep_a,
        out_keep_b,
        sums,
        bias_sums,
        count,
        *_,
    ) = middle(
        total_slots,
        valid.reshape(1),
        valid_lengths,
        ctx_a,
        ctx_b,
        norm_gains,
        shifts,
        x,
        teacher.reshape(seq, width),
        (near, core, far, core_far),
        (out_in, out_in_core, out_in_far),
        (back, back_core),
        (second, second_core),
    )
    ffn_x = swap(to_x, "dp", 0)
    ffn_y = swap(to_y, "tensor", 1)
    grads_b = attend_backward(table, qb, kb, vb, cg_b, lse_b, code, seg)
    away, away_first, bias_far = far_projections(x_low, grads_b, out_send_b, out_keep_b)
    ffn_x, ffn_y, away_first = lax.optimization_barrier((ffn_x, ffn_y, away_first))
    in_away = (rest[1] + ffn_x[1].astype(F32)).astype(LOW)
    back_away = (rest[3] + ffn_y[1].astype(F32)).astype(LOW)
    in_away, back_away, away_first, cg_a = lax.optimization_barrier(
        (in_away, back_away, away_first, cg_a)
    )
    in_y = swap(in_away, "tensor", 1)
    back_x = swap(back_away, "dp", 0)
    qkv_y = swap(away_first, "tensor", 1)
    *grads_a, output = attend_backward(table, qa, ka, va, cg_a, lse_a, code, seg, output)
    small = jnp.concatenate([sums, bias_sums, jnp.zeros((4, width), F32)], axis=0)
    grad_inputs, slabs, small = finish(
        x_low,
        (near, core, far, core_far),
        (*grads_a, *grads_b),
        out_send_a,
        out_keep_a,
        dh_one,
        rest,
        ffn_x,
        ffn_y,
        in_y,
        back_x,
        away,
        qkv_y,
        small,
        bias_far,
    )
    (
        loss,
        grad_w_qkv,
        grad_b_qv,
        grad_w_out,
        grad_w_in,
        grad_b_in,
        grad_w_back,
        grad_gains,
        grad_shifts,
        grad_inputs,
    ) = widen(jnp.stack([side, index]), slabs, small, count, grad_inputs, piece, w_out.shape[0])
    return (
        output.reshape(own_seqs, seq, width),
        loss[0, 0],
        grad_inputs.reshape(own_seqs, seq, width),
        grad_w_qkv.transpose(0, 2, 1),
        grad_b_qv,
        grad_w_out,
        grad_w_in,
        grad_b_in[0],
        grad_w_back,
        grad_gains,
        grad_shifts,
    )


def solution(mesh):
    return jax.shard_map(
        per_device,
        mesh=mesh,
        in_specs=(
            P(("dp", "tensor"), None, None),
            P(None, None, "tensor"),
            P(None, "tensor"),
            P("tensor", None),
            P(None, "tensor"),
            P("tensor"),
            P("tensor", None),
            P(),
            P(),
            P("dp", None),
            P("dp"),
            P(("dp", "tensor"), None, None),
        ),
        out_specs=(
            P(("dp", "tensor"), None, None),
            P(),
            P(("dp", "tensor"), None, None),
            P(None, None, "tensor"),
            P(None, "tensor"),
            P("tensor", None),
            P(None, "tensor"),
            P("tensor"),
            P("tensor", None),
            P(),
            P(),
        ),
        check_vma=False,
    )
```

```python
import functools
import math

import jax
import jax.numpy as jnp
from jax import lax
from jax.experimental import pallas as pl
from jax.experimental.pallas import tpu as pltpu
from jax.sharding import PartitionSpec as P

HD = 64
LN_EPSILON = 1e-05
MASKED_SCORE = -1000000000.0
QB = 256
KB = 128
RB = 256
FR = 256
NT = ((1,), (1,))
TN = ((0,), (0,))
PHI = (
    0.09255110872,
    0.09001568156,
    0.1049848251,
    0.006341010132,
    0.2381524984,
    -0.2150534404,
    0.2551771707,
    -0.07216888208,
)
PHI_STEP = 0.23164188826636045

VMEM_LIMIT = 63 << 20
VMEM = pl.BlockSpec(memory_space=pltpu.VMEM)
SMEM = pl.BlockSpec(memory_space=pltpu.SMEM)
HBM = pl.BlockSpec(memory_space=pl.ANY)
LOW = jnp.bfloat16
F32 = jnp.float32


def dot(left, right, dims=((1,), (0,))):
    return lax.dot_general(left, right, (dims, ((), ())), preferred_element_type=jnp.float32)


def shape(dims, dtype):
    return jax.ShapeDtypeStruct(dims, dtype)


def swap(values, axis, bit):
    size = lax.axis_size(axis)
    return lax.ppermute(values, axis, [(i, i ^ (1 << bit)) for i in range(size)])


def bits_of(axis):
    return int(math.log2(lax.axis_size(axis)))


def partner(axis, bit):
    here = {name: lax.axis_index(name) for name in ("dp", "tensor")}
    here[axis] = here[axis] ^ (1 << bit)
    return here["dp"], here["tensor"]


def greet(partners):
    barrier = pltpu.get_barrier_semaphore()
    for device in partners:
        pl.semaphore_signal(
            barrier, inc=1, device_id=device, device_id_type=pl.DeviceIdType.MESH
        )
    pl.semaphore_wait(barrier, len(partners))


def three_parts(values):
    first = values.astype(LOW)
    rest = values - first.astype(F32)
    second = rest.astype(LOW)
    return first, second, (rest - second.astype(F32)).astype(LOW)


def round_qkv_kernel(side_ref, w_ref, bqv_ref, bin_ref, out_ref):
    piece = w_ref.shape[1]
    width = w_ref.shape[2]
    half = bin_ref.shape[1] // 2
    for i in range(3):
        out_ref[i * piece : (i + 1) * piece, :] = w_ref[i].astype(LOW)
    mine = bin_ref[:, pl.ds(pl.multiple_of(side_ref[0] * half, half), half)]
    other = bin_ref[:, pl.ds(pl.multiple_of((1 - side_ref[0]) * half, half), half)]
    pad = jnp.zeros((1, width - piece), F32)
    rows = [jnp.concatenate([mine, other], axis=1)]
    rows += [jnp.concatenate([bqv_ref[i : i + 1, :], pad], axis=1) for i in range(2)]
    parts = [part.astype(F32) for row in rows for part in three_parts(row)]
    parts += [jnp.zeros((1, width), F32)] * 7
    out_ref[3 * piece :, :] = jnp.concatenate(parts, axis=0).astype(LOW)


def round_qkv(side, w_qkv, b_qv, b_in):
    _, piece, width = w_qkv.shape
    return pl.pallas_call(
        round_qkv_kernel,
        out_shape=shape((3 * piece + 16, width), LOW),
        in_specs=[SMEM, VMEM, VMEM, VMEM],
        out_specs=VMEM,
        compiler_params=pltpu.CompilerParams(vmem_limit_bytes=VMEM_LIMIT),
        name="round_qkv",
    )(side, w_qkv, b_qv, b_in)


def round_rest_kernel(side_ref, wo_ref, wi_ref, wb_ref, x_ref, out_in, back, second, x_low_ref):
    rows, width = wo_ref.shape
    half = width // 2
    for c in range(2):
        out_in[c * rows : (c + 1) * rows, :] = wo_ref[:, c * half : (c + 1) * half].astype(LOW)
    x_low_ref[...] = x_ref[...].astype(LOW)
    parts = (
        (out_in, 2 * rows, back, 0, side_ref[0]),
        (second, 0, second, width, 1 - side_ref[0]),
    )
    for to_in, in_base, to_back, back_base, side in parts:
        at = pl.ds(pl.multiple_of(side * half, half), half)
        to_in[in_base : in_base + width, :] = wi_ref[:, at].astype(LOW)
        for c in range(2):
            start = back_base + c * half
            to_back[start : start + half, :] = wb_ref[at, c * half : (c + 1) * half].astype(LOW)


def round_rest(side, w_out, w_in, w_back, x):
    rows, width = w_out.shape
    half = width // 2
    return pl.pallas_call(
        round_rest_kernel,
        out_shape=(
            shape((2 * rows + width, half), LOW),
            shape((width, half), LOW),
            shape((2 * width, half), LOW),
            shape(x.shape, LOW),
        ),
        in_specs=[SMEM, VMEM, VMEM, VMEM, VMEM],
        out_specs=(VMEM,) * 4,
        compiler_params=pltpu.CompilerParams(vmem_limit_bytes=VMEM_LIMIT),
        name="round_rest",
    )(side, w_out, w_in, w_back, x)


def span_tables(segments, valid, seq):
    blocks = seq // QB
    firsts, lasts = segments[::QB], segments[QB - 1 :: QB]
    low = jnp.sum((segments[None, :] < firsts[:, None]).astype(jnp.int32), axis=1)
    high = jnp.sum((segments[None, :] <= lasts[:, None]).astype(jnp.int32), axis=1)
    own_end = (jnp.arange(blocks, dtype=jnp.int32) + 1) * QB
    high = jnp.maximum(jnp.minimum(high, valid), own_end)
    low_block = low // KB
    high_block = (high + KB - 1) // KB
    return jnp.stack([low_block, high_block - low_block]).astype(jnp.int32)


def make_bias(bias_ref, block, low, count, code_ref, seg_ref):
    dims = (count * KB, QB)
    codes = code_ref[pl.ds(pl.multiple_of(low * KB, KB), count * KB), :]
    segs = seg_ref[:, pl.ds(pl.multiple_of(block * QB, QB), QB)]
    key_at = low * KB + lax.broadcasted_iota(jnp.int32, dims, 0)
    query_at = block * QB + lax.broadcasted_iota(jnp.int32, dims, 1)
    allowed = (codes == segs) | (key_at == query_at)
    bias_ref[: count * KB, :] = jnp.where(allowed, 0.0, MASKED_SCORE)


def one_head(values, head):
    lane = lax.broadcasted_iota(jnp.int32, values.shape, 1)
    keep = (lane < HD) if head == 0 else (lane >= HD)
    return jnp.where(keep, values, jnp.zeros_like(values))


def forward_kernel(
    table_ref,
    x_ref,
    w0_ref,
    w1_ref,
    code_ref,
    seg_ref,
    q_ref,
    k_ref,
    v_ref,
    ctx_ref,
    lse_ref,
    weights,
    biases,
    vt_ref,
    bias_ref,
):
    block = pl.program_id(0)
    low, total = table_ref[0, block], table_ref[1, block]
    piece = (w0_ref.shape[0] - 16) // 3
    pairs = 2 * piece // 128

    @pl.when(block == 0)
    def _():
        for i in range(3):
            for n, ref in enumerate((w0_ref, w1_ref)):
                rows = ref[i * piece : (i + 1) * piece, :]
                weights[i, n * piece : (n + 1) * piece, :] = rows
        lane = lax.broadcasted_iota(jnp.int32, (1, x_ref.shape[1]), 1)
        for i in (0, 2):
            base = 3 * piece + (3 if i == 0 else 6)
            both = [
                sum(ref[base + part : base + part + 1, :].astype(F32) for part in range(3))
                for ref in (w0_ref, w1_ref)
            ]
            row = jnp.where(lane < piece, both[0], pltpu.roll(both[1], piece, 1))
            biases[i : i + 1, :] = row[:, : 2 * piece]
        biases[1:2, :] = jnp.zeros((1, 2 * piece), F32)

        def project(b, carry):
            at = pl.ds(pl.multiple_of(b * QB, QB), QB)
            for i, ref in enumerate((q_ref, k_ref, v_ref)):
                ref[at, :] = (dot(x_ref[at, :], weights[i], NT) + biases[i : i + 1, :]).astype(LOW)
            vt_ref[:, at] = v_ref[at, :].T
            return carry

        lax.fori_loop(0, x_ref.shape[0] // QB, project, 0)

    def run(count):
        make_bias(bias_ref, block, low, count, code_ref, seg_ref)
        bias = bias_ref[: count * KB, :]
        rows = pl.ds(pl.multiple_of(low * KB, KB), count * KB)
        queries = pl.ds(pl.multiple_of(block * QB, QB), QB)

        def scores(head):
            lanes = slice(head // 2 * 128, head // 2 * 128 + 128)
            query = q_ref[queries, lanes] * jnp.asarray(0.125, LOW)
            return dot(k_ref[rows, lanes], one_head(query, head % 2), NT) + bias

        def soft(values, head):
            peak = jnp.max(values, axis=0, keepdims=True)
            powers = jnp.exp(values - peak)
            mass = jnp.sum(powers, axis=0, keepdims=True)
            lse_ref[head : head + 1, :] = peak + jnp.log(mass)
            return (powers * (1.0 / mass)).astype(LOW)

        outs = []

        def context(probs, head):
            outs.append(dot(vt_ref[head * HD : (head + 1) * HD, rows], probs))
            if head % 2 == 1:
                both = jnp.concatenate(outs[-2:], axis=0).T
                ctx_ref[:, head // 2 * 128 : head // 2 * 128 + 128] = both.astype(LOW)

        values, probs = scores(0), None
        for head in range(2 * pairs):
            later = scores(head + 1) if head + 1 < 2 * pairs else None
            now = soft(values, head)
            if head > 0:
                context(probs, head - 1)
            values, probs = later, now
        context(probs, 2 * pairs - 1)

    for count in range(2, k_ref.shape[0] // KB + 1):
        pl.when(total == count)(functools.partial(run, count))


def backward_kernel(carried, table_ref, q_ref, k_ref, v_ref, g_ref, lse_ref, code_ref, seg_ref, *refs):
    block = pl.program_id(0)
    refs = list(refs)
    if carried:
        source, target = refs.pop(0), refs.pop(3)
        target[...] = source[...]
    dq_ref, dk_ref, dv_ref, kt_ref, bias_ref, dk_sum, dv_sum = refs
    low, total = table_ref[0, block], table_ref[1, block]
    heads = q_ref.shape[1] // HD

    @pl.when(block == 0)
    def _():
        kt_ref[...] = k_ref[...].T
        dk_sum[...] = jnp.zeros_like(dk_sum)
        dv_sum[...] = jnp.zeros_like(dv_sum)

    def run(count):
        make_bias(bias_ref, block, low, count, code_ref, seg_ref)
        bias = bias_ref[: count * KB, :]
        rows = pl.ds(pl.multiple_of(low * KB, KB), count * KB)

        def first(head):
            lanes = slice(head // 2 * 128, head // 2 * 128 + 128)
            query = one_head(q_ref[:, lanes] * jnp.asarray(0.125, LOW), head % 2)
            grad = one_head(g_ref[:, lanes], head % 2)
            scores = dot(k_ref[rows, lanes], query, NT) + bias
            return scores, dot(v_ref[rows, lanes], grad, NT), query, grad

        def second(head, scores, prob_grad, query, grad):
            probs = jnp.exp(scores - lse_ref[head : head + 1, :])
            delta = jnp.sum(probs * prob_grad, axis=0, keepdims=True)
            return probs.astype(LOW), (probs * (prob_grad - delta)).astype(LOW), query, grad

        outs = []

        def third(head, probs, score_grad, query, grad):
            lanes = slice(head // 2 * 128, head // 2 * 128 + 128)
            dv_sum[rows, lanes] += dot(probs, grad)
            dk_sum[rows, lanes] += dot(score_grad, query)
            outs.append(dot(kt_ref[head * HD : (head + 1) * HD, rows], score_grad))
            if head % 2 == 1:
                both = jnp.concatenate(outs[-2:], axis=0).T * 0.125
                dq_ref[:, lanes] = both.astype(LOW)

        start, middle_of = first(0), None
        for head in range(heads):
            later = first(head + 1) if head + 1 < heads else None
            now = second(head, *start)
            if head > 0:
                third(head - 1, *middle_of)
            start, middle_of = later, now
        third(heads - 1, *middle_of)

    for count in range(2, k_ref.shape[0] // KB + 1):
        pl.when(total == count)(functools.partial(run, count))

    @pl.when(block == pl.num_programs(0) - 1)
    def _():
        dk_ref[...] = dk_sum[...].astype(LOW)
        dv_ref[...] = dv_sum[...].astype(LOW)


def attend_forward(table, x, first, second, code, seg):
    seq, width = x.shape
    piece = (first.shape[0] - 16) // 3
    heads, blocks = 2 * piece // HD, seq // QB
    whole = lambda i, t: (0, 0)
    column = pl.BlockSpec((seq, 2 * piece), whole)
    return pl.pallas_call(
        forward_kernel,
        out_shape=(shape((seq, 2 * piece), LOW),) * 4 + (shape((8, seq), F32),),
        grid_spec=pltpu.PrefetchScalarGridSpec(
            num_scalar_prefetch=1,
            grid=(blocks,),
            in_specs=[
                pl.BlockSpec((seq, width), whole),
                pl.BlockSpec(first.shape, whole),
                pl.BlockSpec(second.shape, whole),
                pl.BlockSpec((seq, 1), whole),
                pl.BlockSpec((1, seq), whole),
            ],
            out_specs=[
                column,
                column,
                column,
                pl.BlockSpec((QB, 2 * piece), lambda i, t: (i, 0)),
                pl.BlockSpec((8, QB), lambda i, t: (0, i)),
            ],
            scratch_shapes=[
                pltpu.VMEM((3, 2 * piece, width), LOW),
                pltpu.VMEM((3, 2 * piece), F32),
                pltpu.VMEM((2 * piece, seq), LOW),
                pltpu.VMEM((seq, QB), F32),
            ],
        ),
        compiler_params=pltpu.CompilerParams(vmem_limit_bytes=VMEM_LIMIT),
        cost_estimate=pl.CostEstimate(
            flops=16 * seq * seq * piece + 12 * seq * width * piece,
            bytes_accessed=16 * seq * piece,
            transcendentals=seq * seq * heads // 2,
        ),
        name="attend_forward",
    )(table, x, first, second, code, seg)


def attend_backward(table, q, k, v, grad, lse, code, seg, *carried):
    seq, width = grad.shape
    blocks = seq // QB
    block = pl.BlockSpec((QB, width), lambda i, t: (i, 0))
    column = pl.BlockSpec((seq, width), lambda i, t: (0, 0))
    return pl.pallas_call(
        functools.partial(backward_kernel, len(carried)),
        out_shape=(shape((seq, width), LOW),) * 3 + tuple(shape(c.shape, c.dtype) for c in carried),
        grid_spec=pltpu.PrefetchScalarGridSpec(
            num_scalar_prefetch=1,
            grid=(blocks,),
            in_specs=[
                block,
                column,
                column,
                block,
                pl.BlockSpec((8, QB), lambda i, t: (0, i)),
                pl.BlockSpec((seq, 1), lambda i, t: (0, 0)),
                pl.BlockSpec((1, seq), lambda i, t: (0, 0)),
            ]
            + [pl.BlockSpec((QB, c.shape[1]), lambda i, t: (i, 0)) for c in carried],
            out_specs=[block, column, column]
            + [pl.BlockSpec((QB, c.shape[1]), lambda i, t: (i, 0)) for c in carried],
            scratch_shapes=[
                pltpu.VMEM((width, seq), LOW),
                pltpu.VMEM((seq, QB), F32),
                pltpu.VMEM((seq, width), F32),
                pltpu.VMEM((seq, width), F32),
            ],
        ),
        compiler_params=pltpu.CompilerParams(vmem_limit_bytes=VMEM_LIMIT),
        cost_estimate=pl.CostEstimate(
            flops=16 * seq * seq * width,
            bytes_accessed=16 * seq * width,
            transcendentals=seq * seq * width // 128,
        ),
        name="attend_backward",
    )(table, q, k, v, grad, lse, code, seg, *carried)


def gelu_parts(pre):
    t = 1.0 / (1.0 + PHI_STEP * jnp.abs(pre))
    poly = PHI[7] * t + PHI[6]
    for factor in PHI[5::-1]:
        poly = poly * t + factor
    bell = jnp.exp(-0.5 * (pre * pre))
    tail = poly * t * bell
    cdf = jnp.where(pre < 0, tail, 1.0 - tail)
    return pre * cdf, cdf + pre * (bell * 0.3989422804014327)


def norm_stats(values):
    width = values.shape[-1]
    mean = jnp.sum(values, axis=-1, keepdims=True) * (1.0 / width)
    centred = values - mean
    spread = jnp.sum(centred * centred, axis=-1, keepdims=True) * (1.0 / width)
    rate = lax.rsqrt(spread + LN_EPSILON)
    return centred * rate, rate


def norm_back(grad, gain, xhat, rate):
    width = grad.shape[-1]
    scaled = grad * gain
    mean = jnp.sum(scaled, axis=-1, keepdims=True) * (1.0 / width)
    along = jnp.sum(scaled * xhat, axis=-1, keepdims=True) * (1.0 / width)
    return rate * (scaled - mean - xhat * along)


def column_sum(values):
    return jnp.sum(values, axis=0, keepdims=True)


def middle_kernel(
    total_slots,
    dp_bits,
    valid_ref,
    lengths_ref,
    ctx_a,
    ctx_b,
    gains,
    shifts,
    x_hbm,
    teacher_hbm,
    qa,
    qb,
    qc,
    qd,
    outin_own,
    outin_core,
    outin_far,
    back_own,
    back_core,
    second_own,
    second_core,
    out_hbm,
    dh_hbm,
    cg_a,
    cg_b,
    core_hbm,
    to_x,
    to_y,
    rest,
    out_send_a,
    out_send_b,
    out_keep_a,
    out_keep_b,
    sums,
    bias_sums,
    count_ref,
    outin_far_core,
    in_far,
    back_far,
    in_far_core,
    back_far_core,
    w_in,
    w_back,
    w_out,
    bias_parts,
    bias_in,
    xhat_one,
    rate_one,
    mid_low,
    hidden,
    slope,
    acc,
    dh_low,
    pre_grad,
    rows_in,
    rows_out,
    stage16,
    stage32,
    from_core,
    held,
    w_sem,
    in_sem,
    out_sem,
    load_sem,
    store_sem,
    send_sem,
    recv_sem,
    count_send,
    count_recv,
    far_send,
    far_recv,
):
    seq, width = acc.shape
    blocks = seq // RB
    half = width // 2
    out_rows = w_out.shape[0] // 4
    units = w_in.shape[2]
    side = units // 2
    core_at, y_at, x_at = partner("tensor", 0), partner("tensor", 1), partner("dp", 0)
    greet([core_at, y_at] + [partner("dp", bit) for bit in range(dp_bits)])

    def far_copy(n, source, target, device):
        return pltpu.make_async_remote_copy(
            src_ref=source,
            dst_ref=target,
            send_sem=far_send.at[n],
            recv_sem=far_recv.at[n],
            device_id=device,
            device_id_type=pl.DeviceIdType.MESH,
        )

    in_at = pl.ds(2 * out_rows, width)
    far = [
        far_copy(0, outin_far, outin_far_core, core_at),
        far_copy(1, back_own, back_far.at[0], y_at),
        far_copy(2, second_own.at[pl.ds(width, width), :], back_far.at[1], y_at),
        far_copy(3, outin_far.at[in_at, :], in_far, x_at),
        far_copy(4, in_far, in_far_core, core_at),
        far_copy(5, back_far.at[0], back_far_core.at[0], core_at),
        far_copy(6, back_far.at[1], back_far_core.at[1], core_at),
    ]
    for copy in far[:4]:
        copy.start()
    out_in = (outin_own, outin_core, outin_far, outin_far_core)
    in_parts = tuple(ref.at[in_at, :] for ref in out_in)
    in_other = (
        second_own.at[pl.ds(0, width), :],
        second_core.at[pl.ds(0, width), :],
        in_far,
        in_far_core,
    )
    back_parts = (back_own, back_core, back_far.at[0], back_far_core.at[0])
    back_other = (
        second_own.at[pl.ds(width, width), :],
        second_core.at[pl.ds(width, width), :],
        back_far.at[1],
        back_far_core.at[1],
    )

    def rows(i):
        return pl.ds(i * RB, RB)

    def fetch(source, i, slot):
        return pltpu.make_async_copy(source.at[rows(i), :], rows_in.at[slot], in_sem.at[slot])

    def out_weights(p, c):
        return pltpu.make_async_copy(
            out_in[p].at[pl.ds(c * out_rows, out_rows), :],
            w_out.at[pl.ds(p * out_rows, out_rows), pl.ds(c * half, half)],
            w_sem.at[p, c],
        )

    def bias_rows(p):
        source = (qa, qb, qc, qd)[p]
        return pltpu.make_async_copy(
            source.at[pl.ds(source.shape[0] - 16, 16), :], bias_parts.at[p], w_sem.at[p, 8]
        )

    def load_in(source, p, r):
        return pltpu.make_async_copy(
            source, w_in.at[p, :, pl.ds(r * side, side)], w_sem.at[p, 2 + 3 * r]
        )

    def load_back(source, p, r, c):
        return pltpu.make_async_copy(
            source.at[pl.ds(c * side, side), :],
            w_back.at[p, pl.ds(r * side, side), pl.ds(c * half, half)],
            w_sem.at[p, 3 + 3 * r + c],
        )

    def ffn_weights(p):
        load_in(in_parts[p], p, 0).start()
        load_in(in_other[p], p, 1).start()
        for c in range(2):
            load_back(back_parts[p], p, 0, c).start()
            load_back(back_other[p], p, 1, c).start()

    early = [out_weights(p, c) for p in range(4) for c in range(2)]
    for copy in early[:6]:
        copy.start()
    fetch(x_hbm, 0, 0).start()
    for p in range(4):
        bias_rows(p).start()
    for p in range(2):
        ffn_weights(p)

    def count_step(bit):
        return pltpu.make_async_remote_copy(
            src_ref=held.at[2 * bit],
            dst_ref=held.at[2 * bit + 1],
            send_sem=count_send.at[bit],
            recv_sem=count_recv.at[bit],
            device_id=partner("dp", bit),
            device_id_type=pl.DeviceIdType.MESH,
        )

    tokens = jnp.full(held.shape[1:], 0, jnp.int32)
    for i in range(lengths_ref.shape[0]):
        tokens += lengths_ref[i]
    held[0] = tokens
    count_step(0).start()

    def count_on(bit):
        count_step(bit).wait()
        held[2 * bit + 2] = held[2 * bit] + held[2 * bit + 1]
        if bit + 1 < dp_bits:
            count_step(bit + 1).start()

    far[0].wait_recv()
    for copy in early[6:]:
        copy.start()
    for copy in early:
        copy.wait()

    for i in range(blocks):
        if i + 1 < blocks:
            fetch(x_hbm, i + 1, (i + 1) % 2).start()
        fetch(x_hbm, i, i % 2).wait()
        context = jnp.concatenate([ctx_a[rows(i), :], ctx_b[rows(i), :]], axis=1)
        xhat, rate = norm_stats(dot(context, w_out[...]) + shifts[0:1, :] + rows_in[i % 2])
        xhat_one[rows(i), :] = xhat
        rate_one[rows(i), :] = rate
        mid_low[rows(i), :] = (xhat * gains[0:1, :] + shifts[1:2, :]).astype(LOW)
        acc[rows(i), :] = jnp.zeros((RB, width), F32)
        if i < dp_bits:
            count_on(i)
    for bit in range(blocks, dp_bits):
        count_on(bit)
    count_ref[...] = held[2 * dp_bits]
    fetch(teacher_hbm, 0, 0).start()
    for p in range(4):
        bias_rows(p).wait()
        part = bias_parts[p, 0:3, :].astype(F32)
        bias_in[p] = part[0:1] + part[1:2] + part[2:3]

    def up(p, carry):
        @pl.when(p == 2)
        def _():
            for n, then in ((3, 4), (1, 5), (2, 6)):
                far[n].wait_recv()
                far[then].start()
            ffn_weights(2)

        @pl.when(p == 3)
        def _():
            for n in (4, 5, 6):
                far[n].wait_recv()
            ffn_weights(3)

        for r in range(2):
            load_in(in_other[0], p, r).wait()
            for c in range(2):
                load_back(back_own, p, r, c).wait()
        def lift(k):
            return dot(mid_low[pl.ds(k * FR, FR), :], w_in[p]) + bias_in[p]

        def lower(k):
            at = pl.ds(k * FR, FR)
            acc[at, :] += dot(hidden[p, at, :], w_back[p])

        pre = lift(0)
        for k in range(seq // FR):
            later = lift(k + 1) if k + 1 < seq // FR else None
            at = pl.ds(k * FR, FR)
            act, der = gelu_parts(pre)
            hidden[p, at, :] = act.astype(LOW)
            slope[p, at, :] = der
            if k > 0:
                lower(k - 1)
            pre = later
        lower(seq // FR - 1)
        return carry

    lax.fori_loop(0, 4, up, 0)

    zero = jnp.zeros((1, width), F32)
    squares, gain_two, shift_two, shift_mid = zero, zero, zero, zero
    scale = total_slots / held[2 * dp_bits, 0:1, 0:1].astype(F32)
    stores = []
    for i in range(blocks):
        if i + 1 < blocks:
            fetch(teacher_hbm, i + 1, (i + 1) % 2).start()
        fetch(teacher_hbm, i, i % 2).wait()
        mid = xhat_one[rows(i), :] * gains[0:1, :] + shifts[1:2, :]
        xhat, rate = norm_stats(acc[rows(i), :] + shifts[2:3, :] + mid)
        output = xhat * gains[1:2, :] + shifts[3:4, :]
        if i >= 2:
            stores[i - 2].wait()
        rows_out[i % 2] = output
        stores.append(
            pltpu.make_async_copy(rows_out.at[i % 2], out_hbm.at[rows(i), :], out_sem.at[i % 2])
        )
        stores[i].start()
        live = (i * RB + lax.broadcasted_iota(jnp.int32, (RB, 1), 0)) < valid_ref[0]
        distance = jnp.where(live, output - rows_in[i % 2], 0.0)
        squares += column_sum(distance * distance)
        out_grad = scale * distance
        gain_two += column_sum(out_grad * xhat)
        shift_two += column_sum(out_grad)
        dh_two = norm_back(out_grad, gains[1:2, :], xhat, rate)
        shift_mid += column_sum(dh_two)
        acc[rows(i), :] = dh_two
        dh_low[rows(i), :] = dh_two.astype(LOW)
    for store in stores[-2:]:
        store.wait()

    sides = (pl.ds(0, side), pl.ds(side, side))

    def ffn_back(p):
        total = jnp.zeros((1, units), F32)

        def lift(k):
            return dot(dh_low[pl.ds(k * FR, FR), :], w_back[p], NT)

        def lower(k):
            at = pl.ds(k * FR, FR)
            acc[at, :] += dot(pre_grad[at, :], w_in[p], NT)

        raised = lift(0)
        for k in range(seq // FR):
            later = lift(k + 1) if k + 1 < seq // FR else None
            at = pl.ds(k * FR, FR)
            grad = (raised * slope[p, at, :]).astype(LOW)
            pre_grad[at, :] = grad
            total += column_sum(grad.astype(F32))
            if k > 0:
                lower(k - 1)
            raised = later
        lower(seq // FR - 1)
        bias_sums[pl.ds(p, 1), :] = total

    def to_core(pair, w):
        return pltpu.make_async_remote_copy(
            src_ref=stage16.at[w],
            dst_ref=core_hbm.at[pair, w],
            send_sem=send_sem.at[w],
            recv_sem=recv_sem.at[pair, w],
            device_id=core_at,
            device_id_type=pl.DeviceIdType.MESH,
        )

    def away(n, carry):
        p = 2 * n + 1
        ffn_back(p)

        @pl.when(n > 0)
        def _():
            for w in range(2):
                to_core(0, w).wait_send()

        stage16[0] = dot(mid_low[...], pre_grad[...], TN).astype(LOW)
        stage16[1] = dot(hidden[p], dh_low[...], TN).astype(LOW)
        for w in range(2):
            to_core(n, w).start()
        return carry

    lax.fori_loop(0, 2, away, 0)

    def in_moves(pair):
        return [
            pltpu.make_async_copy(stage32.at[0, :, sides[0]], rest.at[pair], store_sem.at[0]),
            pltpu.make_async_copy(stage16.at[0, :, sides[1]], to_x.at[pair], store_sem.at[1]),
        ]

    def back_moves(stage, target):
        return [
            pltpu.make_async_copy(
                stage.at[1, sides[r], sides[c]],
                target.at[r, sides[c], :],
                store_sem.at[2 + 2 * r + c],
            )
            for r in range(2)
            for c in range(2)
        ]

    moves = {1: in_moves(1) + back_moves(stage16, to_y), 0: in_moves(0) + back_moves(stage32, rest.at[pl.ds(2, 2)])}

    def home(n, carry):
        pair = 1 - n
        p = 2 * pair
        for w in range(2):
            to_core(pair, w).wait_recv()
            pltpu.make_async_copy(core_hbm.at[pair, w], from_core.at[w], load_sem.at[w]).start()
        ffn_back(p)

        @pl.when(n == 0)
        def _():
            for w in range(2):
                to_core(1, w).wait_send()

        @pl.when(n == 1)
        def _():
            for copy in moves[1]:
                copy.wait()

        stage32[0] = dot(mid_low[...], pre_grad[...], TN)
        stage32[1] = dot(hidden[p], dh_low[...], TN)
        for w in range(2):
            pltpu.make_async_copy(core_hbm.at[pair, w], from_core.at[w], load_sem.at[w]).wait()
            for k in range(0, width, 128):
                total = stage32[w, k : k + 128, :] + from_core[w, k : k + 128, :].astype(F32)
                stage32[w, k : k + 128, :] = total
                stage16[w, k : k + 128, :] = total.astype(LOW)

        @pl.when(n == 0)
        def _():
            for copy in moves[1]:
                copy.start()

        @pl.when(n == 1)
        def _():
            for copy in moves[0]:
                copy.start()

        return carry

    lax.fori_loop(0, 2, home, 0)

    gain_one, shift_one, shift_out = zero, zero, zero
    stores = []
    for i in range(blocks):
        grad, xhat = acc[rows(i), :], xhat_one[rows(i), :]
        gain_one += column_sum(grad * xhat)
        shift_one += column_sum(grad)
        dh_one = norm_back(grad, gains[0:1, :], xhat, rate_one[rows(i), :])
        shift_out += column_sum(dh_one)
        if i >= 2:
            stores[i - 2].wait()
        rows_out[i % 2] = dh_one
        stores.append(
            pltpu.make_async_copy(rows_out.at[i % 2], dh_hbm.at[rows(i), :], out_sem.at[i % 2])
        )
        stores[i].start()
        dh_one = dh_one.astype(LOW)
        dh_low[rows(i), :] = dh_one
        grad = dot(dh_one, w_out[...], NT).astype(LOW)
        cg_a[rows(i), :] = grad[:, :half]
        cg_b[rows(i), :] = grad[:, half:]
    for context, out_keep, out_send in (
        (ctx_a, out_keep_a, out_send_a),
        (ctx_b, out_keep_b, out_send_b),
    ):
        grad = dot(context[...], dh_low[...], TN)
        out_keep[...] = grad[:out_rows]
        out_send[...] = grad[out_rows:].astype(LOW)
    sums[...] = jnp.concatenate(
        [gain_one, gain_two, shift_out, shift_one, shift_mid, shift_two, squares, zero], axis=0
    )
    for store in stores[-2:]:
        store.wait()
    for copy in moves[0]:
        copy.wait()
    for copy in far:
        copy.wait_send()


def middle(
    total_slots, valid, lengths, ctx_a, ctx_b, gains, shifts, x, teacher, near, out_in, back, second
):
    seq, width = x.shape
    half = width // 2
    out_rows = ctx_a.shape[1] // 2
    units = width
    dp_bits = bits_of("dp")
    slab = (width, units // 2)
    return pl.pallas_call(
        functools.partial(middle_kernel, float(total_slots), dp_bits),
        out_shape=(
            shape((seq, width), F32),
            shape((seq, width), F32),
            shape((seq, half), LOW),
            shape((seq, half), LOW),
            shape((2, 2, width, units), LOW),
            shape((2,) + slab, LOW),
            shape((2,) + slab, LOW),
            shape((4,) + slab, F32),
            shape((out_rows, width), LOW),
            shape((out_rows, width), LOW),
            shape((out_rows, width), F32),
            shape((out_rows, width), F32),
            shape((8, width), F32),
            shape((4, units), F32),
            shape((8, 128), jnp.int32),
            shape(out_in[0].shape, LOW),
            shape(slab, LOW),
            shape((2,) + slab, LOW),
            shape(slab, LOW),
            shape((2,) + slab, LOW),
        ),
        in_specs=[SMEM, SMEM, VMEM, VMEM, VMEM, VMEM, HBM, HBM] + [HBM] * 11,
        out_specs=(HBM, HBM, VMEM, VMEM, HBM, HBM, HBM, HBM) + (VMEM,) * 7 + (HBM,) * 5,
        scratch_shapes=[
            pltpu.VMEM((4, width, units), LOW),
            pltpu.VMEM((4, units, width), LOW),
            pltpu.VMEM((4 * out_rows, width), LOW),
            pltpu.VMEM((4, 16, width), LOW),
            pltpu.VMEM((4, 1, units), F32),
            pltpu.VMEM((seq, width), F32),
            pltpu.VMEM((seq, 1), F32),
            pltpu.VMEM((seq, width), LOW),
            pltpu.VMEM((4, seq, units), LOW),
            pltpu.VMEM((4, seq, units), F32),
            pltpu.VMEM((seq, width), F32),
            pltpu.VMEM((seq, width), LOW),
            pltpu.VMEM((seq, units), LOW),
            pltpu.VMEM((2, RB, width), F32),
            pltpu.VMEM((2, RB, width), F32),
            pltpu.VMEM((2, width, units), LOW),
            pltpu.VMEM((2, width, units), F32),
            pltpu.VMEM((2, width, units), LOW),
            pltpu.VMEM((2 * dp_bits + 1, 8, 128), jnp.int32),
            pltpu.SemaphoreType.DMA((4, 9)),
            pltpu.SemaphoreType.DMA((2,)),
            pltpu.SemaphoreType.DMA((2,)),
            pltpu.SemaphoreType.DMA((2,)),
            pltpu.SemaphoreType.DMA((6,)),
            pltpu.SemaphoreType.DMA((2,)),
            pltpu.SemaphoreType.DMA((2, 2)),
            pltpu.SemaphoreType.DMA((dp_bits,)),
            pltpu.SemaphoreType.DMA((dp_bits,)),
            pltpu.SemaphoreType.DMA((7,)),
            pltpu.SemaphoreType.DMA((7,)),
        ],
        compiler_params=pltpu.CompilerParams(
            vmem_limit_bytes=VMEM_LIMIT, collective_id=1, has_side_effects=True
        ),
        cost_estimate=pl.CostEstimate(
            flops=6 * seq * width * (8 * units + width),
            bytes_accessed=30 << 20,
            transcendentals=2 * seq * 4 * units,
        ),
        name="middle",
    )(valid, lengths, ctx_a, ctx_b, gains, shifts, x, teacher, *near, *out_in, *back, *second)


def add_rows(out, terms, chunk=96):
    rows = out.shape[0]
    chunk = min(chunk, rows)

    def step(i, carry):
        at = pl.ds(pl.multiple_of(i * chunk, chunk), chunk)
        total = terms[0][at, :].astype(F32)
        for term in terms[1:]:
            total += term[at, :].astype(F32)
        out[at, :] = total.astype(out.dtype)
        return carry

    lax.fori_loop(0, rows // chunk, step, 0)


def cross_rows(x_ref, grads, okeep, osend, side, cross, keep, send, bias_ref):
    half = x_ref.shape[1] // 2
    piece = grads[0].shape[1] // 2
    mine = pl.ds(pl.multiple_of(side * half, half), half)
    other = pl.ds(pl.multiple_of((1 - side) * half, half), half)
    for i in range(3):
        cross[...] = dot(grads[i][...], x_ref[...], TN)
        at = slice(i * piece, (i + 1) * piece)
        for n, lanes in enumerate((mine, other)):
            keep[n, at, :] = cross[:piece, lanes]
            send[n, at, :] = cross[piece:, lanes].astype(send.dtype)
        bias_ref[i : i + 1, :] = column_sum(grads[i][...].astype(F32))
    for n, lanes in enumerate((mine, other)):
        keep[n, 3 * piece :, :] = okeep[:, lanes]
        send[n, 3 * piece :, :] = osend[:, lanes].astype(send.dtype)


def far_kernel(
    x_ref,
    dq,
    dk,
    dv,
    osend,
    okeep,
    away,
    away_first,
    bias_ref,
    keep,
    send,
    core,
    cross,
    send_sem,
    recv_sem,
):
    core_at = partner("tensor", 0)
    greet([core_at])
    bias_ref[...] = jnp.zeros(bias_ref.shape, F32)
    cross_rows(
        x_ref, (dq, dk, dv), okeep, osend, lax.axis_index("dp") & 1, cross, keep, send, bias_ref
    )
    copies = [
        pltpu.make_async_remote_copy(
            src_ref=send.at[n],
            dst_ref=core.at[n],
            send_sem=send_sem.at[n],
            recv_sem=recv_sem.at[n],
            device_id=core_at,
            device_id_type=pl.DeviceIdType.MESH,
        )
        for n in range(2)
    ]
    for n in (1, 0):
        copies[n].start()
    for n in (1, 0):
        copies[n].wait_recv()
        add_rows((away, away_first)[n], [keep.at[n], core.at[n]])
    for n in (1, 0):
        copies[n].wait_send()


def far_projections(x, grads, osend, okeep):
    seq, width = x.shape
    half = width // 2
    piece = grads[0].shape[1] // 2
    slabs = (2, width, half)
    return pl.pallas_call(
        far_kernel,
        out_shape=(shape(slabs[1:], LOW), shape(slabs[1:], LOW), shape((8, 2 * piece), F32)),
        in_specs=[VMEM] * 6,
        out_specs=(VMEM, VMEM, VMEM),
        scratch_shapes=[
            pltpu.VMEM(slabs, F32),
            pltpu.VMEM(slabs, F32),
            pltpu.VMEM(slabs, F32),
            pltpu.VMEM((2 * piece, width), F32),
            pltpu.SemaphoreType.DMA((2,)),
            pltpu.SemaphoreType.DMA((2,)),
        ],
        compiler_params=pltpu.CompilerParams(
            vmem_limit_bytes=VMEM_LIMIT, collective_id=3, has_side_effects=True
        ),
        cost_estimate=pl.CostEstimate(
            flops=12 * seq * width * piece, bytes_accessed=10 << 20, transcendentals=0
        ),
        name="far_projections",
    )(x, *grads, osend, okeep)


def finish_kernel(
    dp_bits,
    x_ref,
    w0,
    w1,
    w2,
    w3,
    dqa,
    dka,
    dva,
    dqb,
    dkb,
    dvb,
    osend,
    okeep,
    dh_hbm,
    rest,
    ffn_x,
    ffn_y,
    in_y,
    back_x,
    away,
    away_first,
    small_ref,
    bias_far,
    gx_hbm,
    result,
    small_out,
    own,
    own16,
    keep,
    send,
    core,
    y_recv,
    x_send,
    x_recv,
    total,
    z_send,
    z_recv,
    last_send,
    last_recv,
    extra,
    bias_ref,
    small_held,
    rows_in,
    rows_out,
    cross,
    load_sem,
    send_sem,
    recv_sem,
    in_sem,
    out_sem,
):
    seq, width = x_ref.shape
    half = width // 2
    piece = dqa.shape[1] // 2
    blocks = seq // RB
    place = lax.axis_index("dp")
    index = lax.axis_index("tensor")
    side = place & 1
    core_at, y_at = partner("tensor", 0), partner("tensor", 1)
    dp_at = [partner("dp", bit) for bit in range(dp_bits)]
    greet([core_at, y_at] + dp_at)
    started = {}

    def remote(key, source, target, device):
        n = len(started)
        started[key] = pltpu.make_async_remote_copy(
            src_ref=source,
            dst_ref=target,
            send_sem=send_sem.at[n],
            recv_sem=recv_sem.at[n],
            device_id=device,
            device_id_type=pl.DeviceIdType.MESH,
        )
        started[key].start()

    def arrive(key):
        started[key].wait_recv()

    part = width // 4
    half_bit, part_bit = (place >> 1) & 1, (place >> 2) & 1

    def quarter(i, j):
        at = (half_bit ^ i) * (2 * part) + (part_bit ^ j) * part
        return pl.ds(pl.multiple_of(at, part), part)

    def two_quarters(i):
        return pl.ds(pl.multiple_of((half_bit ^ i) * (2 * part), 2 * part), 2 * part)

    for n, source in ((1, away_first), (0, away)):
        for i in (1, 0):
            rows = two_quarters(i)
            remote(("y", n, i), source.at[rows, :], y_recv.at[n, rows, :], y_at)
    loads = []
    for w, terms in enumerate(((rest.at[0], ffn_x.at[0], in_y), (rest.at[2], ffn_y.at[0], back_x))):
        targets = (own.at[w], own16.at[w, 0], own16.at[w, 1])
        loads.append(
            [
                pltpu.make_async_copy(term, target, load_sem.at[w, n])
                for n, (term, target) in enumerate(zip(terms, targets))
            ]
        )
        for copy in loads[w]:
            copy.start()

    def fetch(i):
        return pltpu.make_async_copy(
            dh_hbm.at[pl.ds(i * RB, RB), :], rows_in.at[i % 2], in_sem.at[i % 2]
        )

    fetch(0).start()

    def scatter(w):
        for j in (1, 0):
            at = pl.ds((1 - j) * part, part)
            add_rows(z_send.at[w, at, :], [total.at[w, quarter(1, j), :]])
            remote((w, "z", j), z_send.at[w, at, :], z_recv.at[w, at, :], dp_at[1])

    def scatter_on(w):
        rows = quarter(0, 1)
        arrive((w, "z", 1))
        add_rows(last_send.at[w], [total.at[w, rows, :], z_recv.at[w, pl.ds(0, part), :]])
        remote((w, "last"), last_send.at[w], last_recv.at[w], dp_at[2])

    def spread(w, i, j):
        rows = result.at[w, 0, quarter(i, j), :]
        if (i, j) == (0, 0):
            remote((w, "gather", 0, 1), rows, rows, dp_at[2])
        if i == 0:
            remote((w, "gather", 1, j), rows, rows, dp_at[1])
        remote((w, "across", i, j), rows, result.at[w, 1, quarter(i, j), :], dp_at[0])

    def settle(w):
        rows = quarter(0, 0)
        own_part = result.at[w, 0, rows, :]
        arrive((w, "z", 0))
        arrive((w, "last"))
        terms = [total.at[w, rows, :], z_recv.at[w, pl.ds(part, part), :], last_recv.at[w]]
        add_rows(own_part, terms)
        for bit in range(3, dp_bits):
            into = extra.at[w, bit - 3]
            remote((w, "all", bit), own_part, into, dp_at[bit])
            started[(w, "all", bit)].wait_send()
            arrive((w, "all", bit))
            add_rows(own_part, [own_part, into])
        spread(w, 0, 0)

    def gather(w, i, j):
        arrive((w, "gather", i, j))
        spread(w, i, j)

    for w in range(2):
        for copy in loads[w]:
            copy.wait()
        add_rows(total.at[w], [own.at[w], own16.at[w, 0], own16.at[w, 1]])
        scatter(w)

    cross_rows(x_ref, (dqa, dka, dva), okeep, osend, side, cross, keep, send, bias_ref)
    for n in (1, 0):
        remote(("core", n), send.at[n], core.at[n], core_at)

    small_held[0] = jnp.zeros(small_held.shape[1:], F32)
    small_held[0, 16:24, :] = small_ref[0:8, :]
    for p in range(4):
        row = 4 * (index ^ p)
        half_mine = small_ref[8 + p : 9 + p, :half]
        half_other = small_ref[8 + p : 9 + p, half:]
        low_half = jnp.where(side == 0, half_mine, half_other)
        high_half = jnp.where(side == 0, half_other, half_mine)
        small_held[0, pl.ds(row, 1), :] = jnp.concatenate([low_half, high_half], axis=1)
        for i, k in enumerate((0, 2)):
            values = (bias_ref, bias_far)[p // 2][k : k + 1, :]
            if p % 2 == 1:
                values = pltpu.roll(values, piece, 1)
            small_held[0, pl.ds(row + 1 + i, 1), :half] = values

    def small_step(n):
        bits = [core_at, y_at] + dp_at
        remote(("small", n), small_held.at[2 * n], small_held.at[2 * n + 1], bits[n])

    def small_sum(n):
        arrive(("small", n))
        out = small_held.at[2 * n + 2] if n < dp_bits + 1 else small_out
        out[...] = small_held[2 * n] + small_held[2 * n + 1]

    weights = ((w0, w1), (w2, w3))
    grads = ((dqa, dka, dva), (dqb, dkb, dvb))
    stores = []

    def inputs_rows(b):
        at = pl.ds(b * RB, RB)
        if b + 1 < blocks:
            fetch(b + 1).start()
        fetch(b).wait()
        grad = rows_in[b % 2]
        for g in range(2):
            for i in range(3):
                rows = slice(i * piece, (i + 1) * piece)
                w = jnp.concatenate([ref[rows, :] for ref in weights[g]], axis=0)
                grad += dot(grads[g][i][at, :], w)
        if b >= 2:
            stores[b - 2].wait()
        rows_out[b % 2] = grad
        stores.append(
            pltpu.make_async_copy(rows_out.at[b % 2], gx_hbm.at[at, :], out_sem.at[b % 2])
        )
        stores[b].start()

    def send_across(i):
        rows = two_quarters(i)
        at = pl.ds((1 - i) * 2 * part, 2 * part)
        arrive(("y", 1, i))
        add_rows(x_send.at[at, :], [keep.at[1, rows, :], core.at[1, rows, :], y_recv.at[1, rows, :]])
        remote(("across", i), x_send.at[at, :], x_recv.at[at, :], dp_at[0])

    def take_across(i):
        rows = two_quarters(i)
        at = pl.ds((1 - i) * 2 * part, 2 * part)
        arrive(("y", 0, i))
        arrive(("across", i))
        add_rows(
            total.at[2, rows, :],
            [keep.at[0, rows, :], core.at[0, rows, :], y_recv.at[0, rows, :], x_recv.at[at, :]],
        )

    small_step(0)
    scatter_on(0)
    arrive(("core", 1))
    send_across(1)
    send_across(0)
    scatter_on(1)
    inputs_rows(0)
    small_sum(0)
    small_step(1)
    settle(0)
    inputs_rows(1)
    small_sum(1)
    small_step(2)
    arrive(("core", 0))
    take_across(1)
    scatter(2)
    settle(1)
    gather(0, 0, 1)
    take_across(0)
    scatter_on(2)
    gather(0, 1, 0)
    inputs_rows(2)
    gather(1, 0, 1)
    small_sum(2)
    small_step(3)
    gather(0, 1, 1)
    settle(2)
    gather(1, 1, 0)
    inputs_rows(3)
    gather(1, 1, 1)
    small_sum(3)
    small_step(4)
    gather(2, 0, 1)
    gather(2, 1, 0)
    for n in range(4, dp_bits + 2):
        small_sum(n)
        if n + 1 < dp_bits + 2:
            small_step(n + 1)
    gather(2, 1, 1)
    for w in range(3):
        for i in range(2):
            for j in range(2):
                arrive((w, "across", i, j))
    for key, copy in started.items():
        if not (isinstance(key, tuple) and key[1] == "all"):
            copy.wait_send()
    for store in stores[-2:]:
        store.wait()


def finish(x, weights, grads, osend, okeep, dh, rest, ffn_x, ffn_y, in_y, back_x, away, away_first, small, bias_far):
    seq, width = x.shape
    half = width // 2
    piece = grads[0].shape[1] // 2
    dp_bits = bits_of("dp")
    slab = (width, half)
    copies = 8 + dp_bits + 2 + 3 * (10 + max(dp_bits - 3, 0))
    assert dp_bits >= 3
    return pl.pallas_call(
        functools.partial(finish_kernel, dp_bits),
        out_shape=(
            shape((seq, width), F32),
            shape((3, 2) + slab, LOW),
            shape((24, width), F32),
        ),
        in_specs=[VMEM] * 13 + [HBM] * 8 + [VMEM, VMEM],
        out_specs=(HBM, VMEM, VMEM),
        scratch_shapes=[
            pltpu.VMEM((2,) + slab, F32),
            pltpu.VMEM((2, 2) + slab, LOW),
            pltpu.VMEM((2,) + slab, F32),
            pltpu.VMEM((2,) + slab, F32),
            pltpu.VMEM((2,) + slab, F32),
            pltpu.VMEM((2,) + slab, LOW),
            pltpu.VMEM(slab, LOW),
            pltpu.VMEM(slab, LOW),
            pltpu.VMEM((3,) + slab, F32),
            pltpu.VMEM((3, width // 2, half), LOW),
            pltpu.VMEM((3, width // 2, half), LOW),
            pltpu.VMEM((3, width // 4, half), LOW),
            pltpu.VMEM((3, width // 4, half), LOW),
            pltpu.VMEM((3, max(dp_bits - 3, 1), width // 4, half), LOW),
            pltpu.VMEM((8, 2 * piece), F32),
            pltpu.VMEM((2 * dp_bits + 4, 24, width), F32),
            pltpu.VMEM((2, RB, width), F32),
            pltpu.VMEM((2, RB, width), F32),
            pltpu.VMEM((2 * piece, width), F32),
            pltpu.SemaphoreType.DMA((2, 3)),
            pltpu.SemaphoreType.DMA((copies,)),
            pltpu.SemaphoreType.DMA((copies,)),
            pltpu.SemaphoreType.DMA((2,)),
            pltpu.SemaphoreType.DMA((2,)),
        ],
        compiler_params=pltpu.CompilerParams(
            vmem_limit_bytes=VMEM_LIMIT, collective_id=2, has_side_effects=True
        ),
        cost_estimate=pl.CostEstimate(
            flops=36 * seq * width * piece, bytes_accessed=50 << 20, transcendentals=0
        ),
        name="finish",
    )(x, *weights, *grads, osend, okeep, dh, rest, ffn_x, ffn_y, in_y, back_x, away, away_first, small, bias_far)


def widen_kernel(
    place_ref,
    result,
    small,
    count,
    source,
    loss_ref,
    qkv_ref,
    bqv_ref,
    out_ref,
    in_ref,
    bin_ref,
    back_ref,
    gains_ref,
    shifts_ref,
    target,
):
    target[...] = source[...]
    half = result.shape[3]
    piece = qkv_ref.shape[1]
    side = place_ref[0]
    for n in range(2):
        natural = (side + n) % 2
        at = pl.ds(pl.multiple_of(natural * half, half), half)
        in_ref[:, at] = result[0, n].astype(F32)
        for c in range(2):
            rows = result[1, n, c * half : (c + 1) * half, :]
            back_ref[at, c * half : (c + 1) * half] = rows.astype(F32)
        for i in range(3):
            qkv_ref[i, :, at] = result[2, n, i * piece : (i + 1) * piece, :].astype(F32)
        out_ref[:, at] = result[2, n, 3 * piece :, :].astype(F32)
    row = 4 * place_ref[1]
    bin_ref[...] = small[pl.ds(row, 1), :]
    for i in range(2):
        bqv_ref[i : i + 1, :] = small[pl.ds(row + 1 + i, 1), :piece]
    gains_ref[...] = small[16:18, :]
    shifts_ref[...] = small[18:22, :]
    tokens = count[0:1, 0:1].astype(F32)
    total = jnp.sum(small[22:23, :], axis=1, keepdims=True)
    loss_ref[...] = total / (2.0 * small.shape[1] * tokens)


def widen(place, result, small, count, inputs_grad, piece, rows):
    width, half = result.shape[2:]
    return pl.pallas_call(
        widen_kernel,
        out_shape=(
            shape((1, 1), F32),
            shape((3, piece, width), F32),
            shape((2, piece), F32),
            shape((rows, width), F32),
            shape((width, 2 * half), F32),
            shape((1, 2 * half), F32),
            shape((2 * half, width), F32),
            shape((2, width), F32),
            shape((4, width), F32),
            shape(inputs_grad.shape, F32),
        ),
        in_specs=[SMEM, VMEM, VMEM, VMEM, VMEM],
        out_specs=(VMEM,) * 10,
        compiler_params=pltpu.CompilerParams(vmem_limit_bytes=VMEM_LIMIT),
        name="widen",
    )(place, result, small, count, inputs_grad)


def per_device(
    inputs,
    w_qkv,
    b_qv,
    w_out,
    w_in,
    b_in,
    w_back,
    norm_gains,
    shifts,
    segment_ids,
    valid_lengths,
    teacher,
):
    own_seqs, seq, width = inputs.shape
    assert own_seqs == 1 and lax.axis_size("tensor") == 4
    total_slots = seq * lax.axis_size("tensor") * lax.axis_size("dp")
    half = width // 2
    piece = w_qkv.shape[2]
    units = w_in.shape[1]
    index = lax.axis_index("tensor")
    side = (lax.axis_index("dp") & 1).astype(jnp.int32)
    side_row = side.reshape(1)
    x = inputs.reshape(seq, width)

    near = round_qkv(side_row, w_qkv.transpose(0, 2, 1), b_qv, b_in[None, :])
    core = swap(near, "tensor", 0)
    far = swap(near, "tensor", 1)
    core, w_in, w_back, w_out = lax.optimization_barrier((core, w_in, w_back, w_out))
    out_in, back, second, x_low = round_rest(side_row, w_out, w_in, w_back, x)
    out_in_far = swap(out_in, "tensor", 1)

    valid = lax.dynamic_index_in_dim(valid_lengths, index, keepdims=False)
    segments = lax.dynamic_index_in_dim(segment_ids, index, keepdims=False)
    positions = jnp.arange(seq, dtype=jnp.int32)
    code = jnp.where(positions < valid, segments, -1)[:, None]
    seg = segments[None, :]
    table = span_tables(segments, valid, seq)

    qa, ka, va, ctx_a, lse_a = attend_forward(table, x_low, near, core, code, seg)
    out_in, back, second, far, ctx_a = lax.optimization_barrier((out_in, back, second, far, ctx_a))
    core_far = swap(far, "tensor", 0)
    out_in_core = swap(out_in, "tensor", 0)
    back_core = swap(back, "tensor", 0)
    second_core = swap(second, "tensor", 0)
    qb, kb, vb, ctx_b, lse_b = attend_forward(table, x_low, far, core_far, code, seg)
    (
        output,
        dh_one,
        cg_a,
        cg_b,
        _,
        to_x,
        to_y,
        rest,
        out_send_a,
        out_send_b,
        out_keep_a,
        out_keep_b,
        sums,
        bias_sums,
        count,
        *_,
    ) = middle(
        total_slots,
        valid.reshape(1),
        valid_lengths,
        ctx_a,
        ctx_b,
        norm_gains,
        shifts,
        x,
        teacher.reshape(seq, width),
        (near, core, far, core_far),
        (out_in, out_in_core, out_in_far),
        (back, back_core),
        (second, second_core),
    )
    ffn_x = swap(to_x, "dp", 0)
    ffn_y = swap(to_y, "tensor", 1)
    grads_b = attend_backward(table, qb, kb, vb, cg_b, lse_b, code, seg)
    away, away_first, bias_far = far_projections(x_low, grads_b, out_send_b, out_keep_b)
    ffn_x, ffn_y, away_first = lax.optimization_barrier((ffn_x, ffn_y, away_first))
    in_away = (rest[1] + ffn_x[1].astype(F32)).astype(LOW)
    back_away = (rest[3] + ffn_y[1].astype(F32)).astype(LOW)
    in_away, back_away, away_first, cg_a = lax.optimization_barrier(
        (in_away, back_away, away_first, cg_a)
    )
    in_y = swap(in_away, "tensor", 1)
    back_x = swap(back_away, "dp", 0)
    *grads_a, output = attend_backward(table, qa, ka, va, cg_a, lse_a, code, seg, output)
    small = jnp.concatenate([sums, bias_sums, jnp.zeros((4, width), F32)], axis=0)
    grad_inputs, slabs, small = finish(
        x_low,
        (near, core, far, core_far),
        (*grads_a, *grads_b),
        out_send_a,
        out_keep_a,
        dh_one,
        rest,
        ffn_x,
        ffn_y,
        in_y,
        back_x,
        away,
        away_first,
        small,
        bias_far,
    )
    (
        loss,
        grad_w_qkv,
        grad_b_qv,
        grad_w_out,
        grad_w_in,
        grad_b_in,
        grad_w_back,
        grad_gains,
        grad_shifts,
        grad_inputs,
    ) = widen(jnp.stack([side, index]), slabs, small, count, grad_inputs, piece, w_out.shape[0])
    return (
        output.reshape(own_seqs, seq, width),
        loss[0, 0],
        grad_inputs.reshape(own_seqs, seq, width),
        grad_w_qkv.transpose(0, 2, 1),
        grad_b_qv,
        grad_w_out,
        grad_w_in,
        grad_b_in[0],
        grad_w_back,
        grad_gains,
        grad_shifts,
    )


def solution(mesh):
    return jax.shard_map(
        per_device,
        mesh=mesh,
        in_specs=(
            P(("dp", "tensor"), None, None),
            P(None, None, "tensor"),
            P(None, "tensor"),
            P("tensor", None),
            P(None, "tensor"),
            P("tensor"),
            P("tensor", None),
            P(),
            P(),
            P("dp", None),
            P("dp"),
            P(("dp", "tensor"), None, None),
        ),
        out_specs=(
            P(("dp", "tensor"), None, None),
            P(),
            P(("dp", "tensor"), None, None),
            P(None, None, "tensor"),
            P(None, "tensor"),
            P("tensor", None),
            P(None, "tensor"),
            P("tensor"),
            P("tensor", None),
            P(),
            P(),
        ),
        check_vma=False,
    )
```

```python
import functools
import math

import jax
import jax.numpy as jnp
from jax import lax
from jax.experimental import pallas as pl
from jax.experimental.pallas import tpu as pltpu
from jax.sharding import PartitionSpec as P

HD = 64
LN_EPSILON = 1e-05
MASKED_SCORE = -1000000000.0
QB = 256
KB = 128
RB = 256
FR = 256
NT = ((1,), (1,))
TN = ((0,), (0,))
PHI = (
    0.1412427189,
    0.1377927593,
    0.1458432541,
    0.005834031383,
    0.2126657205,
    -0.1910292611,
    0.0476509541,
)
PHI_STEP = 0.35355339059327379

VMEM_LIMIT = 63 << 20
VMEM = pl.BlockSpec(memory_space=pltpu.VMEM)
SMEM = pl.BlockSpec(memory_space=pltpu.SMEM)
HBM = pl.BlockSpec(memory_space=pl.ANY)
LOW = jnp.bfloat16
F32 = jnp.float32


def dot(left, right, dims=((1,), (0,))):
    return lax.dot_general(left, right, (dims, ((), ())), preferred_element_type=jnp.float32)


def shape(dims, dtype):
    return jax.ShapeDtypeStruct(dims, dtype)


def swap(values, axis, bit):
    size = lax.axis_size(axis)
    return lax.ppermute(values, axis, [(i, i ^ (1 << bit)) for i in range(size)])


def bits_of(axis):
    return int(math.log2(lax.axis_size(axis)))


def partner(axis, bit):
    here = {name: lax.axis_index(name) for name in ("dp", "tensor")}
    here[axis] = here[axis] ^ (1 << bit)
    return here["dp"], here["tensor"]


def greet(partners):
    barrier = pltpu.get_barrier_semaphore()
    for device in partners:
        pl.semaphore_signal(
            barrier, inc=1, device_id=device, device_id_type=pl.DeviceIdType.MESH
        )
    pl.semaphore_wait(barrier, len(partners))


def three_parts(values):
    first = values.astype(LOW)
    rest = values - first.astype(F32)
    second = rest.astype(LOW)
    return first, second, (rest - second.astype(F32)).astype(LOW)


def round_qkv_kernel(side_ref, w_ref, bqv_ref, bin_ref, out_ref):
    piece = w_ref.shape[1]
    width = w_ref.shape[2]
    half = bin_ref.shape[0] // 2
    for i in range(3):
        out_ref[i * piece : (i + 1) * piece, :] = w_ref[i].astype(LOW)
    row = bin_ref[...].reshape(1, 2 * half)
    mine = jnp.where(side_ref[0] == 0, row[:, :half], row[:, half:])
    other = jnp.where(side_ref[0] == 0, row[:, half:], row[:, :half])
    pad = jnp.zeros((1, width - piece), F32)
    rows = [jnp.concatenate([mine, other], axis=1)]
    rows += [jnp.concatenate([bqv_ref[i : i + 1, :], pad], axis=1) for i in range(2)]
    parts = [part.astype(F32) for row in rows for part in three_parts(row)]
    parts += [jnp.zeros((1, width), F32)] * 7
    out_ref[3 * piece :, :] = jnp.concatenate(parts, axis=0).astype(LOW)


def round_qkv(side, w_qkv, b_qv, b_in):
    _, piece, width = w_qkv.shape
    return pl.pallas_call(
        round_qkv_kernel,
        out_shape=shape((3 * piece + 16, width), LOW),
        in_specs=[SMEM, VMEM, VMEM, VMEM],
        out_specs=VMEM,
        compiler_params=pltpu.CompilerParams(vmem_limit_bytes=VMEM_LIMIT),
        name="round_qkv",
    )(side, w_qkv, b_qv, b_in)


def round_rest_kernel(
    side_ref, wo_hbm, wi_hbm, wb_hbm, x_hbm, out_in, back, second, x_low, *scratch
):
    wo_in, wi_in, wb_in, x_in, oi_out, b_out, s_out, x_out, in_sem, out_sem = scratch
    rows, width = wo_in.shape
    half = width // 2
    loads, stores = [], []

    def load(source, target):
        loads.append(pltpu.make_async_copy(source, target, in_sem.at[len(loads)]))
        loads[-1].start()

    def store(source, target):
        stores.append(pltpu.make_async_copy(source, target, out_sem.at[len(stores)]))
        stores[-1].start()

    load(wo_hbm, wo_in)
    load(wi_hbm, wi_in)
    for side in (side_ref[0], 1 - side_ref[0]):
        at = pl.ds(pl.multiple_of(side * half, half), half)
        load(wb_hbm.at[at, :], wb_in.at[at, :])
    quarters = [pl.ds(i * x_in.shape[0] // 4, x_in.shape[0] // 4) for i in range(4)]
    for at in quarters:
        load(x_hbm.at[at, :], x_in.at[at, :])
    loads[0].wait()
    for c in range(2):
        oi_out[c * rows : (c + 1) * rows, :] = wo_in[:, c * half : (c + 1) * half].astype(LOW)
    loads[1].wait()
    sides = [
        pl.ds(pl.multiple_of(side * half, half), half) for side in (side_ref[0], 1 - side_ref[0])
    ]
    oi_out[2 * rows :, :] = wi_in[:, sides[0]].astype(LOW)
    store(oi_out, out_in)
    s_out[:width, :] = wi_in[:, sides[1]].astype(LOW)
    for n, (to_back, base) in enumerate(((b_out, 0), (s_out, width))):
        loads[2 + n].wait()
        for c in range(2):
            start = base + c * half
            strip = wb_in[sides[n], c * half : (c + 1) * half]
            to_back[start : start + half, :] = strip.astype(LOW)
        store(to_back, (back, second)[n])
    for n, at in enumerate(quarters):
        loads[4 + n].wait()
        x_out[at, :] = x_in[at, :].astype(LOW)
        store(x_out.at[at, :], x_low.at[at, :])
    for copy in stores:
        copy.wait()


def round_rest(side, w_out, w_in, w_back, x):
    rows, width = w_out.shape
    half = width // 2
    shapes = ((2 * rows + width, half), (width, half), (2 * width, half), x.shape)
    return pl.pallas_call(
        round_rest_kernel,
        out_shape=tuple(shape(dims, LOW) for dims in shapes),
        in_specs=[SMEM] + [HBM] * 4,
        out_specs=(HBM,) * 4,
        scratch_shapes=[pltpu.VMEM(a.shape, F32) for a in (w_out, w_in, w_back, x)]
        + [pltpu.VMEM(dims, LOW) for dims in shapes]
        + [pltpu.SemaphoreType.DMA((8,)), pltpu.SemaphoreType.DMA((7,))],
        compiler_params=pltpu.CompilerParams(vmem_limit_bytes=VMEM_LIMIT),
        name="round_rest",
    )(side, w_out, w_in, w_back, x)


def span_tables(segments, valid, seq):
    blocks = seq // QB
    firsts, lasts = segments[::QB], segments[QB - 1 :: QB]
    low = jnp.sum((segments[None, :] < firsts[:, None]).astype(jnp.int32), axis=1)
    high = jnp.sum((segments[None, :] <= lasts[:, None]).astype(jnp.int32), axis=1)
    own_end = (jnp.arange(blocks, dtype=jnp.int32) + 1) * QB
    high = jnp.maximum(jnp.minimum(high, valid), own_end)
    low_block = low // KB
    high_block = (high + KB - 1) // KB
    return jnp.stack([low_block, high_block - low_block]).astype(jnp.int32)


def make_bias(bias_ref, block, low, count, code_ref, seg_ref):
    dims = (count * KB, QB)
    codes = code_ref[pl.ds(pl.multiple_of(low * KB, KB), count * KB), :]
    segs = seg_ref[:, pl.ds(pl.multiple_of(block * QB, QB), QB)]
    key_at = low * KB + lax.broadcasted_iota(jnp.int32, dims, 0)
    query_at = block * QB + lax.broadcasted_iota(jnp.int32, dims, 1)
    allowed = (codes == segs) | (key_at == query_at)
    bias_ref[: count * KB, :] = jnp.where(allowed, 0.0, MASKED_SCORE)


def one_head(values, head):
    lane = lax.broadcasted_iota(jnp.int32, values.shape, 1)
    keep = (lane < HD) if head == 0 else (lane >= HD)
    return jnp.where(keep, values, jnp.zeros_like(values))


def forward_kernel(
    table_ref,
    x_ref,
    w0_ref,
    w1_ref,
    code_ref,
    seg_ref,
    q_ref,
    k_ref,
    v_ref,
    ctx_ref,
    lse_ref,
    weights,
    biases,
    vt_ref,
    bias_ref,
):
    block = pl.program_id(0)
    low, total = table_ref[0, block], table_ref[1, block]
    piece = (w0_ref.shape[0] - 16) // 3
    pairs = 2 * piece // 128

    @pl.when(block == 0)
    def _():
        for i in range(3):
            for n, ref in enumerate((w0_ref, w1_ref)):
                rows = ref[i * piece : (i + 1) * piece, :]
                weights[i, n * piece : (n + 1) * piece, :] = rows
        lane = lax.broadcasted_iota(jnp.int32, (1, x_ref.shape[1]), 1)
        for i in (0, 2):
            base = 3 * piece + (3 if i == 0 else 6)
            both = [
                sum(ref[base + part : base + part + 1, :].astype(F32) for part in range(3))
                for ref in (w0_ref, w1_ref)
            ]
            row = jnp.where(lane < piece, both[0], pltpu.roll(both[1], piece, 1))
            biases[i : i + 1, :] = row[:, : 2 * piece]
        biases[1:2, :] = jnp.zeros((1, 2 * piece), F32)

        def project(b, carry):
            at = pl.ds(pl.multiple_of(b * QB, QB), QB)
            for i, ref in enumerate((q_ref, k_ref, v_ref)):
                ref[at, :] = (dot(x_ref[at, :], weights[i], NT) + biases[i : i + 1, :]).astype(LOW)
            vt_ref[:, at] = v_ref[at, :].T
            return carry

        lax.fori_loop(0, x_ref.shape[0] // QB, project, 0)

    def run(count):
        make_bias(bias_ref, block, low, count, code_ref, seg_ref)
        bias = bias_ref[: count * KB, :]
        rows = pl.ds(pl.multiple_of(low * KB, KB), count * KB)
        queries = pl.ds(pl.multiple_of(block * QB, QB), QB)

        def scores(head):
            lanes = slice(head // 2 * 128, head // 2 * 128 + 128)
            query = q_ref[queries, lanes] * jnp.asarray(0.125, LOW)
            return dot(k_ref[rows, lanes], one_head(query, head % 2), NT) + bias

        def soft(values, head):
            peak = jnp.max(values, axis=0, keepdims=True)
            powers = jnp.exp(values - peak)
            mass = jnp.sum(powers, axis=0, keepdims=True)
            lse_ref[head : head + 1, :] = peak + jnp.log(mass)
            return (powers * (1.0 / mass)).astype(LOW)

        outs = []

        def context(probs, head):
            outs.append(dot(vt_ref[head * HD : (head + 1) * HD, rows], probs))
            if head % 2 == 1:
                both = jnp.concatenate(outs[-2:], axis=0).T
                ctx_ref[:, head // 2 * 128 : head // 2 * 128 + 128] = both.astype(LOW)

        values, probs = scores(0), None
        for head in range(2 * pairs):
            later = scores(head + 1) if head + 1 < 2 * pairs else None
            now = soft(values, head)
            if head > 0:
                context(probs, head - 1)
            values, probs = later, now
        context(probs, 2 * pairs - 1)

    for count in range(2, k_ref.shape[0] // KB + 1):
        pl.when(total == count)(functools.partial(run, count))


def backward_kernel(carried, table_ref, q_ref, k_ref, v_ref, g_ref, lse_ref, code_ref, seg_ref, *refs):
    block = pl.program_id(0)
    refs = list(refs)
    if carried:
        source, target = refs.pop(0), refs.pop(3)
        target[...] = source[...]
    dq_ref, dk_ref, dv_ref, kt_ref, bias_ref, dk_sum, dv_sum = refs
    low, total = table_ref[0, block], table_ref[1, block]
    heads = q_ref.shape[1] // HD

    @pl.when(block == 0)
    def _():
        kt_ref[...] = k_ref[...].T
        dk_sum[...] = jnp.zeros_like(dk_sum)
        dv_sum[...] = jnp.zeros_like(dv_sum)

    def run(count):
        make_bias(bias_ref, block, low, count, code_ref, seg_ref)
        bias = bias_ref[: count * KB, :]
        rows = pl.ds(pl.multiple_of(low * KB, KB), count * KB)

        def first(head):
            lanes = slice(head // 2 * 128, head // 2 * 128 + 128)
            query = one_head(q_ref[:, lanes] * jnp.asarray(0.125, LOW), head % 2)
            grad = one_head(g_ref[:, lanes], head % 2)
            scores = dot(k_ref[rows, lanes], query, NT) + bias
            return scores, dot(v_ref[rows, lanes], grad, NT), query, grad

        def second(head, scores, prob_grad, query, grad):
            probs = jnp.exp(scores - lse_ref[head : head + 1, :])
            delta = jnp.sum(probs * prob_grad, axis=0, keepdims=True)
            return probs.astype(LOW), (probs * (prob_grad - delta)).astype(LOW), query, grad

        outs = []

        def third(head, probs, score_grad, query, grad):
            lanes = slice(head // 2 * 128, head // 2 * 128 + 128)
            dv_sum[rows, lanes] += dot(probs, grad)
            dk_sum[rows, lanes] += dot(score_grad, query)
            outs.append(dot(kt_ref[head * HD : (head + 1) * HD, rows], score_grad))
            if head % 2 == 1:
                both = jnp.concatenate(outs[-2:], axis=0).T * 0.125
                dq_ref[:, lanes] = both.astype(LOW)

        start, middle_of = first(0), None
        for head in range(heads):
            later = first(head + 1) if head + 1 < heads else None
            now = second(head, *start)
            if head > 0:
                third(head - 1, *middle_of)
            start, middle_of = later, now
        third(heads - 1, *middle_of)

    for count in range(2, k_ref.shape[0] // KB + 1):
        pl.when(total == count)(functools.partial(run, count))

    @pl.when(block == pl.num_programs(0) - 1)
    def _():
        dk_ref[...] = dk_sum[...].astype(LOW)
        dv_ref[...] = dv_sum[...].astype(LOW)


def attend_forward(table, x, first, second, code, seg):
    seq, width = x.shape
    piece = (first.shape[0] - 16) // 3
    heads, blocks = 2 * piece // HD, seq // QB
    whole = lambda i, t: (0, 0)
    column = pl.BlockSpec((seq, 2 * piece), whole)
    return pl.pallas_call(
        forward_kernel,
        out_shape=(shape((seq, 2 * piece), LOW),) * 4 + (shape((8, seq), F32),),
        grid_spec=pltpu.PrefetchScalarGridSpec(
            num_scalar_prefetch=1,
            grid=(blocks,),
            in_specs=[
                pl.BlockSpec((seq, width), whole),
                pl.BlockSpec(first.shape, whole),
                pl.BlockSpec(second.shape, whole),
                pl.BlockSpec((seq, 1), whole),
                pl.BlockSpec((1, seq), whole),
            ],
            out_specs=[
                column,
                column,
                column,
                pl.BlockSpec((QB, 2 * piece), lambda i, t: (i, 0)),
                pl.BlockSpec((8, QB), lambda i, t: (0, i)),
            ],
            scratch_shapes=[
                pltpu.VMEM((3, 2 * piece, width), LOW),
                pltpu.VMEM((3, 2 * piece), F32),
                pltpu.VMEM((2 * piece, seq), LOW),
                pltpu.VMEM((seq, QB), F32),
            ],
        ),
        compiler_params=pltpu.CompilerParams(vmem_limit_bytes=VMEM_LIMIT),
        cost_estimate=pl.CostEstimate(
            flops=16 * seq * seq * piece + 12 * seq * width * piece,
            bytes_accessed=16 * seq * piece,
            transcendentals=seq * seq * heads // 2,
        ),
        name="attend_forward",
    )(table, x, first, second, code, seg)


def attend_backward(table, q, k, v, grad, lse, code, seg, *carried):
    seq, width = grad.shape
    blocks = seq // QB
    block = pl.BlockSpec((QB, width), lambda i, t: (i, 0))
    column = pl.BlockSpec((seq, width), lambda i, t: (0, 0))
    return pl.pallas_call(
        functools.partial(backward_kernel, len(carried)),
        out_shape=(shape((seq, width), LOW),) * 3 + tuple(shape(c.shape, c.dtype) for c in carried),
        grid_spec=pltpu.PrefetchScalarGridSpec(
            num_scalar_prefetch=1,
            grid=(blocks,),
            in_specs=[
                block,
                column,
                column,
                block,
                pl.BlockSpec((8, QB), lambda i, t: (0, i)),
                pl.BlockSpec((seq, 1), lambda i, t: (0, 0)),
                pl.BlockSpec((1, seq), lambda i, t: (0, 0)),
            ]
            + [pl.BlockSpec((QB, c.shape[1]), lambda i, t: (i, 0)) for c in carried],
            out_specs=[block, column, column]
            + [pl.BlockSpec((QB, c.shape[1]), lambda i, t: (i, 0)) for c in carried],
            scratch_shapes=[
                pltpu.VMEM((width, seq), LOW),
                pltpu.VMEM((seq, QB), F32),
                pltpu.VMEM((seq, width), F32),
                pltpu.VMEM((seq, width), F32),
            ],
        ),
        compiler_params=pltpu.CompilerParams(vmem_limit_bytes=VMEM_LIMIT),
        cost_estimate=pl.CostEstimate(
            flops=16 * seq * seq * width,
            bytes_accessed=16 * seq * width,
            transcendentals=seq * seq * width // 128,
        ),
        name="attend_backward",
    )(table, q, k, v, grad, lse, code, seg, *carried)


def gelu_parts(pre):
    size = 1.0 + PHI_STEP * jnp.abs(pre)
    t = pl.reciprocal(size, approx=True)
    t = t * (2.0 - size * t)
    poly = PHI[6] * t + PHI[5]
    for factor in PHI[4::-1]:
        poly = poly * t + factor
    bell = jnp.exp2((-0.5 * math.log2(math.e)) * (pre * pre))
    tail = poly * t * bell
    cdf = jnp.where(pre < 0, tail, 1.0 - tail)
    return pre * cdf, cdf + (pre * 0.3989422804014327) * bell


def norm_stats(values):
    width = values.shape[-1]
    mean = jnp.sum(values, axis=-1, keepdims=True) * (1.0 / width)
    centred = values - mean
    spread = jnp.sum(centred * centred, axis=-1, keepdims=True) * (1.0 / width)
    rate = lax.rsqrt(spread + LN_EPSILON)
    return centred * rate, rate


def norm_back(grad, gain, xhat, rate):
    width = grad.shape[-1]
    scaled = grad * gain
    mean = jnp.sum(scaled, axis=-1, keepdims=True) * (1.0 / width)
    along = jnp.sum(scaled * xhat, axis=-1, keepdims=True) * (1.0 / width)
    return rate * (scaled - mean - xhat * along)


def column_sum(values):
    return jnp.sum(values, axis=0, keepdims=True)


def middle_kernel(
    total_slots,
    dp_bits,
    valid_ref,
    lengths_ref,
    ctx_a,
    ctx_b,
    gains,
    shifts,
    x_hbm,
    teacher_hbm,
    qa,
    qb,
    qc,
    qd,
    outin_own,
    outin_core,
    outin_far,
    back_own,
    back_core,
    second_own,
    second_core,
    out_hbm,
    dh_hbm,
    cg_a,
    cg_b,
    core_hbm,
    to_x,
    to_y,
    rest,
    out_send_a,
    out_send_b,
    out_keep_a,
    out_keep_b,
    sums,
    bias_sums,
    count_ref,
    outin_far_core,
    in_far,
    back_far,
    in_far_core,
    back_far_core,
    w_in,
    w_back,
    w_out,
    bias_parts,
    bias_in,
    xhat_one,
    rate_one,
    mid_low,
    hidden,
    slope,
    acc,
    dh_low,
    pre_grad,
    rows_in,
    rows_out,
    stage16,
    stage32,
    from_core,
    held,
    w_sem,
    in_sem,
    out_sem,
    load_sem,
    store_sem,
    send_sem,
    recv_sem,
    count_send,
    count_recv,
    far_send,
    far_recv,
):
    seq, width = acc.shape
    blocks = seq // RB
    half = width // 2
    out_rows = w_out.shape[0] // 4
    units = w_in.shape[2]
    side = units // 2
    core_at, y_at, x_at = partner("tensor", 0), partner("tensor", 1), partner("dp", 0)
    greet([core_at, y_at] + [partner("dp", bit) for bit in range(dp_bits)])

    def far_copy(n, source, target, device):
        return pltpu.make_async_remote_copy(
            src_ref=source,
            dst_ref=target,
            send_sem=far_send.at[n],
            recv_sem=far_recv.at[n],
            device_id=device,
            device_id_type=pl.DeviceIdType.MESH,
        )

    in_at = pl.ds(2 * out_rows, width)
    far = [
        far_copy(
            0,
            outin_far.at[pl.ds(0, 2 * out_rows), :],
            outin_far_core.at[pl.ds(0, 2 * out_rows), :],
            core_at,
        ),
        far_copy(1, back_own, back_far.at[0], y_at),
        far_copy(
            2,
            second_own.at[pl.ds(width, side), :],
            back_far.at[1, pl.ds(0, side), :],
            y_at,
        ),
        far_copy(3, outin_far.at[in_at, :], in_far, x_at),
        far_copy(4, in_far, in_far_core, core_at),
        far_copy(5, back_far.at[0], back_far_core.at[0], core_at),
        far_copy(6, back_far.at[1], back_far_core.at[1], core_at),
        far_copy(
            7,
            back_far.at[0, pl.ds(side, side), :],
            back_far.at[1, pl.ds(side, side), :],
            x_at,
        ),
        far_copy(8, outin_far.at[in_at, :], outin_far_core.at[in_at, :], core_at),
    ]
    for copy in far[:4] + far[8:]:
        copy.start()
    out_in = (outin_own, outin_core, outin_far, outin_far_core)
    in_parts = tuple(ref.at[in_at, :] for ref in out_in)
    in_other = (
        second_own.at[pl.ds(0, width), :],
        second_core.at[pl.ds(0, width), :],
        in_far,
        in_far_core,
    )
    back_parts = (back_own, back_core, back_far.at[0], back_far_core.at[0])
    back_other = (
        second_own.at[pl.ds(width, width), :],
        second_core.at[pl.ds(width, width), :],
        back_far.at[1],
        back_far_core.at[1],
    )

    def rows(i):
        return pl.ds(i * RB, RB)

    def fetch(source, i, slot):
        return pltpu.make_async_copy(source.at[rows(i), :], rows_in.at[slot], in_sem.at[slot])

    def out_weights(p, c):
        return pltpu.make_async_copy(
            out_in[p].at[pl.ds(c * out_rows, out_rows), :],
            w_out.at[pl.ds(p * out_rows, out_rows), pl.ds(c * half, half)],
            w_sem.at[p, c],
        )

    def bias_rows(p):
        source = (qa, qb, qc, qd)[p]
        return pltpu.make_async_copy(
            source.at[pl.ds(source.shape[0] - 16, 16), :], bias_parts.at[p], w_sem.at[p, 8]
        )

    def load_in(source, p, r):
        return pltpu.make_async_copy(
            source, w_in.at[p, :, pl.ds(r * side, side)], w_sem.at[p, 2 + 3 * r]
        )

    def load_back(source, p, r, c):
        return pltpu.make_async_copy(
            source.at[pl.ds(c * side, side), :],
            w_back.at[p, pl.ds(r * side, side), pl.ds(c * half, half)],
            w_sem.at[p, 3 + 3 * r + c],
        )

    def ffn_weights(p):
        load_in(in_parts[p], p, 0).start()
        load_in(in_other[p], p, 1).start()
        for c in range(2):
            load_back(back_parts[p], p, 0, c).start()
            load_back(back_other[p], p, 1, c).start()

    early = [out_weights(p, c) for p in range(4) for c in range(2)]
    for copy in early[:6]:
        copy.start()
    fetch(x_hbm, 0, 0).start()
    for p in range(4):
        bias_rows(p).start()
    for p in range(2):
        ffn_weights(p)

    def count_step(bit):
        return pltpu.make_async_remote_copy(
            src_ref=held.at[2 * bit],
            dst_ref=held.at[2 * bit + 1],
            send_sem=count_send.at[bit],
            recv_sem=count_recv.at[bit],
            device_id=partner("dp", bit),
            device_id_type=pl.DeviceIdType.MESH,
        )

    tokens = jnp.full(held.shape[1:], 0, jnp.int32)
    for i in range(lengths_ref.shape[0]):
        tokens += lengths_ref[i]
    held[0] = tokens
    count_step(0).start()

    def count_on(bit):
        count_step(bit).wait()
        held[2 * bit + 2] = held[2 * bit] + held[2 * bit + 1]
        if bit + 1 < dp_bits:
            count_step(bit + 1).start()

    far[0].wait_recv()
    for copy in early[6:]:
        copy.start()
    for copy in early:
        copy.wait()

    for i in range(blocks):
        if i + 1 < blocks:
            fetch(x_hbm, i + 1, (i + 1) % 2).start()
        fetch(x_hbm, i, i % 2).wait()
        context = jnp.concatenate([ctx_a[rows(i), :], ctx_b[rows(i), :]], axis=1)
        xhat, rate = norm_stats(dot(context, w_out[...]) + shifts[0:1, :] + rows_in[i % 2])
        xhat_one[rows(i), :] = xhat
        rate_one[rows(i), :] = rate
        mid_low[rows(i), :] = (xhat * gains[0:1, :] + shifts[1:2, :]).astype(LOW)
        acc[rows(i), :] = jnp.zeros((RB, width), F32)
    fetch(teacher_hbm, 0, 0).start()
    for p in range(4):
        bias_rows(p).wait()
        part = bias_parts[p, 0:3, :].astype(F32)
        bias_in[p] = part[0:1] + part[1:2] + part[2:3]

    def up(p, carry):
        for bit in range(min(dp_bits, 4)):
            pl.when(p == bit)(functools.partial(count_on, bit))

        @pl.when(p == 1)
        def _():
            far[1].wait_recv()
            far[7].start()
            far[5].start()
            far[3].wait_recv()
            far[4].start()

        @pl.when(p == 2)
        def _():
            far[2].wait_recv()
            far[7].wait_recv()
            far[6].start()
            ffn_weights(2)

        @pl.when(p == 3)
        def _():
            for n in (8, 4, 5, 6):
                far[n].wait_recv()
            ffn_weights(3)

        for r in range(2):
            load_in(in_other[0], p, r).wait()
            for c in range(2):
                load_back(back_own, p, r, c).wait()
        last = seq // FR - 1
        strips = [slice(c, c + 256) for c in range(0, units, 256)]

        def lift(k, cols):
            pre = dot(mid_low[pl.ds(k * FR, FR), :], w_in[p, :, cols])
            return pre + bias_in[p, :, cols]

        def lower(k, cols):
            at = pl.ds(k * FR, FR)
            acc[at, cols] += dot(hidden[p, at, :], w_back[p, :, cols])

        pre = [lift(0, cols) for cols in strips]
        for k in range(last + 1):
            later = []
            for c, cols in enumerate(strips):
                if k < last:
                    later.append(lift(k + 1, cols))
                act, der = gelu_parts(pre[c])
                hidden[p, pl.ds(k * FR, FR), cols] = act.astype(LOW)
                slope[p, pl.ds(k * FR, FR), cols] = der
                if k > 0:
                    lower(k - 1, cols)
            pre = later
        for cols in strips:
            lower(last, cols)
        return carry

    lax.fori_loop(0, 4, up, 0)
    for bit in range(4, dp_bits):
        count_on(bit)
    count_ref[...] = held[2 * dp_bits]

    zero = jnp.zeros((1, width), F32)
    squares, gain_two, shift_two, shift_mid = zero, zero, zero, zero
    scale = total_slots / held[2 * dp_bits, 0:1, 0:1].astype(F32)
    stores = []
    for i in range(blocks):
        if i + 1 < blocks:
            fetch(teacher_hbm, i + 1, (i + 1) % 2).start()
        fetch(teacher_hbm, i, i % 2).wait()
        mid = xhat_one[rows(i), :] * gains[0:1, :] + shifts[1:2, :]
        xhat, rate = norm_stats(acc[rows(i), :] + shifts[2:3, :] + mid)
        output = xhat * gains[1:2, :] + shifts[3:4, :]
        if i >= 2:
            stores[i - 2].wait()
        rows_out[i % 2] = output
        stores.append(
            pltpu.make_async_copy(rows_out.at[i % 2], out_hbm.at[rows(i), :], out_sem.at[i % 2])
        )
        stores[i].start()
        live = (i * RB + lax.broadcasted_iota(jnp.int32, (RB, 1), 0)) < valid_ref[0]
        distance = jnp.where(live, output - rows_in[i % 2], 0.0)
        squares += column_sum(distance * distance)
        out_grad = scale * distance
        gain_two += column_sum(out_grad * xhat)
        shift_two += column_sum(out_grad)
        dh_two = norm_back(out_grad, gains[1:2, :], xhat, rate)
        shift_mid += column_sum(dh_two)
        acc[rows(i), :] = dh_two
        dh_low[rows(i), :] = dh_two.astype(LOW)
    for store in stores[-2:]:
        store.wait()

    sides = (pl.ds(0, side), pl.ds(side, side))

    def ffn_back(p):
        total = jnp.zeros((1, units), F32)

        def lift(k):
            return dot(dh_low[pl.ds(k * FR, FR), :], w_back[p], NT)

        def lower(k):
            at = pl.ds(k * FR, FR)
            acc[at, :] += dot(pre_grad[at, :], w_in[p], NT)

        raised = lift(0)
        for k in range(seq // FR):
            later = lift(k + 1) if k + 1 < seq // FR else None
            at = pl.ds(k * FR, FR)
            grad = (raised * slope[p, at, :]).astype(LOW)
            pre_grad[at, :] = grad
            total += column_sum(grad.astype(F32))
            if k > 0:
                lower(k - 1)
            raised = later
        lower(seq // FR - 1)
        bias_sums[pl.ds(p, 1), :] = total

    def to_core(pair, w):
        return pltpu.make_async_remote_copy(
            src_ref=stage16.at[w],
            dst_ref=core_hbm.at[pair, w],
            send_sem=send_sem.at[w],
            recv_sem=recv_sem.at[pair, w],
            device_id=core_at,
            device_id_type=pl.DeviceIdType.MESH,
        )

    def away(n, carry):
        p = 2 * n + 1
        ffn_back(p)

        @pl.when(n > 0)
        def _():
            for w in range(2):
                to_core(0, w).wait_send()

        stage16[0] = dot(mid_low[...], pre_grad[...], TN).astype(LOW)
        stage16[1] = dot(hidden[p], dh_low[...], TN).astype(LOW)
        for w in range(2):
            to_core(n, w).start()
        return carry

    lax.fori_loop(0, 2, away, 0)

    def in_moves(pair):
        return [
            pltpu.make_async_copy(stage32.at[0, :, sides[0]], rest.at[pair], store_sem.at[0]),
            pltpu.make_async_copy(stage16.at[0, :, sides[1]], to_x.at[pair], store_sem.at[1]),
        ]

    def back_moves(stage, target):
        return [
            pltpu.make_async_copy(
                stage.at[1, sides[r], sides[c]],
                target.at[r, sides[c], :],
                store_sem.at[2 + 2 * r + c],
            )
            for r in range(2)
            for c in range(2)
        ]

    moves = {1: in_moves(1) + back_moves(stage16, to_y), 0: in_moves(0) + back_moves(stage32, rest.at[pl.ds(2, 2)])}

    def home(n, carry):
        pair = n
        p = 2 * pair
        ffn_back(p)
        for w in range(2):
            to_core(pair, w).wait_recv()
            pltpu.make_async_copy(core_hbm.at[pair, w], from_core.at[w], load_sem.at[w]).start()

        @pl.when(n == 0)
        def _():
            for w in range(2):
                to_core(1, w).wait_send()

        @pl.when(n == 1)
        def _():
            for copy in moves[0]:
                copy.wait()

        stage32[0] = dot(mid_low[...], pre_grad[...], TN)
        stage32[1] = dot(hidden[p], dh_low[...], TN)
        for w in range(2):
            pltpu.make_async_copy(core_hbm.at[pair, w], from_core.at[w], load_sem.at[w]).wait()
            for k in range(0, width, 128):
                total = stage32[w, k : k + 128, :] + from_core[w, k : k + 128, :].astype(F32)
                stage32[w, k : k + 128, :] = total
                stage16[w, k : k + 128, :] = total.astype(LOW)

        for turn in range(2):

            @pl.when(n == turn)
            def _(turn=turn):
                for copy in moves[turn]:
                    copy.start()

        return carry

    lax.fori_loop(0, 2, home, 0)

    gain_one, shift_one, shift_out = zero, zero, zero
    stores = []
    for i in range(blocks):
        grad, xhat = acc[rows(i), :], xhat_one[rows(i), :]
        gain_one += column_sum(grad * xhat)
        shift_one += column_sum(grad)
        dh_one = norm_back(grad, gains[0:1, :], xhat, rate_one[rows(i), :])
        shift_out += column_sum(dh_one)
        if i >= 2:
            stores[i - 2].wait()
        rows_out[i % 2] = dh_one
        stores.append(
            pltpu.make_async_copy(rows_out.at[i % 2], dh_hbm.at[rows(i), :], out_sem.at[i % 2])
        )
        stores[i].start()
        dh_one = dh_one.astype(LOW)
        dh_low[rows(i), :] = dh_one
        grad = dot(dh_one, w_out[...], NT).astype(LOW)
        cg_a[rows(i), :] = grad[:, :half]
        cg_b[rows(i), :] = grad[:, half:]
    for context, out_keep, out_send in (
        (ctx_a, out_keep_a, out_send_a),
        (ctx_b, out_keep_b, out_send_b),
    ):
        grad = dot(context[...], dh_low[...], TN)
        out_keep[...] = grad[:out_rows]
        out_send[...] = grad[out_rows:].astype(LOW)
    sums[...] = jnp.concatenate(
        [gain_one, gain_two, shift_out, shift_one, shift_mid, shift_two, squares, zero], axis=0
    )
    for store in stores[-2:]:
        store.wait()
    for copy in moves[1]:
        copy.wait()
    for copy in far:
        copy.wait_send()


def middle(
    total_slots, valid, lengths, ctx_a, ctx_b, gains, shifts, x, teacher, near, out_in, back, second
):
    seq, width = x.shape
    half = width // 2
    out_rows = ctx_a.shape[1] // 2
    units = width
    dp_bits = bits_of("dp")
    slab = (width, units // 2)
    return pl.pallas_call(
        functools.partial(middle_kernel, float(total_slots), dp_bits),
        out_shape=(
            shape((seq, width), F32),
            shape((seq, width), F32),
            shape((seq, half), LOW),
            shape((seq, half), LOW),
            shape((2, 2, width, units), LOW),
            shape((2,) + slab, LOW),
            shape((2,) + slab, LOW),
            shape((4,) + slab, F32),
            shape((out_rows, width), LOW),
            shape((out_rows, width), LOW),
            shape((out_rows, width), F32),
            shape((out_rows, width), F32),
            shape((8, width), F32),
            shape((4, units), F32),
            shape((8, 128), jnp.int32),
            shape(out_in[0].shape, LOW),
            shape(slab, LOW),
            shape((2,) + slab, LOW),
            shape(slab, LOW),
            shape((2,) + slab, LOW),
        ),
        in_specs=[SMEM, SMEM, VMEM, VMEM, VMEM, VMEM, HBM, HBM] + [HBM] * 11,
        out_specs=(HBM, HBM, VMEM, VMEM, HBM, HBM, HBM, HBM) + (VMEM,) * 7 + (HBM,) * 5,
        scratch_shapes=[
            pltpu.VMEM((4, width, units), LOW),
            pltpu.VMEM((4, units, width), LOW),
            pltpu.VMEM((4 * out_rows, width), LOW),
            pltpu.VMEM((4, 16, width), LOW),
            pltpu.VMEM((4, 1, units), F32),
            pltpu.VMEM((seq, width), F32),
            pltpu.VMEM((seq, 1), F32),
            pltpu.VMEM((seq, width), LOW),
            pltpu.VMEM((4, seq, units), LOW),
            pltpu.VMEM((4, seq, units), F32),
            pltpu.VMEM((seq, width), F32),
            pltpu.VMEM((seq, width), LOW),
            pltpu.VMEM((seq, units), LOW),
            pltpu.VMEM((2, RB, width), F32),
            pltpu.VMEM((2, RB, width), F32),
            pltpu.VMEM((2, width, units), LOW),
            pltpu.VMEM((2, width, units), F32),
            pltpu.VMEM((2, width, units), LOW),
            pltpu.VMEM((2 * dp_bits + 1, 8, 128), jnp.int32),
            pltpu.SemaphoreType.DMA((4, 9)),
            pltpu.SemaphoreType.DMA((2,)),
            pltpu.SemaphoreType.DMA((2,)),
            pltpu.SemaphoreType.DMA((2,)),
            pltpu.SemaphoreType.DMA((6,)),
            pltpu.SemaphoreType.DMA((2,)),
            pltpu.SemaphoreType.DMA((2, 2)),
            pltpu.SemaphoreType.DMA((dp_bits,)),
            pltpu.SemaphoreType.DMA((dp_bits,)),
            pltpu.SemaphoreType.DMA((9,)),
            pltpu.SemaphoreType.DMA((9,)),
        ],
        compiler_params=pltpu.CompilerParams(
            vmem_limit_bytes=VMEM_LIMIT, collective_id=1, has_side_effects=True
        ),
        cost_estimate=pl.CostEstimate(
            flops=6 * seq * width * (8 * units + width),
            bytes_accessed=30 << 20,
            transcendentals=2 * seq * 4 * units,
        ),
        name="middle",
    )(valid, lengths, ctx_a, ctx_b, gains, shifts, x, teacher, *near, *out_in, *back, *second)


def add_rows(out, terms, chunk=96):
    rows = out.shape[0]
    chunk = min(chunk, rows)

    def step(i, carry):
        at = pl.ds(pl.multiple_of(i * chunk, chunk), chunk)
        total = terms[0][at, :].astype(F32)
        for term in terms[1:]:
            total += term[at, :].astype(F32)
        out[at, :] = total.astype(out.dtype)
        return carry

    lax.fori_loop(0, rows // chunk, step, 0)


def cross_rows(x_ref, grads, okeep, osend, side, cross, keep, send, bias_ref, emit):
    half = x_ref.shape[1] // 2
    piece = grads[0].shape[1] // 2
    mine = pl.ds(pl.multiple_of(side * half, half), half)
    other = pl.ds(pl.multiple_of((1 - side) * half, half), half)
    sides = ((1, other), (0, mine))
    at = pl.ds(3 * piece, osend.shape[0])
    for n, lanes in sides:
        keep[n, at, :] = okeep[:, lanes]
        send[n, at, :] = osend[:, lanes].astype(send.dtype)
        emit(n, at)
    for i in range(3):
        cross[...] = dot(grads[i][...], x_ref[...], TN)
        at = pl.ds(i * piece, piece)
        for n, lanes in sides:
            keep[n, at, :] = cross[:piece, lanes]
            send[n, at, :] = cross[piece:, lanes].astype(send.dtype)
            emit(n, at)
        bias_ref[i : i + 1, :] = column_sum(grads[i][...].astype(F32))


def far_kernel(
    x_ref,
    dq,
    dk,
    dv,
    osend,
    okeep,
    away,
    away_first,
    bias_ref,
    keep,
    send,
    core,
    cross,
    send_sem,
    recv_sem,
):
    core_at = partner("tensor", 0)
    greet([core_at])
    bias_ref[...] = jnp.zeros(bias_ref.shape, F32)
    copies = []

    def emit(n, rows):
        at = len(copies)
        copies.append(
            pltpu.make_async_remote_copy(
                src_ref=send.at[n, rows, :],
                dst_ref=core.at[n, rows, :],
                send_sem=send_sem.at[at],
                recv_sem=recv_sem.at[at],
                device_id=core_at,
                device_id_type=pl.DeviceIdType.MESH,
            )
        )
        copies[at].start()

    side = lax.axis_index("dp") & 1
    cross_rows(x_ref, (dq, dk, dv), okeep, osend, side, cross, keep, send, bias_ref, emit)
    for n, out in ((1, away_first), (0, away)):
        for copy in copies[1 - n :: 2]:
            copy.wait_recv()
        add_rows(out, [keep.at[n], core.at[n]])
    for copy in copies:
        copy.wait_send()


def far_projections(x, grads, osend, okeep):
    seq, width = x.shape
    half = width // 2
    piece = grads[0].shape[1] // 2
    slabs = (2, width, half)
    return pl.pallas_call(
        far_kernel,
        out_shape=(shape(slabs[1:], LOW), shape(slabs[1:], LOW), shape((8, 2 * piece), F32)),
        in_specs=[VMEM] * 6,
        out_specs=(VMEM, VMEM, VMEM),
        scratch_shapes=[
            pltpu.VMEM(slabs, F32),
            pltpu.VMEM(slabs, F32),
            pltpu.VMEM(slabs, F32),
            pltpu.VMEM((2 * piece, width), F32),
            pltpu.SemaphoreType.DMA((8,)),
            pltpu.SemaphoreType.DMA((8,)),
        ],
        compiler_params=pltpu.CompilerParams(
            vmem_limit_bytes=VMEM_LIMIT, collective_id=3, has_side_effects=True
        ),
        cost_estimate=pl.CostEstimate(
            flops=12 * seq * width * piece, bytes_accessed=10 << 20, transcendentals=0
        ),
        name="far_projections",
    )(x, *grads, osend, okeep)


def finish_kernel(
    dp_bits,
    x_ref,
    w0,
    w1,
    w2,
    w3,
    dqa,
    dka,
    dva,
    dqb,
    dkb,
    dvb,
    osend,
    okeep,
    dh_hbm,
    rest,
    ffn_x,
    ffn_y,
    in_y,
    back_x,
    away,
    away_first,
    small_ref,
    bias_far,
    gx_hbm,
    result,
    small_out,
    own,
    own16,
    keep,
    send,
    core,
    y_recv,
    x_send,
    x_recv,
    total,
    z_send,
    z_recv,
    last_send,
    last_recv,
    extra,
    bias_ref,
    small_held,
    rows_in,
    rows_out,
    cross,
    load_sem,
    send_sem,
    recv_sem,
    in_sem,
    out_sem,
):
    seq, width = x_ref.shape
    half = width // 2
    piece = dqa.shape[1] // 2
    blocks = seq // RB
    place = lax.axis_index("dp")
    index = lax.axis_index("tensor")
    side = place & 1
    core_at, y_at = partner("tensor", 0), partner("tensor", 1)
    dp_at = [partner("dp", bit) for bit in range(dp_bits)]
    greet([core_at, y_at] + dp_at)
    started = {}

    def remote(key, source, target, device):
        n = len(started)
        started[key] = pltpu.make_async_remote_copy(
            src_ref=source,
            dst_ref=target,
            send_sem=send_sem.at[n],
            recv_sem=recv_sem.at[n],
            device_id=device,
            device_id_type=pl.DeviceIdType.MESH,
        )
        started[key].start()

    def arrive(key):
        started[key].wait_recv()

    part = width // 4
    half_bit, part_bit = (place >> 1) & 1, (place >> 2) & 1

    def quarter(i, j):
        at = (half_bit ^ i) * (2 * part) + (part_bit ^ j) * part
        return pl.ds(pl.multiple_of(at, part), part)

    def two_quarters(i):
        return pl.ds(pl.multiple_of((half_bit ^ i) * (2 * part), 2 * part), 2 * part)

    for n, source in ((1, away_first), (0, away)):
        for i in (1, 0):
            rows = two_quarters(i)
            remote(("y", n, i), source.at[rows, :], y_recv.at[n, rows, :], y_at)
    loads = []
    for w, terms in enumerate(((rest.at[0], ffn_x.at[0], in_y), (rest.at[2], ffn_y.at[0], back_x))):
        targets = (own.at[w], own16.at[w, 0], own16.at[w, 1])
        loads.append(
            [
                pltpu.make_async_copy(term, target, load_sem.at[w, n])
                for n, (term, target) in enumerate(zip(terms, targets))
            ]
        )
        for copy in loads[w]:
            copy.start()

    def fetch(i):
        return pltpu.make_async_copy(
            dh_hbm.at[pl.ds(i * RB, RB), :], rows_in.at[i % 2], in_sem.at[i % 2]
        )

    fetch(0).start()

    def scatter(w):
        for j in (1, 0):
            at = pl.ds((1 - j) * part, part)
            add_rows(z_send.at[w, at, :], [total.at[w, quarter(1, j), :]])
            remote((w, "z", j), z_send.at[w, at, :], z_recv.at[w, at, :], dp_at[1])

    def scatter_on(w):
        rows = quarter(0, 1)
        arrive((w, "z", 1))
        add_rows(last_send.at[w], [total.at[w, rows, :], z_recv.at[w, pl.ds(0, part), :]])
        remote((w, "last"), last_send.at[w], last_recv.at[w], dp_at[2])

    def spread(w, i, j):
        rows = result.at[w, 0, quarter(i, j), :]
        if (i, j) == (0, 0):
            remote((w, "gather", 0, 1), rows, rows, dp_at[2])
        if i == 0:
            remote((w, "gather", 1, j), rows, rows, dp_at[1])
        remote((w, "across", i, j), rows, result.at[w, 1, quarter(i, j), :], dp_at[0])

    def settle(w):
        rows = quarter(0, 0)
        own_part = result.at[w, 0, rows, :]
        arrive((w, "z", 0))
        arrive((w, "last"))
        terms = [total.at[w, rows, :], z_recv.at[w, pl.ds(part, part), :], last_recv.at[w]]
        add_rows(own_part, terms)
        for bit in range(3, dp_bits):
            into = extra.at[w, bit - 3]
            remote((w, "all", bit), own_part, into, dp_at[bit])
            started[(w, "all", bit)].wait_send()
            arrive((w, "all", bit))
            add_rows(own_part, [own_part, into])
        spread(w, 0, 0)

    def gather(w, i, j):
        arrive((w, "gather", i, j))
        spread(w, i, j)

    for w in range(2):
        for copy in loads[w]:
            copy.wait()
        add_rows(total.at[w], [own.at[w], own16.at[w, 0], own16.at[w, 1]])
        scatter(w)

    near_parts = ([], [])

    def emit(n, rows):
        near_parts[n].append(("core", n, len(near_parts[n])))
        remote(near_parts[n][-1], send.at[n, rows, :], core.at[n, rows, :], core_at)

    cross_rows(x_ref, (dqa, dka, dva), okeep, osend, side, cross, keep, send, bias_ref, emit)

    small_held[0] = jnp.zeros(small_held.shape[1:], F32)
    small_held[0, 16:24, :] = small_ref[0:8, :]
    for p in range(4):
        row = 4 * (index ^ p)
        half_mine = small_ref[8 + p : 9 + p, :half]
        half_other = small_ref[8 + p : 9 + p, half:]
        low_half = jnp.where(side == 0, half_mine, half_other)
        high_half = jnp.where(side == 0, half_other, half_mine)
        small_held[0, pl.ds(row, 1), :] = jnp.concatenate([low_half, high_half], axis=1)
        for i, k in enumerate((0, 2)):
            values = (bias_ref, bias_far)[p // 2][k : k + 1, :]
            if p % 2 == 1:
                values = pltpu.roll(values, piece, 1)
            small_held[0, pl.ds(row + 1 + i, 1), :half] = values

    def small_step(n):
        bits = [core_at, y_at] + dp_at
        remote(("small", n), small_held.at[2 * n], small_held.at[2 * n + 1], bits[n])

    def small_sum(n):
        arrive(("small", n))
        out = small_held.at[2 * n + 2] if n < dp_bits + 1 else small_out
        out[...] = small_held[2 * n] + small_held[2 * n + 1]

    weights = ((w0, w1), (w2, w3))
    grads = ((dqa, dka, dva), (dqb, dkb, dvb))
    stores = []

    def inputs_rows(b):
        at = pl.ds(b * RB, RB)
        if b + 1 < blocks:
            fetch(b + 1).start()
        fetch(b).wait()
        grad = rows_in[b % 2]
        for g in range(2):
            for i in range(3):
                rows = slice(i * piece, (i + 1) * piece)
                w = jnp.concatenate([ref[rows, :] for ref in weights[g]], axis=0)
                grad += dot(grads[g][i][at, :], w)
        if b >= 2:
            stores[b - 2].wait()
        rows_out[b % 2] = grad
        stores.append(
            pltpu.make_async_copy(rows_out.at[b % 2], gx_hbm.at[at, :], out_sem.at[b % 2])
        )
        stores[b].start()

    def send_across(i):
        rows = two_quarters(i)
        at = pl.ds((1 - i) * 2 * part, 2 * part)
        arrive(("y", 1, i))
        add_rows(x_send.at[at, :], [keep.at[1, rows, :], core.at[1, rows, :], y_recv.at[1, rows, :]])
        remote(("across", i), x_send.at[at, :], x_recv.at[at, :], dp_at[0])

    def take_across(i):
        rows = two_quarters(i)
        at = pl.ds((1 - i) * 2 * part, 2 * part)
        arrive(("y", 0, i))
        arrive(("across", i))
        add_rows(
            total.at[2, rows, :],
            [keep.at[0, rows, :], core.at[0, rows, :], y_recv.at[0, rows, :], x_recv.at[at, :]],
        )

    small_step(0)
    scatter_on(0)
    for key in near_parts[1]:
        arrive(key)
    send_across(1)
    send_across(0)
    scatter_on(1)
    inputs_rows(0)
    small_sum(0)
    small_step(1)
    settle(0)
    inputs_rows(1)
    small_sum(1)
    small_step(2)
    for key in near_parts[0]:
        arrive(key)
    take_across(1)
    scatter(2)
    settle(1)
    gather(0, 0, 1)
    take_across(0)
    scatter_on(2)
    gather(0, 1, 0)
    inputs_rows(2)
    gather(1, 0, 1)
    small_sum(2)
    small_step(3)
    gather(0, 1, 1)
    settle(2)
    gather(1, 1, 0)
    inputs_rows(3)
    gather(1, 1, 1)
    small_sum(3)
    small_step(4)
    gather(2, 0, 1)
    gather(2, 1, 0)
    for n in range(4, dp_bits + 2):
        small_sum(n)
        if n + 1 < dp_bits + 2:
            small_step(n + 1)
    gather(2, 1, 1)
    for w in range(3):
        for i in range(2):
            for j in range(2):
                arrive((w, "across", i, j))
    for key, copy in started.items():
        if not (isinstance(key, tuple) and key[1] == "all"):
            copy.wait_send()
    for store in stores[-2:]:
        store.wait()


def finish(x, weights, grads, osend, okeep, dh, rest, ffn_x, ffn_y, in_y, back_x, away, away_first, small, bias_far):
    seq, width = x.shape
    half = width // 2
    piece = grads[0].shape[1] // 2
    dp_bits = bits_of("dp")
    slab = (width, half)
    copies = 14 + dp_bits + 2 + 3 * (10 + max(dp_bits - 3, 0))
    assert dp_bits >= 3
    return pl.pallas_call(
        functools.partial(finish_kernel, dp_bits),
        out_shape=(
            shape((seq, width), F32),
            shape((3, 2) + slab, LOW),
            shape((24, width), F32),
        ),
        in_specs=[VMEM] * 13 + [HBM] * 8 + [VMEM, VMEM],
        out_specs=(HBM, VMEM, VMEM),
        scratch_shapes=[
            pltpu.VMEM((2,) + slab, F32),
            pltpu.VMEM((2, 2) + slab, LOW),
            pltpu.VMEM((2,) + slab, F32),
            pltpu.VMEM((2,) + slab, F32),
            pltpu.VMEM((2,) + slab, F32),
            pltpu.VMEM((2,) + slab, LOW),
            pltpu.VMEM(slab, LOW),
            pltpu.VMEM(slab, LOW),
            pltpu.VMEM((3,) + slab, F32),
            pltpu.VMEM((3, width // 2, half), LOW),
            pltpu.VMEM((3, width // 2, half), LOW),
            pltpu.VMEM((3, width // 4, half), LOW),
            pltpu.VMEM((3, width // 4, half), LOW),
            pltpu.VMEM((3, max(dp_bits - 3, 1), width // 4, half), LOW),
            pltpu.VMEM((8, 2 * piece), F32),
            pltpu.VMEM((2 * dp_bits + 4, 24, width), F32),
            pltpu.VMEM((2, RB, width), F32),
            pltpu.VMEM((2, RB, width), F32),
            pltpu.VMEM((2 * piece, width), F32),
            pltpu.SemaphoreType.DMA((2, 3)),
            pltpu.SemaphoreType.DMA((copies,)),
            pltpu.SemaphoreType.DMA((copies,)),
            pltpu.SemaphoreType.DMA((2,)),
            pltpu.SemaphoreType.DMA((2,)),
        ],
        compiler_params=pltpu.CompilerParams(
            vmem_limit_bytes=VMEM_LIMIT, collective_id=2, has_side_effects=True
        ),
        cost_estimate=pl.CostEstimate(
            flops=36 * seq * width * piece, bytes_accessed=50 << 20, transcendentals=0
        ),
        name="finish",
    )(x, *weights, *grads, osend, okeep, dh, rest, ffn_x, ffn_y, in_y, back_x, away, away_first, small, bias_far)


def widen_kernel(
    place_ref,
    small,
    count,
    result,
    source,
    loss_ref,
    bqv_ref,
    bin_ref,
    gains_ref,
    shifts_ref,
    qkv_hbm,
    out_hbm,
    in_hbm,
    back_hbm,
    target,
    slabs,
    rows_held,
    qkv_ref,
    out_ref,
    in_ref,
    back_ref,
    in_sem,
    row_sem,
    out_sem,
):
    half = slabs.shape[3]
    piece = qkv_ref.shape[1]
    side = place_ref[0]
    slab_loads = [
        pltpu.make_async_copy(result.at[w], slabs.at[w], in_sem.at[w]) for w in range(3)
    ]
    blocks = source.shape[0] // RB

    def rows(i, out):
        at = pl.ds(i * RB, RB)
        ends = (rows_held.at[i], target.at[at, :]) if out else (source.at[at, :], rows_held.at[i])
        return pltpu.make_async_copy(*ends, row_sem.at[i, out])

    slab_loads[0].start()
    slab_loads[1].start()
    for i in range(blocks):
        rows(i, 0).start()
    slab_loads[2].start()
    stores = []

    def store(value, to):
        stores.append(pltpu.make_async_copy(value, to, out_sem.at[len(stores)]))
        stores[-1].start()

    sides = [
        pl.ds(pl.multiple_of(natural * half, half), half) for natural in (side, 1 - side)
    ]
    slab_loads[0].wait()
    for n in range(2):
        in_ref[:, sides[n]] = slabs[0, n].astype(F32)
    store(in_ref, in_hbm)
    slab_loads[1].wait()
    for n in range(2):
        for c in range(2):
            strip = slabs[1, n, c * half : (c + 1) * half, :]
            back_ref[sides[n], c * half : (c + 1) * half] = strip.astype(F32)
    store(back_ref, back_hbm)
    for i in range(blocks):
        rows(i, 0).wait()
        rows(i, 1).start()
    slab_loads[2].wait()
    for n in range(2):
        for i in range(3):
            qkv_ref[i, :, sides[n]] = slabs[2, n, i * piece : (i + 1) * piece, :].astype(F32)
        out_ref[:, sides[n]] = slabs[2, n, 3 * piece :, :].astype(F32)
    store(qkv_ref, qkv_hbm)
    store(out_ref, out_hbm)
    row = 4 * place_ref[1]
    bin_ref[...] = small[pl.ds(row, 1), :].reshape(bin_ref.shape)
    for i in range(2):
        bqv_ref[i : i + 1, :] = small[pl.ds(row + 1 + i, 1), :piece]
    gains_ref[...] = small[16:18, :]
    shifts_ref[...] = small[18:22, :]
    tokens = count[0:1, 0:1].astype(F32)
    total = jnp.sum(small[22:23, :], axis=1, keepdims=True)
    loss_ref[...] = total / (2.0 * small.shape[1] * tokens)
    for i in range(blocks):
        rows(i, 1).wait()
    for copy in stores:
        copy.wait()


def widen(place, result, small, count, inputs_grad, piece, out_rows):
    width, half = result.shape[2:]
    seq = inputs_grad.shape[0]
    large = ((3, piece, width), (out_rows, width), (width, 2 * half), (2 * half, width))
    return pl.pallas_call(
        widen_kernel,
        out_shape=(
            shape((1, 1), F32),
            shape((2, piece), F32),
            shape((2 * half,), F32),
            shape((2, width), F32),
            shape((4, width), F32),
        )
        + tuple(shape(dims, F32) for dims in large)
        + (shape(inputs_grad.shape, F32),),
        in_specs=[SMEM, VMEM, VMEM, HBM, HBM],
        out_specs=(VMEM,) * 5 + (HBM,) * 5,
        scratch_shapes=[
            pltpu.VMEM(result.shape, LOW),
            pltpu.VMEM((seq // RB, RB, width), F32),
        ]
        + [pltpu.VMEM(dims, F32) for dims in large]
        + [
            pltpu.SemaphoreType.DMA((3,)),
            pltpu.SemaphoreType.DMA((seq // RB, 2)),
            pltpu.SemaphoreType.DMA((4,)),
        ],
        compiler_params=pltpu.CompilerParams(vmem_limit_bytes=VMEM_LIMIT),
        name="widen",
    )(place, small, count, result, inputs_grad)


def per_device(
    inputs,
    w_qkv,
    b_qv,
    w_out,
    w_in,
    b_in,
    w_back,
    norm_gains,
    shifts,
    segment_ids,
    valid_lengths,
    teacher,
):
    own_seqs, seq, width = inputs.shape
    assert own_seqs == 1 and lax.axis_size("tensor") == 4
    total_slots = seq * lax.axis_size("tensor") * lax.axis_size("dp")
    half = width // 2
    piece = w_qkv.shape[2]
    units = w_in.shape[1]
    index = lax.axis_index("tensor")
    side = (lax.axis_index("dp") & 1).astype(jnp.int32)
    side_row = side.reshape(1)
    x = inputs.reshape(seq, width)

    near = round_qkv(side_row, w_qkv.transpose(0, 2, 1), b_qv, b_in)
    core = swap(near, "tensor", 0)
    far = swap(near, "tensor", 1)
    core, w_in, w_back, w_out = lax.optimization_barrier((core, w_in, w_back, w_out))
    out_in, back, second, x_low = round_rest(side_row, w_out, w_in, w_back, x)
    out_in_far = swap(out_in, "tensor", 1)

    valid = lax.dynamic_index_in_dim(valid_lengths, index, keepdims=False)
    segments = lax.dynamic_index_in_dim(segment_ids, index, keepdims=False)
    positions = jnp.arange(seq, dtype=jnp.int32)
    code = jnp.where(positions < valid, segments, -1)[:, None]
    seg = segments[None, :]
    table = span_tables(segments, valid, seq)

    qa, ka, va, ctx_a, lse_a = attend_forward(table, x_low, near, core, code, seg)
    out_in, back, second, far, ctx_a = lax.optimization_barrier((out_in, back, second, far, ctx_a))
    core_far = swap(far, "tensor", 0)
    out_in_core = swap(out_in, "tensor", 0)
    back_core = swap(back, "tensor", 0)
    second_core = swap(second, "tensor", 0)
    qb, kb, vb, ctx_b, lse_b = attend_forward(table, x_low, far, core_far, code, seg)
    (
        output,
        dh_one,
        cg_a,
        cg_b,
        _,
        to_x,
        to_y,
        rest,
        out_send_a,
        out_send_b,
        out_keep_a,
        out_keep_b,
        sums,
        bias_sums,
        count,
        *_,
    ) = middle(
        total_slots,
        valid.reshape(1),
        valid_lengths,
        ctx_a,
        ctx_b,
        norm_gains,
        shifts,
        x,
        teacher.reshape(seq, width),
        (near, core, far, core_far),
        (out_in, out_in_core, out_in_far),
        (back, back_core),
        (second, second_core),
    )
    ffn_x = swap(to_x, "dp", 0)
    ffn_y = swap(to_y, "tensor", 1)
    grads_b = attend_backward(table, qb, kb, vb, cg_b, lse_b, code, seg)
    away, away_first, bias_far = far_projections(x_low, grads_b, out_send_b, out_keep_b)
    ffn_x, ffn_y, away_first = lax.optimization_barrier((ffn_x, ffn_y, away_first))
    in_away = (rest[1] + ffn_x[1].astype(F32)).astype(LOW)
    back_away = (rest[3] + ffn_y[1].astype(F32)).astype(LOW)
    in_away, back_away, away_first, cg_a = lax.optimization_barrier(
        (in_away, back_away, away_first, cg_a)
    )
    in_y = swap(in_away, "tensor", 1)
    back_x = swap(back_away, "dp", 0)
    *grads_a, output = attend_backward(table, qa, ka, va, cg_a, lse_a, code, seg, output)
    small = jnp.concatenate([sums, bias_sums, jnp.zeros((4, width), F32)], axis=0)
    grad_inputs, slabs, small = finish(
        x_low,
        (near, core, far, core_far),
        (*grads_a, *grads_b),
        out_send_a,
        out_keep_a,
        dh_one,
        rest,
        ffn_x,
        ffn_y,
        in_y,
        back_x,
        away,
        away_first,
        small,
        bias_far,
    )
    (
        loss,
        grad_b_qv,
        grad_b_in,
        grad_gains,
        grad_shifts,
        grad_w_qkv,
        grad_w_out,
        grad_w_in,
        grad_w_back,
        grad_inputs,
    ) = widen(jnp.stack([side, index]), slabs, small, count, grad_inputs, piece, w_out.shape[0])
    return (
        output.reshape(own_seqs, seq, width),
        loss[0, 0],
        grad_inputs.reshape(own_seqs, seq, width),
        grad_w_qkv.transpose(0, 2, 1),
        grad_b_qv,
        grad_w_out,
        grad_w_in,
        grad_b_in,
        grad_w_back,
        grad_gains,
        grad_shifts,
    )


def solution(mesh):
    return jax.shard_map(
        per_device,
        mesh=mesh,
        in_specs=(
            P(("dp", "tensor"), None, None),
            P(None, None, "tensor"),
            P(None, "tensor"),
            P("tensor", None),
            P(None, "tensor"),
            P("tensor"),
            P("tensor", None),
            P(),
            P(),
            P("dp", None),
            P("dp"),
            P(("dp", "tensor"), None, None),
        ),
        out_specs=(
            P(("dp", "tensor"), None, None),
            P(),
            P(("dp", "tensor"), None, None),
            P(None, None, "tensor"),
            P(None, "tensor"),
            P("tensor", None),
            P(None, "tensor"),
            P("tensor"),
            P("tensor", None),
            P(),
            P(),
        ),
        check_vma=False,
    )
```

```python
import functools
import math

import jax
import jax.numpy as jnp
from jax import lax
from jax.experimental import pallas as pl
from jax.experimental.pallas import tpu as pltpu
from jax.sharding import PartitionSpec as P

HD = 64
LN_EPSILON = 1e-05
MASKED_SCORE = -1000000000.0
QB = 256
KB = 128
RB = 256
FR = 256
NT = ((1,), (1,))
TN = ((0,), (0,))
PHI = (
    0.1412427189,
    0.1377927593,
    0.1458432541,
    0.005834031383,
    0.2126657205,
    -0.1910292611,
    0.0476509541,
)
PHI_STEP = 0.35355339059327379

VMEM_LIMIT = 63 << 20
VMEM = pl.BlockSpec(memory_space=pltpu.VMEM)
SMEM = pl.BlockSpec(memory_space=pltpu.SMEM)
HBM = pl.BlockSpec(memory_space=pl.ANY)
LOW = jnp.bfloat16
F32 = jnp.float32


def dot(left, right, dims=((1,), (0,))):
    return lax.dot_general(left, right, (dims, ((), ())), preferred_element_type=jnp.float32)


def shape(dims, dtype):
    return jax.ShapeDtypeStruct(dims, dtype)


def swap(values, axis, bit):
    size = lax.axis_size(axis)
    return lax.ppermute(values, axis, [(i, i ^ (1 << bit)) for i in range(size)])


def bits_of(axis):
    return int(math.log2(lax.axis_size(axis)))


def partner(axis, bit):
    here = {name: lax.axis_index(name) for name in ("dp", "tensor")}
    here[axis] = here[axis] ^ (1 << bit)
    return here["dp"], here["tensor"]


def greet(partners):
    barrier = pltpu.get_barrier_semaphore()
    for device in partners:
        pl.semaphore_signal(
            barrier, inc=1, device_id=device, device_id_type=pl.DeviceIdType.MESH
        )
    pl.semaphore_wait(barrier, len(partners))


def three_parts(values):
    first = values.astype(LOW)
    rest = values - first.astype(F32)
    second = rest.astype(LOW)
    return first, second, (rest - second.astype(F32)).astype(LOW)


def span_table(table_ref, seg, valid):
    for block in range(seg.shape[1] // QB):
        start = block * QB
        first = jnp.max(seg[:, start : start + 1])
        last = jnp.max(seg[:, start + QB - 1 : start + QB])
        low = jnp.sum((seg < first).astype(jnp.int32))
        high = jnp.sum((seg <= last).astype(jnp.int32))
        high = jnp.maximum(jnp.minimum(high, valid), start + QB)
        low_block = lax.div(low, jnp.int32(KB))
        table_ref[0, block] = low_block
        table_ref[1, block] = lax.div(high + (KB - 1), jnp.int32(KB)) - low_block


def round_qkv_kernel(
    side_ref, lengths_ref, segments_ref, w_ref, bqv_ref, bin_ref, out_ref, table_ref, code_ref, seg_ref
):
    index = lax.axis_index("tensor")
    valid = lengths_ref[index]
    seg = segments_ref[pl.ds(index, 1), :]
    seg_ref[...] = seg
    span_table(table_ref, seg, valid)
    code = jnp.where(lax.broadcasted_iota(jnp.int32, seg.shape, 1) < valid, seg, -1)
    tall = jnp.broadcast_to(code.astype(F32), (8, seg.shape[1])).T
    code_ref[...] = tall[:, :1].astype(jnp.int32)
    piece = w_ref.shape[1]
    width = w_ref.shape[2]
    half = bin_ref.shape[0] // 2
    for i in range(3):
        out_ref[i * piece : (i + 1) * piece, :] = w_ref[i].astype(LOW)
    row = bin_ref[...].reshape(1, 2 * half)
    mine = jnp.where(side_ref[0] == 0, row[:, :half], row[:, half:])
    other = jnp.where(side_ref[0] == 0, row[:, half:], row[:, :half])
    pad = jnp.zeros((1, width - piece), F32)
    rows = [jnp.concatenate([mine, other], axis=1)]
    rows += [jnp.concatenate([bqv_ref[i : i + 1, :], pad], axis=1) for i in range(2)]
    parts = [part.astype(F32) for row in rows for part in three_parts(row)]
    parts += [jnp.zeros((1, width), F32)] * 7
    out_ref[3 * piece :, :] = jnp.concatenate(parts, axis=0).astype(LOW)


def round_qkv(side, lengths, segments, w_qkv, b_qv, b_in):
    _, piece, width = w_qkv.shape
    seq = segments.shape[1]
    return pl.pallas_call(
        round_qkv_kernel,
        out_shape=(
            shape((3 * piece + 16, width), LOW),
            shape((2, seq // QB), jnp.int32),
            shape((seq, 1), jnp.int32),
            shape((1, seq), jnp.int32),
        ),
        in_specs=[SMEM, SMEM, VMEM, VMEM, VMEM, VMEM],
        out_specs=(VMEM, SMEM, VMEM, VMEM),
        compiler_params=pltpu.CompilerParams(vmem_limit_bytes=VMEM_LIMIT),
        name="round_qkv",
    )(side, lengths, segments, w_qkv, b_qv, b_in)


def round_rest_kernel(
    side_ref, wo_hbm, wi_hbm, wb_hbm, x_hbm, out_in, back, second, x_low, *scratch
):
    wo_in, wi_in, wb_in, x_in, oi_out, b_out, s_out, x_out, in_sem, out_sem = scratch
    rows, width = wo_in.shape
    half = width // 2
    loads, stores = [], []

    def load(source, target):
        loads.append(pltpu.make_async_copy(source, target, in_sem.at[len(loads)]))
        loads[-1].start()

    def store(source, target):
        stores.append(pltpu.make_async_copy(source, target, out_sem.at[len(stores)]))
        stores[-1].start()

    load(wo_hbm, wo_in)
    load(wi_hbm, wi_in)
    for side in (side_ref[0], 1 - side_ref[0]):
        at = pl.ds(pl.multiple_of(side * half, half), half)
        load(wb_hbm.at[at, :], wb_in.at[at, :])
    quarters = [pl.ds(i * x_in.shape[0] // 4, x_in.shape[0] // 4) for i in range(4)]
    for at in quarters:
        load(x_hbm.at[at, :], x_in.at[at, :])
    loads[0].wait()
    for c in range(2):
        oi_out[c * rows : (c + 1) * rows, :] = wo_in[:, c * half : (c + 1) * half].astype(LOW)
    loads[1].wait()
    sides = [
        pl.ds(pl.multiple_of(side * half, half), half) for side in (side_ref[0], 1 - side_ref[0])
    ]
    oi_out[2 * rows :, :] = wi_in[:, sides[0]].astype(LOW)
    store(oi_out, out_in)
    s_out[:width, :] = wi_in[:, sides[1]].astype(LOW)
    for n, (to_back, base) in enumerate(((b_out, 0), (s_out, width))):
        loads[2 + n].wait()
        for c in range(2):
            start = base + c * half
            strip = wb_in[sides[n], c * half : (c + 1) * half]
            to_back[start : start + half, :] = strip.astype(LOW)
        store(to_back, (back, second)[n])
    for n, at in enumerate(quarters):
        loads[4 + n].wait()
        x_out[at, :] = x_in[at, :].astype(LOW)
        store(x_out.at[at, :], x_low.at[at, :])
    for copy in stores:
        copy.wait()


def round_rest(side, w_out, w_in, w_back, x):
    rows, width = w_out.shape
    half = width // 2
    shapes = ((2 * rows + width, half), (width, half), (2 * width, half), x.shape)
    return pl.pallas_call(
        round_rest_kernel,
        out_shape=tuple(shape(dims, LOW) for dims in shapes),
        in_specs=[SMEM] + [HBM] * 4,
        out_specs=(HBM,) * 4,
        scratch_shapes=[pltpu.VMEM(a.shape, F32) for a in (w_out, w_in, w_back, x)]
        + [pltpu.VMEM(dims, LOW) for dims in shapes]
        + [pltpu.SemaphoreType.DMA((8,)), pltpu.SemaphoreType.DMA((7,))],
        compiler_params=pltpu.CompilerParams(vmem_limit_bytes=VMEM_LIMIT),
        name="round_rest",
    )(side, w_out, w_in, w_back, x)


def make_bias(bias_ref, block, low, count, code_ref, seg_ref):
    dims = (count * KB, QB)
    codes = code_ref[pl.ds(pl.multiple_of(low * KB, KB), count * KB), :]
    segs = seg_ref[:, pl.ds(pl.multiple_of(block * QB, QB), QB)]
    key_at = low * KB + lax.broadcasted_iota(jnp.int32, dims, 0)
    query_at = block * QB + lax.broadcasted_iota(jnp.int32, dims, 1)
    allowed = (codes == segs) | (key_at == query_at)
    bias_ref[: count * KB, :] = jnp.where(allowed, 0.0, MASKED_SCORE)


def one_head(values, head):
    lane = lax.broadcasted_iota(jnp.int32, values.shape, 1)
    keep = (lane < HD) if head == 0 else (lane >= HD)
    return jnp.where(keep, values, jnp.zeros_like(values))


def forward_kernel(
    table_ref,
    x_ref,
    w0_ref,
    w1_ref,
    code_ref,
    seg_ref,
    q_ref,
    k_ref,
    v_ref,
    ctx_ref,
    lse_ref,
    weights,
    biases,
    vt_ref,
    bias_ref,
):
    block = pl.program_id(0)
    low, total = table_ref[0, block], table_ref[1, block]
    piece = (w0_ref.shape[0] - 16) // 3
    pairs = 2 * piece // 128

    @pl.when(block == 0)
    def _():
        for i in range(3):
            for n, ref in enumerate((w0_ref, w1_ref)):
                rows = ref[i * piece : (i + 1) * piece, :]
                weights[i, n * piece : (n + 1) * piece, :] = rows
        lane = lax.broadcasted_iota(jnp.int32, (1, x_ref.shape[1]), 1)
        for i in (0, 2):
            base = 3 * piece + (3 if i == 0 else 6)
            both = [
                sum(ref[base + part : base + part + 1, :].astype(F32) for part in range(3))
                for ref in (w0_ref, w1_ref)
            ]
            row = jnp.where(lane < piece, both[0], pltpu.roll(both[1], piece, 1))
            biases[i : i + 1, :] = row[:, : 2 * piece]
        biases[1:2, :] = jnp.zeros((1, 2 * piece), F32)

        def project(b, carry):
            at = pl.ds(pl.multiple_of(b * QB, QB), QB)
            for i, ref in enumerate((q_ref, k_ref, v_ref)):
                ref[at, :] = (dot(x_ref[at, :], weights[i], NT) + biases[i : i + 1, :]).astype(LOW)
            vt_ref[:, at] = v_ref[at, :].T
            return carry

        lax.fori_loop(0, x_ref.shape[0] // QB, project, 0)

    def run(count):
        make_bias(bias_ref, block, low, count, code_ref, seg_ref)
        bias = bias_ref[: count * KB, :]
        rows = pl.ds(pl.multiple_of(low * KB, KB), count * KB)
        queries = pl.ds(pl.multiple_of(block * QB, QB), QB)

        def scores(head):
            lanes = slice(head // 2 * 128, head // 2 * 128 + 128)
            query = q_ref[queries, lanes] * jnp.asarray(0.125, LOW)
            return dot(k_ref[rows, lanes], one_head(query, head % 2), NT) + bias

        def soft(values, head):
            peak = jnp.max(values, axis=0, keepdims=True)
            powers = jnp.exp(values - peak)
            mass = jnp.sum(powers, axis=0, keepdims=True)
            lse_ref[head : head + 1, :] = peak + jnp.log(mass)
            return (powers * (1.0 / mass)).astype(LOW)

        outs = []

        def context(probs, head):
            outs.append(dot(vt_ref[head * HD : (head + 1) * HD, rows], probs))
            if head % 2 == 1:
                both = jnp.concatenate(outs[-2:], axis=0).T
                ctx_ref[:, head // 2 * 128 : head // 2 * 128 + 128] = both.astype(LOW)

        values, probs = scores(0), None
        for head in range(2 * pairs):
            later = scores(head + 1) if head + 1 < 2 * pairs else None
            now = soft(values, head)
            if head > 0:
                context(probs, head - 1)
            values, probs = later, now
        context(probs, 2 * pairs - 1)

    for count in range(QB // KB, k_ref.shape[0] // KB + 1):
        pl.when(total == count)(functools.partial(run, count))


def backward_kernel(carried, table_ref, q_ref, k_ref, v_ref, g_ref, lse_ref, code_ref, seg_ref, *refs):
    block = pl.program_id(0)
    refs = list(refs)
    if carried:
        source, target = refs.pop(0), refs.pop(3)
        target[...] = source[...]
    dq_ref, dk_ref, dv_ref, kt_ref, bias_ref, dk_sum, dv_sum = refs
    low, total = table_ref[0, block], table_ref[1, block]
    heads = q_ref.shape[1] // HD

    @pl.when(block == 0)
    def _():
        kt_ref[...] = k_ref[...].T
        dk_sum[...] = jnp.zeros_like(dk_sum)
        dv_sum[...] = jnp.zeros_like(dv_sum)

    def run(count):
        make_bias(bias_ref, block, low, count, code_ref, seg_ref)
        bias = bias_ref[: count * KB, :]
        rows = pl.ds(pl.multiple_of(low * KB, KB), count * KB)

        def first(head):
            lanes = slice(head // 2 * 128, head // 2 * 128 + 128)
            query = one_head(q_ref[:, lanes] * jnp.asarray(0.125, LOW), head % 2)
            grad = one_head(g_ref[:, lanes], head % 2)
            scores = dot(k_ref[rows, lanes], query, NT) + bias
            return scores, dot(v_ref[rows, lanes], grad, NT), query, grad

        def second(head, scores, prob_grad, query, grad):
            probs = jnp.exp(scores - lse_ref[head : head + 1, :])
            delta = jnp.sum(probs * prob_grad, axis=0, keepdims=True)
            return probs.astype(LOW), (probs * (prob_grad - delta)).astype(LOW), query, grad

        outs = []

        def third(head, probs, score_grad, query, grad):
            lanes = slice(head // 2 * 128, head // 2 * 128 + 128)
            dv_sum[rows, lanes] += dot(probs, grad)
            dk_sum[rows, lanes] += dot(score_grad, query)
            outs.append(dot(kt_ref[head * HD : (head + 1) * HD, rows], score_grad))
            if head % 2 == 1:
                both = jnp.concatenate(outs[-2:], axis=0).T * 0.125
                dq_ref[:, lanes] = both.astype(LOW)

        start, middle_of = first(0), None
        for head in range(heads):
            later = first(head + 1) if head + 1 < heads else None
            now = second(head, *start)
            if head > 0:
                third(head - 1, *middle_of)
            start, middle_of = later, now
        third(heads - 1, *middle_of)

    for count in range(QB // KB, k_ref.shape[0] // KB + 1):
        pl.when(total == count)(functools.partial(run, count))

    @pl.when(block == pl.num_programs(0) - 1)
    def _():
        dk_ref[...] = dk_sum[...].astype(LOW)
        dv_ref[...] = dv_sum[...].astype(LOW)


def attend_forward(table, x, first, second, code, seg):
    seq, width = x.shape
    piece = (first.shape[0] - 16) // 3
    heads, blocks = 2 * piece // HD, seq // QB
    whole = lambda i, t: (0, 0)
    column = pl.BlockSpec((seq, 2 * piece), whole)
    return pl.pallas_call(
        forward_kernel,
        out_shape=(shape((seq, 2 * piece), LOW),) * 4 + (shape((8, seq), F32),),
        grid_spec=pltpu.PrefetchScalarGridSpec(
            num_scalar_prefetch=1,
            grid=(blocks,),
            in_specs=[
                pl.BlockSpec((seq, width), whole),
                pl.BlockSpec(first.shape, whole),
                pl.BlockSpec(second.shape, whole),
                pl.BlockSpec((seq, 1), whole),
                pl.BlockSpec((1, seq), whole),
            ],
            out_specs=[
                column,
                column,
                column,
                pl.BlockSpec((QB, 2 * piece), lambda i, t: (i, 0)),
                pl.BlockSpec((8, QB), lambda i, t: (0, i)),
            ],
            scratch_shapes=[
                pltpu.VMEM((3, 2 * piece, width), LOW),
                pltpu.VMEM((3, 2 * piece), F32),
                pltpu.VMEM((2 * piece, seq), LOW),
                pltpu.VMEM((seq, QB), F32),
            ],
        ),
        compiler_params=pltpu.CompilerParams(vmem_limit_bytes=VMEM_LIMIT),
        cost_estimate=pl.CostEstimate(
            flops=16 * seq * seq * piece + 12 * seq * width * piece,
            bytes_accessed=16 * seq * piece,
            transcendentals=seq * seq * heads // 2,
        ),
        name="attend_forward",
    )(table, x, first, second, code, seg)


def attend_backward(table, q, k, v, grad, lse, code, seg, *carried):
    seq, width = grad.shape
    blocks = seq // QB
    block = pl.BlockSpec((QB, width), lambda i, t: (i, 0))
    column = pl.BlockSpec((seq, width), lambda i, t: (0, 0))
    return pl.pallas_call(
        functools.partial(backward_kernel, len(carried)),
        out_shape=(shape((seq, width), LOW),) * 3 + tuple(shape(c.shape, c.dtype) for c in carried),
        grid_spec=pltpu.PrefetchScalarGridSpec(
            num_scalar_prefetch=1,
            grid=(blocks,),
            in_specs=[
                block,
                column,
                column,
                block,
                pl.BlockSpec((8, QB), lambda i, t: (0, i)),
                pl.BlockSpec((seq, 1), lambda i, t: (0, 0)),
                pl.BlockSpec((1, seq), lambda i, t: (0, 0)),
            ]
            + [pl.BlockSpec((QB, c.shape[1]), lambda i, t: (i, 0)) for c in carried],
            out_specs=[block, column, column]
            + [pl.BlockSpec((QB, c.shape[1]), lambda i, t: (i, 0)) for c in carried],
            scratch_shapes=[
                pltpu.VMEM((width, seq), LOW),
                pltpu.VMEM((seq, QB), F32),
                pltpu.VMEM((seq, width), F32),
                pltpu.VMEM((seq, width), F32),
            ],
        ),
        compiler_params=pltpu.CompilerParams(vmem_limit_bytes=VMEM_LIMIT),
        cost_estimate=pl.CostEstimate(
            flops=16 * seq * seq * width,
            bytes_accessed=16 * seq * width,
            transcendentals=seq * seq * width // 128,
        ),
        name="attend_backward",
    )(table, q, k, v, grad, lse, code, seg, *carried)


def gelu_parts(pre):
    size = 1.0 + PHI_STEP * jnp.abs(pre)
    t = pl.reciprocal(size, approx=True)
    t = t * (2.0 - size * t)
    poly = PHI[6] * t + PHI[5]
    for factor in PHI[4::-1]:
        poly = poly * t + factor
    bell = jnp.exp2((-0.5 * math.log2(math.e)) * (pre * pre))
    tail = poly * t * bell
    cdf = jnp.where(pre < 0, tail, 1.0 - tail)
    return pre * cdf, cdf + (pre * 0.3989422804014327) * bell


def norm_stats(values):
    width = values.shape[-1]
    mean = jnp.sum(values, axis=-1, keepdims=True) * (1.0 / width)
    centred = values - mean
    spread = jnp.sum(centred * centred, axis=-1, keepdims=True) * (1.0 / width)
    rate = lax.rsqrt(spread + LN_EPSILON)
    return centred * rate, rate


def norm_back(grad, gain, xhat, rate):
    width = grad.shape[-1]
    scaled = grad * gain
    mean = jnp.sum(scaled, axis=-1, keepdims=True) * (1.0 / width)
    along = jnp.sum(scaled * xhat, axis=-1, keepdims=True) * (1.0 / width)
    return rate * (scaled - mean - xhat * along)


def column_sum(values):
    return jnp.sum(values, axis=0, keepdims=True)


def middle_kernel(
    total_slots,
    dp_bits,
    lengths_ref,
    ctx_a,
    ctx_b,
    gains,
    shifts,
    x_hbm,
    teacher_hbm,
    qa,
    qb,
    qc,
    qd,
    outin_own,
    outin_core,
    outin_far,
    back_own,
    back_core,
    second_own,
    second_core,
    out_hbm,
    dh_hbm,
    cg_a,
    cg_b,
    core_hbm,
    to_x,
    to_y,
    rest,
    out_send_a,
    out_send_b,
    out_keep_a,
    out_keep_b,
    sums,
    bias_sums,
    count_ref,
    outin_far_core,
    in_far,
    back_far,
    in_far_core,
    back_far_core,
    w_in,
    w_back,
    w_out,
    bias_parts,
    bias_in,
    xhat_one,
    rate_one,
    mid_low,
    hidden,
    slope,
    acc,
    dh_low,
    pre_grad,
    rows_in,
    rows_out,
    stage16,
    stage32,
    from_core,
    held,
    w_sem,
    in_sem,
    out_sem,
    load_sem,
    store_sem,
    send_sem,
    recv_sem,
    count_send,
    count_recv,
    far_send,
    far_recv,
):
    seq, width = acc.shape
    blocks = seq // RB
    half = width // 2
    out_rows = w_out.shape[0] // 4
    units = w_in.shape[2]
    side = units // 2
    core_at, y_at, x_at = partner("tensor", 0), partner("tensor", 1), partner("dp", 0)
    greet([core_at, y_at] + [partner("dp", bit) for bit in range(dp_bits)])

    def far_copy(n, source, target, device):
        return pltpu.make_async_remote_copy(
            src_ref=source,
            dst_ref=target,
            send_sem=far_send.at[n],
            recv_sem=far_recv.at[n],
            device_id=device,
            device_id_type=pl.DeviceIdType.MESH,
        )

    in_at = pl.ds(2 * out_rows, width)
    far = [
        far_copy(
            0,
            outin_far.at[pl.ds(0, 2 * out_rows), :],
            outin_far_core.at[pl.ds(0, 2 * out_rows), :],
            core_at,
        ),
        far_copy(1, back_own, back_far.at[0], y_at),
        far_copy(
            2,
            second_own.at[pl.ds(width, side), :],
            back_far.at[1, pl.ds(0, side), :],
            y_at,
        ),
        far_copy(3, outin_far.at[in_at, :], in_far, x_at),
        far_copy(4, in_far, in_far_core, core_at),
        far_copy(5, back_far.at[0], back_far_core.at[0], core_at),
        far_copy(6, back_far.at[1], back_far_core.at[1], core_at),
        far_copy(
            7,
            back_far.at[0, pl.ds(side, side), :],
            back_far.at[1, pl.ds(side, side), :],
            x_at,
        ),
        far_copy(8, outin_far.at[in_at, :], outin_far_core.at[in_at, :], core_at),
    ]
    for copy in far[:4] + far[8:]:
        copy.start()
    out_in = (outin_own, outin_core, outin_far, outin_far_core)
    in_parts = tuple(ref.at[in_at, :] for ref in out_in)
    in_other = (
        second_own.at[pl.ds(0, width), :],
        second_core.at[pl.ds(0, width), :],
        in_far,
        in_far_core,
    )
    back_parts = (back_own, back_core, back_far.at[0], back_far_core.at[0])
    back_other = (
        second_own.at[pl.ds(width, width), :],
        second_core.at[pl.ds(width, width), :],
        back_far.at[1],
        back_far_core.at[1],
    )

    def rows(i):
        return pl.ds(i * RB, RB)

    def fetch(source, i, slot):
        return pltpu.make_async_copy(source.at[rows(i), :], rows_in.at[slot], in_sem.at[slot])

    def out_weights(p, c):
        return pltpu.make_async_copy(
            out_in[p].at[pl.ds(c * out_rows, out_rows), :],
            w_out.at[pl.ds(p * out_rows, out_rows), pl.ds(c * half, half)],
            w_sem.at[p, c],
        )

    def bias_rows(p):
        source = (qa, qb, qc, qd)[p]
        return pltpu.make_async_copy(
            source.at[pl.ds(source.shape[0] - 16, 16), :], bias_parts.at[p], w_sem.at[p, 8]
        )

    def load_in(source, p, r):
        return pltpu.make_async_copy(
            source, w_in.at[p, :, pl.ds(r * side, side)], w_sem.at[p, 2 + 3 * r]
        )

    def load_back(source, p, r, c):
        return pltpu.make_async_copy(
            source.at[pl.ds(c * side, side), :],
            w_back.at[p, pl.ds(r * side, side), pl.ds(c * half, half)],
            w_sem.at[p, 3 + 3 * r + c],
        )

    def ffn_weights(p):
        load_in(in_parts[p], p, 0).start()
        load_in(in_other[p], p, 1).start()
        for c in range(2):
            load_back(back_parts[p], p, 0, c).start()
            load_back(back_other[p], p, 1, c).start()

    early = [out_weights(p, c) for p in range(4) for c in range(2)]
    for copy in early[:6]:
        copy.start()
    fetch(x_hbm, 0, 0).start()
    for p in range(4):
        bias_rows(p).start()
    for p in range(2):
        ffn_weights(p)

    def count_step(bit):
        return pltpu.make_async_remote_copy(
            src_ref=held.at[2 * bit],
            dst_ref=held.at[2 * bit + 1],
            send_sem=count_send.at[bit],
            recv_sem=count_recv.at[bit],
            device_id=partner("dp", bit),
            device_id_type=pl.DeviceIdType.MESH,
        )

    tokens = jnp.full(held.shape[1:], 0, jnp.int32)
    for i in range(lengths_ref.shape[0]):
        tokens += lengths_ref[i]
    held[0] = tokens
    count_step(0).start()

    def count_on(bit):
        count_step(bit).wait()
        held[2 * bit + 2] = held[2 * bit] + held[2 * bit + 1]
        if bit + 1 < dp_bits:
            count_step(bit + 1).start()

    far[0].wait_recv()
    for copy in early[6:]:
        copy.start()
    for copy in early:
        copy.wait()

    for i in range(blocks):
        if i + 1 < blocks:
            fetch(x_hbm, i + 1, (i + 1) % 2).start()
        fetch(x_hbm, i, i % 2).wait()
        context = jnp.concatenate([ctx_a[rows(i), :], ctx_b[rows(i), :]], axis=1)
        xhat, rate = norm_stats(dot(context, w_out[...]) + shifts[0:1, :] + rows_in[i % 2])
        xhat_one[rows(i), :] = xhat
        rate_one[rows(i), :] = rate
        mid_low[rows(i), :] = (xhat * gains[0:1, :] + shifts[1:2, :]).astype(LOW)
        acc[rows(i), :] = jnp.zeros((RB, width), F32)
    fetch(teacher_hbm, 0, 0).start()
    for p in range(4):
        bias_rows(p).wait()
        part = bias_parts[p, 0:3, :].astype(F32)
        bias_in[p] = part[0:1] + part[1:2] + part[2:3]

    def up(p, carry):
        for bit in range(min(dp_bits, 4)):
            pl.when(p == bit)(functools.partial(count_on, bit))

        @pl.when(p == 1)
        def _():
            far[1].wait_recv()
            far[7].start()
            far[5].start()
            far[3].wait_recv()
            far[4].start()

        @pl.when(p == 2)
        def _():
            far[2].wait_recv()
            far[7].wait_recv()
            far[6].start()
            ffn_weights(2)

        @pl.when(p == 3)
        def _():
            for n in (8, 4, 5, 6):
                far[n].wait_recv()
            ffn_weights(3)

        for r in range(2):
            load_in(in_other[0], p, r).wait()
            for c in range(2):
                load_back(back_own, p, r, c).wait()
        last = seq // FR - 1
        strips = [slice(c, c + 256) for c in range(0, units, 256)]

        def lift(k, cols):
            pre = dot(mid_low[pl.ds(k * FR, FR), :], w_in[p, :, cols])
            return pre + bias_in[p, :, cols]

        def lower(k, acts, cols):
            acc[pl.ds(k * FR, FR), cols] += dot(acts, w_back[p, :, cols])

        pre, before = [lift(0, cols) for cols in strips], None
        for k in range(last + 1):
            later, acts = [], []
            for c, cols in enumerate(strips):
                if k < last:
                    later.append(lift(k + 1, cols))
                act, der = gelu_parts(pre[c])
                acts.append(act.astype(LOW))
                hidden[p, pl.ds(k * FR, FR), cols] = acts[c]
                slope[p, pl.ds(k * FR, FR), cols] = der
                if k > 0:
                    lower(k - 1, before, cols)
            pre, before = later, jnp.concatenate(acts, axis=1)
        for cols in strips:
            lower(last, before, cols)
        return carry

    lax.fori_loop(0, 4, up, 0)
    for bit in range(4, dp_bits):
        count_on(bit)
    count_ref[...] = held[2 * dp_bits]

    zero = jnp.zeros((1, width), F32)
    squares, gain_two, shift_two, shift_mid = zero, zero, zero, zero
    scale = total_slots / held[2 * dp_bits, 0:1, 0:1].astype(F32)
    valid = lengths_ref[lax.axis_index("tensor")]
    stores = []
    for i in range(blocks):
        if i + 1 < blocks:
            fetch(teacher_hbm, i + 1, (i + 1) % 2).start()
        fetch(teacher_hbm, i, i % 2).wait()
        mid = xhat_one[rows(i), :] * gains[0:1, :] + shifts[1:2, :]
        xhat, rate = norm_stats(acc[rows(i), :] + shifts[2:3, :] + mid)
        output = xhat * gains[1:2, :] + shifts[3:4, :]
        if i >= 2:
            stores[i - 2].wait()
        rows_out[i % 2] = output
        stores.append(
            pltpu.make_async_copy(rows_out.at[i % 2], out_hbm.at[rows(i), :], out_sem.at[i % 2])
        )
        stores[i].start()
        live = (i * RB + lax.broadcasted_iota(jnp.int32, (RB, 1), 0)) < valid
        distance = jnp.where(live, output - rows_in[i % 2], 0.0)
        squares += column_sum(distance * distance)
        out_grad = scale * distance
        gain_two += column_sum(out_grad * xhat)
        shift_two += column_sum(out_grad)
        dh_two = norm_back(out_grad, gains[1:2, :], xhat, rate)
        shift_mid += column_sum(dh_two)
        acc[rows(i), :] = dh_two
        dh_low[rows(i), :] = dh_two.astype(LOW)
    for store in stores[-2:]:
        store.wait()

    sides = (pl.ds(0, side), pl.ds(side, side))

    def ffn_back(p):
        total = jnp.zeros((1, units), F32)

        def lift(k):
            return dot(dh_low[pl.ds(k * FR, FR), :], w_back[p], NT)

        def lower(k):
            at = pl.ds(k * FR, FR)
            acc[at, :] += dot(pre_grad[at, :], w_in[p], NT)

        raised = lift(0)
        for k in range(seq // FR):
            later = lift(k + 1) if k + 1 < seq // FR else None
            at = pl.ds(k * FR, FR)
            grad = (raised * slope[p, at, :]).astype(LOW)
            pre_grad[at, :] = grad
            total += column_sum(grad.astype(F32))
            if k > 0:
                lower(k - 1)
            raised = later
        lower(seq // FR - 1)
        bias_sums[pl.ds(p, 1), :] = total

    def to_core(pair, w):
        return pltpu.make_async_remote_copy(
            src_ref=stage16.at[w],
            dst_ref=core_hbm.at[pair, w],
            send_sem=send_sem.at[w],
            recv_sem=recv_sem.at[pair, w],
            device_id=core_at,
            device_id_type=pl.DeviceIdType.MESH,
        )

    def away(n, carry):
        p = 2 * n + 1
        ffn_back(p)

        @pl.when(n > 0)
        def _():
            for w in range(2):
                to_core(0, w).wait_send()

        stage16[0] = dot(mid_low[...], pre_grad[...], TN).astype(LOW)
        stage16[1] = dot(hidden[p], dh_low[...], TN).astype(LOW)
        for w in range(2):
            to_core(n, w).start()
        return carry

    lax.fori_loop(0, 2, away, 0)

    def in_moves(pair):
        return [
            pltpu.make_async_copy(stage32.at[0, :, sides[0]], rest.at[pair], store_sem.at[0]),
            pltpu.make_async_copy(stage16.at[0, :, sides[1]], to_x.at[pair], store_sem.at[1]),
        ]

    def back_moves(stage, target):
        return [
            pltpu.make_async_copy(
                stage.at[1, sides[r], sides[c]],
                target.at[r, sides[c], :],
                store_sem.at[2 + 2 * r + c],
            )
            for r in range(2)
            for c in range(2)
        ]

    moves = {1: in_moves(1) + back_moves(stage16, to_y), 0: in_moves(0) + back_moves(stage32, rest.at[pl.ds(2, 2)])}

    def home(n, carry):
        pair = n
        p = 2 * pair
        ffn_back(p)
        for w in range(2):
            to_core(pair, w).wait_recv()
            pltpu.make_async_copy(core_hbm.at[pair, w], from_core.at[w], load_sem.at[w]).start()

        @pl.when(n == 0)
        def _():
            for w in range(2):
                to_core(1, w).wait_send()

        @pl.when(n == 1)
        def _():
            for copy in moves[0]:
                copy.wait()

        stage32[0] = dot(mid_low[...], pre_grad[...], TN)
        stage32[1] = dot(hidden[p], dh_low[...], TN)
        for w in range(2):
            pltpu.make_async_copy(core_hbm.at[pair, w], from_core.at[w], load_sem.at[w]).wait()
            for k in range(0, width, 128):
                total = stage32[w, k : k + 128, :] + from_core[w, k : k + 128, :].astype(F32)
                stage32[w, k : k + 128, :] = total
                stage16[w, k : k + 128, :] = total.astype(LOW)

        for turn in range(2):

            @pl.when(n == turn)
            def _(turn=turn):
                for copy in moves[turn]:
                    copy.start()

        return carry

    lax.fori_loop(0, 2, home, 0)

    gain_one, shift_one, shift_out = zero, zero, zero
    stores = []
    for i in range(blocks):
        grad, xhat = acc[rows(i), :], xhat_one[rows(i), :]
        gain_one += column_sum(grad * xhat)
        shift_one += column_sum(grad)
        dh_one = norm_back(grad, gains[0:1, :], xhat, rate_one[rows(i), :])
        shift_out += column_sum(dh_one)
        if i >= 2:
            stores[i - 2].wait()
        rows_out[i % 2] = dh_one
        stores.append(
            pltpu.make_async_copy(rows_out.at[i % 2], dh_hbm.at[rows(i), :], out_sem.at[i % 2])
        )
        stores[i].start()
        dh_one = dh_one.astype(LOW)
        dh_low[rows(i), :] = dh_one
        grad = dot(dh_one, w_out[...], NT).astype(LOW)
        cg_a[rows(i), :] = grad[:, :half]
        cg_b[rows(i), :] = grad[:, half:]
    for context, out_keep, out_send in (
        (ctx_a, out_keep_a, out_send_a),
        (ctx_b, out_keep_b, out_send_b),
    ):
        grad = dot(context[...], dh_low[...], TN)
        out_keep[...] = grad[:out_rows]
        out_send[...] = grad[out_rows:].astype(LOW)
    sums[...] = jnp.concatenate(
        [gain_one, gain_two, shift_out, shift_one, shift_mid, shift_two, squares, zero], axis=0
    )
    for store in stores[-2:]:
        store.wait()
    for copy in moves[1]:
        copy.wait()
    for copy in far:
        copy.wait_send()


def middle(
    total_slots, lengths, ctx_a, ctx_b, gains, shifts, x, teacher, near, out_in, back, second
):
    seq, width = x.shape
    half = width // 2
    out_rows = ctx_a.shape[1] // 2
    units = width
    dp_bits = bits_of("dp")
    slab = (width, units // 2)
    return pl.pallas_call(
        functools.partial(middle_kernel, float(total_slots), dp_bits),
        out_shape=(
            shape((seq, width), F32),
            shape((seq, width), F32),
            shape((seq, half), LOW),
            shape((seq, half), LOW),
            shape((2, 2, width, units), LOW),
            shape((2,) + slab, LOW),
            shape((2,) + slab, LOW),
            shape((4,) + slab, F32),
            shape((out_rows, width), LOW),
            shape((out_rows, width), LOW),
            shape((out_rows, width), F32),
            shape((out_rows, width), F32),
            shape((8, width), F32),
            shape((4, units), F32),
            shape((8, 128), jnp.int32),
            shape(out_in[0].shape, LOW),
            shape(slab, LOW),
            shape((2,) + slab, LOW),
            shape(slab, LOW),
            shape((2,) + slab, LOW),
        ),
        in_specs=[SMEM, VMEM, VMEM, VMEM, VMEM, HBM, HBM] + [HBM] * 11,
        out_specs=(HBM, HBM, VMEM, VMEM, HBM, HBM, HBM, HBM) + (VMEM,) * 7 + (HBM,) * 5,
        scratch_shapes=[
            pltpu.VMEM((4, width, units), LOW),
            pltpu.VMEM((4, units, width), LOW),
            pltpu.VMEM((4 * out_rows, width), LOW),
            pltpu.VMEM((4, 16, width), LOW),
            pltpu.VMEM((4, 1, units), F32),
            pltpu.VMEM((seq, width), F32),
            pltpu.VMEM((seq, 1), F32),
            pltpu.VMEM((seq, width), LOW),
            pltpu.VMEM((4, seq, units), LOW),
            pltpu.VMEM((4, seq, units), F32),
            pltpu.VMEM((seq, width), F32),
            pltpu.VMEM((seq, width), LOW),
            pltpu.VMEM((seq, units), LOW),
            pltpu.VMEM((2, RB, width), F32),
            pltpu.VMEM((2, RB, width), F32),
            pltpu.VMEM((2, width, units), LOW),
            pltpu.VMEM((2, width, units), F32),
            pltpu.VMEM((2, width, units), LOW),
            pltpu.VMEM((2 * dp_bits + 1, 8, 128), jnp.int32),
            pltpu.SemaphoreType.DMA((4, 9)),
            pltpu.SemaphoreType.DMA((2,)),
            pltpu.SemaphoreType.DMA((2,)),
            pltpu.SemaphoreType.DMA((2,)),
            pltpu.SemaphoreType.DMA((6,)),
            pltpu.SemaphoreType.DMA((2,)),
            pltpu.SemaphoreType.DMA((2, 2)),
            pltpu.SemaphoreType.DMA((dp_bits,)),
            pltpu.SemaphoreType.DMA((dp_bits,)),
            pltpu.SemaphoreType.DMA((9,)),
            pltpu.SemaphoreType.DMA((9,)),
        ],
        compiler_params=pltpu.CompilerParams(
            vmem_limit_bytes=VMEM_LIMIT, collective_id=1, has_side_effects=True
        ),
        cost_estimate=pl.CostEstimate(
            flops=6 * seq * width * (8 * units + width),
            bytes_accessed=30 << 20,
            transcendentals=2 * seq * 4 * units,
        ),
        name="middle",
    )(lengths, ctx_a, ctx_b, gains, shifts, x, teacher, *near, *out_in, *back, *second)


def add_rows(out, terms, chunk=96):
    rows = out.shape[0]
    chunk = min(chunk, rows)

    def step(i, carry):
        at = pl.ds(pl.multiple_of(i * chunk, chunk), chunk)
        total = terms[0][at, :].astype(F32)
        for term in terms[1:]:
            total += term[at, :].astype(F32)
        out[at, :] = total.astype(out.dtype)
        return carry

    lax.fori_loop(0, rows // chunk, step, 0)


def cross_rows(x_ref, grads, okeep, osend, side, cross, keep, send, bias_ref, emit, between=None):
    half = x_ref.shape[1] // 2
    piece = grads[0].shape[1] // 2
    mine = pl.ds(pl.multiple_of(side * half, half), half)
    other = pl.ds(pl.multiple_of((1 - side) * half, half), half)
    sides = ((1, other), (0, mine))
    at = pl.ds(3 * piece, osend.shape[0])
    for n, lanes in sides:
        keep[n, at, :] = okeep[:, lanes]
        send[n, at, :] = osend[:, lanes].astype(send.dtype)
        emit(n, at)
    for i in range(3):
        cross[...] = dot(grads[i][...], x_ref[...], TN)
        at = pl.ds(i * piece, piece)
        for n, lanes in sides:
            keep[n, at, :] = cross[:piece, lanes]
            send[n, at, :] = cross[piece:, lanes].astype(send.dtype)
            emit(n, at)
        bias_ref[i : i + 1, :] = column_sum(grads[i][...].astype(F32))
        if i == 0 and between is not None:
            between()


def far_kernel(
    x_ref,
    dq,
    dk,
    dv,
    osend,
    okeep,
    away,
    away_first,
    bias_ref,
    keep,
    send,
    core,
    cross,
    send_sem,
    recv_sem,
):
    core_at = partner("tensor", 0)
    greet([core_at])
    bias_ref[...] = jnp.zeros(bias_ref.shape, F32)
    copies = []

    def emit(n, rows):
        at = len(copies)
        copies.append(
            pltpu.make_async_remote_copy(
                src_ref=send.at[n, rows, :],
                dst_ref=core.at[n, rows, :],
                send_sem=send_sem.at[at],
                recv_sem=recv_sem.at[at],
                device_id=core_at,
                device_id_type=pl.DeviceIdType.MESH,
            )
        )
        copies[at].start()

    side = lax.axis_index("dp") & 1
    cross_rows(x_ref, (dq, dk, dv), okeep, osend, side, cross, keep, send, bias_ref, emit)
    for n, out in ((1, away_first), (0, away)):
        for copy in copies[1 - n :: 2]:
            copy.wait_recv()
        add_rows(out, [keep.at[n], core.at[n]])
    for copy in copies:
        copy.wait_send()


def far_projections(x, grads, osend, okeep):
    seq, width = x.shape
    half = width // 2
    piece = grads[0].shape[1] // 2
    slabs = (2, width, half)
    return pl.pallas_call(
        far_kernel,
        out_shape=(shape(slabs[1:], LOW), shape(slabs[1:], LOW), shape((8, 2 * piece), F32)),
        in_specs=[VMEM] * 6,
        out_specs=(VMEM, VMEM, VMEM),
        scratch_shapes=[
            pltpu.VMEM(slabs, F32),
            pltpu.VMEM(slabs, F32),
            pltpu.VMEM(slabs, F32),
            pltpu.VMEM((2 * piece, width), F32),
            pltpu.SemaphoreType.DMA((8,)),
            pltpu.SemaphoreType.DMA((8,)),
        ],
        compiler_params=pltpu.CompilerParams(
            vmem_limit_bytes=VMEM_LIMIT, collective_id=3, has_side_effects=True
        ),
        cost_estimate=pl.CostEstimate(
            flops=12 * seq * width * piece, bytes_accessed=10 << 20, transcendentals=0
        ),
        name="far_projections",
    )(x, *grads, osend, okeep)


def finish_kernel(
    dp_bits,
    x_hbm,
    w0_hbm,
    w1_hbm,
    w2_hbm,
    w3_hbm,
    dqa_hbm,
    dka_hbm,
    dva_hbm,
    dqb_hbm,
    dkb_hbm,
    dvb_hbm,
    osend,
    okeep,
    dh_hbm,
    rest,
    ffn_x,
    ffn_y,
    in_z,
    back_x,
    away,
    qkv_y,
    small_ref,
    bias_far,
    gx_hbm,
    result,
    small_out,
    x_ref,
    w0,
    w1,
    w2,
    w3,
    dqa,
    dka,
    dva,
    dqb,
    dkb,
    dvb,
    own,
    own16,
    in_send,
    in_recv,
    keep,
    send,
    core,
    y_recv,
    x_send,
    x_recv,
    total,
    z_send,
    z_recv,
    last_send,
    last_recv,
    extra,
    bias_ref,
    small_held,
    rows_in,
    rows_out,
    cross,
    operand_sem,
    load_sem,
    send_sem,
    recv_sem,
    in_sem,
    out_sem,
):
    seq, width = x_ref.shape
    half = width // 2
    piece = dqa.shape[1] // 2
    blocks = seq // RB
    place = lax.axis_index("dp")
    index = lax.axis_index("tensor")
    side = place & 1
    core_at, y_at = partner("tensor", 0), partner("tensor", 1)
    dp_at = [partner("dp", bit) for bit in range(dp_bits)]
    greet([core_at, y_at] + dp_at)
    started = {}

    def remote(key, source, target, device):
        n = len(started)
        started[key] = pltpu.make_async_remote_copy(
            src_ref=source,
            dst_ref=target,
            send_sem=send_sem.at[n],
            recv_sem=recv_sem.at[n],
            device_id=device,
            device_id_type=pl.DeviceIdType.MESH,
        )
        started[key].start()

    def arrive(key):
        started[key].wait_recv()

    part = width // 4
    half_bit, part_bit = (place >> 1) & 1, (place >> 2) & 1

    def quarter(i, j):
        at = (half_bit ^ i) * (2 * part) + (part_bit ^ j) * part
        return pl.ds(pl.multiple_of(at, part), part)

    def two_quarters(i):
        return pl.ds(pl.multiple_of((half_bit ^ i) * (2 * part), 2 * part), 2 * part)

    for i in (1, 0):
        rows = two_quarters(i)
        remote(("y", 0, i), away.at[rows, :], y_recv.at[0, rows, :], y_at)
    mine = two_quarters(0)
    loads = [[], []]

    def load(w, source, target):
        loads[w].append(pltpu.make_async_copy(source, target, load_sem.at[w, len(loads[w])]))
        loads[w][-1].start()

    load(1, rest.at[2], own.at[1])
    load(1, ffn_y.at[0], own16.at[1, 0])
    load(1, back_x, own16.at[1, 1])
    for pair in range(2):
        at = pl.ds(pair * 2 * part, 2 * part)
        load(0, rest.at[pair, mine, :], own.at[0, at, :])
        load(0, ffn_x.at[pair, mine, :], own16.at[0, 0, at, :])
        load(0, in_z.at[pair], own16.at[0, 1, at, :])
    load(1, qkv_y, y_recv.at[1])
    operands = [
        pltpu.make_async_copy(source, target, operand_sem.at[n])
        for n, (source, target) in enumerate(
            (
                (dqa_hbm, dqa),
                (x_hbm, x_ref),
                (dka_hbm, dka),
                (dva_hbm, dva),
                (dqb_hbm, dqb),
                (dkb_hbm, dkb),
                (dvb_hbm, dvb),
                (w0_hbm, w0),
                (w1_hbm, w1),
                (w2_hbm, w2),
                (w3_hbm, w3),
            )
        )
    ]
    for copy in operands:
        copy.start()

    def fetch(i):
        return pltpu.make_async_copy(
            dh_hbm.at[pl.ds(i * RB, RB), :], rows_in.at[i % 2], in_sem.at[i % 2]
        )

    fetch(0).start()

    def scatter(w):
        for j in (1, 0):
            at = pl.ds((1 - j) * part, part)
            add_rows(z_send.at[w, at, :], [total.at[w, quarter(1, j), :]])
            remote((w, "z", j), z_send.at[w, at, :], z_recv.at[w, at, :], dp_at[1])

    def in_part(j):
        return in_recv.at[pl.ds(pl.multiple_of((part_bit ^ j) * part, part), part), :]

    def scatter_on(w):
        rows = quarter(0, 1)
        arrive("in y" if w == 0 else (w, "z", 1))
        came = in_part(1) if w == 0 else z_recv.at[w, pl.ds(0, part), :]
        add_rows(last_send.at[w], [total.at[w, rows, :], came])
        remote((w, "last"), last_send.at[w], last_recv.at[w], dp_at[2])

    def spread(w, i, j):
        rows = result.at[w, 0, quarter(i, j), :]
        if (i, j) == (0, 0):
            remote((w, "gather", 0, 1), rows, rows, dp_at[2])
        if i == 0:
            remote((w, "gather", 1, j), rows, rows, dp_at[1])
        remote((w, "across", i, j), rows, result.at[w, 1, quarter(i, j), :], dp_at[0])

    def settle(w):
        rows = quarter(0, 0)
        own_part = result.at[w, 0, rows, :]
        if w > 0:
            arrive((w, "z", 0))
        arrive((w, "last"))
        came = in_part(0) if w == 0 else z_recv.at[w, pl.ds(part, part), :]
        terms = [total.at[w, rows, :], came, last_recv.at[w]]
        add_rows(own_part, terms)
        for bit in range(3, dp_bits):
            into = extra.at[w, bit - 3]
            remote((w, "all", bit), own_part, into, dp_at[bit])
            started[(w, "all", bit)].wait_send()
            arrive((w, "all", bit))
            add_rows(own_part, [own_part, into])
        spread(w, 0, 0)

    def gather(w, i, j):
        arrive((w, "gather", i, j))
        spread(w, i, j)

    for copy in loads[1]:
        copy.wait()
    add_rows(total.at[1], [own.at[1], own16.at[1, 0], own16.at[1, 1]])
    scatter(1)
    for copy in loads[0]:
        copy.wait()
    for pair, out in ((1, in_send), (0, total.at[0, mine, :])):
        at = pl.ds(pair * 2 * part, 2 * part)
        add_rows(out, [own.at[0, at, :], own16.at[0, 0, at, :], own16.at[0, 1, at, :]])
    remote("in y", in_send, in_recv, y_at)
    for copy in operands[:4]:
        copy.wait()

    near_parts = ([], [])

    def emit(n, rows):
        near_parts[n].append(("core", n, len(near_parts[n])))
        remote(near_parts[n][-1], send.at[n, rows, :], core.at[n, rows, :], core_at)

    near_grads = (dqa, dka, dva)
    cross_rows(
        x_ref,
        near_grads,
        okeep,
        osend,
        side,
        cross,
        keep,
        send,
        bias_ref,
        emit,
    )
    for copy in operands[4:]:
        copy.wait()

    small_held[0] = jnp.zeros(small_held.shape[1:], F32)
    small_held[0, 16:24, :] = small_ref[0:8, :]
    for p in range(4):
        row = 4 * (index ^ p)
        half_mine = small_ref[8 + p : 9 + p, :half]
        half_other = small_ref[8 + p : 9 + p, half:]
        low_half = jnp.where(side == 0, half_mine, half_other)
        high_half = jnp.where(side == 0, half_other, half_mine)
        small_held[0, pl.ds(row, 1), :] = jnp.concatenate([low_half, high_half], axis=1)
        for i, k in enumerate((0, 2)):
            values = (bias_ref, bias_far)[p // 2][k : k + 1, :]
            if p % 2 == 1:
                values = pltpu.roll(values, piece, 1)
            small_held[0, pl.ds(row + 1 + i, 1), :half] = values

    def small_step(n):
        bits = [core_at, y_at] + dp_at
        remote(("small", n), small_held.at[2 * n], small_held.at[2 * n + 1], bits[n])

    def small_sum(n):
        arrive(("small", n))
        out = small_held.at[2 * n + 2] if n < dp_bits + 1 else small_out
        out[...] = small_held[2 * n] + small_held[2 * n + 1]

    weights = ((w0, w1), (w2, w3))
    grads = ((dqa, dka, dva), (dqb, dkb, dvb))
    stores = []

    def inputs_rows(b):
        at = pl.ds(b * RB, RB)
        if b + 1 < blocks:
            fetch(b + 1).start()
        fetch(b).wait()
        grad = rows_in[b % 2]
        for g in range(2):
            for i in range(3):
                rows = slice(i * piece, (i + 1) * piece)
                w = jnp.concatenate([ref[rows, :] for ref in weights[g]], axis=0)
                grad += dot(grads[g][i][at, :], w)
        if b >= 2:
            stores[b - 2].wait()
        rows_out[b % 2] = grad
        stores.append(
            pltpu.make_async_copy(rows_out.at[b % 2], gx_hbm.at[at, :], out_sem.at[b % 2])
        )
        stores[b].start()

    def send_across(i):
        rows = two_quarters(i)
        at = pl.ds((1 - i) * 2 * part, 2 * part)
        add_rows(x_send.at[at, :], [keep.at[1, rows, :], core.at[1, rows, :], y_recv.at[1, rows, :]])
        remote(("across", i), x_send.at[at, :], x_recv.at[at, :], dp_at[0])

    def take_across(i):
        rows = two_quarters(i)
        at = pl.ds((1 - i) * 2 * part, 2 * part)
        arrive(("y", 0, i))
        arrive(("across", i))
        add_rows(
            total.at[2, rows, :],
            [keep.at[0, rows, :], core.at[0, rows, :], y_recv.at[0, rows, :], x_recv.at[at, :]],
        )

    small_step(0)
    for key in near_parts[1]:
        arrive(key)
    send_across(1)
    send_across(0)
    scatter_on(1)
    inputs_rows(0)
    settle(1)
    small_sum(0)
    small_step(1)
    for key in near_parts[0]:
        arrive(key)
    take_across(1)
    scatter(2)
    scatter_on(0)
    inputs_rows(1)
    gather(1, 0, 1)
    small_sum(1)
    small_step(2)
    take_across(0)
    scatter_on(2)
    gather(1, 1, 0)
    settle(0)
    inputs_rows(2)
    gather(1, 1, 1)
    small_sum(2)
    small_step(3)
    gather(0, 0, 1)
    settle(2)
    gather(0, 1, 0)
    inputs_rows(3)
    gather(0, 1, 1)
    small_sum(3)
    small_step(4)
    gather(2, 0, 1)
    gather(2, 1, 0)
    for n in range(4, dp_bits + 2):
        small_sum(n)
        if n + 1 < dp_bits + 2:
            small_step(n + 1)
    gather(2, 1, 1)
    for w in range(3):
        for i in range(2):
            for j in range(2):
                arrive((w, "across", i, j))
    for key, copy in started.items():
        if not (isinstance(key, tuple) and key[1] == "all"):
            copy.wait_send()
    for store in stores[-2:]:
        store.wait()


def finish(x, weights, grads, osend, okeep, dh, rest, ffn_x, ffn_y, in_z, back_x, away, qkv_y, small, bias_far):
    seq, width = x.shape
    half = width // 2
    piece = grads[0].shape[1] // 2
    dp_bits = bits_of("dp")
    slab = (width, half)
    copies = 14 + dp_bits + 2 + 3 * (10 + max(dp_bits - 3, 0))
    assert dp_bits >= 3
    return pl.pallas_call(
        functools.partial(finish_kernel, dp_bits),
        out_shape=(
            shape((seq, width), F32),
            shape((3, 2) + slab, LOW),
            shape((24, width), F32),
        ),
        in_specs=[HBM] * 11 + [VMEM] * 2 + [HBM] * 8 + [VMEM, VMEM],
        out_specs=(HBM, VMEM, VMEM),
        scratch_shapes=[pltpu.VMEM(a.shape, LOW) for a in (x, *weights, *grads)]
        + [
            pltpu.VMEM((2,) + slab, F32),
            pltpu.VMEM((2, 2) + slab, LOW),
            pltpu.VMEM((width // 2, half), LOW),
            pltpu.VMEM((width // 2, half), LOW),
            pltpu.VMEM((2,) + slab, F32),
            pltpu.VMEM((2,) + slab, F32),
            pltpu.VMEM((2,) + slab, F32),
            pltpu.VMEM((2,) + slab, LOW),
            pltpu.VMEM(slab, LOW),
            pltpu.VMEM(slab, LOW),
            pltpu.VMEM((3,) + slab, F32),
            pltpu.VMEM((3, width // 2, half), LOW),
            pltpu.VMEM((3, width // 2, half), LOW),
            pltpu.VMEM((3, width // 4, half), LOW),
            pltpu.VMEM((3, width // 4, half), LOW),
            pltpu.VMEM((3, max(dp_bits - 3, 1), width // 4, half), LOW),
            pltpu.VMEM((8, 2 * piece), F32),
            pltpu.VMEM((2 * dp_bits + 4, 24, width), F32),
            pltpu.VMEM((2, RB, width), F32),
            pltpu.VMEM((2, RB, width), F32),
            pltpu.VMEM((2 * piece, width), F32),
            pltpu.SemaphoreType.DMA((11,)),
            pltpu.SemaphoreType.DMA((2, 6)),
            pltpu.SemaphoreType.DMA((copies,)),
            pltpu.SemaphoreType.DMA((copies,)),
            pltpu.SemaphoreType.DMA((2,)),
            pltpu.SemaphoreType.DMA((2,)),
        ],
        compiler_params=pltpu.CompilerParams(
            vmem_limit_bytes=VMEM_LIMIT, collective_id=2, has_side_effects=True
        ),
        cost_estimate=pl.CostEstimate(
            flops=36 * seq * width * piece, bytes_accessed=50 << 20, transcendentals=0
        ),
        name="finish",
    )(x, *weights, *grads, osend, okeep, dh, rest, ffn_x, ffn_y, in_z, back_x, away, qkv_y, small, bias_far)


def widen_kernel(
    place_ref,
    small,
    count,
    result,
    source,
    loss_ref,
    bqv_ref,
    bin_ref,
    gains_ref,
    shifts_ref,
    qkv_hbm,
    out_hbm,
    in_hbm,
    back_hbm,
    target,
    slabs,
    rows_held,
    qkv_ref,
    out_ref,
    in_ref,
    back_ref,
    in_sem,
    row_sem,
    out_sem,
):
    half = slabs.shape[3]
    piece = qkv_ref.shape[1]
    side = place_ref[0]
    slab_loads = [
        pltpu.make_async_copy(result.at[w], slabs.at[w], in_sem.at[w]) for w in range(3)
    ]
    blocks = source.shape[0] // RB

    def rows(i, out):
        at = pl.ds(i * RB, RB)
        ends = (rows_held.at[i], target.at[at, :]) if out else (source.at[at, :], rows_held.at[i])
        return pltpu.make_async_copy(*ends, row_sem.at[i, out])

    slab_loads[0].start()
    slab_loads[1].start()
    for i in range(blocks):
        rows(i, 0).start()
    slab_loads[2].start()
    stores = []

    def store(value, to):
        stores.append(pltpu.make_async_copy(value, to, out_sem.at[len(stores)]))
        stores[-1].start()

    sides = [
        pl.ds(pl.multiple_of(natural * half, half), half) for natural in (side, 1 - side)
    ]
    slab_loads[0].wait()
    for n in range(2):
        in_ref[:, sides[n]] = slabs[0, n].astype(F32)
    store(in_ref, in_hbm)
    slab_loads[1].wait()
    for n in range(2):
        for c in range(2):
            strip = slabs[1, n, c * half : (c + 1) * half, :]
            back_ref[sides[n], c * half : (c + 1) * half] = strip.astype(F32)
    store(back_ref, back_hbm)
    for i in range(blocks):
        rows(i, 0).wait()
        rows(i, 1).start()
    slab_loads[2].wait()
    for n in range(2):
        for i in range(3):
            qkv_ref[i, :, sides[n]] = slabs[2, n, i * piece : (i + 1) * piece, :].astype(F32)
        out_ref[:, sides[n]] = slabs[2, n, 3 * piece :, :].astype(F32)
    store(qkv_ref, qkv_hbm)
    store(out_ref, out_hbm)
    row = 4 * place_ref[1]
    bin_ref[...] = small[pl.ds(row, 1), :].reshape(bin_ref.shape)
    for i in range(2):
        bqv_ref[i : i + 1, :] = small[pl.ds(row + 1 + i, 1), :piece]
    gains_ref[...] = small[16:18, :]
    shifts_ref[...] = small[18:22, :]
    tokens = count[0:1, 0:1].astype(F32)
    total = jnp.sum(small[22:23, :], axis=1, keepdims=True)
    loss_ref[...] = total / (2.0 * small.shape[1] * tokens)
    for i in range(blocks):
        rows(i, 1).wait()
    for copy in stores:
        copy.wait()


def widen(place, result, small, count, inputs_grad, piece, out_rows):
    width, half = result.shape[2:]
    seq = inputs_grad.shape[0]
    large = ((3, piece, width), (out_rows, width), (width, 2 * half), (2 * half, width))
    return pl.pallas_call(
        widen_kernel,
        out_shape=(
            shape((1, 1), F32),
            shape((2, piece), F32),
            shape((2 * half,), F32),
            shape((2, width), F32),
            shape((4, width), F32),
        )
        + tuple(shape(dims, F32) for dims in large)
        + (shape(inputs_grad.shape, F32),),
        in_specs=[SMEM, VMEM, VMEM, HBM, HBM],
        out_specs=(VMEM,) * 5 + (HBM,) * 5,
        scratch_shapes=[
            pltpu.VMEM(result.shape, LOW),
            pltpu.VMEM((seq // RB, RB, width), F32),
        ]
        + [pltpu.VMEM(dims, F32) for dims in large]
        + [
            pltpu.SemaphoreType.DMA((3,)),
            pltpu.SemaphoreType.DMA((seq // RB, 2)),
            pltpu.SemaphoreType.DMA((4,)),
        ],
        compiler_params=pltpu.CompilerParams(vmem_limit_bytes=VMEM_LIMIT),
        name="widen",
    )(place, small, count, result, inputs_grad)


def per_device(
    inputs,
    w_qkv,
    b_qv,
    w_out,
    w_in,
    b_in,
    w_back,
    norm_gains,
    shifts,
    segment_ids,
    valid_lengths,
    teacher,
):
    own_seqs, seq, width = inputs.shape
    assert own_seqs == 1 and lax.axis_size("tensor") == 4
    total_slots = seq * lax.axis_size("tensor") * lax.axis_size("dp")
    half = width // 2
    piece = w_qkv.shape[2]
    units = w_in.shape[1]
    index = lax.axis_index("tensor")
    side = (lax.axis_index("dp") & 1).astype(jnp.int32)
    side_row = side.reshape(1)
    x = inputs.reshape(seq, width)

    near, table, code, seg = round_qkv(
        side_row, valid_lengths, segment_ids, w_qkv.transpose(0, 2, 1), b_qv, b_in
    )
    core = swap(near, "tensor", 0)
    far = swap(near, "tensor", 1)
    core, w_in, w_back, w_out = lax.optimization_barrier((core, w_in, w_back, w_out))
    out_in, back, second, x_low = round_rest(side_row, w_out, w_in, w_back, x)
    out_in_far = swap(out_in, "tensor", 1)

    qa, ka, va, ctx_a, lse_a = attend_forward(table, x_low, near, core, code, seg)
    out_in, back, second, far, ctx_a = lax.optimization_barrier((out_in, back, second, far, ctx_a))
    core_far = swap(far, "tensor", 0)
    out_in_core = swap(out_in, "tensor", 0)
    back_core = swap(back, "tensor", 0)
    second_core = swap(second, "tensor", 0)
    qb, kb, vb, ctx_b, lse_b = attend_forward(table, x_low, far, core_far, code, seg)
    (
        output,
        dh_one,
        cg_a,
        cg_b,
        _,
        to_x,
        to_y,
        rest,
        out_send_a,
        out_send_b,
        out_keep_a,
        out_keep_b,
        sums,
        bias_sums,
        count,
        *_,
    ) = middle(
        total_slots,
        valid_lengths,
        ctx_a,
        ctx_b,
        norm_gains,
        shifts,
        x,
        teacher.reshape(seq, width),
        (near, core, far, core_far),
        (out_in, out_in_core, out_in_far),
        (back, back_core),
        (second, second_core),
    )
    ffn_x = swap(to_x, "dp", 0)
    ffn_y = swap(to_y, "tensor", 1)
    grads_b = attend_backward(table, qb, kb, vb, cg_b, lse_b, code, seg)
    away, away_first, bias_far = far_projections(x_low, grads_b, out_send_b, out_keep_b)
    ffn_x, ffn_y, away_first = lax.optimization_barrier((ffn_x, ffn_y, away_first))
    half_other = 1 - ((lax.axis_index("dp") >> 1) & 1)
    in_away = (
        lax.dynamic_slice_in_dim(rest[:2], half_other * half, half, 1)
        + lax.dynamic_slice_in_dim(ffn_x, half_other * half, half, 1).astype(F32)
    ).astype(LOW)
    back_away = (rest[3] + ffn_y[1].astype(F32)).astype(LOW)
    in_away, back_away, away_first, cg_a = lax.optimization_barrier(
        (in_away, back_away, away_first, cg_a)
    )
    in_z = swap(in_away, "dp", 1)
    qkv_y = swap(away_first, "tensor", 1)
    back_x = swap(back_away, "dp", 0)
    *grads_a, output = attend_backward(table, qa, ka, va, cg_a, lse_a, code, seg, output)
    small = jnp.concatenate([sums, bias_sums, jnp.zeros((4, width), F32)], axis=0)
    grad_inputs, slabs, small = finish(
        x_low,
        (near, core, far, core_far),
        (*grads_a, *grads_b),
        out_send_a,
        out_keep_a,
        dh_one,
        rest,
        ffn_x,
        ffn_y,
        in_z,
        back_x,
        away,
        qkv_y,
        small,
        bias_far,
    )
    (
        loss,
        grad_b_qv,
        grad_b_in,
        grad_gains,
        grad_shifts,
        grad_w_qkv,
        grad_w_out,
        grad_w_in,
        grad_w_back,
        grad_inputs,
    ) = widen(jnp.stack([side, index]), slabs, small, count, grad_inputs, piece, w_out.shape[0])
    return (
        output.reshape(own_seqs, seq, width),
        loss[0, 0],
        grad_inputs.reshape(own_seqs, seq, width),
        grad_w_qkv.transpose(0, 2, 1),
        grad_b_qv,
        grad_w_out,
        grad_w_in,
        grad_b_in,
        grad_w_back,
        grad_gains,
        grad_shifts,
    )


def solution(mesh):
    return jax.shard_map(
        per_device,
        mesh=mesh,
        in_specs=(
            P(("dp", "tensor"), None, None),
            P(None, None, "tensor"),
            P(None, "tensor"),
            P("tensor", None),
            P(None, "tensor"),
            P("tensor"),
            P("tensor", None),
            P(),
            P(),
            P("dp", None),
            P("dp"),
            P(("dp", "tensor"), None, None),
        ),
        out_specs=(
            P(("dp", "tensor"), None, None),
            P(),
            P(("dp", "tensor"), None, None),
            P(None, None, "tensor"),
            P(None, "tensor"),
            P("tensor", None),
            P(None, "tensor"),
            P("tensor"),
            P("tensor", None),
            P(),
            P(),
        ),
        check_vma=False,
    )
```

```python
import functools
import math

import jax
import jax.numpy as jnp
from jax import lax
from jax.experimental import pallas as pl
from jax.experimental.pallas import tpu as pltpu
from jax.sharding import PartitionSpec as P

HD = 64
LN_EPSILON = 1e-05
MASKED_SCORE = -1000000000.0
QB = 256
KB = 128
RB = 256
FR = 256
NT = ((1,), (1,))
TN = ((0,), (0,))
PHI = (
    0.1412427189,
    0.1377927593,
    0.1458432541,
    0.005834031383,
    0.2126657205,
    -0.1910292611,
    0.0476509541,
)
PHI_STEP = 0.35355339059327379

VMEM_LIMIT = 63 << 20
VMEM = pl.BlockSpec(memory_space=pltpu.VMEM)
SMEM = pl.BlockSpec(memory_space=pltpu.SMEM)
HBM = pl.BlockSpec(memory_space=pl.ANY)
LOW = jnp.bfloat16
F32 = jnp.float32


def dot(left, right, dims=((1,), (0,))):
    return lax.dot_general(left, right, (dims, ((), ())), preferred_element_type=jnp.float32)


def shape(dims, dtype):
    return jax.ShapeDtypeStruct(dims, dtype)


def swap(values, axis, bit):
    size = lax.axis_size(axis)
    return lax.ppermute(values, axis, [(i, i ^ (1 << bit)) for i in range(size)])


def bits_of(axis):
    return int(math.log2(lax.axis_size(axis)))


def partner(axis, bit):
    here = {name: lax.axis_index(name) for name in ("dp", "tensor")}
    here[axis] = here[axis] ^ (1 << bit)
    return here["dp"], here["tensor"]


def greet(partners):
    barrier = pltpu.get_barrier_semaphore()
    for device in partners:
        pl.semaphore_signal(
            barrier, inc=1, device_id=device, device_id_type=pl.DeviceIdType.MESH
        )
    pl.semaphore_wait(barrier, len(partners))


def three_parts(values):
    first = values.astype(LOW)
    rest = values - first.astype(F32)
    second = rest.astype(LOW)
    return first, second, (rest - second.astype(F32)).astype(LOW)


def span_table(table_ref, seg, valid):
    for block in range(seg.shape[1] // QB):
        start = block * QB
        first = jnp.max(seg[:, start : start + 1])
        last = jnp.max(seg[:, start + QB - 1 : start + QB])
        low = jnp.sum((seg < first).astype(jnp.int32))
        high = jnp.sum((seg <= last).astype(jnp.int32))
        high = jnp.maximum(jnp.minimum(high, valid), start + QB)
        low_block = lax.div(low, jnp.int32(KB))
        table_ref[0, block] = low_block
        table_ref[1, block] = lax.div(high + (KB - 1), jnp.int32(KB)) - low_block


def round_qkv_kernel(
    lengths_ref, segments_ref, w_ref, bqv_ref, bin_ref, out_ref, table_ref, code_ref, seg_ref
):
    index = lax.axis_index("tensor")
    valid = lengths_ref[index]
    seg = segments_ref[pl.ds(index, 1), :]
    seg_ref[...] = seg
    span_table(table_ref, seg, valid)
    code = jnp.where(lax.broadcasted_iota(jnp.int32, seg.shape, 1) < valid, seg, -1)
    tall = jnp.broadcast_to(code.astype(F32), (8, seg.shape[1])).T
    code_ref[...] = tall[:, :1].astype(jnp.int32)
    piece = w_ref.shape[1]
    width = w_ref.shape[2]
    half = bin_ref.shape[0] // 2
    for i in range(3):
        out_ref[i * piece : (i + 1) * piece, :] = w_ref[i].astype(LOW)
    row = bin_ref[...].reshape(1, 2 * half)
    side = lax.axis_index("dp") & 1
    mine = jnp.where(side == 0, row[:, :half], row[:, half:])
    other = jnp.where(side == 0, row[:, half:], row[:, :half])
    pad = jnp.zeros((1, width - piece), F32)
    rows = [jnp.concatenate([mine, other], axis=1)]
    rows += [jnp.concatenate([bqv_ref[i : i + 1, :], pad], axis=1) for i in range(2)]
    parts = [part.astype(F32) for row in rows for part in three_parts(row)]
    parts += [jnp.zeros((1, width), F32)] * 7
    out_ref[3 * piece :, :] = jnp.concatenate(parts, axis=0).astype(LOW)


def round_qkv(lengths, segments, w_qkv, b_qv, b_in):
    _, piece, width = w_qkv.shape
    seq = segments.shape[1]
    return pl.pallas_call(
        round_qkv_kernel,
        out_shape=(
            shape((3 * piece + 16, width), LOW),
            shape((2, seq // QB), jnp.int32),
            shape((seq, 1), jnp.int32),
            shape((1, seq), jnp.int32),
        ),
        in_specs=[SMEM, VMEM, VMEM, VMEM, VMEM],
        out_specs=(VMEM, SMEM, VMEM, VMEM),
        compiler_params=pltpu.CompilerParams(vmem_limit_bytes=VMEM_LIMIT),
        name="round_qkv",
    )(lengths, segments, w_qkv, b_qv, b_in)


def round_rest_kernel(
    wo_hbm, wi_hbm, wb_hbm, x_hbm, out_in, back, second, x_low, *scratch
):
    wo_in, wi_in, wb_in, x_in, oi_out, b_out, s_out, x_out, in_sem, out_sem = scratch
    rows, width = wo_in.shape
    half = width // 2
    own_side = lax.axis_index("dp") & 1
    loads, stores = [], []

    def load(source, target):
        loads.append(pltpu.make_async_copy(source, target, in_sem.at[len(loads)]))
        loads[-1].start()

    def store(source, target):
        stores.append(pltpu.make_async_copy(source, target, out_sem.at[len(stores)]))
        stores[-1].start()

    load(wo_hbm, wo_in)
    load(wi_hbm, wi_in)
    for side in (own_side, 1 - own_side):
        at = pl.ds(pl.multiple_of(side * half, half), half)
        load(wb_hbm.at[at, :], wb_in.at[at, :])
    quarters = [pl.ds(i * x_in.shape[0] // 4, x_in.shape[0] // 4) for i in range(4)]
    for at in quarters:
        load(x_hbm.at[at, :], x_in.at[at, :])
    loads[0].wait()
    for c in range(2):
        oi_out[c * rows : (c + 1) * rows, :] = wo_in[:, c * half : (c + 1) * half].astype(LOW)
    loads[1].wait()
    sides = [
        pl.ds(pl.multiple_of(side * half, half), half) for side in (own_side, 1 - own_side)
    ]
    oi_out[2 * rows :, :] = wi_in[:, sides[0]].astype(LOW)
    store(oi_out, out_in)
    s_out[:width, :] = wi_in[:, sides[1]].astype(LOW)
    for n, (to_back, base) in enumerate(((b_out, 0), (s_out, width))):
        loads[2 + n].wait()
        for c in range(2):
            start = base + c * half
            strip = wb_in[sides[n], c * half : (c + 1) * half]
            to_back[start : start + half, :] = strip.astype(LOW)
        store(to_back, (back, second)[n])
    for n, at in enumerate(quarters):
        loads[4 + n].wait()
        x_out[at, :] = x_in[at, :].astype(LOW)
        store(x_out.at[at, :], x_low.at[at, :])
    for copy in stores:
        copy.wait()


def round_rest(w_out, w_in, w_back, x):
    rows, width = w_out.shape
    half = width // 2
    shapes = ((2 * rows + width, half), (width, half), (2 * width, half), x.shape)
    return pl.pallas_call(
        round_rest_kernel,
        out_shape=tuple(shape(dims, LOW) for dims in shapes),
        in_specs=[HBM] * 4,
        out_specs=(HBM,) * 4,
        scratch_shapes=[pltpu.VMEM(a.shape, F32) for a in (w_out, w_in, w_back, x)]
        + [pltpu.VMEM(dims, LOW) for dims in shapes]
        + [pltpu.SemaphoreType.DMA((8,)), pltpu.SemaphoreType.DMA((7,))],
        compiler_params=pltpu.CompilerParams(vmem_limit_bytes=VMEM_LIMIT),
        name="round_rest",
    )(w_out, w_in, w_back, x)


def make_bias(bias_ref, block, low, count, code_ref, seg_ref):
    dims = (count * KB, QB)
    codes = code_ref[pl.ds(pl.multiple_of(low * KB, KB), count * KB), :]
    segs = seg_ref[:, pl.ds(pl.multiple_of(block * QB, QB), QB)]
    key_at = low * KB + lax.broadcasted_iota(jnp.int32, dims, 0)
    query_at = block * QB + lax.broadcasted_iota(jnp.int32, dims, 1)
    allowed = (codes == segs) | (key_at == query_at)
    bias_ref[: count * KB, :] = jnp.where(allowed, 0.0, MASKED_SCORE)


def one_head(values, head):
    lane = lax.broadcasted_iota(jnp.int32, values.shape, 1)
    keep = (lane < HD) if head == 0 else (lane >= HD)
    return jnp.where(keep, values, jnp.zeros_like(values))


def forward_kernel(
    table_ref,
    x_ref,
    w0_ref,
    w1_ref,
    code_ref,
    seg_ref,
    q_ref,
    k_ref,
    v_ref,
    ctx_ref,
    lse_ref,
    weights,
    biases,
    vt_ref,
    bias_ref,
):
    block = pl.program_id(0)
    low, total = table_ref[0, block], table_ref[1, block]
    piece = (w0_ref.shape[0] - 16) // 3
    pairs = 2 * piece // 128

    @pl.when(block == 0)
    def _():
        for i in range(3):
            for n, ref in enumerate((w0_ref, w1_ref)):
                rows = ref[i * piece : (i + 1) * piece, :]
                weights[i, n * piece : (n + 1) * piece, :] = rows
        lane = lax.broadcasted_iota(jnp.int32, (1, x_ref.shape[1]), 1)
        for i in (0, 2):
            base = 3 * piece + (3 if i == 0 else 6)
            both = [
                sum(ref[base + part : base + part + 1, :].astype(F32) for part in range(3))
                for ref in (w0_ref, w1_ref)
            ]
            row = jnp.where(lane < piece, both[0], pltpu.roll(both[1], piece, 1))
            biases[i : i + 1, :] = row[:, : 2 * piece]
        biases[1:2, :] = jnp.zeros((1, 2 * piece), F32)

        def project(b, carry):
            at = pl.ds(pl.multiple_of(b * QB, QB), QB)
            for i, ref in enumerate((q_ref, k_ref, v_ref)):
                ref[at, :] = (dot(x_ref[at, :], weights[i], NT) + biases[i : i + 1, :]).astype(LOW)
            vt_ref[:, at] = v_ref[at, :].T
            return carry

        lax.fori_loop(0, x_ref.shape[0] // QB, project, 0)

    def run(count):
        make_bias(bias_ref, block, low, count, code_ref, seg_ref)
        bias = bias_ref[: count * KB, :]
        rows = pl.ds(pl.multiple_of(low * KB, KB), count * KB)
        queries = pl.ds(pl.multiple_of(block * QB, QB), QB)

        def scores(head):
            lanes = slice(head // 2 * 128, head // 2 * 128 + 128)
            query = q_ref[queries, lanes] * jnp.asarray(0.125, LOW)
            return dot(k_ref[rows, lanes], one_head(query, head % 2), NT) + bias

        def soft(values, head):
            peak = jnp.max(values, axis=0, keepdims=True)
            powers = jnp.exp(values - peak)
            mass = jnp.sum(powers, axis=0, keepdims=True)
            lse_ref[head : head + 1, :] = peak + jnp.log(mass)
            return (powers * (1.0 / mass)).astype(LOW)

        outs = []

        def context(probs, head):
            outs.append(dot(vt_ref[head * HD : (head + 1) * HD, rows], probs))
            if head % 2 == 1:
                both = jnp.concatenate(outs[-2:], axis=0).T
                ctx_ref[:, head // 2 * 128 : head // 2 * 128 + 128] = both.astype(LOW)

        values, probs = scores(0), None
        for head in range(2 * pairs):
            later = scores(head + 1) if head + 1 < 2 * pairs else None
            now = soft(values, head)
            if head > 0:
                context(probs, head - 1)
            values, probs = later, now
        context(probs, 2 * pairs - 1)

    for count in range(QB // KB, k_ref.shape[0] // KB + 1):
        pl.when(total == count)(functools.partial(run, count))


def backward_kernel(carried, table_ref, q_ref, k_ref, v_ref, g_ref, lse_ref, code_ref, seg_ref, *refs):
    block = pl.program_id(0)
    refs = list(refs)
    if carried:
        source, target = refs.pop(0), refs.pop(3)
        target[...] = source[...]
    dq_ref, dk_ref, dv_ref, kt_ref, bias_ref, dk_sum, dv_sum = refs
    low, total = table_ref[0, block], table_ref[1, block]
    heads = q_ref.shape[1] // HD

    @pl.when(block == 0)
    def _():
        kt_ref[...] = k_ref[...].T
        dk_sum[...] = jnp.zeros_like(dk_sum)
        dv_sum[...] = jnp.zeros_like(dv_sum)

    def run(count):
        make_bias(bias_ref, block, low, count, code_ref, seg_ref)
        bias = bias_ref[: count * KB, :]
        rows = pl.ds(pl.multiple_of(low * KB, KB), count * KB)

        def first(head):
            lanes = slice(head // 2 * 128, head // 2 * 128 + 128)
            query = one_head(q_ref[:, lanes] * jnp.asarray(0.125, LOW), head % 2)
            grad = one_head(g_ref[:, lanes], head % 2)
            scores = dot(k_ref[rows, lanes], query, NT) + bias
            return scores, dot(v_ref[rows, lanes], grad, NT), query, grad

        def second(head, scores, prob_grad, query, grad):
            probs = jnp.exp(scores - lse_ref[head : head + 1, :])
            delta = jnp.sum(probs * prob_grad, axis=0, keepdims=True)
            return probs.astype(LOW), (probs * (prob_grad - delta)).astype(LOW), query, grad

        outs = []

        def third(head, probs, score_grad, query, grad):
            lanes = slice(head // 2 * 128, head // 2 * 128 + 128)
            dv_sum[rows, lanes] += dot(probs, grad)
            dk_sum[rows, lanes] += dot(score_grad, query)
            outs.append(dot(kt_ref[head * HD : (head + 1) * HD, rows], score_grad))
            if head % 2 == 1:
                both = jnp.concatenate(outs[-2:], axis=0).T * 0.125
                dq_ref[:, lanes] = both.astype(LOW)

        start, middle_of = first(0), None
        for head in range(heads):
            later = first(head + 1) if head + 1 < heads else None
            now = second(head, *start)
            if head > 0:
                third(head - 1, *middle_of)
            start, middle_of = later, now
        third(heads - 1, *middle_of)

    for count in range(QB // KB, k_ref.shape[0] // KB + 1):
        pl.when(total == count)(functools.partial(run, count))

    @pl.when(block == pl.num_programs(0) - 1)
    def _():
        dk_ref[...] = dk_sum[...].astype(LOW)
        dv_ref[...] = dv_sum[...].astype(LOW)


def attend_forward(table, x, first, second, code, seg):
    seq, width = x.shape
    piece = (first.shape[0] - 16) // 3
    heads, blocks = 2 * piece // HD, seq // QB
    whole = lambda i, t: (0, 0)
    column = pl.BlockSpec((seq, 2 * piece), whole)
    return pl.pallas_call(
        forward_kernel,
        out_shape=(shape((seq, 2 * piece), LOW),) * 4 + (shape((8, seq), F32),),
        grid_spec=pltpu.PrefetchScalarGridSpec(
            num_scalar_prefetch=1,
            grid=(blocks,),
            in_specs=[
                pl.BlockSpec((seq, width), whole),
                pl.BlockSpec(first.shape, whole),
                pl.BlockSpec(second.shape, whole),
                pl.BlockSpec((seq, 1), whole),
                pl.BlockSpec((1, seq), whole),
            ],
            out_specs=[
                column,
                column,
                column,
                pl.BlockSpec((QB, 2 * piece), lambda i, t: (i, 0)),
                pl.BlockSpec((8, QB), lambda i, t: (0, i)),
            ],
            scratch_shapes=[
                pltpu.VMEM((3, 2 * piece, width), LOW),
                pltpu.VMEM((3, 2 * piece), F32),
                pltpu.VMEM((2 * piece, seq), LOW),
                pltpu.VMEM((seq, QB), F32),
            ],
        ),
        compiler_params=pltpu.CompilerParams(vmem_limit_bytes=VMEM_LIMIT),
        cost_estimate=pl.CostEstimate(
            flops=16 * seq * seq * piece + 12 * seq * width * piece,
            bytes_accessed=16 * seq * piece,
            transcendentals=seq * seq * heads // 2,
        ),
        name="attend_forward",
    )(table, x, first, second, code, seg)


def attend_backward(table, q, k, v, grad, lse, code, seg, *carried):
    seq, width = grad.shape
    blocks = seq // QB
    block = pl.BlockSpec((QB, width), lambda i, t: (i, 0))
    column = pl.BlockSpec((seq, width), lambda i, t: (0, 0))
    return pl.pallas_call(
        functools.partial(backward_kernel, len(carried)),
        out_shape=(shape((seq, width), LOW),) * 3 + tuple(shape(c.shape, c.dtype) for c in carried),
        grid_spec=pltpu.PrefetchScalarGridSpec(
            num_scalar_prefetch=1,
            grid=(blocks,),
            in_specs=[
                block,
                column,
                column,
                block,
                pl.BlockSpec((8, QB), lambda i, t: (0, i)),
                pl.BlockSpec((seq, 1), lambda i, t: (0, 0)),
                pl.BlockSpec((1, seq), lambda i, t: (0, 0)),
            ]
            + [pl.BlockSpec((QB, c.shape[1]), lambda i, t: (i, 0)) for c in carried],
            out_specs=[block, column, column]
            + [pl.BlockSpec((QB, c.shape[1]), lambda i, t: (i, 0)) for c in carried],
            scratch_shapes=[
                pltpu.VMEM((width, seq), LOW),
                pltpu.VMEM((seq, QB), F32),
                pltpu.VMEM((seq, width), F32),
                pltpu.VMEM((seq, width), F32),
            ],
        ),
        compiler_params=pltpu.CompilerParams(vmem_limit_bytes=VMEM_LIMIT),
        cost_estimate=pl.CostEstimate(
            flops=16 * seq * seq * width,
            bytes_accessed=16 * seq * width,
            transcendentals=seq * seq * width // 128,
        ),
        name="attend_backward",
    )(table, q, k, v, grad, lse, code, seg, *carried)


def gelu_parts(pre):
    size = 1.0 + PHI_STEP * jnp.abs(pre)
    t = pl.reciprocal(size, approx=True)
    t = t * (2.0 - size * t)
    poly = PHI[6] * t + PHI[5]
    for factor in PHI[4::-1]:
        poly = poly * t + factor
    bell = jnp.exp2((-0.5 * math.log2(math.e)) * (pre * pre))
    tail = poly * t * bell
    cdf = jnp.where(pre < 0, tail, 1.0 - tail)
    return pre * cdf, cdf + (pre * 0.3989422804014327) * bell


def norm_stats(values):
    width = values.shape[-1]
    mean = jnp.sum(values, axis=-1, keepdims=True) * (1.0 / width)
    centred = values - mean
    spread = jnp.sum(centred * centred, axis=-1, keepdims=True) * (1.0 / width)
    rate = lax.rsqrt(spread + LN_EPSILON)
    return centred * rate, rate


def norm_back(grad, gain, xhat, rate):
    width = grad.shape[-1]
    scaled = grad * gain
    mean = jnp.sum(scaled, axis=-1, keepdims=True) * (1.0 / width)
    along = jnp.sum(scaled * xhat, axis=-1, keepdims=True) * (1.0 / width)
    return rate * (scaled - mean - xhat * along)


def column_sum(values):
    return jnp.sum(values, axis=0, keepdims=True)


def middle_kernel(
    total_slots,
    dp_bits,
    lengths_ref,
    ctx_a,
    ctx_b,
    gains,
    shifts,
    x_hbm,
    teacher_hbm,
    qa,
    qb,
    qc,
    qd,
    outin_own,
    outin_core,
    outin_far,
    back_own,
    back_core,
    second_own,
    second_core,
    out_hbm,
    dh_hbm,
    cg_a,
    cg_b,
    core_hbm,
    to_x,
    to_y,
    rest,
    out_send_a,
    out_send_b,
    out_keep_a,
    out_keep_b,
    sums,
    bias_sums,
    count_ref,
    outin_far_core,
    in_far,
    back_far,
    in_far_core,
    back_far_core,
    w_in,
    w_back,
    w_out,
    bias_parts,
    bias_in,
    xhat_one,
    rate_one,
    mid_low,
    hidden,
    slope,
    acc,
    dh_low,
    pre_grad,
    rows_in,
    rows_out,
    stage16,
    stage32,
    from_core,
    held,
    w_sem,
    in_sem,
    out_sem,
    load_sem,
    store_sem,
    send_sem,
    recv_sem,
    count_send,
    count_recv,
    far_send,
    far_recv,
):
    seq, width = acc.shape
    blocks = seq // RB
    half = width // 2
    out_rows = w_out.shape[0] // 4
    units = w_in.shape[2]
    side = units // 2
    core_at, y_at, x_at = partner("tensor", 0), partner("tensor", 1), partner("dp", 0)
    greet([core_at, y_at] + [partner("dp", bit) for bit in range(dp_bits)])

    def far_copy(n, source, target, device):
        return pltpu.make_async_remote_copy(
            src_ref=source,
            dst_ref=target,
            send_sem=far_send.at[n],
            recv_sem=far_recv.at[n],
            device_id=device,
            device_id_type=pl.DeviceIdType.MESH,
        )

    in_at = pl.ds(2 * out_rows, width)
    far = [
        far_copy(
            0,
            outin_far.at[pl.ds(0, 2 * out_rows), :],
            outin_far_core.at[pl.ds(0, 2 * out_rows), :],
            core_at,
        ),
        far_copy(1, back_own, back_far.at[0], y_at),
        far_copy(
            2,
            second_own.at[pl.ds(width, side), :],
            back_far.at[1, pl.ds(0, side), :],
            y_at,
        ),
        far_copy(3, outin_far.at[in_at, :], in_far, x_at),
        far_copy(4, in_far, in_far_core, core_at),
        far_copy(5, back_far.at[0], back_far_core.at[0], core_at),
        far_copy(6, back_far.at[1], back_far_core.at[1], core_at),
        far_copy(
            7,
            back_far.at[0, pl.ds(side, side), :],
            back_far.at[1, pl.ds(side, side), :],
            x_at,
        ),
        far_copy(8, outin_far.at[in_at, :], outin_far_core.at[in_at, :], core_at),
    ]
    for copy in far[:4] + far[8:]:
        copy.start()
    out_in = (outin_own, outin_core, outin_far, outin_far_core)
    in_parts = tuple(ref.at[in_at, :] for ref in out_in)
    in_other = (
        second_own.at[pl.ds(0, width), :],
        second_core.at[pl.ds(0, width), :],
        in_far,
        in_far_core,
    )
    back_parts = (back_own, back_core, back_far.at[0], back_far_core.at[0])
    back_other = (
        second_own.at[pl.ds(width, width), :],
        second_core.at[pl.ds(width, width), :],
        back_far.at[1],
        back_far_core.at[1],
    )

    def rows(i):
        return pl.ds(i * RB, RB)

    def fetch(source, i, slot):
        return pltpu.make_async_copy(source.at[rows(i), :], rows_in.at[slot], in_sem.at[slot])

    def out_weights(p, c):
        return pltpu.make_async_copy(
            out_in[p].at[pl.ds(c * out_rows, out_rows), :],
            w_out.at[pl.ds(p * out_rows, out_rows), pl.ds(c * half, half)],
            w_sem.at[p, c],
        )

    def bias_rows(p):
        source = (qa, qb, qc, qd)[p]
        return pltpu.make_async_copy(
            source.at[pl.ds(source.shape[0] - 16, 16), :], bias_parts.at[p], w_sem.at[p, 8]
        )

    def load_in(source, p, r):
        return pltpu.make_async_copy(
            source, w_in.at[p, :, pl.ds(r * side, side)], w_sem.at[p, 2 + 3 * r]
        )

    def load_back(source, p, r, c):
        return pltpu.make_async_copy(
            source.at[pl.ds(c * side, side), :],
            w_back.at[p, pl.ds(r * side, side), pl.ds(c * half, half)],
            w_sem.at[p, 3 + 3 * r + c],
        )

    def ffn_weights(p):
        load_in(in_parts[p], p, 0).start()
        load_in(in_other[p], p, 1).start()
        for c in range(2):
            load_back(back_parts[p], p, 0, c).start()
            load_back(back_other[p], p, 1, c).start()

    early = [out_weights(p, c) for p in range(4) for c in range(2)]
    for copy in early[:6]:
        copy.start()
    fetch(x_hbm, 0, 0).start()
    for p in range(4):
        bias_rows(p).start()
    for p in range(2):
        ffn_weights(p)

    def count_step(bit):
        return pltpu.make_async_remote_copy(
            src_ref=held.at[2 * bit],
            dst_ref=held.at[2 * bit + 1],
            send_sem=count_send.at[bit],
            recv_sem=count_recv.at[bit],
            device_id=partner("dp", bit),
            device_id_type=pl.DeviceIdType.MESH,
        )

    tokens = jnp.full(held.shape[1:], 0, jnp.int32)
    for i in range(lengths_ref.shape[0]):
        tokens += lengths_ref[i]
    held[0] = tokens
    count_step(0).start()

    def count_on(bit):
        count_step(bit).wait()
        held[2 * bit + 2] = held[2 * bit] + held[2 * bit + 1]
        if bit + 1 < dp_bits:
            count_step(bit + 1).start()

    far[0].wait_recv()
    for copy in early[6:]:
        copy.start()
    for copy in early:
        copy.wait()

    for i in range(blocks):
        if i + 1 < blocks:
            fetch(x_hbm, i + 1, (i + 1) % 2).start()
        fetch(x_hbm, i, i % 2).wait()
        context = jnp.concatenate([ctx_a[rows(i), :], ctx_b[rows(i), :]], axis=1)
        xhat, rate = norm_stats(dot(context, w_out[...]) + shifts[0:1, :] + rows_in[i % 2])
        xhat_one[rows(i), :] = xhat
        rate_one[rows(i), :] = rate
        mid_low[rows(i), :] = (xhat * gains[0:1, :] + shifts[1:2, :]).astype(LOW)
        acc[rows(i), :] = jnp.zeros((RB, width), F32)
    fetch(teacher_hbm, 0, 0).start()
    for p in range(4):
        bias_rows(p).wait()
        part = bias_parts[p, 0:3, :].astype(F32)
        bias_in[p] = part[0:1] + part[1:2] + part[2:3]

    def up(p, carry):
        for bit in range(min(dp_bits, 4)):
            pl.when(p == bit)(functools.partial(count_on, bit))

        @pl.when(p == 1)
        def _():
            far[1].wait_recv()
            far[7].start()
            far[5].start()
            far[3].wait_recv()
            far[4].start()

        @pl.when(p == 2)
        def _():
            far[2].wait_recv()
            far[7].wait_recv()
            far[6].start()
            ffn_weights(2)

        @pl.when(p == 3)
        def _():
            for n in (8, 4, 5, 6):
                far[n].wait_recv()
            ffn_weights(3)

        for r in range(2):
            load_in(in_other[0], p, r).wait()
            for c in range(2):
                load_back(back_own, p, r, c).wait()
        last = seq // FR - 1
        strips = [slice(c, c + 256) for c in range(0, units, 256)]

        def lift(k, cols):
            pre = dot(mid_low[pl.ds(k * FR, FR), :], w_in[p, :, cols])
            return pre + bias_in[p, :, cols]

        def lower(k, acts, cols):
            acc[pl.ds(k * FR, FR), cols] += dot(acts, w_back[p, :, cols])

        pre, before = [lift(0, cols) for cols in strips], None
        for k in range(last + 1):
            later, acts = [], []
            for c, cols in enumerate(strips):
                if k < last:
                    later.append(lift(k + 1, cols))
                act, der = gelu_parts(pre[c])
                acts.append(act.astype(LOW))
                hidden[p, pl.ds(k * FR, FR), cols] = acts[c]
                slope[p, pl.ds(k * FR, FR), cols] = der
                if k > 0:
                    lower(k - 1, before, cols)
            pre, before = later, jnp.concatenate(acts, axis=1)
        for cols in strips:
            lower(last, before, cols)
        return carry

    lax.fori_loop(0, 4, up, 0)
    for bit in range(4, dp_bits):
        count_on(bit)
    count_ref[...] = held[2 * dp_bits]

    zero = jnp.zeros((1, width), F32)
    squares, gain_two, shift_two, shift_mid = zero, zero, zero, zero
    scale = total_slots / held[2 * dp_bits, 0:1, 0:1].astype(F32)
    valid = lengths_ref[lax.axis_index("tensor")]
    stores = []
    for i in range(blocks):
        if i + 1 < blocks:
            fetch(teacher_hbm, i + 1, (i + 1) % 2).start()
        fetch(teacher_hbm, i, i % 2).wait()
        mid = xhat_one[rows(i), :] * gains[0:1, :] + shifts[1:2, :]
        xhat, rate = norm_stats(acc[rows(i), :] + shifts[2:3, :] + mid)
        output = xhat * gains[1:2, :] + shifts[3:4, :]
        if i >= 2:
            stores[i - 2].wait()
        rows_out[i % 2] = output
        stores.append(
            pltpu.make_async_copy(rows_out.at[i % 2], out_hbm.at[rows(i), :], out_sem.at[i % 2])
        )
        stores[i].start()
        live = (i * RB + lax.broadcasted_iota(jnp.int32, (RB, 1), 0)) < valid
        distance = jnp.where(live, output - rows_in[i % 2], 0.0)
        squares += column_sum(distance * distance)
        out_grad = scale * distance
        gain_two += column_sum(out_grad * xhat)
        shift_two += column_sum(out_grad)
        dh_two = norm_back(out_grad, gains[1:2, :], xhat, rate)
        shift_mid += column_sum(dh_two)
        acc[rows(i), :] = dh_two
        dh_low[rows(i), :] = dh_two.astype(LOW)
    for store in stores[-2:]:
        store.wait()

    sides = (pl.ds(0, side), pl.ds(side, side))

    def ffn_back(p):
        total = jnp.zeros((1, units), F32)

        def lift(k):
            return dot(dh_low[pl.ds(k * FR, FR), :], w_back[p], NT)

        def lower(k):
            at = pl.ds(k * FR, FR)
            acc[at, :] += dot(pre_grad[at, :], w_in[p], NT)

        raised = lift(0)
        for k in range(seq // FR):
            later = lift(k + 1) if k + 1 < seq // FR else None
            at = pl.ds(k * FR, FR)
            grad = (raised * slope[p, at, :]).astype(LOW)
            pre_grad[at, :] = grad
            total += column_sum(grad.astype(F32))
            if k > 0:
                lower(k - 1)
            raised = later
        lower(seq // FR - 1)
        bias_sums[pl.ds(p, 1), :] = total

    def to_core(pair, w):
        return pltpu.make_async_remote_copy(
            src_ref=stage16.at[w],
            dst_ref=core_hbm.at[pair, w],
            send_sem=send_sem.at[w],
            recv_sem=recv_sem.at[pair, w],
            device_id=core_at,
            device_id_type=pl.DeviceIdType.MESH,
        )

    def away(n, carry):
        p = 2 * n + 1
        ffn_back(p)

        @pl.when(n > 0)
        def _():
            for w in range(2):
                to_core(0, w).wait_send()

        stage16[0] = dot(mid_low[...], pre_grad[...], TN).astype(LOW)
        stage16[1] = dot(hidden[p], dh_low[...], TN).astype(LOW)
        for w in range(2):
            to_core(n, w).start()
        return carry

    lax.fori_loop(0, 2, away, 0)

    def in_moves(pair):
        return [
            pltpu.make_async_copy(stage32.at[0, :, sides[0]], rest.at[pair], store_sem.at[0]),
            pltpu.make_async_copy(stage16.at[0, :, sides[1]], to_x.at[pair], store_sem.at[1]),
        ]

    def back_moves(stage, target):
        return [
            pltpu.make_async_copy(
                stage.at[1, sides[r], sides[c]],
                target.at[r, sides[c], :],
                store_sem.at[2 + 2 * r + c],
            )
            for r in range(2)
            for c in range(2)
        ]

    moves = {1: in_moves(1) + back_moves(stage16, to_y), 0: in_moves(0) + back_moves(stage32, rest.at[pl.ds(2, 2)])}

    def home(n, carry):
        pair = n
        p = 2 * pair
        ffn_back(p)
        for w in range(2):
            to_core(pair, w).wait_recv()
            pltpu.make_async_copy(core_hbm.at[pair, w], from_core.at[w], load_sem.at[w]).start()

        @pl.when(n == 0)
        def _():
            for w in range(2):
                to_core(1, w).wait_send()

        @pl.when(n == 1)
        def _():
            for copy in moves[0]:
                copy.wait()

        stage32[0] = dot(mid_low[...], pre_grad[...], TN)
        stage32[1] = dot(hidden[p], dh_low[...], TN)
        for w in range(2):
            pltpu.make_async_copy(core_hbm.at[pair, w], from_core.at[w], load_sem.at[w]).wait()
            for k in range(0, width, 128):
                total = stage32[w, k : k + 128, :] + from_core[w, k : k + 128, :].astype(F32)
                stage32[w, k : k + 128, :] = total
                stage16[w, k : k + 128, :] = total.astype(LOW)

        for turn in range(2):

            @pl.when(n == turn)
            def _(turn=turn):
                for copy in moves[turn]:
                    copy.start()

        return carry

    lax.fori_loop(0, 2, home, 0)

    gain_one, shift_one, shift_out = zero, zero, zero
    stores = []
    for i in range(blocks):
        grad, xhat = acc[rows(i), :], xhat_one[rows(i), :]
        gain_one += column_sum(grad * xhat)
        shift_one += column_sum(grad)
        dh_one = norm_back(grad, gains[0:1, :], xhat, rate_one[rows(i), :])
        shift_out += column_sum(dh_one)
        if i >= 2:
            stores[i - 2].wait()
        rows_out[i % 2] = dh_one
        stores.append(
            pltpu.make_async_copy(rows_out.at[i % 2], dh_hbm.at[rows(i), :], out_sem.at[i % 2])
        )
        stores[i].start()
        dh_one = dh_one.astype(LOW)
        dh_low[rows(i), :] = dh_one
        grad = dot(dh_one, w_out[...], NT).astype(LOW)
        cg_a[rows(i), :] = grad[:, :half]
        cg_b[rows(i), :] = grad[:, half:]
    for context, out_keep, out_send in (
        (ctx_a, out_keep_a, out_send_a),
        (ctx_b, out_keep_b, out_send_b),
    ):
        grad = dot(context[...], dh_low[...], TN)
        out_keep[...] = grad[:out_rows]
        out_send[...] = grad[out_rows:].astype(LOW)
    sums[...] = jnp.concatenate(
        [gain_one, gain_two, shift_out, shift_one, shift_mid, shift_two, squares, zero], axis=0
    )
    for store in stores[-2:]:
        store.wait()
    for copy in moves[1]:
        copy.wait()
    for copy in far:
        copy.wait_send()


def middle(
    total_slots, lengths, ctx_a, ctx_b, gains, shifts, x, teacher, near, out_in, back, second
):
    seq, width = x.shape
    half = width // 2
    out_rows = ctx_a.shape[1] // 2
    units = width
    dp_bits = bits_of("dp")
    slab = (width, units // 2)
    return pl.pallas_call(
        functools.partial(middle_kernel, float(total_slots), dp_bits),
        out_shape=(
            shape((seq, width), F32),
            shape((seq, width), F32),
            shape((seq, half), LOW),
            shape((seq, half), LOW),
            shape((2, 2, width, units), LOW),
            shape((2,) + slab, LOW),
            shape((2,) + slab, LOW),
            shape((4,) + slab, F32),
            shape((out_rows, width), LOW),
            shape((out_rows, width), LOW),
            shape((out_rows, width), F32),
            shape((out_rows, width), F32),
            shape((8, width), F32),
            shape((4, units), F32),
            shape((8, 128), jnp.int32),
            shape(out_in[0].shape, LOW),
            shape(slab, LOW),
            shape((2,) + slab, LOW),
            shape(slab, LOW),
            shape((2,) + slab, LOW),
        ),
        in_specs=[SMEM, VMEM, VMEM, VMEM, VMEM, HBM, HBM] + [HBM] * 11,
        out_specs=(HBM, HBM, VMEM, VMEM, HBM, HBM, HBM, HBM) + (VMEM,) * 7 + (HBM,) * 5,
        scratch_shapes=[
            pltpu.VMEM((4, width, units), LOW),
            pltpu.VMEM((4, units, width), LOW),
            pltpu.VMEM((4 * out_rows, width), LOW),
            pltpu.VMEM((4, 16, width), LOW),
            pltpu.VMEM((4, 1, units), F32),
            pltpu.VMEM((seq, width), F32),
            pltpu.VMEM((seq, 1), F32),
            pltpu.VMEM((seq, width), LOW),
            pltpu.VMEM((4, seq, units), LOW),
            pltpu.VMEM((4, seq, units), F32),
            pltpu.VMEM((seq, width), F32),
            pltpu.VMEM((seq, width), LOW),
            pltpu.VMEM((seq, units), LOW),
            pltpu.VMEM((2, RB, width), F32),
            pltpu.VMEM((2, RB, width), F32),
            pltpu.VMEM((2, width, units), LOW),
            pltpu.VMEM((2, width, units), F32),
            pltpu.VMEM((2, width, units), LOW),
            pltpu.VMEM((2 * dp_bits + 1, 8, 128), jnp.int32),
            pltpu.SemaphoreType.DMA((4, 9)),
            pltpu.SemaphoreType.DMA((2,)),
            pltpu.SemaphoreType.DMA((2,)),
            pltpu.SemaphoreType.DMA((2,)),
            pltpu.SemaphoreType.DMA((6,)),
            pltpu.SemaphoreType.DMA((2,)),
            pltpu.SemaphoreType.DMA((2, 2)),
            pltpu.SemaphoreType.DMA((dp_bits,)),
            pltpu.SemaphoreType.DMA((dp_bits,)),
            pltpu.SemaphoreType.DMA((9,)),
            pltpu.SemaphoreType.DMA((9,)),
        ],
        compiler_params=pltpu.CompilerParams(
            vmem_limit_bytes=VMEM_LIMIT, collective_id=1, has_side_effects=True
        ),
        cost_estimate=pl.CostEstimate(
            flops=6 * seq * width * (8 * units + width),
            bytes_accessed=30 << 20,
            transcendentals=2 * seq * 4 * units,
        ),
        name="middle",
    )(lengths, ctx_a, ctx_b, gains, shifts, x, teacher, *near, *out_in, *back, *second)


def add_rows(out, terms, chunk=96):
    rows = out.shape[0]
    chunk = min(chunk, rows)

    def step(i, carry):
        at = pl.ds(pl.multiple_of(i * chunk, chunk), chunk)
        total = terms[0][at, :].astype(F32)
        for term in terms[1:]:
            total += term[at, :].astype(F32)
        out[at, :] = total.astype(out.dtype)
        return carry

    lax.fori_loop(0, rows // chunk, step, 0)


def cross_rows(x_ref, grads, okeep, osend, side, cross, keep, send, bias_ref, emit, between=None):
    half = x_ref.shape[1] // 2
    piece = grads[0].shape[1] // 2
    mine = pl.ds(pl.multiple_of(side * half, half), half)
    other = pl.ds(pl.multiple_of((1 - side) * half, half), half)
    sides = ((1, other), (0, mine))
    at = pl.ds(3 * piece, osend.shape[0])
    for n, lanes in sides:
        keep[n, at, :] = okeep[:, lanes]
        send[n, at, :] = osend[:, lanes].astype(send.dtype)
        emit(n, at)
    for i in range(3):
        cross[...] = dot(grads[i][...], x_ref[...], TN)
        at = pl.ds(i * piece, piece)
        for n, lanes in sides:
            keep[n, at, :] = cross[:piece, lanes]
            send[n, at, :] = cross[piece:, lanes].astype(send.dtype)
            emit(n, at)
        bias_ref[i : i + 1, :] = column_sum(grads[i][...].astype(F32))
        if i == 0 and between is not None:
            between()


def far_kernel(
    x_ref,
    dq,
    dk,
    dv,
    osend,
    okeep,
    away,
    away_first,
    bias_ref,
    keep,
    send,
    core,
    cross,
    send_sem,
    recv_sem,
):
    core_at = partner("tensor", 0)
    greet([core_at])
    bias_ref[...] = jnp.zeros(bias_ref.shape, F32)
    copies = []

    def emit(n, rows):
        at = len(copies)
        copies.append(
            pltpu.make_async_remote_copy(
                src_ref=send.at[n, rows, :],
                dst_ref=core.at[n, rows, :],
                send_sem=send_sem.at[at],
                recv_sem=recv_sem.at[at],
                device_id=core_at,
                device_id_type=pl.DeviceIdType.MESH,
            )
        )
        copies[at].start()

    side = lax.axis_index("dp") & 1
    cross_rows(x_ref, (dq, dk, dv), okeep, osend, side, cross, keep, send, bias_ref, emit)
    for n, out in ((1, away_first), (0, away)):
        for copy in copies[1 - n :: 2]:
            copy.wait_recv()
        add_rows(out, [keep.at[n], core.at[n]])
    for copy in copies:
        copy.wait_send()


def far_projections(x, grads, osend, okeep):
    seq, width = x.shape
    half = width // 2
    piece = grads[0].shape[1] // 2
    slabs = (2, width, half)
    return pl.pallas_call(
        far_kernel,
        out_shape=(shape(slabs[1:], LOW), shape(slabs[1:], LOW), shape((8, 2 * piece), F32)),
        in_specs=[VMEM] * 6,
        out_specs=(VMEM, VMEM, VMEM),
        scratch_shapes=[
            pltpu.VMEM(slabs, F32),
            pltpu.VMEM(slabs, F32),
            pltpu.VMEM(slabs, F32),
            pltpu.VMEM((2 * piece, width), F32),
            pltpu.SemaphoreType.DMA((8,)),
            pltpu.SemaphoreType.DMA((8,)),
        ],
        compiler_params=pltpu.CompilerParams(
            vmem_limit_bytes=VMEM_LIMIT, collective_id=3, has_side_effects=True
        ),
        cost_estimate=pl.CostEstimate(
            flops=12 * seq * width * piece, bytes_accessed=10 << 20, transcendentals=0
        ),
        name="far_projections",
    )(x, *grads, osend, okeep)


def finish_kernel(
    dp_bits,
    x_hbm,
    w0_hbm,
    w1_hbm,
    w2_hbm,
    w3_hbm,
    dqa_hbm,
    dka_hbm,
    dva_hbm,
    dqb_hbm,
    dkb_hbm,
    dvb_hbm,
    osend,
    okeep,
    dh_hbm,
    rest,
    ffn_x,
    ffn_y,
    in_z,
    back_x,
    away,
    qkv_y,
    sums_ref,
    bias_in_ref,
    bias_far,
    gx_hbm,
    result,
    small_out,
    x_ref,
    w0,
    w1,
    w2,
    w3,
    dqa,
    dka,
    dva,
    dqb,
    dkb,
    dvb,
    own,
    own16,
    in_send,
    in_recv,
    keep,
    send,
    core,
    y_recv,
    x_send,
    x_recv,
    total,
    z_send,
    z_recv,
    last_send,
    last_recv,
    extra,
    bias_ref,
    small_held,
    rows_in,
    rows_out,
    cross,
    operand_sem,
    load_sem,
    send_sem,
    recv_sem,
    in_sem,
    out_sem,
):
    seq, width = x_ref.shape
    half = width // 2
    piece = dqa.shape[1] // 2
    blocks = seq // RB
    place = lax.axis_index("dp")
    index = lax.axis_index("tensor")
    side = place & 1
    core_at, y_at = partner("tensor", 0), partner("tensor", 1)
    dp_at = [partner("dp", bit) for bit in range(dp_bits)]
    greet([core_at, y_at] + dp_at)
    started = {}

    def remote(key, source, target, device):
        n = len(started)
        started[key] = pltpu.make_async_remote_copy(
            src_ref=source,
            dst_ref=target,
            send_sem=send_sem.at[n],
            recv_sem=recv_sem.at[n],
            device_id=device,
            device_id_type=pl.DeviceIdType.MESH,
        )
        started[key].start()

    def arrive(key):
        started[key].wait_recv()

    part = width // 4
    half_bit, part_bit = (place >> 1) & 1, (place >> 2) & 1

    def quarter(i, j):
        at = (half_bit ^ i) * (2 * part) + (part_bit ^ j) * part
        return pl.ds(pl.multiple_of(at, part), part)

    def two_quarters(i):
        return pl.ds(pl.multiple_of((half_bit ^ i) * (2 * part), 2 * part), 2 * part)

    for i in (1, 0):
        rows = two_quarters(i)
        remote(("y", 0, i), away.at[rows, :], y_recv.at[0, rows, :], y_at)
    mine = two_quarters(0)
    loads = [[], []]

    def load(w, source, target):
        loads[w].append(pltpu.make_async_copy(source, target, load_sem.at[w, len(loads[w])]))
        loads[w][-1].start()

    load(1, rest.at[2], own.at[1])
    load(1, ffn_y.at[0], own16.at[1, 0])
    load(1, back_x, own16.at[1, 1])
    for pair in range(2):
        at = pl.ds(pair * 2 * part, 2 * part)
        load(0, rest.at[pair, mine, :], own.at[0, at, :])
        load(0, ffn_x.at[pair, mine, :], own16.at[0, 0, at, :])
        load(0, in_z.at[pair], own16.at[0, 1, at, :])
    load(1, qkv_y, y_recv.at[1])
    operands = [
        pltpu.make_async_copy(source, target, operand_sem.at[n])
        for n, (source, target) in enumerate(
            (
                (dqa_hbm, dqa),
                (x_hbm, x_ref),
                (dka_hbm, dka),
                (dva_hbm, dva),
                (dqb_hbm, dqb),
                (dkb_hbm, dkb),
                (dvb_hbm, dvb),
                (w0_hbm, w0),
                (w1_hbm, w1),
                (w2_hbm, w2),
                (w3_hbm, w3),
            )
        )
    ]
    for copy in operands:
        copy.start()

    def fetch(i):
        return pltpu.make_async_copy(
            dh_hbm.at[pl.ds(i * RB, RB), :], rows_in.at[i % 2], in_sem.at[i % 2]
        )

    fetch(0).start()

    def scatter(w):
        for j in (1, 0):
            at = pl.ds((1 - j) * part, part)
            add_rows(z_send.at[w, at, :], [total.at[w, quarter(1, j), :]])
            remote((w, "z", j), z_send.at[w, at, :], z_recv.at[w, at, :], dp_at[1])

    def in_part(j):
        return in_recv.at[pl.ds(pl.multiple_of((part_bit ^ j) * part, part), part), :]

    def scatter_on(w):
        rows = quarter(0, 1)
        arrive("in y" if w == 0 else (w, "z", 1))
        came = in_part(1) if w == 0 else z_recv.at[w, pl.ds(0, part), :]
        add_rows(last_send.at[w], [total.at[w, rows, :], came])
        remote((w, "last"), last_send.at[w], last_recv.at[w], dp_at[2])

    def spread(w, i, j):
        rows = result.at[w, 0, quarter(i, j), :]
        if (i, j) == (0, 0):
            remote((w, "gather", 0, 1), rows, rows, dp_at[2])
        if i == 0:
            remote((w, "gather", 1, j), rows, rows, dp_at[1])
        remote((w, "across", i, j), rows, result.at[w, 1, quarter(i, j), :], dp_at[0])

    def settle(w):
        rows = quarter(0, 0)
        own_part = result.at[w, 0, rows, :]
        if w > 0:
            arrive((w, "z", 0))
        arrive((w, "last"))
        came = in_part(0) if w == 0 else z_recv.at[w, pl.ds(part, part), :]
        terms = [total.at[w, rows, :], came, last_recv.at[w]]
        add_rows(own_part, terms)
        for bit in range(3, dp_bits):
            into = extra.at[w, bit - 3]
            remote((w, "all", bit), own_part, into, dp_at[bit])
            started[(w, "all", bit)].wait_send()
            arrive((w, "all", bit))
            add_rows(own_part, [own_part, into])
        spread(w, 0, 0)

    def gather(w, i, j):
        arrive((w, "gather", i, j))
        spread(w, i, j)

    for copy in loads[1]:
        copy.wait()
    add_rows(total.at[1], [own.at[1], own16.at[1, 0], own16.at[1, 1]])
    scatter(1)
    for copy in loads[0]:
        copy.wait()
    for pair, out in ((1, in_send), (0, total.at[0, mine, :])):
        at = pl.ds(pair * 2 * part, 2 * part)
        add_rows(out, [own.at[0, at, :], own16.at[0, 0, at, :], own16.at[0, 1, at, :]])
    remote("in y", in_send, in_recv, y_at)
    for copy in operands[:4]:
        copy.wait()

    near_parts = ([], [])

    def emit(n, rows):
        near_parts[n].append(("core", n, len(near_parts[n])))
        remote(near_parts[n][-1], send.at[n, rows, :], core.at[n, rows, :], core_at)

    near_grads = (dqa, dka, dva)
    cross_rows(
        x_ref,
        near_grads,
        okeep,
        osend,
        side,
        cross,
        keep,
        send,
        bias_ref,
        emit,
    )
    for copy in operands[4:]:
        copy.wait()

    small_held[0] = jnp.zeros(small_held.shape[1:], F32)
    small_held[0, 16:24, :] = sums_ref[...]
    for p in range(4):
        row = 4 * (index ^ p)
        half_mine = bias_in_ref[p : p + 1, :half]
        half_other = bias_in_ref[p : p + 1, half:]
        low_half = jnp.where(side == 0, half_mine, half_other)
        high_half = jnp.where(side == 0, half_other, half_mine)
        small_held[0, pl.ds(row, 1), :] = jnp.concatenate([low_half, high_half], axis=1)
        for i, k in enumerate((0, 2)):
            values = (bias_ref, bias_far)[p // 2][k : k + 1, :]
            if p % 2 == 1:
                values = pltpu.roll(values, piece, 1)
            small_held[0, pl.ds(row + 1 + i, 1), :half] = values

    def small_step(n):
        bits = [core_at, y_at] + dp_at
        remote(("small", n), small_held.at[2 * n], small_held.at[2 * n + 1], bits[n])

    def small_sum(n):
        arrive(("small", n))
        out = small_held.at[2 * n + 2] if n < dp_bits + 1 else small_out
        out[...] = small_held[2 * n] + small_held[2 * n + 1]

    weights = ((w0, w1), (w2, w3))
    grads = ((dqa, dka, dva), (dqb, dkb, dvb))
    stores = []

    def inputs_rows(b):
        at = pl.ds(b * RB, RB)
        if b + 1 < blocks:
            fetch(b + 1).start()
        fetch(b).wait()
        grad = rows_in[b % 2]
        for g in range(2):
            for i in range(3):
                rows = slice(i * piece, (i + 1) * piece)
                w = jnp.concatenate([ref[rows, :] for ref in weights[g]], axis=0)
                grad += dot(grads[g][i][at, :], w)
        if b >= 2:
            stores[b - 2].wait()
        rows_out[b % 2] = grad
        stores.append(
            pltpu.make_async_copy(rows_out.at[b % 2], gx_hbm.at[at, :], out_sem.at[b % 2])
        )
        stores[b].start()

    def send_across(i):
        rows = two_quarters(i)
        at = pl.ds((1 - i) * 2 * part, 2 * part)
        add_rows(x_send.at[at, :], [keep.at[1, rows, :], core.at[1, rows, :], y_recv.at[1, rows, :]])
        remote(("across", i), x_send.at[at, :], x_recv.at[at, :], dp_at[0])

    def take_across(i):
        rows = two_quarters(i)
        at = pl.ds((1 - i) * 2 * part, 2 * part)
        arrive(("y", 0, i))
        arrive(("across", i))
        add_rows(
            total.at[2, rows, :],
            [keep.at[0, rows, :], core.at[0, rows, :], y_recv.at[0, rows, :], x_recv.at[at, :]],
        )

    small_step(0)
    for key in near_parts[1]:
        arrive(key)
    send_across(1)
    send_across(0)
    scatter_on(1)
    inputs_rows(0)
    settle(1)
    small_sum(0)
    small_step(1)
    for key in near_parts[0]:
        arrive(key)
    take_across(1)
    scatter(2)
    scatter_on(0)
    inputs_rows(1)
    gather(1, 0, 1)
    small_sum(1)
    small_step(2)
    take_across(0)
    scatter_on(2)
    gather(1, 1, 0)
    settle(0)
    inputs_rows(2)
    gather(1, 1, 1)
    small_sum(2)
    small_step(3)
    gather(0, 0, 1)
    settle(2)
    gather(0, 1, 0)
    inputs_rows(3)
    gather(0, 1, 1)
    small_sum(3)
    small_step(4)
    gather(2, 0, 1)
    gather(2, 1, 0)
    for n in range(4, dp_bits + 2):
        small_sum(n)
        if n + 1 < dp_bits + 2:
            small_step(n + 1)
    gather(2, 1, 1)
    for w in range(3):
        for i in range(2):
            for j in range(2):
                arrive((w, "across", i, j))
    for key, copy in started.items():
        if not (isinstance(key, tuple) and key[1] == "all"):
            copy.wait_send()
    for store in stores[-2:]:
        store.wait()


def finish(
    x, weights, grads, osend, okeep, dh, rest, ffn_x, ffn_y, in_z, back_x, away, qkv_y, sums, bias_in, bias_far
):
    seq, width = x.shape
    half = width // 2
    piece = grads[0].shape[1] // 2
    dp_bits = bits_of("dp")
    slab = (width, half)
    copies = 14 + dp_bits + 2 + 3 * (10 + max(dp_bits - 3, 0))
    assert dp_bits >= 3
    return pl.pallas_call(
        functools.partial(finish_kernel, dp_bits),
        out_shape=(
            shape((seq, width), F32),
            shape((3, 2) + slab, LOW),
            shape((24, width), F32),
        ),
        in_specs=[HBM] * 11 + [VMEM] * 2 + [HBM] * 8 + [VMEM] * 3,
        out_specs=(HBM, VMEM, VMEM),
        scratch_shapes=[pltpu.VMEM(a.shape, LOW) for a in (x, *weights, *grads)]
        + [
            pltpu.VMEM((2,) + slab, F32),
            pltpu.VMEM((2, 2) + slab, LOW),
            pltpu.VMEM((width // 2, half), LOW),
            pltpu.VMEM((width // 2, half), LOW),
            pltpu.VMEM((2,) + slab, F32),
            pltpu.VMEM((2,) + slab, F32),
            pltpu.VMEM((2,) + slab, F32),
            pltpu.VMEM((2,) + slab, LOW),
            pltpu.VMEM(slab, LOW),
            pltpu.VMEM(slab, LOW),
            pltpu.VMEM((3,) + slab, F32),
            pltpu.VMEM((3, width // 2, half), LOW),
            pltpu.VMEM((3, width // 2, half), LOW),
            pltpu.VMEM((3, width // 4, half), LOW),
            pltpu.VMEM((3, width // 4, half), LOW),
            pltpu.VMEM((3, max(dp_bits - 3, 1), width // 4, half), LOW),
            pltpu.VMEM((8, 2 * piece), F32),
            pltpu.VMEM((2 * dp_bits + 4, 24, width), F32),
            pltpu.VMEM((2, RB, width), F32),
            pltpu.VMEM((2, RB, width), F32),
            pltpu.VMEM((2 * piece, width), F32),
            pltpu.SemaphoreType.DMA((11,)),
            pltpu.SemaphoreType.DMA((2, 6)),
            pltpu.SemaphoreType.DMA((copies,)),
            pltpu.SemaphoreType.DMA((copies,)),
            pltpu.SemaphoreType.DMA((2,)),
            pltpu.SemaphoreType.DMA((2,)),
        ],
        compiler_params=pltpu.CompilerParams(
            vmem_limit_bytes=VMEM_LIMIT, collective_id=2, has_side_effects=True
        ),
        cost_estimate=pl.CostEstimate(
            flops=36 * seq * width * piece, bytes_accessed=50 << 20, transcendentals=0
        ),
        name="finish",
    )(x, *weights, *grads, osend, okeep, dh, rest, ffn_x, ffn_y, in_z, back_x, away, qkv_y, sums, bias_in, bias_far)


def widen_kernel(
    small,
    count,
    result,
    source,
    loss_ref,
    bqv_ref,
    bin_ref,
    gains_ref,
    shifts_ref,
    qkv_hbm,
    out_hbm,
    in_hbm,
    back_hbm,
    target,
    slabs,
    rows_held,
    qkv_ref,
    out_ref,
    in_ref,
    back_ref,
    in_sem,
    row_sem,
    out_sem,
):
    half = slabs.shape[3]
    piece = qkv_ref.shape[1]
    side = lax.axis_index("dp") & 1
    slab_loads = [
        pltpu.make_async_copy(result.at[w], slabs.at[w], in_sem.at[w]) for w in range(3)
    ]
    blocks = source.shape[0] // RB

    def rows(i, out):
        at = pl.ds(i * RB, RB)
        ends = (rows_held.at[i], target.at[at, :]) if out else (source.at[at, :], rows_held.at[i])
        return pltpu.make_async_copy(*ends, row_sem.at[i, out])

    slab_loads[0].start()
    slab_loads[1].start()
    for i in range(blocks):
        rows(i, 0).start()
    slab_loads[2].start()
    stores = []

    def store(value, to):
        stores.append(pltpu.make_async_copy(value, to, out_sem.at[len(stores)]))
        stores[-1].start()

    sides = [
        pl.ds(pl.multiple_of(natural * half, half), half) for natural in (side, 1 - side)
    ]
    slab_loads[0].wait()
    for n in range(2):
        in_ref[:, sides[n]] = slabs[0, n].astype(F32)
    store(in_ref, in_hbm)
    slab_loads[1].wait()
    for n in range(2):
        for c in range(2):
            strip = slabs[1, n, c * half : (c + 1) * half, :]
            back_ref[sides[n], c * half : (c + 1) * half] = strip.astype(F32)
    store(back_ref, back_hbm)
    for i in range(blocks):
        rows(i, 0).wait()
        rows(i, 1).start()
    slab_loads[2].wait()
    for n in range(2):
        for i in range(3):
            qkv_ref[i, :, sides[n]] = slabs[2, n, i * piece : (i + 1) * piece, :].astype(F32)
        out_ref[:, sides[n]] = slabs[2, n, 3 * piece :, :].astype(F32)
    store(qkv_ref, qkv_hbm)
    store(out_ref, out_hbm)
    row = 4 * lax.axis_index("tensor")
    bin_ref[...] = small[pl.ds(row, 1), :].reshape(bin_ref.shape)
    for i in range(2):
        bqv_ref[i : i + 1, :] = small[pl.ds(row + 1 + i, 1), :piece]
    gains_ref[...] = small[16:18, :]
    shifts_ref[...] = small[18:22, :]
    tokens = count[0:1, 0:1].astype(F32)
    total = jnp.sum(small[22:23, :], axis=1, keepdims=True)
    loss_ref[...] = total / (2.0 * small.shape[1] * tokens)
    for i in range(blocks):
        rows(i, 1).wait()
    for copy in stores:
        copy.wait()


def widen(result, small, count, inputs_grad, piece, out_rows):
    width, half = result.shape[2:]
    seq = inputs_grad.shape[0]
    large = ((3, piece, width), (out_rows, width), (width, 2 * half), (2 * half, width))
    return pl.pallas_call(
        widen_kernel,
        out_shape=(
            shape((1, 1), F32),
            shape((2, piece), F32),
            shape((2 * half,), F32),
            shape((2, width), F32),
            shape((4, width), F32),
        )
        + tuple(shape(dims, F32) for dims in large)
        + (shape(inputs_grad.shape, F32),),
        in_specs=[VMEM, VMEM, HBM, HBM],
        out_specs=(VMEM,) * 5 + (HBM,) * 5,
        scratch_shapes=[
            pltpu.VMEM(result.shape, LOW),
            pltpu.VMEM((seq // RB, RB, width), F32),
        ]
        + [pltpu.VMEM(dims, F32) for dims in large]
        + [
            pltpu.SemaphoreType.DMA((3,)),
            pltpu.SemaphoreType.DMA((seq // RB, 2)),
            pltpu.SemaphoreType.DMA((4,)),
        ],
        compiler_params=pltpu.CompilerParams(vmem_limit_bytes=VMEM_LIMIT),
        name="widen",
    )(small, count, result, inputs_grad)


def per_device(
    inputs,
    w_qkv,
    b_qv,
    w_out,
    w_in,
    b_in,
    w_back,
    norm_gains,
    shifts,
    segment_ids,
    valid_lengths,
    teacher,
):
    own_seqs, seq, width = inputs.shape
    assert own_seqs == 1 and lax.axis_size("tensor") == 4
    total_slots = seq * lax.axis_size("tensor") * lax.axis_size("dp")
    half = width // 2
    piece = w_qkv.shape[2]
    units = w_in.shape[1]
    x = inputs.reshape(seq, width)

    near, table, code, seg = round_qkv(
        valid_lengths, segment_ids, w_qkv.transpose(0, 2, 1), b_qv, b_in
    )
    core = swap(near, "tensor", 0)
    far = swap(near, "tensor", 1)
    core, w_in, w_back, w_out = lax.optimization_barrier((core, w_in, w_back, w_out))
    out_in, back, second, x_low = round_rest(w_out, w_in, w_back, x)
    out_in_far = swap(out_in, "tensor", 1)

    qa, ka, va, ctx_a, lse_a = attend_forward(table, x_low, near, core, code, seg)
    out_in, back, second, far, ctx_a = lax.optimization_barrier((out_in, back, second, far, ctx_a))
    core_far = swap(far, "tensor", 0)
    out_in_core = swap(out_in, "tensor", 0)
    back_core = swap(back, "tensor", 0)
    second_core = swap(second, "tensor", 0)
    qb, kb, vb, ctx_b, lse_b = attend_forward(table, x_low, far, core_far, code, seg)
    (
        output,
        dh_one,
        cg_a,
        cg_b,
        _,
        to_x,
        to_y,
        rest,
        out_send_a,
        out_send_b,
        out_keep_a,
        out_keep_b,
        sums,
        bias_sums,
        count,
        *_,
    ) = middle(
        total_slots,
        valid_lengths,
        ctx_a,
        ctx_b,
        norm_gains,
        shifts,
        x,
        teacher.reshape(seq, width),
        (near, core, far, core_far),
        (out_in, out_in_core, out_in_far),
        (back, back_core),
        (second, second_core),
    )
    ffn_x = swap(to_x, "dp", 0)
    ffn_y = swap(to_y, "tensor", 1)
    grads_b = attend_backward(table, qb, kb, vb, cg_b, lse_b, code, seg)
    away, away_first, bias_far = far_projections(x_low, grads_b, out_send_b, out_keep_b)
    ffn_x, ffn_y, away_first = lax.optimization_barrier((ffn_x, ffn_y, away_first))
    half_other = 1 - ((lax.axis_index("dp") >> 1) & 1)
    in_away = (
        lax.dynamic_slice(rest, (0, half_other * half, 0), (2, half, half))
        + lax.dynamic_slice_in_dim(ffn_x, half_other * half, half, 1).astype(F32)
    ).astype(LOW)
    back_away = (rest[3] + ffn_y[1].astype(F32)).astype(LOW)
    in_away, back_away, away_first, cg_a = lax.optimization_barrier(
        (in_away, back_away, away_first, cg_a)
    )
    in_z = swap(in_away, "dp", 1)
    qkv_y = swap(away_first, "tensor", 1)
    back_x = swap(back_away, "dp", 0)
    *grads_a, output = attend_backward(table, qa, ka, va, cg_a, lse_a, code, seg, output)
    grad_inputs, slabs, small = finish(
        x_low,
        (near, core, far, core_far),
        (*grads_a, *grads_b),
        out_send_a,
        out_keep_a,
        dh_one,
        rest,
        ffn_x,
        ffn_y,
        in_z,
        back_x,
        away,
        qkv_y,
        sums,
        bias_sums,
        bias_far,
    )
    (
        loss,
        grad_b_qv,
        grad_b_in,
        grad_gains,
        grad_shifts,
        grad_w_qkv,
        grad_w_out,
        grad_w_in,
        grad_w_back,
        grad_inputs,
    ) = widen(slabs, small, count, grad_inputs, piece, w_out.shape[0])
    return (
        output.reshape(own_seqs, seq, width),
        loss[0, 0],
        grad_inputs.reshape(own_seqs, seq, width),
        grad_w_qkv.transpose(0, 2, 1),
        grad_b_qv,
        grad_w_out,
        grad_w_in,
        grad_b_in,
        grad_w_back,
        grad_gains,
        grad_shifts,
    )


def solution(mesh):
    return jax.shard_map(
        per_device,
        mesh=mesh,
        in_specs=(
            P(("dp", "tensor"), None, None),
            P(None, None, "tensor"),
            P(None, "tensor"),
            P("tensor", None),
            P(None, "tensor"),
            P("tensor"),
            P("tensor", None),
            P(),
            P(),
            P("dp", None),
            P("dp"),
            P(("dp", "tensor"), None, None),
        ),
        out_specs=(
            P(("dp", "tensor"), None, None),
            P(),
            P(("dp", "tensor"), None, None),
            P(None, None, "tensor"),
            P(None, "tensor"),
            P("tensor", None),
            P(None, "tensor"),
            P("tensor"),
            P("tensor", None),
            P(),
            P(),
        ),
        check_vma=False,
    )
```

```python
import functools
import math

import jax
import jax.numpy as jnp
from jax import lax
from jax.experimental import pallas as pl
from jax.experimental.pallas import tpu as pltpu
from jax.sharding import PartitionSpec as P

HD = 64
LN_EPSILON = 1e-05
MASKED_SCORE = -1000000000.0
QB = 256
KB = 128
RB = 256
FR = 256
BR = 512
NT = ((1,), (1,))
TN = ((0,), (0,))
PHI = (
    0.1412427189,
    0.1377927593,
    0.1458432541,
    0.005834031383,
    0.2126657205,
    -0.1910292611,
    0.0476509541,
)
PHI_STEP = 0.35355339059327379

VMEM_LIMIT = 63 << 20
VMEM = pl.BlockSpec(memory_space=pltpu.VMEM)
SMEM = pl.BlockSpec(memory_space=pltpu.SMEM)
HBM = pl.BlockSpec(memory_space=pl.ANY)
LOW = jnp.bfloat16
F32 = jnp.float32


def dot(left, right, dims=((1,), (0,))):
    return lax.dot_general(left, right, (dims, ((), ())), preferred_element_type=jnp.float32)


def shape(dims, dtype):
    return jax.ShapeDtypeStruct(dims, dtype)


def swap(values, axis, bit):
    size = lax.axis_size(axis)
    return lax.ppermute(values, axis, [(i, i ^ (1 << bit)) for i in range(size)])


def bits_of(axis):
    return int(math.log2(lax.axis_size(axis)))


def partner(axis, bit):
    here = {name: lax.axis_index(name) for name in ("dp", "tensor")}
    here[axis] = here[axis] ^ (1 << bit)
    return here["dp"], here["tensor"]


def greet(partners):
    barrier = pltpu.get_barrier_semaphore()
    for device in partners:
        pl.semaphore_signal(
            barrier, inc=1, device_id=device, device_id_type=pl.DeviceIdType.MESH
        )
    pl.semaphore_wait(barrier, len(partners))


def three_parts(values):
    first = values.astype(LOW)
    rest = values - first.astype(F32)
    second = rest.astype(LOW)
    return first, second, (rest - second.astype(F32)).astype(LOW)


def span_table(table_ref, seg, valid):
    for block in range(seg.shape[1] // QB):
        start = block * QB
        first = jnp.max(seg[:, start : start + 1])
        last = jnp.max(seg[:, start + QB - 1 : start + QB])
        low = jnp.sum((seg < first).astype(jnp.int32))
        high = jnp.sum((seg <= last).astype(jnp.int32))
        high = jnp.maximum(jnp.minimum(high, valid), start + QB)
        low_block = lax.div(low, jnp.int32(KB))
        table_ref[0, block] = low_block
        table_ref[1, block] = lax.div(high + (KB - 1), jnp.int32(KB)) - low_block


def round_qkv_kernel(
    lengths_ref, segments_ref, w_ref, bqv_ref, bin_ref, out_ref, table_ref, code_ref, seg_ref
):
    index = lax.axis_index("tensor")
    valid = lengths_ref[index]
    seg = segments_ref[pl.ds(index, 1), :]
    seg_ref[...] = seg
    span_table(table_ref, seg, valid)
    code = jnp.where(lax.broadcasted_iota(jnp.int32, seg.shape, 1) < valid, seg, -1)
    tall = jnp.broadcast_to(code.astype(F32), (8, seg.shape[1])).T
    code_ref[...] = tall[:, :1].astype(jnp.int32)
    piece = w_ref.shape[1]
    width = w_ref.shape[2]
    half = bin_ref.shape[0] // 2
    for i in range(3):
        out_ref[i * piece : (i + 1) * piece, :] = w_ref[i].astype(LOW)
    row = bin_ref[...].reshape(1, 2 * half)
    side = lax.axis_index("dp") & 1
    mine = jnp.where(side == 0, row[:, :half], row[:, half:])
    other = jnp.where(side == 0, row[:, half:], row[:, :half])
    pad = jnp.zeros((1, width - piece), F32)
    rows = [jnp.concatenate([mine, other], axis=1)]
    rows += [jnp.concatenate([bqv_ref[i : i + 1, :], pad], axis=1) for i in range(2)]
    parts = [part.astype(F32) for row in rows for part in three_parts(row)]
    parts += [jnp.zeros((1, width), F32)] * 7
    out_ref[3 * piece :, :] = jnp.concatenate(parts, axis=0).astype(LOW)


def round_qkv(lengths, segments, w_qkv, b_qv, b_in):
    _, piece, width = w_qkv.shape
    seq = segments.shape[1]
    return pl.pallas_call(
        round_qkv_kernel,
        out_shape=(
            shape((3 * piece + 16, width), LOW),
            shape((2, seq // QB), jnp.int32),
            shape((seq, 1), jnp.int32),
            shape((1, seq), jnp.int32),
        ),
        in_specs=[SMEM, VMEM, VMEM, VMEM, VMEM],
        out_specs=(VMEM, SMEM, VMEM, VMEM),
        compiler_params=pltpu.CompilerParams(vmem_limit_bytes=VMEM_LIMIT),
        name="round_qkv",
    )(lengths, segments, w_qkv, b_qv, b_in)


def round_rest_kernel(
    wo_hbm, wi_hbm, wb_hbm, x_hbm, out_in, back, second, x_low, *scratch
):
    wo_in, wi_in, wb_in, x_in, oi_out, b_out, s_out, x_out, in_sem, out_sem = scratch
    rows, width = wo_in.shape
    half = width // 2
    own_side = lax.axis_index("dp") & 1
    loads, stores = [], []

    def load(source, target):
        loads.append(pltpu.make_async_copy(source, target, in_sem.at[len(loads)]))
        loads[-1].start()

    def store(source, target):
        stores.append(pltpu.make_async_copy(source, target, out_sem.at[len(stores)]))
        stores[-1].start()

    load(wo_hbm, wo_in)
    load(wi_hbm, wi_in)
    for side in (own_side, 1 - own_side):
        at = pl.ds(pl.multiple_of(side * half, half), half)
        load(wb_hbm.at[at, :], wb_in.at[at, :])
    quarters = [pl.ds(i * x_in.shape[0] // 4, x_in.shape[0] // 4) for i in range(4)]
    for at in quarters:
        load(x_hbm.at[at, :], x_in.at[at, :])
    loads[0].wait()
    for c in range(2):
        oi_out[c * rows : (c + 1) * rows, :] = wo_in[:, c * half : (c + 1) * half].astype(LOW)
    loads[1].wait()
    sides = [
        pl.ds(pl.multiple_of(side * half, half), half) for side in (own_side, 1 - own_side)
    ]
    oi_out[2 * rows :, :] = wi_in[:, sides[0]].astype(LOW)
    store(oi_out, out_in)
    s_out[:width, :] = wi_in[:, sides[1]].astype(LOW)
    for n, (to_back, base) in enumerate(((b_out, 0), (s_out, width))):
        loads[2 + n].wait()
        for c in range(2):
            start = base + c * half
            strip = wb_in[sides[n], c * half : (c + 1) * half]
            to_back[start : start + half, :] = strip.astype(LOW)
        store(to_back, (back, second)[n])
    for n, at in enumerate(quarters):
        loads[4 + n].wait()
        x_out[at, :] = x_in[at, :].astype(LOW)
        store(x_out.at[at, :], x_low.at[at, :])
    for copy in stores:
        copy.wait()


def round_rest(w_out, w_in, w_back, x):
    rows, width = w_out.shape
    half = width // 2
    shapes = ((2 * rows + width, half), (width, half), (2 * width, half), x.shape)
    return pl.pallas_call(
        round_rest_kernel,
        out_shape=tuple(shape(dims, LOW) for dims in shapes),
        in_specs=[HBM] * 4,
        out_specs=(HBM,) * 4,
        scratch_shapes=[pltpu.VMEM(a.shape, F32) for a in (w_out, w_in, w_back, x)]
        + [pltpu.VMEM(dims, LOW) for dims in shapes]
        + [pltpu.SemaphoreType.DMA((8,)), pltpu.SemaphoreType.DMA((7,))],
        compiler_params=pltpu.CompilerParams(vmem_limit_bytes=VMEM_LIMIT),
        name="round_rest",
    )(w_out, w_in, w_back, x)


def make_bias(bias_ref, block, low, count, code_ref, seg_ref):
    dims = (count * KB, QB)
    codes = code_ref[pl.ds(pl.multiple_of(low * KB, KB), count * KB), :]
    segs = seg_ref[:, pl.ds(pl.multiple_of(block * QB, QB), QB)]
    key_at = low * KB + lax.broadcasted_iota(jnp.int32, dims, 0)
    query_at = block * QB + lax.broadcasted_iota(jnp.int32, dims, 1)
    allowed = (codes == segs) | (key_at == query_at)
    bias_ref[: count * KB, :] = jnp.where(allowed, 0.0, MASKED_SCORE)


def one_head(values, head):
    lane = lax.broadcasted_iota(jnp.int32, values.shape, 1)
    keep = (lane < HD) if head == 0 else (lane >= HD)
    return jnp.where(keep, values, jnp.zeros_like(values))


def forward_kernel(
    table_ref,
    x_ref,
    w0_ref,
    w1_ref,
    code_ref,
    seg_ref,
    q_ref,
    k_ref,
    v_ref,
    ctx_ref,
    lse_ref,
    weights,
    biases,
    vt_ref,
    bias_ref,
):
    block = pl.program_id(0)
    low, total = table_ref[0, block], table_ref[1, block]
    piece = (w0_ref.shape[0] - 16) // 3
    pairs = 2 * piece // 128

    @pl.when(block == 0)
    def _():
        for i in range(3):
            for n, ref in enumerate((w0_ref, w1_ref)):
                rows = ref[i * piece : (i + 1) * piece, :]
                weights[i, n * piece : (n + 1) * piece, :] = rows
        lane = lax.broadcasted_iota(jnp.int32, (1, x_ref.shape[1]), 1)
        for i in (0, 2):
            base = 3 * piece + (3 if i == 0 else 6)
            both = [
                sum(ref[base + part : base + part + 1, :].astype(F32) for part in range(3))
                for ref in (w0_ref, w1_ref)
            ]
            row = jnp.where(lane < piece, both[0], pltpu.roll(both[1], piece, 1))
            biases[i : i + 1, :] = row[:, : 2 * piece]
        biases[1:2, :] = jnp.zeros((1, 2 * piece), F32)

        def project(b, carry):
            at = pl.ds(pl.multiple_of(b * QB, QB), QB)
            for i, ref in enumerate((q_ref, k_ref, v_ref)):
                ref[at, :] = (dot(x_ref[at, :], weights[i], NT) + biases[i : i + 1, :]).astype(LOW)
            vt_ref[:, at] = v_ref[at, :].T
            return carry

        lax.fori_loop(0, x_ref.shape[0] // QB, project, 0)

    def run(count):
        make_bias(bias_ref, block, low, count, code_ref, seg_ref)
        bias = bias_ref[: count * KB, :]
        rows = pl.ds(pl.multiple_of(low * KB, KB), count * KB)
        queries = pl.ds(pl.multiple_of(block * QB, QB), QB)

        def scores(head):
            lanes = slice(head // 2 * 128, head // 2 * 128 + 128)
            query = q_ref[queries, lanes] * jnp.asarray(0.125, LOW)
            return dot(k_ref[rows, lanes], one_head(query, head % 2), NT) + bias

        def soft(values, head):
            peak = jnp.max(values, axis=0, keepdims=True)
            powers = jnp.exp(values - peak)
            mass = jnp.sum(powers, axis=0, keepdims=True)
            lse_ref[head : head + 1, :] = peak + jnp.log(mass)
            return (powers * (1.0 / mass)).astype(LOW)

        outs = []

        def context(probs, head):
            outs.append(dot(vt_ref[head * HD : (head + 1) * HD, rows], probs))
            if head % 2 == 1:
                both = jnp.concatenate(outs[-2:], axis=0).T
                ctx_ref[:, head // 2 * 128 : head // 2 * 128 + 128] = both.astype(LOW)

        values, probs = scores(0), None
        for head in range(2 * pairs):
            later = scores(head + 1) if head + 1 < 2 * pairs else None
            now = soft(values, head)
            if head > 0:
                context(probs, head - 1)
            values, probs = later, now
        context(probs, 2 * pairs - 1)

    for count in range(QB // KB, k_ref.shape[0] // KB + 1):
        pl.when(total == count)(functools.partial(run, count))


def backward_kernel(carried, table_ref, q_ref, k_ref, v_ref, g_ref, lse_ref, code_ref, seg_ref, *refs):
    block = pl.program_id(0)
    refs = list(refs)
    if carried:
        source, target = refs.pop(0), refs.pop(3)
        target[...] = source[...]
    dq_ref, dk_ref, dv_ref, kt_ref, bias_ref, dk_sum, dv_sum = refs
    low, total = table_ref[0, block], table_ref[1, block]
    heads = q_ref.shape[1] // HD

    @pl.when(block == 0)
    def _():
        kt_ref[...] = k_ref[...].T
        dk_sum[...] = jnp.zeros_like(dk_sum)
        dv_sum[...] = jnp.zeros_like(dv_sum)

    def run(count):
        make_bias(bias_ref, block, low, count, code_ref, seg_ref)
        bias = bias_ref[: count * KB, :]
        rows = pl.ds(pl.multiple_of(low * KB, KB), count * KB)

        def first(head):
            lanes = slice(head // 2 * 128, head // 2 * 128 + 128)
            query = one_head(q_ref[:, lanes] * jnp.asarray(0.125, LOW), head % 2)
            grad = one_head(g_ref[:, lanes], head % 2)
            scores = dot(k_ref[rows, lanes], query, NT) + bias
            return scores, dot(v_ref[rows, lanes], grad, NT), query, grad

        def second(head, scores, prob_grad, query, grad):
            probs = jnp.exp(scores - lse_ref[head : head + 1, :])
            delta = jnp.sum(probs * prob_grad, axis=0, keepdims=True)
            return probs.astype(LOW), (probs * (prob_grad - delta)).astype(LOW), query, grad

        outs = []

        def third(head, probs, score_grad, query, grad):
            lanes = slice(head // 2 * 128, head // 2 * 128 + 128)
            dv_sum[rows, lanes] += dot(probs, grad)
            dk_sum[rows, lanes] += dot(score_grad, query)
            outs.append(dot(kt_ref[head * HD : (head + 1) * HD, rows], score_grad))
            if head % 2 == 1:
                both = jnp.concatenate(outs[-2:], axis=0).T * 0.125
                dq_ref[:, lanes] = both.astype(LOW)

        start, middle_of = first(0), None
        for head in range(heads):
            later = first(head + 1) if head + 1 < heads else None
            now = second(head, *start)
            if head > 0:
                third(head - 1, *middle_of)
            start, middle_of = later, now
        third(heads - 1, *middle_of)

    for count in range(QB // KB, k_ref.shape[0] // KB + 1):
        pl.when(total == count)(functools.partial(run, count))

    @pl.when(block == pl.num_programs(0) - 1)
    def _():
        dk_ref[...] = dk_sum[...].astype(LOW)
        dv_ref[...] = dv_sum[...].astype(LOW)


def attend_forward(table, x, first, second, code, seg):
    seq, width = x.shape
    piece = (first.shape[0] - 16) // 3
    heads, blocks = 2 * piece // HD, seq // QB
    whole = lambda i, t: (0, 0)
    column = pl.BlockSpec((seq, 2 * piece), whole)
    return pl.pallas_call(
        forward_kernel,
        out_shape=(shape((seq, 2 * piece), LOW),) * 4 + (shape((8, seq), F32),),
        grid_spec=pltpu.PrefetchScalarGridSpec(
            num_scalar_prefetch=1,
            grid=(blocks,),
            in_specs=[
                pl.BlockSpec((seq, width), whole),
                pl.BlockSpec(first.shape, whole),
                pl.BlockSpec(second.shape, whole),
                pl.BlockSpec((seq, 1), whole),
                pl.BlockSpec((1, seq), whole),
            ],
            out_specs=[
                column,
                column,
                column,
                pl.BlockSpec((QB, 2 * piece), lambda i, t: (i, 0)),
                pl.BlockSpec((8, QB), lambda i, t: (0, i)),
            ],
            scratch_shapes=[
                pltpu.VMEM((3, 2 * piece, width), LOW),
                pltpu.VMEM((3, 2 * piece), F32),
                pltpu.VMEM((2 * piece, seq), LOW),
                pltpu.VMEM((seq, QB), F32),
            ],
        ),
        compiler_params=pltpu.CompilerParams(vmem_limit_bytes=VMEM_LIMIT),
        cost_estimate=pl.CostEstimate(
            flops=16 * seq * seq * piece + 12 * seq * width * piece,
            bytes_accessed=16 * seq * piece,
            transcendentals=seq * seq * heads // 2,
        ),
        name="attend_forward",
    )(table, x, first, second, code, seg)


def attend_backward(table, q, k, v, grad, lse, code, seg, *carried):
    seq, width = grad.shape
    blocks = seq // QB
    block = pl.BlockSpec((QB, width), lambda i, t: (i, 0))
    column = pl.BlockSpec((seq, width), lambda i, t: (0, 0))
    return pl.pallas_call(
        functools.partial(backward_kernel, len(carried)),
        out_shape=(shape((seq, width), LOW),) * 3 + tuple(shape(c.shape, c.dtype) for c in carried),
        grid_spec=pltpu.PrefetchScalarGridSpec(
            num_scalar_prefetch=1,
            grid=(blocks,),
            in_specs=[
                block,
                column,
                column,
                block,
                pl.BlockSpec((8, QB), lambda i, t: (0, i)),
                pl.BlockSpec((seq, 1), lambda i, t: (0, 0)),
                pl.BlockSpec((1, seq), lambda i, t: (0, 0)),
            ]
            + [pl.BlockSpec((QB, c.shape[1]), lambda i, t: (i, 0)) for c in carried],
            out_specs=[block, column, column]
            + [pl.BlockSpec((QB, c.shape[1]), lambda i, t: (i, 0)) for c in carried],
            scratch_shapes=[
                pltpu.VMEM((width, seq), LOW),
                pltpu.VMEM((seq, QB), F32),
                pltpu.VMEM((seq, width), F32),
                pltpu.VMEM((seq, width), F32),
            ],
        ),
        compiler_params=pltpu.CompilerParams(vmem_limit_bytes=VMEM_LIMIT),
        cost_estimate=pl.CostEstimate(
            flops=16 * seq * seq * width,
            bytes_accessed=16 * seq * width,
            transcendentals=seq * seq * width // 128,
        ),
        name="attend_backward",
    )(table, q, k, v, grad, lse, code, seg, *carried)


def gelu_parts(pre):
    size = 1.0 + PHI_STEP * jnp.abs(pre)
    t = pl.reciprocal(size, approx=True)
    t = t * (2.0 - size * t)
    poly = PHI[6] * t + PHI[5]
    for factor in PHI[4::-1]:
        poly = poly * t + factor
    bell = jnp.exp2((-0.5 * math.log2(math.e)) * (pre * pre))
    tail = poly * t * bell
    cdf = jnp.where(pre < 0, tail, 1.0 - tail)
    return pre * cdf, cdf + (pre * 0.3989422804014327) * bell


def norm_stats(values):
    width = values.shape[-1]
    mean = jnp.sum(values, axis=-1, keepdims=True) * (1.0 / width)
    centred = values - mean
    spread = jnp.sum(centred * centred, axis=-1, keepdims=True) * (1.0 / width)
    rate = lax.rsqrt(spread + LN_EPSILON)
    return centred * rate, rate


def norm_back(grad, gain, xhat, rate):
    width = grad.shape[-1]
    scaled = grad * gain
    mean = jnp.sum(scaled, axis=-1, keepdims=True) * (1.0 / width)
    along = jnp.sum(scaled * xhat, axis=-1, keepdims=True) * (1.0 / width)
    return rate * (scaled - mean - xhat * along)


def column_sum(values):
    return jnp.sum(values, axis=0, keepdims=True)


def middle_kernel(
    total_slots,
    dp_bits,
    lengths_ref,
    ctx_a,
    ctx_b,
    gains,
    shifts,
    x_hbm,
    teacher_hbm,
    qa,
    qb,
    qc,
    qd,
    outin_own,
    outin_core,
    outin_far,
    back_own,
    back_core,
    second_own,
    second_core,
    out_hbm,
    dh_hbm,
    cg_a,
    cg_b,
    core_hbm,
    to_x,
    to_y,
    rest,
    out_send_a,
    out_send_b,
    out_keep_a,
    out_keep_b,
    sums,
    bias_sums,
    count_ref,
    outin_far_core,
    in_far,
    back_far,
    in_far_core,
    back_far_core,
    w_in,
    w_back,
    w_out,
    bias_parts,
    bias_in,
    xhat_one,
    rate_one,
    mid_low,
    hidden,
    slope,
    acc,
    dh_low,
    pre_grad,
    rows_in,
    rows_out,
    stage16,
    stage32,
    from_core,
    held,
    w_sem,
    in_sem,
    out_sem,
    load_sem,
    store_sem,
    send_sem,
    recv_sem,
    count_send,
    count_recv,
    far_send,
    far_recv,
):
    seq, width = acc.shape
    blocks = seq // RB
    half = width // 2
    out_rows = w_out.shape[0] // 4
    units = w_in.shape[2]
    side = units // 2
    core_at, y_at, x_at = partner("tensor", 0), partner("tensor", 1), partner("dp", 0)
    greet([core_at, y_at] + [partner("dp", bit) for bit in range(dp_bits)])

    def far_copy(n, source, target, device):
        return pltpu.make_async_remote_copy(
            src_ref=source,
            dst_ref=target,
            send_sem=far_send.at[n],
            recv_sem=far_recv.at[n],
            device_id=device,
            device_id_type=pl.DeviceIdType.MESH,
        )

    in_at = pl.ds(2 * out_rows, width)
    far = [
        far_copy(
            0,
            outin_far.at[pl.ds(0, 2 * out_rows), :],
            outin_far_core.at[pl.ds(0, 2 * out_rows), :],
            core_at,
        ),
        far_copy(1, back_own, back_far.at[0], y_at),
        far_copy(
            2,
            second_own.at[pl.ds(width, side), :],
            back_far.at[1, pl.ds(0, side), :],
            y_at,
        ),
        far_copy(3, outin_far.at[in_at, :], in_far, x_at),
        far_copy(4, in_far, in_far_core, core_at),
        far_copy(5, back_far.at[0], back_far_core.at[0], core_at),
        far_copy(6, back_far.at[1], back_far_core.at[1], core_at),
        far_copy(
            7,
            back_far.at[0, pl.ds(side, side), :],
            back_far.at[1, pl.ds(side, side), :],
            x_at,
        ),
        far_copy(8, outin_far.at[in_at, :], outin_far_core.at[in_at, :], core_at),
    ]
    for copy in far[:4] + far[8:]:
        copy.start()
    out_in = (outin_own, outin_core, outin_far, outin_far_core)
    in_parts = tuple(ref.at[in_at, :] for ref in out_in)
    in_other = (
        second_own.at[pl.ds(0, width), :],
        second_core.at[pl.ds(0, width), :],
        in_far,
        in_far_core,
    )
    back_parts = (back_own, back_core, back_far.at[0], back_far_core.at[0])
    back_other = (
        second_own.at[pl.ds(width, width), :],
        second_core.at[pl.ds(width, width), :],
        back_far.at[1],
        back_far_core.at[1],
    )

    def rows(i):
        return pl.ds(pl.multiple_of(i * RB, RB), RB)

    def keep_rows(i, target):
        return pltpu.make_async_copy(
            rows_out.at[i & 1], target.at[rows(i), :], out_sem.at[i & 1]
        )

    def fetch(source, i, slot):
        return pltpu.make_async_copy(source.at[rows(i), :], rows_in.at[slot], in_sem.at[slot])

    def out_weights(p, c):
        return pltpu.make_async_copy(
            out_in[p].at[pl.ds(c * out_rows, out_rows), :],
            w_out.at[pl.ds(p * out_rows, out_rows), pl.ds(c * half, half)],
            w_sem.at[p, c],
        )

    def bias_rows(p):
        source = (qa, qb, qc, qd)[p]
        return pltpu.make_async_copy(
            source.at[pl.ds(source.shape[0] - 16, 16), :], bias_parts.at[p], w_sem.at[p, 8]
        )

    def load_in(source, p, r):
        return pltpu.make_async_copy(
            source, w_in.at[p, :, pl.ds(r * side, side)], w_sem.at[p, 2 + 3 * r]
        )

    def load_back(source, p, r, c):
        return pltpu.make_async_copy(
            source.at[pl.ds(c * side, side), :],
            w_back.at[p, pl.ds(r * side, side), pl.ds(c * half, half)],
            w_sem.at[p, 3 + 3 * r + c],
        )

    def ffn_weights(p):
        load_in(in_parts[p], p, 0).start()
        load_in(in_other[p], p, 1).start()
        for c in range(2):
            load_back(back_parts[p], p, 0, c).start()
            load_back(back_other[p], p, 1, c).start()

    early = [out_weights(p, c) for p in range(4) for c in range(2)]
    for copy in early[:6]:
        copy.start()
    fetch(x_hbm, 0, 0).start()
    for p in range(4):
        bias_rows(p).start()
    for p in range(2):
        ffn_weights(p)

    def count_step(bit):
        return pltpu.make_async_remote_copy(
            src_ref=held.at[2 * bit],
            dst_ref=held.at[2 * bit + 1],
            send_sem=count_send.at[bit],
            recv_sem=count_recv.at[bit],
            device_id=partner("dp", bit),
            device_id_type=pl.DeviceIdType.MESH,
        )

    tokens = jnp.full(held.shape[1:], 0, jnp.int32)
    for i in range(lengths_ref.shape[0]):
        tokens += lengths_ref[i]
    held[0] = tokens
    count_step(0).start()

    def count_on(bit):
        count_step(bit).wait()
        held[2 * bit + 2] = held[2 * bit] + held[2 * bit + 1]
        if bit + 1 < dp_bits:
            count_step(bit + 1).start()

    far[0].wait_recv()
    for copy in early[6:]:
        copy.start()
    for copy in early:
        copy.wait()

    for i in range(blocks):
        if i + 1 < blocks:
            fetch(x_hbm, i + 1, (i + 1) % 2).start()
        fetch(x_hbm, i, i % 2).wait()
        context = jnp.concatenate([ctx_a[rows(i), :], ctx_b[rows(i), :]], axis=1)
        xhat, rate = norm_stats(dot(context, w_out[...]) + shifts[0:1, :] + rows_in[i % 2])
        xhat_one[rows(i), :] = xhat
        rate_one[rows(i), :] = rate
        mid_low[rows(i), :] = (xhat * gains[0:1, :] + shifts[1:2, :]).astype(LOW)
        acc[rows(i), :] = jnp.zeros((RB, width), F32)
    fetch(teacher_hbm, 0, 0).start()
    for p in range(4):
        bias_rows(p).wait()
        part = bias_parts[p, 0:3, :].astype(F32)
        bias_in[p] = part[0:1] + part[1:2] + part[2:3]

    def up(p, carry):
        for bit in range(min(dp_bits, 4)):
            pl.when(p == bit)(functools.partial(count_on, bit))

        @pl.when(p == 1)
        def _():
            far[1].wait_recv()
            far[7].start()
            far[5].start()
            far[3].wait_recv()
            far[4].start()

        @pl.when(p == 2)
        def _():
            far[2].wait_recv()
            far[7].wait_recv()
            far[6].start()
            ffn_weights(2)

        @pl.when(p == 3)
        def _():
            for n in (8, 4, 5, 6):
                far[n].wait_recv()
            ffn_weights(3)

        for r in range(2):
            load_in(in_other[0], p, r).wait()
            for c in range(2):
                load_back(back_own, p, r, c).wait()
        last = seq // FR - 1
        strips = [slice(c, c + 256) for c in range(0, units, 256)]

        def lift(k, cols):
            pre = dot(mid_low[pl.ds(k * FR, FR), :], w_in[p, :, cols])
            return pre + bias_in[p, :, cols]

        def lower(k, acts, cols):
            acc[pl.ds(k * FR, FR), cols] += dot(acts, w_back[p, :, cols])

        pre, before = [lift(0, cols) for cols in strips], None
        for k in range(last + 1):
            later, acts = [], []
            for c, cols in enumerate(strips):
                if k < last:
                    later.append(lift(k + 1, cols))
                act, der = gelu_parts(pre[c])
                acts.append(act.astype(LOW))
                hidden[p, pl.ds(k * FR, FR), cols] = acts[c]
                slope[p, pl.ds(k * FR, FR), cols] = der
                if k > 0:
                    lower(k - 1, before, cols)
            pre, before = later, jnp.concatenate(acts, axis=1)
        for cols in strips:
            lower(last, before, cols)
        return carry

    lax.fori_loop(0, 4, up, 0)
    for bit in range(4, dp_bits):
        count_on(bit)
    count_ref[...] = held[2 * dp_bits]

    zero = jnp.zeros((1, width), F32)
    scale = total_slots / held[2 * dp_bits, 0:1, 0:1].astype(F32)
    valid = lengths_ref[lax.axis_index("tensor")]

    def norm_two(i, totals):
        squares, gain_two, shift_two, shift_mid = totals

        @pl.when(i + 1 < blocks)
        def _():
            fetch(teacher_hbm, i + 1, (i + 1) & 1).start()

        fetch(teacher_hbm, i, i & 1).wait()
        mid = xhat_one[rows(i), :] * gains[0:1, :] + shifts[1:2, :]
        xhat, rate = norm_stats(acc[rows(i), :] + shifts[2:3, :] + mid)
        output = xhat * gains[1:2, :] + shifts[3:4, :]

        @pl.when(i >= 2)
        def _():
            keep_rows(i, out_hbm).wait()

        rows_out[i & 1] = output
        keep_rows(i, out_hbm).start()
        live = (i * RB + lax.broadcasted_iota(jnp.int32, (RB, 1), 0)) < valid
        distance = jnp.where(live, output - rows_in[i & 1], 0.0)
        out_grad = scale * distance
        dh_two = norm_back(out_grad, gains[1:2, :], xhat, rate)
        acc[rows(i), :] = dh_two
        dh_low[rows(i), :] = dh_two.astype(LOW)
        return (
            squares + column_sum(distance * distance),
            gain_two + column_sum(out_grad * xhat),
            shift_two + column_sum(out_grad),
            shift_mid + column_sum(dh_two),
        )

    squares, gain_two, shift_two, shift_mid = lax.fori_loop(
        0, blocks, norm_two, (zero, zero, zero, zero)
    )
    for i in range(blocks - 2, blocks):
        keep_rows(i, out_hbm).wait()

    sides = (pl.ds(0, side), pl.ds(side, side))

    def ffn_back(p):
        total = jnp.zeros((1, units), F32)

        def lift(k):
            return dot(dh_low[pl.ds(k * BR, BR), :], w_back[p], NT)

        def lower(k):
            at = pl.ds(k * BR, BR)
            acc[at, :] += dot(pre_grad[at, :], w_in[p], NT)

        raised = lift(0)
        for k in range(seq // BR):
            later = lift(k + 1) if k + 1 < seq // BR else None
            at = pl.ds(k * BR, BR)
            grad = (raised * slope[p, at, :]).astype(LOW)
            pre_grad[at, :] = grad
            total += column_sum(grad.astype(F32))
            if k > 0:
                lower(k - 1)
            raised = later
        lower(seq // BR - 1)
        bias_sums[pl.ds(p, 1), :] = total

    def to_core(pair, w):
        return pltpu.make_async_remote_copy(
            src_ref=stage16.at[w],
            dst_ref=core_hbm.at[pair, w],
            send_sem=send_sem.at[w],
            recv_sem=recv_sem.at[pair, w],
            device_id=core_at,
            device_id_type=pl.DeviceIdType.MESH,
        )

    def away(n, carry):
        p = 2 * n + 1
        ffn_back(p)

        @pl.when(n > 0)
        def _():
            for w in range(2):
                to_core(0, w).wait_send()

        stage16[0] = dot(mid_low[...], pre_grad[...], TN).astype(LOW)
        stage16[1] = dot(hidden[p], dh_low[...], TN).astype(LOW)
        for w in range(2):
            to_core(n, w).start()
        return carry

    lax.fori_loop(0, 2, away, 0)

    def in_moves(pair):
        return [
            pltpu.make_async_copy(stage32.at[0, :, sides[0]], rest.at[pair], store_sem.at[0]),
            pltpu.make_async_copy(stage16.at[0, :, sides[1]], to_x.at[pair], store_sem.at[1]),
        ]

    def back_moves(stage, target):
        return [
            pltpu.make_async_copy(
                stage.at[1, sides[r], sides[c]],
                target.at[r, sides[c], :],
                store_sem.at[2 + 2 * r + c],
            )
            for r in range(2)
            for c in range(2)
        ]

    moves = {1: in_moves(1) + back_moves(stage16, to_y), 0: in_moves(0) + back_moves(stage32, rest.at[pl.ds(2, 2)])}

    def home(n, carry):
        pair = n
        p = 2 * pair
        ffn_back(p)
        for w in range(2):
            to_core(pair, w).wait_recv()
            pltpu.make_async_copy(core_hbm.at[pair, w], from_core.at[w], load_sem.at[w]).start()

        @pl.when(n == 0)
        def _():
            for w in range(2):
                to_core(1, w).wait_send()

        @pl.when(n == 1)
        def _():
            for copy in moves[0]:
                copy.wait()

        stage32[0] = dot(mid_low[...], pre_grad[...], TN)
        stage32[1] = dot(hidden[p], dh_low[...], TN)
        for w in range(2):
            pltpu.make_async_copy(core_hbm.at[pair, w], from_core.at[w], load_sem.at[w]).wait()
            for k in range(0, width, 128):
                total = stage32[w, k : k + 128, :] + from_core[w, k : k + 128, :].astype(F32)
                stage32[w, k : k + 128, :] = total
                stage16[w, k : k + 128, :] = total.astype(LOW)

        for turn in range(2):

            @pl.when(n == turn)
            def _(turn=turn):
                for copy in moves[turn]:
                    copy.start()

        return carry

    lax.fori_loop(0, 2, home, 0)

    def norm_one(i, totals):
        gain_one, shift_one, shift_out = totals
        grad, xhat = acc[rows(i), :], xhat_one[rows(i), :]
        dh_one = norm_back(grad, gains[0:1, :], xhat, rate_one[rows(i), :])

        @pl.when(i >= 2)
        def _():
            keep_rows(i, dh_hbm).wait()

        rows_out[i & 1] = dh_one
        keep_rows(i, dh_hbm).start()
        dh_one_low = dh_one.astype(LOW)
        dh_low[rows(i), :] = dh_one_low
        context_grad = dot(dh_one_low, w_out[...], NT).astype(LOW)
        cg_a[rows(i), :] = context_grad[:, :half]
        cg_b[rows(i), :] = context_grad[:, half:]
        return (
            gain_one + column_sum(grad * xhat),
            shift_one + column_sum(grad),
            shift_out + column_sum(dh_one),
        )

    gain_one, shift_one, shift_out = lax.fori_loop(0, blocks, norm_one, (zero, zero, zero))
    for context, out_keep, out_send in (
        (ctx_a, out_keep_a, out_send_a),
        (ctx_b, out_keep_b, out_send_b),
    ):
        grad = dot(context[...], dh_low[...], TN)
        out_keep[...] = grad[:out_rows]
        out_send[...] = grad[out_rows:].astype(LOW)
    sums[...] = jnp.concatenate(
        [gain_one, gain_two, shift_out, shift_one, shift_mid, shift_two, squares, zero], axis=0
    )
    for i in range(blocks - 2, blocks):
        keep_rows(i, dh_hbm).wait()
    for copy in moves[1]:
        copy.wait()
    for copy in far:
        copy.wait_send()


def middle(
    total_slots, lengths, ctx_a, ctx_b, gains, shifts, x, teacher, near, out_in, back, second
):
    seq, width = x.shape
    half = width // 2
    out_rows = ctx_a.shape[1] // 2
    units = width
    dp_bits = bits_of("dp")
    slab = (width, units // 2)
    return pl.pallas_call(
        functools.partial(middle_kernel, float(total_slots), dp_bits),
        out_shape=(
            shape((seq, width), F32),
            shape((seq, width), F32),
            shape((seq, half), LOW),
            shape((seq, half), LOW),
            shape((2, 2, width, units), LOW),
            shape((2,) + slab, LOW),
            shape((2,) + slab, LOW),
            shape((4,) + slab, F32),
            shape((out_rows, width), LOW),
            shape((out_rows, width), LOW),
            shape((out_rows, width), F32),
            shape((out_rows, width), F32),
            shape((8, width), F32),
            shape((4, units), F32),
            shape((8, 128), jnp.int32),
            shape(out_in[0].shape, LOW),
            shape(slab, LOW),
            shape((2,) + slab, LOW),
            shape(slab, LOW),
            shape((2,) + slab, LOW),
        ),
        in_specs=[SMEM, VMEM, VMEM, VMEM, VMEM, HBM, HBM] + [HBM] * 11,
        out_specs=(HBM, HBM, VMEM, VMEM, HBM, HBM, HBM, HBM) + (VMEM,) * 7 + (HBM,) * 5,
        scratch_shapes=[
            pltpu.VMEM((4, width, units), LOW),
            pltpu.VMEM((4, units, width), LOW),
            pltpu.VMEM((4 * out_rows, width), LOW),
            pltpu.VMEM((4, 16, width), LOW),
            pltpu.VMEM((4, 1, units), F32),
            pltpu.VMEM((seq, width), F32),
            pltpu.VMEM((seq, 1), F32),
            pltpu.VMEM((seq, width), LOW),
            pltpu.VMEM((4, seq, units), LOW),
            pltpu.VMEM((4, seq, units), F32),
            pltpu.VMEM((seq, width), F32),
            pltpu.VMEM((seq, width), LOW),
            pltpu.VMEM((seq, units), LOW),
            pltpu.VMEM((2, RB, width), F32),
            pltpu.VMEM((2, RB, width), F32),
            pltpu.VMEM((2, width, units), LOW),
            pltpu.VMEM((2, width, units), F32),
            pltpu.VMEM((2, width, units), LOW),
            pltpu.VMEM((2 * dp_bits + 1, 8, 128), jnp.int32),
            pltpu.SemaphoreType.DMA((4, 9)),
            pltpu.SemaphoreType.DMA((2,)),
            pltpu.SemaphoreType.DMA((2,)),
            pltpu.SemaphoreType.DMA((2,)),
            pltpu.SemaphoreType.DMA((6,)),
            pltpu.SemaphoreType.DMA((2,)),
            pltpu.SemaphoreType.DMA((2, 2)),
            pltpu.SemaphoreType.DMA((dp_bits,)),
            pltpu.SemaphoreType.DMA((dp_bits,)),
            pltpu.SemaphoreType.DMA((9,)),
            pltpu.SemaphoreType.DMA((9,)),
        ],
        compiler_params=pltpu.CompilerParams(
            vmem_limit_bytes=VMEM_LIMIT, collective_id=1, has_side_effects=True
        ),
        cost_estimate=pl.CostEstimate(
            flops=6 * seq * width * (8 * units + width),
            bytes_accessed=30 << 20,
            transcendentals=2 * seq * 4 * units,
        ),
        name="middle",
    )(lengths, ctx_a, ctx_b, gains, shifts, x, teacher, *near, *out_in, *back, *second)


def add_rows(out, terms, chunk=96):
    rows = out.shape[0]
    chunk = min(chunk, rows)

    def step(i, carry):
        at = pl.ds(pl.multiple_of(i * chunk, chunk), chunk)
        total = terms[0][at, :].astype(F32)
        for term in terms[1:]:
            total += term[at, :].astype(F32)
        out[at, :] = total.astype(out.dtype)
        return carry

    lax.fori_loop(0, rows // chunk, step, 0)


def cross_rows(x_ref, grads, okeep, osend, side, cross, keep, send, bias_ref, emit, between=None):
    half = x_ref.shape[1] // 2
    piece = grads[0].shape[1] // 2
    mine = pl.ds(pl.multiple_of(side * half, half), half)
    other = pl.ds(pl.multiple_of((1 - side) * half, half), half)
    sides = ((1, other), (0, mine))
    at = pl.ds(3 * piece, osend.shape[0])
    for n, lanes in sides:
        keep[n, at, :] = okeep[:, lanes]
        send[n, at, :] = osend[:, lanes].astype(send.dtype)
        emit(n, at)
    for i in range(3):
        cross[...] = dot(grads[i][...], x_ref[...], TN)
        at = pl.ds(i * piece, piece)
        for n, lanes in sides:
            keep[n, at, :] = cross[:piece, lanes]
            send[n, at, :] = cross[piece:, lanes].astype(send.dtype)
            emit(n, at)
        bias_ref[i : i + 1, :] = column_sum(grads[i][...].astype(F32))
        if i == 0 and between is not None:
            between()


def far_kernel(
    x_ref,
    dq,
    dk,
    dv,
    osend,
    okeep,
    away,
    away_first,
    bias_ref,
    keep,
    send,
    core,
    cross,
    send_sem,
    recv_sem,
):
    core_at = partner("tensor", 0)
    greet([core_at])
    bias_ref[...] = jnp.zeros(bias_ref.shape, F32)
    copies = []

    def emit(n, rows):
        at = len(copies)
        copies.append(
            pltpu.make_async_remote_copy(
                src_ref=send.at[n, rows, :],
                dst_ref=core.at[n, rows, :],
                send_sem=send_sem.at[at],
                recv_sem=recv_sem.at[at],
                device_id=core_at,
                device_id_type=pl.DeviceIdType.MESH,
            )
        )
        copies[at].start()

    side = lax.axis_index("dp") & 1
    cross_rows(x_ref, (dq, dk, dv), okeep, osend, side, cross, keep, send, bias_ref, emit)
    for n, out in ((1, away_first), (0, away)):
        for copy in copies[1 - n :: 2]:
            copy.wait_recv()
        add_rows(out, [keep.at[n], core.at[n]])
    for copy in copies:
        copy.wait_send()


def far_projections(x, grads, osend, okeep):
    seq, width = x.shape
    half = width // 2
    piece = grads[0].shape[1] // 2
    slabs = (2, width, half)
    return pl.pallas_call(
        far_kernel,
        out_shape=(shape(slabs[1:], LOW), shape(slabs[1:], LOW), shape((8, 2 * piece), F32)),
        in_specs=[VMEM] * 6,
        out_specs=(VMEM, VMEM, VMEM),
        scratch_shapes=[
            pltpu.VMEM(slabs, F32),
            pltpu.VMEM(slabs, F32),
            pltpu.VMEM(slabs, F32),
            pltpu.VMEM((2 * piece, width), F32),
            pltpu.SemaphoreType.DMA((8,)),
            pltpu.SemaphoreType.DMA((8,)),
        ],
        compiler_params=pltpu.CompilerParams(
            vmem_limit_bytes=VMEM_LIMIT, collective_id=3, has_side_effects=True
        ),
        cost_estimate=pl.CostEstimate(
            flops=12 * seq * width * piece, bytes_accessed=10 << 20, transcendentals=0
        ),
        name="far_projections",
    )(x, *grads, osend, okeep)


def finish_kernel(
    dp_bits,
    x_hbm,
    w0_hbm,
    w1_hbm,
    w2_hbm,
    w3_hbm,
    dqa_hbm,
    dka_hbm,
    dva_hbm,
    dqb_hbm,
    dkb_hbm,
    dvb_hbm,
    osend,
    okeep,
    dh_hbm,
    rest,
    ffn_x,
    ffn_y,
    in_z,
    back_x,
    away,
    qkv_y,
    sums_ref,
    bias_in_ref,
    bias_far,
    gx_hbm,
    result,
    small_out,
    x_ref,
    w0,
    w1,
    w2,
    w3,
    dqa,
    dka,
    dva,
    dqb,
    dkb,
    dvb,
    own,
    own16,
    in_send,
    in_recv,
    keep,
    send,
    core,
    y_recv,
    x_send,
    x_recv,
    total,
    z_send,
    z_recv,
    last_send,
    last_recv,
    extra,
    bias_ref,
    small_held,
    rows_in,
    rows_out,
    cross,
    operand_sem,
    load_sem,
    send_sem,
    recv_sem,
    in_sem,
    out_sem,
):
    seq, width = x_ref.shape
    half = width // 2
    piece = dqa.shape[1] // 2
    blocks = seq // RB
    place = lax.axis_index("dp")
    index = lax.axis_index("tensor")
    side = place & 1
    core_at, y_at = partner("tensor", 0), partner("tensor", 1)
    dp_at = [partner("dp", bit) for bit in range(dp_bits)]
    greet([core_at, y_at] + dp_at)
    started = {}

    def remote(key, source, target, device):
        n = len(started)
        started[key] = pltpu.make_async_remote_copy(
            src_ref=source,
            dst_ref=target,
            send_sem=send_sem.at[n],
            recv_sem=recv_sem.at[n],
            device_id=device,
            device_id_type=pl.DeviceIdType.MESH,
        )
        started[key].start()

    def arrive(key):
        started[key].wait_recv()

    part = width // 4
    half_bit, part_bit = (place >> 1) & 1, (place >> 2) & 1

    def quarter(i, j):
        at = (half_bit ^ i) * (2 * part) + (part_bit ^ j) * part
        return pl.ds(pl.multiple_of(at, part), part)

    def two_quarters(i):
        return pl.ds(pl.multiple_of((half_bit ^ i) * (2 * part), 2 * part), 2 * part)

    for i in (1, 0):
        rows = two_quarters(i)
        remote(("y", 0, i), away.at[rows, :], y_recv.at[0, rows, :], y_at)
    mine = two_quarters(0)
    loads = [[], []]

    def load(w, source, target):
        loads[w].append(pltpu.make_async_copy(source, target, load_sem.at[w, len(loads[w])]))
        loads[w][-1].start()

    load(1, rest.at[2], own.at[1])
    load(1, ffn_y.at[0], own16.at[1, 0])
    load(1, back_x, own16.at[1, 1])
    for pair in range(2):
        at = pl.ds(pair * 2 * part, 2 * part)
        load(0, rest.at[pair, mine, :], own.at[0, at, :])
        load(0, ffn_x.at[pair, mine, :], own16.at[0, 0, at, :])
        load(0, in_z.at[pair], own16.at[0, 1, at, :])
    load(1, qkv_y, y_recv.at[1])
    operands = [
        pltpu.make_async_copy(source, target, operand_sem.at[n])
        for n, (source, target) in enumerate(
            (
                (dqa_hbm, dqa),
                (x_hbm, x_ref),
                (dka_hbm, dka),
                (dva_hbm, dva),
                (dqb_hbm, dqb),
                (dkb_hbm, dkb),
                (dvb_hbm, dvb),
                (w0_hbm, w0),
                (w1_hbm, w1),
                (w2_hbm, w2),
                (w3_hbm, w3),
            )
        )
    ]
    for copy in operands:
        copy.start()

    def fetch(i):
        return pltpu.make_async_copy(
            dh_hbm.at[pl.ds(i * RB, RB), :], rows_in.at[i % 2], in_sem.at[i % 2]
        )

    fetch(0).start()

    def scatter(w):
        for j in (1, 0):
            at = pl.ds((1 - j) * part, part)
            add_rows(z_send.at[w, at, :], [total.at[w, quarter(1, j), :]])
            remote((w, "z", j), z_send.at[w, at, :], z_recv.at[w, at, :], dp_at[1])

    def in_part(j):
        return in_recv.at[pl.ds(pl.multiple_of((part_bit ^ j) * part, part), part), :]

    def scatter_on(w):
        rows = quarter(0, 1)
        arrive("in y" if w == 0 else (w, "z", 1))
        came = in_part(1) if w == 0 else z_recv.at[w, pl.ds(0, part), :]
        add_rows(last_send.at[w], [total.at[w, rows, :], came])
        remote((w, "last"), last_send.at[w], last_recv.at[w], dp_at[2])

    def spread(w, i, j):
        rows = result.at[w, 0, quarter(i, j), :]
        if (i, j) == (0, 0):
            remote((w, "gather", 0, 1), rows, rows, dp_at[2])
        if i == 0:
            remote((w, "gather", 1, j), rows, rows, dp_at[1])
        remote((w, "across", i, j), rows, result.at[w, 1, quarter(i, j), :], dp_at[0])

    def settle(w):
        rows = quarter(0, 0)
        own_part = result.at[w, 0, rows, :]
        if w > 0:
            arrive((w, "z", 0))
        arrive((w, "last"))
        came = in_part(0) if w == 0 else z_recv.at[w, pl.ds(part, part), :]
        terms = [total.at[w, rows, :], came, last_recv.at[w]]
        add_rows(own_part, terms)
        for bit in range(3, dp_bits):
            into = extra.at[w, bit - 3]
            remote((w, "all", bit), own_part, into, dp_at[bit])
            started[(w, "all", bit)].wait_send()
            arrive((w, "all", bit))
            add_rows(own_part, [own_part, into])
        spread(w, 0, 0)

    def gather(w, i, j):
        arrive((w, "gather", i, j))
        spread(w, i, j)

    for copy in loads[1]:
        copy.wait()
    add_rows(total.at[1], [own.at[1], own16.at[1, 0], own16.at[1, 1]])
    scatter(1)
    for copy in loads[0]:
        copy.wait()
    for pair, out in ((1, in_send), (0, total.at[0, mine, :])):
        at = pl.ds(pair * 2 * part, 2 * part)
        add_rows(out, [own.at[0, at, :], own16.at[0, 0, at, :], own16.at[0, 1, at, :]])
    remote("in y", in_send, in_recv, y_at)
    for copy in operands[:4]:
        copy.wait()

    near_parts = ([], [])

    def emit(n, rows):
        near_parts[n].append(("core", n, len(near_parts[n])))
        remote(near_parts[n][-1], send.at[n, rows, :], core.at[n, rows, :], core_at)

    near_grads = (dqa, dka, dva)
    cross_rows(
        x_ref,
        near_grads,
        okeep,
        osend,
        side,
        cross,
        keep,
        send,
        bias_ref,
        emit,
    )
    for copy in operands[4:]:
        copy.wait()

    small_held[0] = jnp.zeros(small_held.shape[1:], F32)
    small_held[0, 16:24, :] = sums_ref[...]
    for p in range(4):
        row = 4 * (index ^ p)
        half_mine = bias_in_ref[p : p + 1, :half]
        half_other = bias_in_ref[p : p + 1, half:]
        low_half = jnp.where(side == 0, half_mine, half_other)
        high_half = jnp.where(side == 0, half_other, half_mine)
        small_held[0, pl.ds(row, 1), :] = jnp.concatenate([low_half, high_half], axis=1)
        for i, k in enumerate((0, 2)):
            values = (bias_ref, bias_far)[p // 2][k : k + 1, :]
            if p % 2 == 1:
                values = pltpu.roll(values, piece, 1)
            small_held[0, pl.ds(row + 1 + i, 1), :half] = values

    def small_step(n):
        bits = [core_at, y_at] + dp_at
        remote(("small", n), small_held.at[2 * n], small_held.at[2 * n + 1], bits[n])

    def small_sum(n):
        arrive(("small", n))
        out = small_held.at[2 * n + 2] if n < dp_bits + 1 else small_out
        out[...] = small_held[2 * n] + small_held[2 * n + 1]

    weights = ((w0, w1), (w2, w3))
    grads = ((dqa, dka, dva), (dqb, dkb, dvb))
    stores = []

    def inputs_rows(b):
        at = pl.ds(b * RB, RB)
        if b + 1 < blocks:
            fetch(b + 1).start()
        fetch(b).wait()
        grad = rows_in[b % 2]
        for g in range(2):
            for i in range(3):
                rows = slice(i * piece, (i + 1) * piece)
                w = jnp.concatenate([ref[rows, :] for ref in weights[g]], axis=0)
                grad += dot(grads[g][i][at, :], w)
        if b >= 2:
            stores[b - 2].wait()
        rows_out[b % 2] = grad
        stores.append(
            pltpu.make_async_copy(rows_out.at[b % 2], gx_hbm.at[at, :], out_sem.at[b % 2])
        )
        stores[b].start()

    def send_across(i):
        rows = two_quarters(i)
        at = pl.ds((1 - i) * 2 * part, 2 * part)
        add_rows(x_send.at[at, :], [keep.at[1, rows, :], core.at[1, rows, :], y_recv.at[1, rows, :]])
        remote(("across", i), x_send.at[at, :], x_recv.at[at, :], dp_at[0])

    def take_across(i):
        rows = two_quarters(i)
        at = pl.ds((1 - i) * 2 * part, 2 * part)
        arrive(("y", 0, i))
        arrive(("across", i))
        add_rows(
            total.at[2, rows, :],
            [keep.at[0, rows, :], core.at[0, rows, :], y_recv.at[0, rows, :], x_recv.at[at, :]],
        )

    small_step(0)
    for key in near_parts[1]:
        arrive(key)
    send_across(1)
    send_across(0)
    scatter_on(1)
    inputs_rows(0)
    settle(1)
    small_sum(0)
    small_step(1)
    for key in near_parts[0]:
        arrive(key)
    take_across(1)
    scatter(2)
    scatter_on(0)
    inputs_rows(1)
    gather(1, 0, 1)
    small_sum(1)
    small_step(2)
    take_across(0)
    scatter_on(2)
    gather(1, 1, 0)
    settle(0)
    inputs_rows(2)
    gather(1, 1, 1)
    small_sum(2)
    small_step(3)
    gather(0, 0, 1)
    settle(2)
    gather(0, 1, 0)
    inputs_rows(3)
    gather(0, 1, 1)
    small_sum(3)
    small_step(4)
    gather(2, 0, 1)
    gather(2, 1, 0)
    for n in range(4, dp_bits + 2):
        small_sum(n)
        if n + 1 < dp_bits + 2:
            small_step(n + 1)
    gather(2, 1, 1)
    for w in range(3):
        for i in range(2):
            for j in range(2):
                arrive((w, "across", i, j))
    for key, copy in started.items():
        if not (isinstance(key, tuple) and key[1] == "all"):
            copy.wait_send()
    for store in stores[-2:]:
        store.wait()


def finish(
    x, weights, grads, osend, okeep, dh, rest, ffn_x, ffn_y, in_z, back_x, away, qkv_y, sums, bias_in, bias_far
):
    seq, width = x.shape
    half = width // 2
    piece = grads[0].shape[1] // 2
    dp_bits = bits_of("dp")
    slab = (width, half)
    copies = 14 + dp_bits + 2 + 3 * (10 + max(dp_bits - 3, 0))
    assert dp_bits >= 3
    return pl.pallas_call(
        functools.partial(finish_kernel, dp_bits),
        out_shape=(
            shape((seq, width), F32),
            shape((3, 2) + slab, LOW),
            shape((24, width), F32),
        ),
        in_specs=[HBM] * 11 + [VMEM] * 2 + [HBM] * 8 + [VMEM] * 3,
        out_specs=(HBM, VMEM, VMEM),
        scratch_shapes=[pltpu.VMEM(a.shape, LOW) for a in (x, *weights, *grads)]
        + [
            pltpu.VMEM((2,) + slab, F32),
            pltpu.VMEM((2, 2) + slab, LOW),
            pltpu.VMEM((width // 2, half), LOW),
            pltpu.VMEM((width // 2, half), LOW),
            pltpu.VMEM((2,) + slab, F32),
            pltpu.VMEM((2,) + slab, F32),
            pltpu.VMEM((2,) + slab, F32),
            pltpu.VMEM((2,) + slab, LOW),
            pltpu.VMEM(slab, LOW),
            pltpu.VMEM(slab, LOW),
            pltpu.VMEM((3,) + slab, F32),
            pltpu.VMEM((3, width // 2, half), LOW),
            pltpu.VMEM((3, width // 2, half), LOW),
            pltpu.VMEM((3, width // 4, half), LOW),
            pltpu.VMEM((3, width // 4, half), LOW),
            pltpu.VMEM((3, max(dp_bits - 3, 1), width // 4, half), LOW),
            pltpu.VMEM((8, 2 * piece), F32),
            pltpu.VMEM((2 * dp_bits + 4, 24, width), F32),
            pltpu.VMEM((2, RB, width), F32),
            pltpu.VMEM((2, RB, width), F32),
            pltpu.VMEM((2 * piece, width), F32),
            pltpu.SemaphoreType.DMA((11,)),
            pltpu.SemaphoreType.DMA((2, 6)),
            pltpu.SemaphoreType.DMA((copies,)),
            pltpu.SemaphoreType.DMA((copies,)),
            pltpu.SemaphoreType.DMA((2,)),
            pltpu.SemaphoreType.DMA((2,)),
        ],
        compiler_params=pltpu.CompilerParams(
            vmem_limit_bytes=VMEM_LIMIT, collective_id=2, has_side_effects=True
        ),
        cost_estimate=pl.CostEstimate(
            flops=36 * seq * width * piece, bytes_accessed=50 << 20, transcendentals=0
        ),
        name="finish",
    )(x, *weights, *grads, osend, okeep, dh, rest, ffn_x, ffn_y, in_z, back_x, away, qkv_y, sums, bias_in, bias_far)


def widen_kernel(
    small,
    count,
    result,
    source,
    loss_ref,
    bqv_ref,
    bin_ref,
    gains_ref,
    shifts_ref,
    qkv_hbm,
    out_hbm,
    in_hbm,
    back_hbm,
    target,
    slabs,
    rows_held,
    qkv_ref,
    out_ref,
    in_ref,
    back_ref,
    in_sem,
    row_sem,
    out_sem,
):
    half = slabs.shape[3]
    piece = qkv_ref.shape[1]
    side = lax.axis_index("dp") & 1
    slab_loads = [
        pltpu.make_async_copy(result.at[w], slabs.at[w], in_sem.at[w]) for w in range(3)
    ]
    blocks = source.shape[0] // RB

    def rows(i, out):
        at = pl.ds(i * RB, RB)
        ends = (rows_held.at[i], target.at[at, :]) if out else (source.at[at, :], rows_held.at[i])
        return pltpu.make_async_copy(*ends, row_sem.at[i, out])

    slab_loads[0].start()
    slab_loads[1].start()
    for i in range(blocks):
        rows(i, 0).start()
    slab_loads[2].start()
    stores = []

    def store(value, to):
        stores.append(pltpu.make_async_copy(value, to, out_sem.at[len(stores)]))
        stores[-1].start()

    sides = [
        pl.ds(pl.multiple_of(natural * half, half), half) for natural in (side, 1 - side)
    ]
    slab_loads[0].wait()
    for n in range(2):
        in_ref[:, sides[n]] = slabs[0, n].astype(F32)
    store(in_ref, in_hbm)
    slab_loads[1].wait()
    for n in range(2):
        for c in range(2):
            strip = slabs[1, n, c * half : (c + 1) * half, :]
            back_ref[sides[n], c * half : (c + 1) * half] = strip.astype(F32)
    store(back_ref, back_hbm)
    for i in range(blocks):
        rows(i, 0).wait()
        rows(i, 1).start()
    slab_loads[2].wait()
    for n in range(2):
        for i in range(3):
            qkv_ref[i, :, sides[n]] = slabs[2, n, i * piece : (i + 1) * piece, :].astype(F32)
        out_ref[:, sides[n]] = slabs[2, n, 3 * piece :, :].astype(F32)
    store(qkv_ref, qkv_hbm)
    store(out_ref, out_hbm)
    row = 4 * lax.axis_index("tensor")
    bin_ref[...] = small[pl.ds(row, 1), :].reshape(bin_ref.shape)
    for i in range(2):
        bqv_ref[i : i + 1, :] = small[pl.ds(row + 1 + i, 1), :piece]
    gains_ref[...] = small[16:18, :]
    shifts_ref[...] = small[18:22, :]
    tokens = count[0:1, 0:1].astype(F32)
    total = jnp.sum(small[22:23, :], axis=1, keepdims=True)
    loss_ref[...] = total / (2.0 * small.shape[1] * tokens)
    for i in range(blocks):
        rows(i, 1).wait()
    for copy in stores:
        copy.wait()


def widen(result, small, count, inputs_grad, piece, out_rows):
    width, half = result.shape[2:]
    seq = inputs_grad.shape[0]
    large = ((3, piece, width), (out_rows, width), (width, 2 * half), (2 * half, width))
    return pl.pallas_call(
        widen_kernel,
        out_shape=(
            shape((1, 1), F32),
            shape((2, piece), F32),
            shape((2 * half,), F32),
            shape((2, width), F32),
            shape((4, width), F32),
        )
        + tuple(shape(dims, F32) for dims in large)
        + (shape(inputs_grad.shape, F32),),
        in_specs=[VMEM, VMEM, HBM, HBM],
        out_specs=(VMEM,) * 5 + (HBM,) * 5,
        scratch_shapes=[
            pltpu.VMEM(result.shape, LOW),
            pltpu.VMEM((seq // RB, RB, width), F32),
        ]
        + [pltpu.VMEM(dims, F32) for dims in large]
        + [
            pltpu.SemaphoreType.DMA((3,)),
            pltpu.SemaphoreType.DMA((seq // RB, 2)),
            pltpu.SemaphoreType.DMA((4,)),
        ],
        compiler_params=pltpu.CompilerParams(vmem_limit_bytes=VMEM_LIMIT),
        name="widen",
    )(small, count, result, inputs_grad)


def per_device(
    inputs,
    w_qkv,
    b_qv,
    w_out,
    w_in,
    b_in,
    w_back,
    norm_gains,
    shifts,
    segment_ids,
    valid_lengths,
    teacher,
):
    own_seqs, seq, width = inputs.shape
    assert own_seqs == 1 and lax.axis_size("tensor") == 4
    total_slots = seq * lax.axis_size("tensor") * lax.axis_size("dp")
    half = width // 2
    piece = w_qkv.shape[2]
    units = w_in.shape[1]
    x = inputs.reshape(seq, width)

    near, table, code, seg = round_qkv(
        valid_lengths, segment_ids, w_qkv.transpose(0, 2, 1), b_qv, b_in
    )
    core = swap(near, "tensor", 0)
    far = swap(near, "tensor", 1)
    core, w_in, w_back, w_out = lax.optimization_barrier((core, w_in, w_back, w_out))
    out_in, back, second, x_low = round_rest(w_out, w_in, w_back, x)
    out_in_far = swap(out_in, "tensor", 1)

    qa, ka, va, ctx_a, lse_a = attend_forward(table, x_low, near, core, code, seg)
    out_in, back, second, far, ctx_a = lax.optimization_barrier((out_in, back, second, far, ctx_a))
    core_far = swap(far, "tensor", 0)
    out_in_core = swap(out_in, "tensor", 0)
    back_core = swap(back, "tensor", 0)
    second_core = swap(second, "tensor", 0)
    qb, kb, vb, ctx_b, lse_b = attend_forward(table, x_low, far, core_far, code, seg)
    (
        output,
        dh_one,
        cg_a,
        cg_b,
        _,
        to_x,
        to_y,
        rest,
        out_send_a,
        out_send_b,
        out_keep_a,
        out_keep_b,
        sums,
        bias_sums,
        count,
        *_,
    ) = middle(
        total_slots,
        valid_lengths,
        ctx_a,
        ctx_b,
        norm_gains,
        shifts,
        x,
        teacher.reshape(seq, width),
        (near, core, far, core_far),
        (out_in, out_in_core, out_in_far),
        (back, back_core),
        (second, second_core),
    )
    ffn_x = swap(to_x, "dp", 0)
    ffn_y = swap(to_y, "tensor", 1)
    grads_b = attend_backward(table, qb, kb, vb, cg_b, lse_b, code, seg)
    away, away_first, bias_far = far_projections(x_low, grads_b, out_send_b, out_keep_b)
    ffn_x, ffn_y, away_first = lax.optimization_barrier((ffn_x, ffn_y, away_first))
    half_other = 1 - ((lax.axis_index("dp") >> 1) & 1)
    in_away = (
        lax.dynamic_slice(rest, (0, half_other * half, 0), (2, half, half))
        + lax.dynamic_slice_in_dim(ffn_x, half_other * half, half, 1).astype(F32)
    ).astype(LOW)
    back_away = (rest[3] + ffn_y[1].astype(F32)).astype(LOW)
    in_away, back_away, away_first, cg_a = lax.optimization_barrier(
        (in_away, back_away, away_first, cg_a)
    )
    in_z = swap(in_away, "dp", 1)
    qkv_y = swap(away_first, "tensor", 1)
    back_x = swap(back_away, "dp", 0)
    *grads_a, output = attend_backward(table, qa, ka, va, cg_a, lse_a, code, seg, output)
    grad_inputs, slabs, small = finish(
        x_low,
        (near, core, far, core_far),
        (*grads_a, *grads_b),
        out_send_a,
        out_keep_a,
        dh_one,
        rest,
        ffn_x,
        ffn_y,
        in_z,
        back_x,
        away,
        qkv_y,
        sums,
        bias_sums,
        bias_far,
    )
    (
        loss,
        grad_b_qv,
        grad_b_in,
        grad_gains,
        grad_shifts,
        grad_w_qkv,
        grad_w_out,
        grad_w_in,
        grad_w_back,
        grad_inputs,
    ) = widen(slabs, small, count, grad_inputs, piece, w_out.shape[0])
    return (
        output.reshape(own_seqs, seq, width),
        loss[0, 0],
        grad_inputs.reshape(own_seqs, seq, width),
        grad_w_qkv.transpose(0, 2, 1),
        grad_b_qv,
        grad_w_out,
        grad_w_in,
        grad_b_in,
        grad_w_back,
        grad_gains,
        grad_shifts,
    )


def solution(mesh):
    return jax.shard_map(
        per_device,
        mesh=mesh,
        in_specs=(
            P(("dp", "tensor"), None, None),
            P(None, None, "tensor"),
            P(None, "tensor"),
            P("tensor", None),
            P(None, "tensor"),
            P("tensor"),
            P("tensor", None),
            P(),
            P(),
            P("dp", None),
            P("dp"),
            P(("dp", "tensor"), None, None),
        ),
        out_specs=(
            P(("dp", "tensor"), None, None),
            P(),
            P(("dp", "tensor"), None, None),
            P(None, None, "tensor"),
            P(None, "tensor"),
            P("tensor", None),
            P(None, "tensor"),
            P("tensor"),
            P("tensor", None),
            P(),
            P(),
        ),
        check_vma=False,
    )
```
